32 devices in a mesh: batch: 4 (over x, core), blk: 8 (over z, y).
Axes of the slice: x: 2, y: 2, z: 4, core: 2. Of those that a mesh axis runs over, the one named last changes fastest.
Arguments:
- inputs: bfloat16 [8, 1024, 1024], P('batch', 'blk'), may hold values from -6 to 6
- time_embed: bfloat16 [8, 1024], P('batch'), may hold values from -6 to 6
- lengths: int32 [8], P('batch'), may hold values from 64 to 1024, as said below
- cotangent: bfloat16 [8, 1024, 1024], P('batch', 'blk'), may hold values from -6 to 6
- w_mod: bfloat16 [1024, 6144], replicated, may hold values from -0.1875 to 0.1875
- b_mod: bfloat16 [6144], replicated, may hold values from -3 to 3
- w_qkv: bfloat16 [1024, 3072], replicated, may hold values from -0.1875 to 0.1875
- b_qkv: bfloat16 [3072], replicated, may hold values from -2 to 2
- w_out: bfloat16 [1024, 1024], replicated, may hold values from -2 to 2
- b_out: bfloat16 [1024], replicated, may hold values from -2 to 2
- w_up: bfloat16 [1024, 2048], replicated, may hold values from -0.1875 to 0.1875
- b_up: bfloat16 [2048], replicated, may hold values from -3 to 3
- w_down: bfloat16 [2048, 1024], replicated, may hold values from -0.125 to 0.125
- b_down: bfloat16 [1024], replicated, may hold values from -2 to 2
Outputs:
- output: float32 [8, 1024, 1024], P('batch', 'blk')
- grad_inputs: float32 [8, 1024, 1024], P('batch', 'blk')
- grad_time: float32 [8, 1024], P('batch')
- grad_w_mod: float32 [1024, 6144], P('blk')
- grad_b_mod: float32 [6144], P('blk')
- grad_w_qkv: float32 [1024, 3072], P('blk')
- grad_b_qkv: float32 [3072], P('blk')
- grad_w_out: float32 [1024, 1024], P('blk')
- grad_b_out: float32 [1024], P('blk')
- grad_w_up: float32 [1024, 2048], P('blk')
- grad_b_up: float32 [2048], P('blk')
- grad_w_down: float32 [2048, 1024], P('blk')
- grad_b_down: float32 [1024], P('blk')
The draws below stay inside these ranges and needn't reach their ends.
Inputs may be any that keep to these rules, and one draw needn't show every extreme that they name: `lengths`: lengths are counted in mel frames, from 64 to 1024. Among the 2 utterances of each index of batch, one drawn from the seed has exactly 1024 frames and another exactly 64.
All inputs are finite; a program needn't handle non-finite values.
Results may differ from the reference program's by a relative error of at most 0.017.
Values may be sent and summed in bfloat16 or wider, within the bound.
A program may use at most 192 MiB of HBM per device.

```python
import jax
import jax.numpy as jnp
from jax import lax

D = 1024
HEADS = 16
FF = 2048
DH = 64
SEQS = 2
FRAMES = 1024
UTTS = 8


def draw_lengths(key, part):
    groups = UTTS // SEQS
    drawn = jax.random.randint(jax.random.fold_in(key, 11), (UTTS,), FRAMES // 16, FRAMES + 1, dtype=jnp.int32)
    full_slot = jax.random.randint(jax.random.fold_in(key, 12), (groups,), 0, SEQS, dtype=jnp.int32)
    offset = jax.random.randint(jax.random.fold_in(key, 13), (groups,), 1, SEQS, dtype=jnp.int32)
    short_slot = (full_slot + offset) % SEQS
    slot = jnp.arange(UTTS, dtype=jnp.int32) % SEQS
    group_of = jnp.arange(UTTS, dtype=jnp.int32) // SEQS
    full_mark = slot == full_slot[group_of]
    short_mark = slot == short_slot[group_of]
    lengths = jnp.where(full_mark, FRAMES, jnp.where(short_mark, FRAMES // 16, drawn))
    return lengths.astype(jnp.int32)


def block_scale(rng, extent, pieces, low, high):
    level = 1.0
    for position, shards_of in pieces:
        steps = jax.random.uniform(jax.random.fold_in(jax.random.fold_in(rng, 6), position), (shards_of,), jnp.float32, low / len(pieces), high / len(pieces))
        level = level * jnp.repeat(jnp.exp(steps), extent[position] // shards_of).reshape((-1,) + (1,) * (len(extent) - 1 - position))
    return level


def centred(own_key, shape, scale, limit, shards=(), kind=jnp.bfloat16):
    values = jax.random.normal(own_key, shape, jnp.float32) * scale
    if len(shards) > 0:
        values = block_scale(own_key, shape, shards, -0.22, 0.18) * values
    return jnp.clip(values, min=-limit, max=limit).astype(kind)


def setup_inputs(seed: int = 0) -> dict:
    seeds = jax.random.split(jax.random.key(seed), 15)
    return {
        "inputs": centred(seeds[0], (UTTS, FRAMES, D), 1.0, 6.0, ((0, 4), (1, 8))),
        "time_embed": centred(seeds[1], (UTTS, D), 1.0, 6.0, ((0, 4),)),
        "lengths": draw_lengths(jax.random.fold_in(seeds[14], 71), 0),
        "cotangent": centred(seeds[3], (UTTS, FRAMES, D), 1.0, 6.0, ((0, 4), (1, 8))),
        "w_mod": centred(seeds[4], (D, 6 * D), D ** -0.5, 0.1875),
        "b_mod": centred(seeds[5], (6 * D,), 0.5, 3.0),
        "w_qkv": centred(seeds[6], (D, 3 * D), D ** -0.5, 0.1875),
        "b_qkv": centred(seeds[7], (3 * D,), 0.3, 2.0),
        "w_out": centred(seeds[8], (D, D), (max(D // 128, 4)) ** -0.5, 2.0),
        "b_out": centred(seeds[9], (D,), 0.3, 2.0),
        "w_up": centred(seeds[10], (D, FF), D ** -0.5, 0.1875),
        "b_up": centred(seeds[11], (FF,), 0.5, 3.0),
        "w_down": centred(seeds[12], (FF, D), FF ** -0.5, 0.125),
        "b_down": centred(seeds[13], (D,), 0.3, 2.0),
    }


EPS = 1e-06
NEG = -1e+30
HIGH = lax.Precision.HIGHEST

@jax.custom_vjp
def low(v):
    return lax.optimization_barrier(v.astype(jnp.bfloat16)).astype(jnp.float32)

@jax.custom_vjp
def low_back(v):
    return v

def low_keep(v):
    return (low(v), None)

def low_pass(kept, grad):
    return (grad,)

def back_keep(v):
    return (v, None)

def back_low(kept, grad):
    return (low(grad),)
low.defvjp(low_keep, low_pass)
low_back.defvjp(back_keep, back_low)

def matmul(left, right):
    return jnp.dot(left, right, precision=HIGH, preferred_element_type=jnp.float32)

def layer_norm(rows):
    mean = lax.optimization_barrier(jnp.mean(rows, axis=-1, keepdims=True))
    centered = rows - mean
    variance = lax.optimization_barrier(jnp.mean(centered * centered, axis=-1, keepdims=True))
    return centered * lax.rsqrt(variance + EPS)

def angle_tables(count):
    half = DH // 2
    freqs = 10000.0 ** (-jnp.arange(half, dtype=jnp.float32) / half)
    angle = jnp.arange(count, dtype=jnp.int32).astype(jnp.float32)[:, None] * freqs[None, :]
    return (jnp.cos(angle)[:, None, :], jnp.sin(angle)[:, None, :])

def rotate(parts, cosines, sines):
    half = parts.shape[-1] // 2
    first = parts[..., :half]
    second = parts[..., half:]
    return jnp.concatenate([first * cosines - second * sines, second * cosines + first * sines], axis=-1)

def attend(queries, keys, values, valid):
    frames = queries.shape[0]
    size = min(512, frames)
    blocks = queries.reshape(frames // size, size, HEADS, DH)

    def one_block(block):
        raw = low_back(jnp.einsum('qhd,khd->hqk', block, keys, precision=HIGH) * DH ** (-0.5))
        raw = jnp.where(valid[None, None, :], raw, NEG)
        probs = low(jax.nn.softmax(raw, axis=-1))
        return jnp.einsum('hqk,khd->qhd', probs, values, precision=HIGH)
    return lax.map(jax.checkpoint(one_block), blocks).reshape(frames, HEADS * DH)

def forward_one(rows, embed, length, w_mod, b_mod, w_qkv, b_qkv, w_out, b_out, w_up, b_up, w_down, b_down):
    frames, width = rows.shape
    time_act = low(jax.nn.silu(embed))
    mods = matmul(time_act[None, :], w_mod)[0] + b_mod
    shift_a, scale_a, gate_a, shift_f, scale_f, gate_f = jnp.split(mods, 6)
    hidden_a = low(layer_norm(rows) * (1.0 + scale_a) + shift_a)
    qkv = low_back(matmul(hidden_a, w_qkv) + b_qkv)
    queries, keys, values = jnp.split(qkv, 3, axis=-1)
    cosines, sines = angle_tables(frames)
    queries = low(rotate(queries.reshape(frames, HEADS, DH), cosines, sines))
    keys = low(rotate(keys.reshape(frames, HEADS, DH), cosines, sines))
    values = low(values.reshape(frames, HEADS, DH))
    valid = jnp.arange(frames, dtype=jnp.int32) < length
    attn = low(low_back(attend(queries, keys, values, valid)))
    branch_a = low_back(matmul(attn, w_out) + b_out)
    mixed = rows + gate_a * branch_a
    hidden_f = low(layer_norm(mixed) * (1.0 + scale_f) + shift_f)
    pre_act = low_back(matmul(hidden_f, w_up) + b_up)
    act_low = low(jax.nn.gelu(pre_act, approximate=True))
    branch_f = low_back(matmul(act_low, w_down) + b_down)
    return mixed + gate_f * branch_f

def reference(inputs, time_embed, lengths, cotangent, w_mod, b_mod, w_qkv, b_qkv, w_out, b_out, w_up, b_up, w_down, b_down):
    weights = tuple((weight.astype(jnp.float32) for weight in (w_mod, b_mod, w_qkv, b_qkv, w_out, b_out, w_up, b_up, w_down, b_down)))
    zeros = tuple((jnp.zeros(weight.shape, jnp.float32) for weight in weights))

    def visit(totals, item):
        rows, embed, length, grad_rows = item

        def layer(rows_in, embed_in, *params):
            return forward_one(rows_in, embed_in, length, *params)
        result, pull = jax.vjp(layer, rows.astype(jnp.float32), embed.astype(jnp.float32), *weights)
        grads = pull(grad_rows.astype(jnp.float32))
        totals = tuple((total + grad for total, grad in zip(totals, grads[2:])))
        return (totals, (result, grads[0], grads[1]))
    totals, outs = lax.scan(visit, zeros, (inputs, time_embed, lengths, cotangent))
    return (outs[0], outs[1], outs[2], totals[0], totals[1], totals[2], totals[3], totals[4], totals[5], totals[6], totals[7], totals[8], totals[9])
```

```python
from functools import partial

import jax
import jax.numpy as jnp
from jax import lax
from jax.experimental import pallas as pl
from jax.experimental.pallas import tpu as pltpu
from jax.sharding import PartitionSpec as P

HEADS = 16
EPS = 1e-06
LANES = 128
SHORT = 16
MESH = pl.DeviceIdType.MESH
BF16 = jnp.bfloat16
F32 = jnp.float32
MIB = 1 << 20


def dot(left, right):
    return jnp.dot(left, right, preferred_element_type=F32)


def dot_rows(left, right):
    return lax.dot_general(left, right, (((1,), (1,)), ((), ())), preferred_element_type=F32)


def dot_frames(left, right):
    return lax.dot_general(left, right, (((0,), (0,)), ((), ())), preferred_element_type=F32)


def normalize(rows):
    mean = jnp.mean(rows, axis=-1, keepdims=True)
    centered = rows - mean
    inverse = lax.rsqrt(jnp.mean(centered * centered, axis=-1, keepdims=True) + EPS)
    return (centered * inverse, inverse)


def norm_back(normed, inverse, grad):
    return inverse * (
        grad
        - jnp.mean(grad, axis=-1, keepdims=True)
        - normed * jnp.mean(grad * normed, axis=-1, keepdims=True)
    )


def whole(shape):
    return pl.BlockSpec(shape, lambda *_: (0,) * len(shape))


def in_hbm():
    return pl.BlockSpec(memory_space=pltpu.HBM)


def rotary_tables(first, frames, seqs, half):
    positions = (first + jnp.arange(frames, dtype=jnp.int32)).astype(F32)
    freqs = 10000.0 ** (-jnp.arange(half, dtype=F32) / half)
    angle = positions[:, None] * freqs[None, :]
    cosines, sines = jnp.cos(angle), jnp.sin(angle)
    reps = LANES // (2 * half)
    cos_table = jnp.tile(jnp.concatenate([cosines, cosines], axis=1), (seqs, reps))
    sin_table = jnp.tile(jnp.concatenate([-sines, sines], axis=1), (seqs, reps))
    return cos_table, sin_table


def rotate(rows, cos_table, sin_table, half):
    lane = lax.broadcasted_iota(jnp.int32, rows.shape, 1)
    partner = jnp.where(
        lax.rem(lane, 2 * half) < half,
        pltpu.roll(rows, LANES - half, 1),
        pltpu.roll(rows, half, 1),
    )
    return rows * cos_table + partner * sin_table


def pre_kernel(sizes, x_ref, time_ref, cos_ref, sin_ref, w_mod, b_mod, w_qkv, b_qkv, mods, hidden, qkv):
    seqs, frames, width, half, mod_steps, span, qkv_span = sizes
    step = pl.program_id(0)

    @pl.when(step < mod_steps)
    def _():
        cols = pl.ds(pl.multiple_of(step * span, span), span)
        mods[:, cols] = dot(time_ref[...], w_mod[...]) + b_mod[...].astype(F32)

    @pl.when(step == mod_steps)
    def _():
        for s in range(seqs):
            normed, _ = normalize(x_ref[s * frames : (s + 1) * frames, :].astype(F32))
            shift, scale = mods[s : s + 1, :width], mods[s : s + 1, width : 2 * width]
            hidden[s * frames : (s + 1) * frames, :] = (normed * (1.0 + scale) + shift).astype(BF16)

    @pl.when(step >= mod_steps)
    def _():
        rows = dot(hidden[...], w_qkv[...]) + b_qkv[...].astype(F32)
        kind = (step - mod_steps) // (width // qkv_span)

        @pl.when(kind < 2)
        def _():
            factor = jnp.where(kind == 0, (2.0 * half) ** (-0.5), 1.0)
            for c in range(qkv_span // LANES):
                part = rows[:, c * LANES : (c + 1) * LANES]
                turned = rotate(part, cos_ref[...], sin_ref[...], half)
                qkv[c] = (turned * factor).astype(BF16)

        @pl.when(kind == 2)
        def _():
            for c in range(qkv_span // LANES):
                qkv[c] = rows[:, c * LANES : (c + 1) * LANES].astype(BF16)


def pre_attention(x, time_act, cos_table, sin_table, w_mod, b_mod, w_qkv, b_qkv, frames):
    tokens, width = x.shape
    seqs = tokens // frames
    half = width // HEADS // 2
    span, qkv_span = 512, 512
    mod_steps = w_mod.shape[1] // span
    per_kind = width // qkv_span
    groups = width // LANES
    sizes = (seqs, frames, width, half, mod_steps, span, qkv_span)

    def at(i):
        return jnp.minimum(i, mod_steps - 1)

    def past(i):
        return jnp.maximum(i - mod_steps, 0)

    return pl.pallas_call(
        partial(pre_kernel, sizes),
        grid=(mod_steps + 3 * per_kind,),
        in_specs=[
            whole((tokens, width)),
            whole((seqs, width)),
            whole((tokens, LANES)),
            whole((tokens, LANES)),
            pl.BlockSpec((width, span), lambda i: (0, at(i))),
            pl.BlockSpec((1, span), lambda i: (0, at(i))),
            pl.BlockSpec((width, qkv_span), lambda i: (0, past(i))),
            pl.BlockSpec((1, qkv_span), lambda i: (0, past(i))),
        ],
        out_specs=[
            whole((seqs, w_mod.shape[1])),
            whole((tokens, width)),
            pl.BlockSpec(
                (qkv_span // LANES, tokens, LANES),
                lambda i: (lax.rem(past(i), per_kind), 0, past(i) // per_kind),
            ),
        ],
        out_shape=[
            jax.ShapeDtypeStruct((seqs, w_mod.shape[1]), F32),
            jax.ShapeDtypeStruct((tokens, width), BF16),
            jax.ShapeDtypeStruct((groups, tokens, 3 * LANES), BF16),
        ],
        compiler_params=pltpu.CompilerParams(vmem_limit_bytes=40 * MIB),
        name="pre_attention",
    )(x, time_act, cos_table, sin_table, w_mod, b_mod[None], w_qkv, b_qkv[None])


class Plan:
    def __init__(self, count, frames, width):
        self.count = count
        self.frames = frames
        self.width = width
        self.groups = min(count, width // LANES)
        self.splits = count // self.groups
        total = count * frames
        short = total // SHORT
        self.total = total
        self.short_rows = min(short, frames)
        self.short_blocks = -(-short // frames)
        self.short = short


def greet_all(count, me, barrier):
    for step in range(1, count):
        pl.semaphore_signal(
            barrier, inc=1, device_id={"blk": lax.rem(me + step, count)}, device_id_type=MESH
        )
    pl.semaphore_wait(barrier, count - 1)


def send(src, dst, send_sem, recv_sem, peer):
    copy = pltpu.make_async_remote_copy(
        src_ref=src, dst_ref=dst, send_sem=send_sem, recv_sem=recv_sem,
        device_id={"blk": peer}, device_id_type=MESH,
    )
    copy.start()
    return copy


def spread_kernel(plan, with_keys, *refs):
    n, g, f = plan.count, plan.groups, plan.frames
    if with_keys:
        rows, q_out, kv_out, short_out, q_send, q_recv, k_send, k_recv, s_send, s_recv = refs
    else:
        rows, q_out, q_send, q_recv = refs
    me = lax.axis_index("blk")
    group, split = lax.rem(me, g), me // g
    greet_all(n, me, pltpu.get_barrier_semaphore())
    waits = []
    if with_keys:
        for step in range(n):
            peer = lax.rem(me + step, n)
            src, dst = rows.at[lax.rem(peer, g), 0:f, LANES : 3 * LANES], kv_out.at[me]
            if step == 0:
                waits.append(pltpu.make_async_copy(src, dst, k_recv.at[0]))
                waits[-1].start()
            else:
                waits.append(send(src, dst, k_send.at[step], k_recv.at[step], peer))
    for step in range(g):
        peer = split * g + lax.rem(group + step, g)
        if with_keys:
            src = rows.at[lax.rem(peer, g), :, 0:LANES]
        else:
            src = rows.at[:, pl.ds(pl.multiple_of(lax.rem(peer, g) * LANES, LANES), LANES)]
        dst = q_out.at[group]
        if step == 0:
            waits.append(pltpu.make_async_copy(src, dst, q_recv.at[0]))
            waits[-1].start()
        else:
            waits.append(send(src, dst, q_send.at[step], q_recv.at[step], peer))
    if with_keys:
        for block in range(plan.short_blocks):
            own = rows.at[group, f : f + plan.short_rows, LANES : 3 * LANES]

            @pl.when(me == block)
            def _():
                copies = []
                for step in range(1, n):
                    peer = lax.rem(me + step, n)
                    src = rows.at[lax.rem(peer, g), f : f + plan.short_rows, LANES : 3 * LANES]
                    copies.append(
                        send(src, short_out.at[block], s_send.at[step], s_recv.at[block], peer)
                    )
                local = pltpu.make_async_copy(own, short_out.at[block], s_recv.at[block])
                local.start()
                for copy in copies:
                    copy.wait_send()

            pltpu.make_async_copy(own, short_out.at[block], s_recv.at[block]).wait()
    for copy in waits:
        copy.wait()


def spread(plan, rows, with_keys, collective_id, name):
    n, g, f = plan.count, plan.groups, plan.frames
    tokens = 2 * f
    outs = [jax.ShapeDtypeStruct((g, tokens, LANES), BF16)]
    sems = [pltpu.SemaphoreType.DMA((g,))] * 2
    if with_keys:
        outs += [
            jax.ShapeDtypeStruct((n, f, 2 * LANES), BF16),
            jax.ShapeDtypeStruct((plan.short_blocks, plan.short_rows, 2 * LANES), BF16),
        ]
        sems += [pltpu.SemaphoreType.DMA((n,))] * 3 + [pltpu.SemaphoreType.DMA((plan.short_blocks,))]
    return pl.pallas_call(
        partial(spread_kernel, plan, with_keys),
        in_specs=[in_hbm()],
        out_specs=[in_hbm()] * len(outs),
        out_shape=outs,
        scratch_shapes=sems,
        compiler_params=pltpu.CompilerParams(collective_id=collective_id, has_side_effects=True),
        name=name,
    )(rows)


def gather_kernel(plan, with_keys, *refs):
    n, g, f = plan.count, plan.groups, plan.frames
    if with_keys:
        q_in, kv_in, short_in, q_out, kv_out, short_out, q_send, q_recv, k_send, k_recv, s_send, s_recv = refs
    else:
        q_in, q_out, q_send, q_recv = refs
    me = lax.axis_index("blk")
    group, split = lax.rem(me, g), me // g
    greet_all(n, me, pltpu.get_barrier_semaphore())
    waits = []
    own_cols = pl.ds(pl.multiple_of(group * LANES, LANES), LANES)
    if with_keys:
        for step in range(n):
            peer = lax.rem(me + step, n)
            for which in range(2):
                src = kv_in.at[which, peer]
                dst = kv_out.at[which, split, :, own_cols]
                if step == 0:
                    waits.append(pltpu.make_async_copy(src, dst, k_recv.at[which, 0]))
                    waits[-1].start()
                else:
                    waits.append(send(src, dst, k_send.at[which, step], k_recv.at[which, step], peer))
    for step in range(g):
        peer = split * g + lax.rem(group + step, g)
        src, dst = q_in.at[lax.rem(peer, g)], q_out.at[:, own_cols]
        if step == 0:
            waits.append(pltpu.make_async_copy(src, dst, q_recv.at[0]))
            waits[-1].start()
        else:
            waits.append(send(src, dst, q_send.at[step], q_recv.at[step], peer))
    if with_keys:
        for block in range(plan.short_blocks):
            dst = short_out.at[:, split, :, own_cols]

            @pl.when(me != block)
            def _():
                send(short_in.at[block], dst, s_send, s_recv.at[me], block).wait_send()

            @pl.when(me == block)
            def _():
                local = pltpu.make_async_copy(short_in.at[block], dst, s_recv.at[block])
                local.start()
                for source in range(n):
                    pltpu.make_async_copy(short_in.at[block], dst, s_recv.at[source]).wait()
    for copy in waits:
        copy.wait()


def gather(plan, parts, with_keys, collective_id, name):
    n, g, f = plan.count, plan.groups, plan.frames
    tokens = 2 * f
    outs = [jax.ShapeDtypeStruct((tokens, plan.width), BF16)]
    sems = [pltpu.SemaphoreType.DMA((g,))] * 2
    if with_keys:
        outs += [
            jax.ShapeDtypeStruct((2, plan.splits, f, plan.width), BF16),
            jax.ShapeDtypeStruct((2, plan.splits, plan.short_rows, plan.width), BF16),
        ]
        sems += [pltpu.SemaphoreType.DMA((2, n))] * 2
        sems += [pltpu.SemaphoreType.DMA(()), pltpu.SemaphoreType.DMA((n,))]
    return pl.pallas_call(
        partial(gather_kernel, plan, with_keys),
        in_specs=[in_hbm()] * len(parts),
        out_specs=[in_hbm()] * len(outs),
        out_shape=outs,
        scratch_shapes=sems,
        compiler_params=pltpu.CompilerParams(collective_id=collective_id, has_side_effects=True),
        name=name,
    )(*parts)


def stacked(rows, head_dim):
    lane = lax.broadcasted_iota(jnp.int32, rows.shape, 1)
    heads = LANES // head_dim
    return jnp.concatenate(
        [jnp.where(lane // head_dim == h, rows, jnp.zeros_like(rows)) for h in range(heads)], axis=0
    )


def unstacked(turned, frames, head_dim):
    heads = LANES // head_dim
    return jnp.concatenate(
        [
            turned[h * head_dim : (h + 1) * head_dim, h * frames : (h + 1) * frames]
            for h in range(heads)
        ],
        axis=0,
    ).T


def attend(queries, keys, values_t, head_dim):
    frames = queries.shape[0]
    scores = dot_rows(keys, stacked(queries, head_dim))
    top = jnp.max(scores, axis=0, keepdims=True)
    weights = jnp.exp(scores - top)
    total = jnp.sum(weights, axis=0, keepdims=True)
    out = dot(values_t, weights.astype(BF16)) / total
    return unstacked(out, frames, head_dim).astype(BF16), top + jnp.log(total)


def attention_kernel(plan, head_dim, q_ref, kv_ref, short_ref, out_ref, lse_ref, long_vt, short_vt):
    f, total, short = plan.frames, plan.total, plan.short

    @pl.when(pl.program_id(0) == 0)
    def _():
        long_vt[...] = kv_ref[:, :, LANES:].reshape(total, LANES).T
        short_vt[...] = short_ref[:, :, LANES:].reshape(short, LANES).T

    long_out, long_lse = attend(
        q_ref[0, :f], kv_ref[:, :, :LANES].reshape(total, LANES), long_vt[...], head_dim
    )
    short_out, short_lse = attend(
        q_ref[0, f:], short_ref[:, :, :LANES].reshape(short, LANES), short_vt[...], head_dim
    )
    out_ref[0, :f] = long_out
    out_ref[0, f:] = short_out
    lse_ref[0, 0:1] = long_lse
    lse_ref[0, 1:2] = short_lse


def attention(plan, head_dim, queries, kv, short_kv):
    g, f = plan.groups, plan.frames
    wide = f * (LANES // head_dim)
    return pl.pallas_call(
        partial(attention_kernel, plan, head_dim),
        grid=(g,),
        in_specs=[
            pl.BlockSpec((1, 2 * f, LANES), lambda i: (i, 0, 0)),
            whole(kv.shape),
            whole(short_kv.shape),
        ],
        out_specs=[
            pl.BlockSpec((1, 2 * f, LANES), lambda i: (i, 0, 0)),
            pl.BlockSpec((1, 2, wide), lambda i: (i, 0, 0)),
        ],
        out_shape=[
            jax.ShapeDtypeStruct((g, 2 * f, LANES), BF16),
            jax.ShapeDtypeStruct((g, 2, wide), F32),
        ],
        scratch_shapes=[
            pltpu.VMEM((LANES, plan.total), BF16),
            pltpu.VMEM((LANES, plan.short), BF16),
        ],
        compiler_params=pltpu.CompilerParams(vmem_limit_bytes=48 * MIB),
        name="attention",
    )(queries, kv, short_kv)


def attend_back(queries, grads, lse, keys, keys_t, values, head_dim):
    frames = queries.shape[0]
    q_heads, g_heads = stacked(queries, head_dim), stacked(grads, head_dim)
    probs = jnp.exp(dot_rows(keys, q_heads) - lse)
    grad_probs = dot_rows(values, g_heads)
    delta = jnp.sum(probs * grad_probs, axis=0, keepdims=True)
    grad_scores = (probs * (grad_probs - delta)).astype(BF16)
    grad_values = dot(probs.astype(BF16), g_heads)
    grad_keys = dot(grad_scores, q_heads)
    grad_queries = unstacked(dot(keys_t, grad_scores), frames, head_dim) * head_dim ** (-0.5)
    return grad_queries.astype(BF16), grad_keys, grad_values


def attention_back_kernel(plan, head_dim, *refs):
    q_ref, g_ref, lse_ref, kv_ref, short_ref, dq_ref, dkv_ref, dshort_ref, long_kt, short_kt, dlong, dsmall = refs
    f, total, short = plan.frames, plan.total, plan.short
    step = pl.program_id(0)

    @pl.when(step == 0)
    def _():
        long_kt[...] = kv_ref[:, :, :LANES].reshape(total, LANES).T
        short_kt[...] = short_ref[:, :, :LANES].reshape(short, LANES).T
        dlong[...] = jnp.zeros_like(dlong)
        dsmall[...] = jnp.zeros_like(dsmall)

    for rows, kv, kt, lse, acc in (
        (slice(0, f), kv_ref, long_kt, lse_ref[0, 0:1], dlong),
        (slice(f, 2 * f), short_ref, short_kt, lse_ref[0, 1:2], dsmall),
    ):
        size = acc.shape[1]
        dq, dk, dv = attend_back(
            q_ref[0, rows],
            g_ref[0, rows],
            lse,
            kv[:, :, :LANES].reshape(size, LANES),
            kt[...],
            kv[:, :, LANES:].reshape(size, LANES),
            head_dim,
        )
        dq_ref[0, rows] = dq
        acc[0] += dk
        acc[1] += dv

    @pl.when(step == pl.num_programs(0) - 1)
    def _():
        dkv_ref[...] = dlong[...].astype(BF16).reshape(dkv_ref.shape)
        for block in range(plan.short_blocks):
            rows = slice(block * plan.short_rows, (block + 1) * plan.short_rows)
            dshort_ref[block] = dsmall[:, rows].astype(BF16)


def attention_back(plan, head_dim, queries, grads, lse, kv, short_kv):
    n, g, f = plan.count, plan.groups, plan.frames
    per_block = pl.BlockSpec((1, 2 * f, LANES), lambda i: (i, 0, 0))
    outs = [
        jax.ShapeDtypeStruct((g, 2 * f, LANES), BF16),
        jax.ShapeDtypeStruct((2, n, f, LANES), BF16),
        jax.ShapeDtypeStruct((plan.short_blocks, 2, plan.short_rows, LANES), BF16),
    ]
    return pl.pallas_call(
        partial(attention_back_kernel, plan, head_dim),
        grid=(g,),
        in_specs=[
            per_block,
            per_block,
            pl.BlockSpec((1,) + lse.shape[1:], lambda i: (i, 0, 0)),
            whole(kv.shape),
            whole(short_kv.shape),
        ],
        out_specs=[per_block, whole(outs[1].shape), whole(outs[2].shape)],
        out_shape=outs,
        scratch_shapes=[
            pltpu.VMEM((LANES, plan.total), BF16),
            pltpu.VMEM((LANES, plan.short), BF16),
            pltpu.VMEM((2, plan.total, LANES), F32),
            pltpu.VMEM((2, plan.short, LANES), F32),
        ],
        compiler_params=pltpu.CompilerParams(vmem_limit_bytes=48 * MIB),
        name="attention_back",
    )(queries, grads, lse, kv, short_kv)


def xy_peers(count, batch):
    b, j = lax.axis_index("batch"), lax.axis_index("blk")
    core, half = lax.rem(b, 2), b // 2
    near, far = lax.rem(j, 2), j // 2
    at_core = (half * 2 + 1 - core, j)
    at_x = ((1 - half) * 2 + core, j)
    at_near = (b, far * 2 + 1 - near)
    return b, j, core, half, near, far, at_core, at_x, at_near


def push(src, dst, sems, index, device):
    copy = pltpu.make_async_remote_copy(
        src_ref=src, dst_ref=dst, send_sem=sems.at[0, index], recv_sem=sems.at[1, index],
        device_id=device, device_id_type=MESH,
    )
    copy.start()
    return copy


def add_into(target, other):
    target[...] = (target[...].astype(F32) + other.astype(F32)).astype(BF16)


def reduce_kernel(count, chunk, parts, out, *scratch):
    rows, columns = parts.shape[1:]
    half_chunk = chunk // 2
    pairs = columns // chunk // 2
    far_count = count // 2
    a_one, a_two, b_one, b_two, far_buf, a1, a2, b1, b2, far_sems, out_x, out_c = scratch
    b, j, core, half, near, far, at_core, at_x, at_near = xy_peers(count, 4)
    barrier = pltpu.get_barrier_semaphore()
    far_peers = [
        (b, lax.rem(far + step, far_count) * 2 + near) for step in range(1, far_count)
    ]
    for device in [at_core, at_x, at_near] + far_peers:
        pl.semaphore_signal(barrier, inc=1, device_id=device, device_id_type=MESH)
    pl.semaphore_wait(barrier, 2 + far_count)

    def cols(base, which):
        return pl.ds(pl.multiple_of(base + which * half_chunk, half_chunk), half_chunk)

    def base_of(k, second):
        return (k + (pairs if second else 0)) * chunk

    parts4 = parts.reshape(far_count, 2, rows, columns)
    stage_one, stage_two, stage_far, stage_x, stage_c = {}, {}, {}, {}, {}

    def start_one(k):
        if k < pairs:
            src = parts.at[:, :, cols(base_of(k, False), 1 - half)]
            stage_one[k, 0] = push(src, a_one.at[k], a1, k, at_x)
            base = base_of(k, True)
            src = parts4.at[:, 1 - near, :, base : base + chunk]
            stage_one[k, 1] = push(src, b_one.at[k], b1, k, at_near)

    def finish_one(k):
        stage_one[k, 0].wait()
        add_into(a_one.at[k], parts[:, :, cols(base_of(k, False), half)])
        src = a_one.at[k].reshape(far_count, 2, rows, half_chunk).at[:, 1 - near]
        stage_two[k, 0] = push(src, a_two.at[k], a2, k, at_near)
        stage_one[k, 1].wait()
        base = base_of(k, True)
        add_into(b_one.at[k], parts4[:, near, :, base : base + chunk])
        src = b_one.at[k, :, :, cols(0, 1 - half)]
        stage_two[k, 1] = push(src, b_two.at[k], b2, k, at_x)

    def finish_two(k):
        stage_two[k, 0].wait()
        add_into(a_two.at[k], a_one.at[k].reshape(far_count, 2, rows, half_chunk)[:, near])
        stage_two[k, 1].wait()
        add_into(b_two.at[k], b_one[k, :, :, cols(0, half)])
        for which, buf in enumerate((a_two, b_two)):
            for step in range(1, far_count):
                peer = lax.rem(far + step, far_count)
                stage_far[k, which, step] = push(
                    buf.at[k, peer],
                    far_buf.at[which, k, step - 1],
                    far_sems,
                    (which * pairs + k) * far_count + step,
                    (b, peer * 2 + near),
                )

    def finish_far(k):
        for which, buf in enumerate((a_two, b_two)):
            total = buf[k, far].astype(F32)
            for step in range(1, far_count):
                stage_far[k, which, step].wait()
                total = total + far_buf[which, k, step - 1].astype(F32)
            own = cols(base_of(k, which), half)
            out[core, :, own] = total.astype(BF16)
            place = out.at[core, :, own]
            stage_x[k, which] = push(place, place, out_x, which * pairs + k, at_x)
            stage_c[k, which, 0] = push(place, place, out_c, (which * pairs + k) * 2, at_core)

    def finish_x(k):
        for which in range(2):
            stage_x[k, which].wait()
            place = out.at[core, :, cols(base_of(k, which), 1 - half)]
            stage_c[k, which, 1] = push(place, place, out_c, (which * pairs + k) * 2 + 1, at_core)

    start_one(0)
    start_one(1)
    for t in range(pairs + 3):
        if t < pairs:
            finish_one(t)
            start_one(t + 2)
        if 0 <= t - 1 < pairs:
            finish_two(t - 1)
        if 0 <= t - 2 < pairs:
            finish_far(t - 2)
        if 0 <= t - 3 < pairs:
            finish_x(t - 3)
    for copy in stage_c.values():
        copy.wait()


def reduce_weights(parts, chunk, collective_id):
    count, rows, columns = parts.shape
    half_chunk, pairs, far_count = chunk // 2, columns // chunk // 2, count // 2

    def sems(size):
        return pltpu.SemaphoreType.DMA((2, size))

    vmem = pl.BlockSpec(memory_space=pltpu.VMEM)
    return pl.pallas_call(
        partial(reduce_kernel, count, chunk),
        in_specs=[vmem],
        out_specs=vmem,
        out_shape=jax.ShapeDtypeStruct((2, rows, columns), BF16),
        scratch_shapes=[
            pltpu.VMEM((pairs, count, rows, half_chunk), BF16),
            pltpu.VMEM((pairs, far_count, rows, half_chunk), BF16),
            pltpu.VMEM((pairs, far_count, rows, chunk), BF16),
            pltpu.VMEM((pairs, far_count, rows, half_chunk), BF16),
            pltpu.VMEM((2, pairs, far_count - 1, rows, half_chunk), BF16),
            sems(pairs),
            sems(pairs),
            sems(pairs),
            sems(pairs),
            sems(2 * pairs * far_count),
            sems(2 * pairs),
            sems(4 * pairs),
        ],
        compiler_params=pltpu.CompilerParams(
            collective_id=collective_id, has_side_effects=True, vmem_limit_bytes=56 * MIB
        ),
        name="reduce_weights",
    )(parts)


def small_kernel(count, batch, parts, out, arrived, mine, first, second, third):
    b, j = lax.axis_index("batch"), lax.axis_index("blk")
    barrier = pltpu.get_barrier_semaphore()
    along = [(b, lax.rem(j + step, count)) for step in range(1, count)]
    across = [(lax.rem(b + step, batch), j) for step in range(1, batch)]
    for device in along + across:
        pl.semaphore_signal(barrier, inc=1, device_id=device, device_id_type=MESH)
    pl.semaphore_wait(barrier, count + batch - 2)
    copies = []
    for step, device in enumerate(along):
        copies.append(push(parts.at[device[1]], arrived.at[step], first, step, device))
    total = parts[j]
    for step in range(count - 1):
        copies[step].wait()
        total = total + arrived[step]
    mine[...] = total
    out[b, j] = total
    copies = []
    for step, device in enumerate(along):
        copies.append(push(mine, out.at[b, j], second, step, device))
    for copy in copies:
        copy.wait()
    copies = []
    for step, device in enumerate(across):
        copies.append(push(out.at[b], out.at[b], third, step, device))
    for copy in copies:
        copy.wait()


def small_sums(parts, batch, collective_id):
    count = parts.shape[0]
    vmem = pl.BlockSpec(memory_space=pltpu.VMEM)
    return pl.pallas_call(
        partial(small_kernel, count, batch),
        in_specs=[vmem],
        out_specs=vmem,
        out_shape=jax.ShapeDtypeStruct((batch,) + parts.shape, F32),
        scratch_shapes=[
            pltpu.VMEM((count - 1,) + parts.shape[1:], F32),
            pltpu.VMEM(parts.shape[1:], F32),
            pltpu.SemaphoreType.DMA((2, count - 1)),
            pltpu.SemaphoreType.DMA((2, count - 1)),
            pltpu.SemaphoreType.DMA((2, batch - 1)),
        ],
        compiler_params=pltpu.CompilerParams(collective_id=collective_id, has_side_effects=True),
        name="small_sums",
    )(parts)


def core_swap(array, batch):
    return lax.ppermute(array, "batch", [(i, i ^ 1) for i in range(batch)])


def half_columns(array, which):
    size = array.shape[1] // 2
    return lax.dynamic_slice_in_dim(array, which * size, size, axis=1)


def weight_part(left, right, core, batch):
    other_left = core_swap(left, batch)
    other_right = core_swap(half_columns(right, 1 - core), batch)
    both_left = jnp.concatenate([left, other_left], axis=0)
    both_right = jnp.concatenate([half_columns(right, core), other_right], axis=0)
    return dot_frames(both_left, both_right).astype(BF16)


def on_device(
    inputs,
    time_embed,
    lengths,
    cotangent,
    w_mod,
    b_mod,
    w_qkv,
    b_qkv,
    w_out,
    b_out,
    w_up,
    b_up,
    w_down,
    b_down,
):
    seqs, frames, width = inputs.shape
    tokens = seqs * frames
    head_dim = width // HEADS
    count, batch = lax.axis_size("blk"), lax.axis_size("batch")
    me = lax.axis_index("blk")
    core = lax.rem(lax.axis_index("batch"), 2)
    plan = Plan(count, frames, width)
    swap = lengths[0] < lengths[1]

    def ordered(array):
        return jnp.where(swap, array[::-1], array)

    embed = ordered(time_embed).astype(F32)
    time_silu, silu_pull = jax.vjp(jax.nn.silu, embed)
    time_act = time_silu.astype(BF16)
    cos_table, sin_table = rotary_tables(me * frames, frames, seqs, head_dim // 2)
    x = ordered(inputs).reshape(tokens, width)
    mods, hidden_a, qkv = pre_attention(
        x, time_act, cos_table, sin_table, w_mod, b_mod, w_qkv, b_qkv, frames
    )
    queries, kv, short_kv = spread(plan, qkv, True, 0, "spread_qkv")
    attn_groups, lse = attention(plan, head_dim, queries, kv, short_kv)
    (attn_low,) = gather(plan, (attn_groups,), False, 1, "gather_attention")

    def per_frame(piece):
        return jnp.repeat(piece, frames, axis=0)

    def per_seq(rows):
        return jnp.sum(rows.reshape(seqs, frames, -1), axis=1)

    shift_a, scale_a, gate_a, shift_f, scale_f, gate_f = [
        per_frame(piece) for piece in jnp.split(mods, 6, axis=-1)
    ]
    residual = x.astype(F32)
    branch_a = dot(attn_low, w_out) + b_out.astype(F32)
    mixed = residual + gate_a * branch_a
    norm_f, inverse_f = normalize(mixed)
    hidden_f = (norm_f * (1.0 + scale_f) + shift_f).astype(BF16)
    pre_act = dot(hidden_f, w_up) + b_up.astype(F32)
    act_f32, gelu_pull = jax.vjp(partial(jax.nn.gelu, approximate=True), pre_act)
    act_low = act_f32.astype(BF16)
    branch_f = dot(act_low, w_down) + b_down.astype(F32)
    output = mixed + gate_f * branch_f
    grad_out = ordered(cotangent).reshape(tokens, width).astype(F32)
    grad_gate_f = per_seq(grad_out * branch_f)
    grad_ff = (gate_f * grad_out).astype(BF16)
    part_down = weight_part(act_low, grad_ff, core, batch)
    grad_pre = gelu_pull(dot_rows(grad_ff, w_down))[0].astype(BF16)
    part_up = weight_part(hidden_f, grad_pre, core, batch)
    grad_hidden_f = dot_rows(grad_pre, w_up)
    grad_scale_f = per_seq(grad_hidden_f * norm_f)
    grad_shift_f = per_seq(grad_hidden_f)
    grad_mixed = grad_out + norm_back(norm_f, inverse_f, grad_hidden_f * (1.0 + scale_f))
    grad_gate_a = per_seq(grad_mixed * branch_a)
    grad_branch_a = (gate_a * grad_mixed).astype(BF16)
    part_out = weight_part(attn_low, grad_branch_a, core, batch)
    grad_attn = dot_rows(grad_branch_a, w_out).astype(BF16)

    (grads,) = spread(plan, grad_attn, False, 2, "spread_grad")
    dq, dkv, dshort = attention_back(plan, head_dim, queries, grads, lse, kv, short_kv)
    dq, dkv, dshort = gather(plan, (dq, dkv, dshort), True, 3, "gather_grads")
    dkv = jnp.sum(dkv.astype(F32), axis=1)
    dshort = jnp.where(me < plan.short_blocks, jnp.sum(dshort.astype(F32), axis=1), 0.0)
    dshort = jnp.pad(dshort, ((0, 0), (0, frames - plan.short_rows), (0, 0)))
    grad_kv = jnp.concatenate([dkv, dshort], axis=1)

    def turned_back(rows):
        groups = rows.reshape(tokens, -1, 2, head_dim // 2)
        cosines = cos_table[:, None, : head_dim // 2]
        sines = sin_table[:, None, head_dim // 2 : head_dim]
        first, second = groups[:, :, 0], groups[:, :, 1]
        return jnp.stack(
            [first * cosines + second * sines, second * cosines - first * sines], axis=2
        ).reshape(tokens, width)

    grad_qkv = jnp.concatenate(
        [turned_back(dq.astype(F32)), turned_back(grad_kv[0]), grad_kv[1]], axis=1
    ).astype(BF16)
    part_qkv = weight_part(hidden_a, grad_qkv, core, batch)
    grad_hidden_a = dot_rows(grad_qkv, w_qkv)
    norm_a, inverse_a = normalize(residual)
    grad_scale_a = per_seq(grad_hidden_a * norm_a)
    grad_shift_a = per_seq(grad_hidden_a)
    grad_inputs = grad_mixed + norm_back(norm_a, inverse_a, grad_hidden_a * (1.0 + scale_a))
    grad_mods = jnp.concatenate(
        [grad_shift_a, grad_scale_a, grad_gate_a, grad_shift_f, grad_scale_f, grad_gate_f], axis=-1
    )
    biases = [jnp.sum(g.astype(F32), axis=0) for g in (grad_qkv, grad_branch_a, grad_pre, grad_ff)]

    mod_cols = mods.shape[1] // count
    bias_sizes = [bias.shape[0] // count for bias in biases]
    own = (jnp.arange(count) == me)[:, None]
    pieces = [
        grad_mods.reshape(seqs, count, mod_cols).transpose(1, 0, 2).reshape(count, -1),
        *[bias.reshape(count, -1) for bias in biases],
        jnp.where(
            own,
            time_act.astype(F32).reshape(seqs, count, -1).transpose(1, 0, 2).reshape(count, -1),
            0.0,
        ),
    ]
    flat = jnp.concatenate(pieces, axis=1)
    size = flat.shape[1]
    flat = jnp.pad(flat, ((0, 0), (0, -size % (8 * LANES))))
    sums = small_sums(flat.reshape(count, -1, LANES), batch, 4).reshape(batch, count, -1)
    mods_all = sums[:, :, : seqs * mod_cols].reshape(batch, count, seqs, mod_cols)
    mods_all = mods_all.transpose(0, 2, 1, 3).reshape(batch * seqs, -1)
    mine = lax.dynamic_index_in_dim(sums, me, axis=1, keepdims=False)
    grad_b_mod = jnp.sum(mine[:, : seqs * mod_cols].reshape(batch * seqs, mod_cols), axis=0)
    offset = seqs * mod_cols
    bias_total = jnp.sum(mine, axis=0)
    grad_biases = []
    for bias_size in bias_sizes:
        grad_biases.append(bias_total[offset : offset + bias_size])
        offset += bias_size
    times = mine[:, offset : offset + seqs * (width // count)].reshape(batch * seqs, -1)
    grad_w_mod = dot_frames(times.astype(BF16), mods_all.astype(BF16))
    own_mods = lax.dynamic_slice_in_dim(mods_all, lax.axis_index("batch") * seqs, seqs, axis=0)
    grad_silu = dot_rows(own_mods.astype(BF16), w_mod)
    grad_time = ordered(silu_pull(grad_silu)[0])

    rows = width // count
    split_down = part_down.reshape(count, -1, rows, width // 2)
    split_down = [split_down[:, i] for i in range(split_down.shape[1])]
    parts = jnp.concatenate(
        [p.reshape(count, rows, -1) for p in (part_qkv, part_out, part_up)] + split_down, axis=2
    )
    totals = reduce_weights(parts, 512, 5).astype(F32)
    ends = [3 * width // 2, 2 * width, 3 * width]
    grad_w_qkv, grad_w_out, grad_w_up, down = [
        jnp.concatenate([piece[0], piece[1]], axis=1) for piece in jnp.split(totals, ends, axis=2)
    ]
    down = down.reshape(rows, 2, -1, width // 2).transpose(2, 0, 1, 3)
    grad_w_down = down.reshape(-1, width)
    return (
        ordered(output.reshape(seqs, frames, width)),
        ordered(grad_inputs.reshape(seqs, frames, width)),
        grad_time,
        grad_w_mod,
        grad_b_mod,
        grad_w_qkv,
        grad_biases[0],
        grad_w_out,
        grad_biases[1],
        grad_w_up,
        grad_biases[2],
        grad_w_down,
        grad_biases[3],
    )


def solution(mesh):
    frame_spec, weight_spec = P("batch", "blk", None), P("blk", None)
    return jax.shard_map(
        on_device,
        mesh=mesh,
        in_specs=(frame_spec, P("batch", None), P("batch"), frame_spec) + (P(),) * 10,
        out_specs=(frame_spec, frame_spec, P("batch", None)) + (weight_spec, P("blk")) * 5,
        check_vma=False,
    )
```

```python
from functools import partial

import jax
import jax.numpy as jnp
from jax import lax
from jax.experimental import pallas as pl
from jax.experimental.pallas import tpu as pltpu
from jax.sharding import PartitionSpec as P

HEADS = 16
EPS = 1e-06
LANES = 128
SHORT = 16
MESH = pl.DeviceIdType.MESH
BF16 = jnp.bfloat16
F32 = jnp.float32
MIB = 1 << 20


def dot(left, right):
    return jnp.dot(left, right, preferred_element_type=F32)


def dot_rows(left, right):
    return lax.dot_general(left, right, (((1,), (1,)), ((), ())), preferred_element_type=F32)


def dot_frames(left, right):
    return lax.dot_general(left, right, (((0,), (0,)), ((), ())), preferred_element_type=F32)


def normalize(rows):
    mean = jnp.mean(rows, axis=-1, keepdims=True)
    centered = rows - mean
    inverse = lax.rsqrt(jnp.mean(centered * centered, axis=-1, keepdims=True) + EPS)
    return (centered * inverse, inverse)


def norm_back(normed, inverse, grad):
    return inverse * (
        grad
        - jnp.mean(grad, axis=-1, keepdims=True)
        - normed * jnp.mean(grad * normed, axis=-1, keepdims=True)
    )


def whole(shape):
    return pl.BlockSpec(shape, lambda *_: (0,) * len(shape))


def in_hbm():
    return pl.BlockSpec(memory_space=pltpu.HBM)


def rotary_tables(first, frames, seqs, half):
    positions = (first + jnp.arange(frames, dtype=jnp.int32)).astype(F32)
    freqs = 10000.0 ** (-jnp.arange(half, dtype=F32) / half)
    angle = positions[:, None] * freqs[None, :]
    cosines, sines = jnp.cos(angle), jnp.sin(angle)
    reps = LANES // (2 * half)
    cos_table = jnp.tile(jnp.concatenate([cosines, cosines], axis=1), (seqs, reps))
    sin_table = jnp.tile(jnp.concatenate([-sines, sines], axis=1), (seqs, reps))
    return cos_table, sin_table


def rotate(rows, cos_table, sin_table, half):
    lane = lax.broadcasted_iota(jnp.int32, rows.shape, 1)
    partner = jnp.where(
        lax.rem(lane, 2 * half) < half,
        pltpu.roll(rows, LANES - half, 1),
        pltpu.roll(rows, half, 1),
    )
    return rows * cos_table + partner * sin_table


def pre_kernel(sizes, x_ref, time_ref, cos_ref, sin_ref, w_mod, b_mod, w_qkv, b_qkv, mods, hidden, qkv):
    seqs, frames, width, half, mod_steps, span, qkv_span, cols = sizes
    step = pl.program_id(0)

    @pl.when(step < mod_steps)
    def _():
        cols = pl.ds(pl.multiple_of(step * span, span), span)
        mods[:, cols] = dot(time_ref[...], w_mod[...]) + b_mod[...].astype(F32)

    @pl.when(step == mod_steps)
    def _():
        for s in range(seqs):
            normed, _ = normalize(x_ref[s * frames : (s + 1) * frames, :].astype(F32))
            shift, scale = mods[s : s + 1, :width], mods[s : s + 1, width : 2 * width]
            hidden[s * frames : (s + 1) * frames, :] = (normed * (1.0 + scale) + shift).astype(BF16)

    @pl.when(step >= mod_steps)
    def _():
        rows = dot(hidden[...], w_qkv[...]) + b_qkv[...].astype(F32)
        kind = (step - mod_steps) // (width // qkv_span)

        def store(c, part):
            start = c * LANES % cols
            qkv[c * LANES // cols, :, start : start + LANES] = part

        @pl.when(kind < 2)
        def _():
            factor = jnp.where(kind == 0, (2.0 * half) ** (-0.5), 1.0)
            for c in range(qkv_span // LANES):
                part = rows[:, c * LANES : (c + 1) * LANES]
                turned = rotate(part, cos_ref[...], sin_ref[...], half)
                store(c, (turned * factor).astype(BF16))

        @pl.when(kind == 2)
        def _():
            for c in range(qkv_span // LANES):
                store(c, rows[:, c * LANES : (c + 1) * LANES].astype(BF16))


def pre_attention(x, time_act, cos_table, sin_table, w_mod, b_mod, w_qkv, b_qkv, frames, cols):
    tokens, width = x.shape
    seqs = tokens // frames
    half = width // HEADS // 2
    span, qkv_span = 512, 512
    mod_steps = w_mod.shape[1] // span
    per_kind = width // qkv_span
    sizes = (seqs, frames, width, half, mod_steps, span, qkv_span, cols)

    def at(i):
        return jnp.minimum(i, mod_steps - 1)

    def past(i):
        return jnp.maximum(i - mod_steps, 0)

    return pl.pallas_call(
        partial(pre_kernel, sizes),
        grid=(mod_steps + 3 * per_kind,),
        in_specs=[
            whole((tokens, width)),
            whole((seqs, width)),
            whole((tokens, LANES)),
            whole((tokens, LANES)),
            pl.BlockSpec((width, span), lambda i: (0, at(i))),
            pl.BlockSpec((1, span), lambda i: (0, at(i))),
            pl.BlockSpec((width, qkv_span), lambda i: (0, past(i))),
            pl.BlockSpec((1, qkv_span), lambda i: (0, past(i))),
        ],
        out_specs=[
            whole((seqs, w_mod.shape[1])),
            whole((tokens, width)),
            pl.BlockSpec(
                (qkv_span // cols, tokens, cols),
                lambda i: (lax.rem(past(i), per_kind), 0, past(i) // per_kind),
            ),
        ],
        out_shape=[
            jax.ShapeDtypeStruct((seqs, w_mod.shape[1]), F32),
            jax.ShapeDtypeStruct((tokens, width), BF16),
            jax.ShapeDtypeStruct((width // cols, tokens, 3 * cols), BF16),
        ],
        compiler_params=pltpu.CompilerParams(vmem_limit_bytes=40 * MIB),
        name="pre_attention",
    )(x, time_act, cos_table, sin_table, w_mod, b_mod[None], w_qkv, b_qkv[None])


class Plan:
    def __init__(self, count, frames, width):
        self.count = count
        self.frames = frames
        self.width = width
        self.groups = min(max(count // 2, 1), 4)
        self.cols = width // self.groups
        self.splits = count // self.groups
        self.total = count * frames
        self.short = self.total // SHORT
        self.short_rows = min(self.short, frames)
        self.short_blocks = -(-self.short // frames)


def greet(devices, barrier):
    for device in devices:
        pl.semaphore_signal(barrier, inc=1, device_id=device, device_id_type=MESH)
    pl.semaphore_wait(barrier, len(devices))


def push(src, dst, sems, index, device):
    copy = pltpu.make_async_remote_copy(
        src_ref=src, dst_ref=dst, send_sem=sems.at[(0,) + index], recv_sem=sems.at[(1,) + index],
        device_id=device, device_id_type=MESH,
    )
    copy.start()
    return copy


def local(src, dst, sem):
    copy = pltpu.make_async_copy(src, dst, sem)
    copy.start()
    return copy


def stacked(rows, head_dim):
    lane = lax.broadcasted_iota(jnp.int32, rows.shape, 1)
    heads = LANES // head_dim
    return jnp.concatenate(
        [jnp.where(lane // head_dim == h, rows, jnp.zeros_like(rows)) for h in range(heads)], axis=0
    )


def unstacked(turned, frames, head_dim):
    heads = LANES // head_dim
    return jnp.concatenate(
        [
            turned[h * head_dim : (h + 1) * head_dim, h * frames : (h + 1) * frames]
            for h in range(heads)
        ],
        axis=0,
    ).T


def attend(queries, keys, values_t, head_dim):
    frames = queries.shape[0]
    scores = dot_rows(keys, stacked(queries, head_dim))
    top = jnp.max(scores, axis=0, keepdims=True)
    weights = jnp.exp(scores - top)
    total = jnp.sum(weights, axis=0, keepdims=True)
    out = dot(values_t, weights.astype(BF16)) / total
    return unstacked(out, frames, head_dim).astype(BF16), top + jnp.log(total)


def forward_kernel(plan, head_dim, rows, out, q_buf, kv_buf, short_buf, lse, o_buf, long_vt, short_vt, q_sems, k_sems, s_sems, o_sems):
    n, g, f, cols = plan.count, plan.groups, plan.frames, plan.cols
    b, me = lax.axis_index("batch"), lax.axis_index("blk")
    group, split = lax.rem(me, g), me // g
    others = [lax.rem(me + step, n) for step in range(1, n)]
    mates = [split * g + lax.rem(group + step, g) for step in range(1, g)]
    greet([(b, peer) for peer in others], pltpu.get_barrier_semaphore())
    waits = []
    for step, peer in enumerate(others):
        src = rows.at[lax.rem(peer, g), 0:f, cols : 3 * cols]
        waits.append(push(src, kv_buf.at[me], k_sems, (step,), (b, peer)))
    for block in range(plan.short_blocks):

        @pl.when(me == block)
        def _():
            for step, peer in enumerate(others):
                src = rows.at[lax.rem(peer, g), f : f + plan.short_rows, cols : 3 * cols]
                push(src, short_buf.at[block], s_sems, (block, step), (b, peer))

    for step, peer in enumerate(mates):
        src = rows.at[lax.rem(peer, g), :, 0:cols]
        waits.append(push(src, q_buf.at[group], q_sems, (step,), (b, peer)))
    kv_buf[me] = rows[group, 0:f, cols : 3 * cols]
    q_buf[group] = rows[group, :, 0:cols]
    for copy in waits:
        copy.wait()
    for block in range(plan.short_blocks):

        @pl.when(me == block)
        def _():
            short_buf[block] = rows[group, f : f + plan.short_rows, cols : 3 * cols]
            for step, peer in enumerate(others):
                src = rows.at[lax.rem(peer, g), f : f + plan.short_rows, cols : 3 * cols]
                pltpu.make_async_copy(src, src, s_sems.at[0, block, step]).wait()

        for step, peer in enumerate(others):

            @pl.when(lax.rem(block + step + 1, n) == me)
            def _():
                dst = short_buf.at[block]
                pltpu.make_async_copy(dst, dst, s_sems.at[1, block, step]).wait()

    long_vt[...] = kv_buf[:, :, cols:].reshape(plan.total, cols).T
    short_vt[...] = short_buf[:, :, cols:].reshape(plan.short, cols).T
    sends = []
    own_cols = pl.ds(pl.multiple_of(group * cols, LANES), cols)
    for step in range(g):
        slot = lax.rem(group + step, g)
        for u in range(cols // LANES):
            lanes = slice(u * LANES, (u + 1) * LANES)
            keys = kv_buf[:, :, lanes].reshape(plan.total, LANES)
            o_buf[slot, :f, lanes], lse[slot, u : u + 1] = attend(
                q_buf[slot, :f, lanes], keys, long_vt[lanes], head_dim
            )
            keys = short_buf[:, :, lanes].reshape(plan.short, LANES)
            row = cols // LANES + u
            o_buf[slot, f:, lanes], lse[slot, row : row + 1] = attend(
                q_buf[slot, f:, lanes], keys, short_vt[lanes], head_dim
            )
        if step == 0:
            out[:, own_cols] = o_buf[slot]
        else:
            peer = mates[step - 1]
            sends.append(push(o_buf.at[slot], out.at[:, own_cols], o_sems, (step - 1,), (b, peer)))
    for copy in sends:
        copy.wait()


def forward_attention(plan, head_dim, rows, collective_id):
    n, g, f, cols = plan.count, plan.groups, plan.frames, plan.cols
    wide = f * (LANES // head_dim)
    sems = pltpu.SemaphoreType.DMA
    vmem = pl.BlockSpec(memory_space=pltpu.VMEM)
    return pl.pallas_call(
        partial(forward_kernel, plan, head_dim),
        in_specs=[vmem],
        out_specs=[vmem] * 5,
        out_shape=[
            jax.ShapeDtypeStruct((2 * f, plan.width), BF16),
            jax.ShapeDtypeStruct((g, 2 * f, cols), BF16),
            jax.ShapeDtypeStruct((n, f, 2 * cols), BF16),
            jax.ShapeDtypeStruct((plan.short_blocks, plan.short_rows, 2 * cols), BF16),
            jax.ShapeDtypeStruct((g, 2 * (cols // LANES), wide), F32),
        ],
        scratch_shapes=[
            pltpu.VMEM((g, 2 * f, cols), BF16),
            pltpu.VMEM((cols, plan.total), BF16),
            pltpu.VMEM((cols, plan.short), BF16),
            sems((2, g - 1)),
            sems((2, n - 1)),
            sems((2, plan.short_blocks, n - 1)),
            sems((2, g - 1)),
        ],
        compiler_params=pltpu.CompilerParams(
            collective_id=collective_id, has_side_effects=True, vmem_limit_bytes=48 * MIB
        ),
        name="forward_attention",
    )(rows)


def attend_back(queries, grads, lse, keys, keys_t, values, head_dim):
    frames = queries.shape[0]
    q_heads, g_heads = stacked(queries, head_dim), stacked(grads, head_dim)
    probs = jnp.exp(dot_rows(keys, q_heads) - lse)
    grad_probs = dot_rows(values, g_heads)
    delta = jnp.sum(probs * grad_probs, axis=0, keepdims=True)
    grad_scores = (probs * (grad_probs - delta)).astype(BF16)
    grad_values = dot(probs.astype(BF16), g_heads)
    grad_keys = dot(grad_scores, q_heads)
    grad_queries = unstacked(dot(keys_t, grad_scores), frames, head_dim) * head_dim ** (-0.5)
    return grad_queries.astype(BF16), grad_keys, grad_values


def backward_kernel(plan, head_dim, grads, q_buf, kv_buf, short_buf, lse, dq_out, dkv_out, dshort_out, g_buf, dq_buf, dlong, dsmall, dkv_buf, dshort_buf, long_kt, short_kt, g_sems, q_sems, k_sems, s_sems):
    n, g, f, cols = plan.count, plan.groups, plan.frames, plan.cols
    b, me = lax.axis_index("batch"), lax.axis_index("blk")
    group, split = lax.rem(me, g), me // g
    others = [lax.rem(me + step, n) for step in range(1, n)]
    mates = [split * g + lax.rem(group + step, g) for step in range(1, g)]
    greet([(b, peer) for peer in others], pltpu.get_barrier_semaphore())

    def cols_of(which):
        return pl.ds(pl.multiple_of(which * cols, LANES), cols)

    waits = []
    for step, peer in enumerate(mates):
        src = grads.at[:, cols_of(lax.rem(peer, g))]
        waits.append(push(src, g_buf.at[group], g_sems, (step,), (b, peer)))
    g_buf[group] = grads[:, cols_of(group)]
    long_kt[...] = kv_buf[:, :, :cols].reshape(plan.total, cols).T
    short_kt[...] = short_buf[:, :, :cols].reshape(plan.short, cols).T
    for copy in waits:
        copy.wait()
    sends = []
    for step in range(g):
        slot = lax.rem(group + step, g)
        for u in range(cols // LANES):
            lanes = slice(u * LANES, (u + 1) * LANES)
            high = slice(cols + u * LANES, cols + (u + 1) * LANES)
            for rows, kv, kt, row, acc in (
                (slice(0, f), kv_buf, long_kt, u, dlong),
                (slice(f, 2 * f), short_buf, short_kt, cols // LANES + u, dsmall),
            ):
                size = acc.shape[1]
                dq, dk, dv = attend_back(
                    q_buf[slot, rows, lanes],
                    g_buf[slot, rows, lanes],
                    lse[slot, row : row + 1],
                    kv[:, :, lanes].reshape(size, LANES),
                    kt[lanes],
                    kv[:, :, high].reshape(size, LANES),
                    head_dim,
                )
                dq_buf[slot, rows, lanes] = dq
                if step == 0:
                    acc[0, :, lanes] = dk
                    acc[1, :, lanes] = dv
                else:
                    acc[0, :, lanes] += dk
                    acc[1, :, lanes] += dv
        if step == 0:
            dq_out[:, cols_of(group)] = dq_buf[slot]
        else:
            peer = mates[step - 1]
            dst = dq_out.at[:, cols_of(group)]
            sends.append(push(dq_buf.at[slot], dst, q_sems, (step - 1,), (b, peer)))
    dkv_buf[...] = dlong[...].astype(BF16).reshape(dkv_buf.shape)
    for step, peer in enumerate(others):
        for which in range(2):
            dst = dkv_out.at[which, split, :, cols_of(group)]
            sends.append(push(dkv_buf.at[which, peer], dst, k_sems, (which, step), (b, peer)))
    for which in range(2):
        dkv_out[which, split, :, cols_of(group)] = dkv_buf[which, me]
    for block in range(plan.short_blocks):
        span = slice(block * plan.short_rows, (block + 1) * plan.short_rows)
        dshort_buf[block] = dsmall[:, span].astype(BF16)
        dst = dshort_out.at[:, split, :, cols_of(group)]
        for step, peer in enumerate(others):

            @pl.when(peer == block)
            def _():
                push(dshort_buf.at[block], dst, s_sems, (step,), (b, peer)).wait_send()

        @pl.when(me == block)
        def _():
            dshort_out[:, split, :, cols_of(group)] = dshort_buf[block]
            for step in range(n - 1):
                pltpu.make_async_copy(dshort_buf.at[block], dshort_buf.at[block], s_sems.at[1, step]).wait()

    for copy in sends:
        copy.wait()


def backward_attention(plan, head_dim, grads, q_buf, kv_buf, short_buf, lse, collective_id):
    n, g, f, cols = plan.count, plan.groups, plan.frames, plan.cols
    sems = pltpu.SemaphoreType.DMA
    vmem = pl.BlockSpec(memory_space=pltpu.VMEM)
    return pl.pallas_call(
        partial(backward_kernel, plan, head_dim),
        in_specs=[vmem] * 5,
        out_specs=[vmem] * 3,
        out_shape=[
            jax.ShapeDtypeStruct((2 * f, plan.width), BF16),
            jax.ShapeDtypeStruct((2, plan.splits, f, plan.width), BF16),
            jax.ShapeDtypeStruct((2, plan.splits, plan.short_rows, plan.width), BF16),
        ],
        scratch_shapes=[
            pltpu.VMEM((g, 2 * f, cols), BF16),
            pltpu.VMEM((g, 2 * f, cols), BF16),
            pltpu.VMEM((2, plan.total, cols), F32),
            pltpu.VMEM((2, plan.short, cols), F32),
            pltpu.VMEM((2, n, f, cols), BF16),
            pltpu.VMEM((plan.short_blocks, 2, plan.short_rows, cols), BF16),
            pltpu.VMEM((cols, plan.total), BF16),
            pltpu.VMEM((cols, plan.short), BF16),
            sems((2, g - 1)),
            sems((2, g - 1)),
            sems((2, 2, n - 1)),
            sems((2, n - 1)),
        ],
        compiler_params=pltpu.CompilerParams(
            collective_id=collective_id, has_side_effects=True, vmem_limit_bytes=56 * MIB
        ),
        name="backward_attention",
    )(grads, q_buf, kv_buf, short_buf, lse)


def xy_peers(count, batch):
    b, j = lax.axis_index("batch"), lax.axis_index("blk")
    core, half = lax.rem(b, 2), b // 2
    near, far = lax.rem(j, 2), j // 2
    at_core = (half * 2 + 1 - core, j)
    at_x = ((1 - half) * 2 + core, j)
    at_near = (b, far * 2 + 1 - near)
    return b, j, core, half, near, far, at_core, at_x, at_near


def add_into(target, other):
    target[...] = (target[...].astype(F32) + other.astype(F32)).astype(BF16)


def reduce_kernel(count, chunk, parts, out, *scratch):
    rows, columns = parts.shape[1:]
    half_chunk = chunk // 2
    pairs = columns // chunk // 2
    far_count = count // 2
    a_one, a_two, b_one, b_two, far_buf, a1, a2, b1, b2, far_sems, out_x, out_c = scratch
    b, j, core, half, near, far, at_core, at_x, at_near = xy_peers(count, 4)
    barrier = pltpu.get_barrier_semaphore()
    far_peers = [
        (b, lax.rem(far + step, far_count) * 2 + near) for step in range(1, far_count)
    ]
    for device in [at_core, at_x, at_near] + far_peers:
        pl.semaphore_signal(barrier, inc=1, device_id=device, device_id_type=MESH)
    pl.semaphore_wait(barrier, 2 + far_count)

    def cols(base, which):
        return pl.ds(pl.multiple_of(base + which * half_chunk, half_chunk), half_chunk)

    def base_of(k, second):
        return (k + (pairs if second else 0)) * chunk

    parts4 = parts.reshape(far_count, 2, rows, columns)
    stage_one, stage_two, stage_far, stage_x, stage_c = {}, {}, {}, {}, {}

    def start_one(k):
        if k < pairs:
            src = parts.at[:, :, cols(base_of(k, False), 1 - half)]
            stage_one[k, 0] = push(src, a_one.at[k], a1, (k,), at_x)
            base = base_of(k, True)
            src = parts4.at[:, 1 - near, :, base : base + chunk]
            stage_one[k, 1] = push(src, b_one.at[k], b1, (k,), at_near)

    def finish_one(k):
        stage_one[k, 0].wait()
        add_into(a_one.at[k], parts[:, :, cols(base_of(k, False), half)])
        src = a_one.at[k].reshape(far_count, 2, rows, half_chunk).at[:, 1 - near]
        stage_two[k, 0] = push(src, a_two.at[k], a2, (k,), at_near)
        stage_one[k, 1].wait()
        base = base_of(k, True)
        add_into(b_one.at[k], parts4[:, near, :, base : base + chunk])
        src = b_one.at[k, :, :, cols(0, 1 - half)]
        stage_two[k, 1] = push(src, b_two.at[k], b2, (k,), at_x)

    def finish_two(k):
        stage_two[k, 0].wait()
        add_into(a_two.at[k], a_one.at[k].reshape(far_count, 2, rows, half_chunk)[:, near])
        stage_two[k, 1].wait()
        add_into(b_two.at[k], b_one[k, :, :, cols(0, half)])
        for which, buf in enumerate((a_two, b_two)):
            for step in range(1, far_count):
                peer = lax.rem(far + step, far_count)
                stage_far[k, which, step] = push(
                    buf.at[k, peer],
                    far_buf.at[which, k, step - 1],
                    far_sems,
                    ((which * pairs + k) * far_count + step,),
                    (b, peer * 2 + near),
                )

    def finish_far(k):
        for which, buf in enumerate((a_two, b_two)):
            total = buf[k, far].astype(F32)
            for step in range(1, far_count):
                stage_far[k, which, step].wait()
                total = total + far_buf[which, k, step - 1].astype(F32)
            own = cols(base_of(k, which), half)
            out[core, :, own] = total.astype(BF16)
            place = out.at[core, :, own]
            stage_x[k, which] = push(place, place, out_x, (which * pairs + k,), at_x)
            stage_c[k, which, 0] = push(place, place, out_c, ((which * pairs + k) * 2,), at_core)

    def finish_x(k):
        for which in range(2):
            stage_x[k, which].wait()
            place = out.at[core, :, cols(base_of(k, which), 1 - half)]
            stage_c[k, which, 1] = push(place, place, out_c, ((which * pairs + k) * 2 + 1,), at_core)

    start_one(0)
    start_one(1)
    for t in range(pairs + 3):
        if t < pairs:
            finish_one(t)
            start_one(t + 2)
        if 0 <= t - 1 < pairs:
            finish_two(t - 1)
        if 0 <= t - 2 < pairs:
            finish_far(t - 2)
        if 0 <= t - 3 < pairs:
            finish_x(t - 3)
    for copy in stage_c.values():
        copy.wait()


def reduce_weights(parts, chunk, collective_id):
    count, rows, columns = parts.shape
    half_chunk, pairs, far_count = chunk // 2, columns // chunk // 2, count // 2

    def sems(size):
        return pltpu.SemaphoreType.DMA((2, size))

    vmem = pl.BlockSpec(memory_space=pltpu.VMEM)
    return pl.pallas_call(
        partial(reduce_kernel, count, chunk),
        in_specs=[vmem],
        out_specs=vmem,
        out_shape=jax.ShapeDtypeStruct((2, rows, columns), BF16),
        scratch_shapes=[
            pltpu.VMEM((pairs, count, rows, half_chunk), BF16),
            pltpu.VMEM((pairs, far_count, rows, half_chunk), BF16),
            pltpu.VMEM((pairs, far_count, rows, chunk), BF16),
            pltpu.VMEM((pairs, far_count, rows, half_chunk), BF16),
            pltpu.VMEM((2, pairs, far_count - 1, rows, half_chunk), BF16),
            sems(pairs),
            sems(pairs),
            sems(pairs),
            sems(pairs),
            sems(2 * pairs * far_count),
            sems(2 * pairs),
            sems(4 * pairs),
        ],
        compiler_params=pltpu.CompilerParams(
            collective_id=collective_id, has_side_effects=True, vmem_limit_bytes=56 * MIB
        ),
        name="reduce_weights",
    )(parts)


def small_kernel(count, batch, parts, out, arrived, mine, first, second, third):
    b, j = lax.axis_index("batch"), lax.axis_index("blk")
    barrier = pltpu.get_barrier_semaphore()
    along = [(b, lax.rem(j + step, count)) for step in range(1, count)]
    across = [(lax.rem(b + step, batch), j) for step in range(1, batch)]
    for device in along + across:
        pl.semaphore_signal(barrier, inc=1, device_id=device, device_id_type=MESH)
    pl.semaphore_wait(barrier, count + batch - 2)
    copies = []
    for step, device in enumerate(along):
        copies.append(push(parts.at[device[1]], arrived.at[step], first, (step,), device))
    total = parts[j]
    for step in range(count - 1):
        copies[step].wait()
        total = total + arrived[step]
    mine[...] = total
    out[b, j] = total
    copies = []
    for step, device in enumerate(along):
        copies.append(push(mine, out.at[b, j], second, (step,), device))
    for copy in copies:
        copy.wait()
    copies = []
    for step, device in enumerate(across):
        copies.append(push(out.at[b], out.at[b], third, (step,), device))
    for copy in copies:
        copy.wait()


def small_sums(parts, batch, collective_id):
    count = parts.shape[0]
    vmem = pl.BlockSpec(memory_space=pltpu.VMEM)
    return pl.pallas_call(
        partial(small_kernel, count, batch),
        in_specs=[vmem],
        out_specs=vmem,
        out_shape=jax.ShapeDtypeStruct((batch,) + parts.shape, F32),
        scratch_shapes=[
            pltpu.VMEM((count - 1,) + parts.shape[1:], F32),
            pltpu.VMEM(parts.shape[1:], F32),
            pltpu.SemaphoreType.DMA((2, count - 1)),
            pltpu.SemaphoreType.DMA((2, count - 1)),
            pltpu.SemaphoreType.DMA((2, batch - 1)),
        ],
        compiler_params=pltpu.CompilerParams(collective_id=collective_id, has_side_effects=True),
        name="small_sums",
    )(parts)


def core_swap(array, batch):
    return lax.ppermute(array, "batch", [(i, i ^ 1) for i in range(batch)])


def half_columns(array, which):
    size = array.shape[1] // 2
    return lax.dynamic_slice_in_dim(array, which * size, size, axis=1)


def weight_part(left, right, core, batch):
    other_left = core_swap(left, batch)
    other_right = core_swap(half_columns(right, 1 - core), batch)
    both_left = jnp.concatenate([left, other_left], axis=0)
    both_right = jnp.concatenate([half_columns(right, core), other_right], axis=0)
    return dot_frames(both_left, both_right).astype(BF16)


def on_device(
    inputs,
    time_embed,
    lengths,
    cotangent,
    w_mod,
    b_mod,
    w_qkv,
    b_qkv,
    w_out,
    b_out,
    w_up,
    b_up,
    w_down,
    b_down,
):
    seqs, frames, width = inputs.shape
    tokens = seqs * frames
    head_dim = width // HEADS
    count, batch = lax.axis_size("blk"), lax.axis_size("batch")
    me = lax.axis_index("blk")
    core = lax.rem(lax.axis_index("batch"), 2)
    plan = Plan(count, frames, width)
    swap = lengths[0] < lengths[1]

    def ordered(array):
        return jnp.where(swap, array[::-1], array)

    embed = ordered(time_embed).astype(F32)
    time_silu, silu_pull = jax.vjp(jax.nn.silu, embed)
    time_act = time_silu.astype(BF16)
    cos_table, sin_table = rotary_tables(me * frames, frames, seqs, head_dim // 2)
    x = ordered(inputs).reshape(tokens, width)
    mods, hidden_a, qkv = pre_attention(
        x, time_act, cos_table, sin_table, w_mod, b_mod, w_qkv, b_qkv, frames, plan.cols
    )
    attn_low, queries, kv, short_kv, lse = forward_attention(plan, head_dim, qkv, 0)

    def per_frame(piece):
        return jnp.repeat(piece, frames, axis=0)

    def per_seq(rows):
        return jnp.sum(rows.reshape(seqs, frames, -1), axis=1)

    shift_a, scale_a, gate_a, shift_f, scale_f, gate_f = [
        per_frame(piece) for piece in jnp.split(mods, 6, axis=-1)
    ]
    residual = x.astype(F32)
    branch_a = dot(attn_low, w_out) + b_out.astype(F32)
    mixed = residual + gate_a * branch_a
    norm_f, inverse_f = normalize(mixed)
    hidden_f = (norm_f * (1.0 + scale_f) + shift_f).astype(BF16)
    pre_act = dot(hidden_f, w_up) + b_up.astype(F32)
    act_f32, gelu_pull = jax.vjp(partial(jax.nn.gelu, approximate=True), pre_act)
    act_low = act_f32.astype(BF16)
    branch_f = dot(act_low, w_down) + b_down.astype(F32)
    output = mixed + gate_f * branch_f
    grad_out = ordered(cotangent).reshape(tokens, width).astype(F32)
    grad_gate_f = per_seq(grad_out * branch_f)
    grad_ff = (gate_f * grad_out).astype(BF16)
    part_down = weight_part(act_low, grad_ff, core, batch)
    grad_pre = gelu_pull(dot_rows(grad_ff, w_down))[0].astype(BF16)
    part_up = weight_part(hidden_f, grad_pre, core, batch)
    grad_hidden_f = dot_rows(grad_pre, w_up)
    grad_scale_f = per_seq(grad_hidden_f * norm_f)
    grad_shift_f = per_seq(grad_hidden_f)
    grad_mixed = grad_out + norm_back(norm_f, inverse_f, grad_hidden_f * (1.0 + scale_f))
    grad_gate_a = per_seq(grad_mixed * branch_a)
    grad_branch_a = (gate_a * grad_mixed).astype(BF16)
    part_out = weight_part(attn_low, grad_branch_a, core, batch)
    grad_attn = dot_rows(grad_branch_a, w_out).astype(BF16)

    dq, dkv, dshort = backward_attention(plan, head_dim, grad_attn, queries, kv, short_kv, lse, 1)
    dkv = jnp.sum(dkv.astype(F32), axis=1)
    dshort = jnp.where(me < plan.short_blocks, jnp.sum(dshort.astype(F32), axis=1), 0.0)
    dshort = jnp.pad(dshort, ((0, 0), (0, frames - plan.short_rows), (0, 0)))
    grad_kv = jnp.concatenate([dkv, dshort], axis=1)

    def turned_back(rows):
        groups = rows.reshape(tokens, -1, 2, head_dim // 2)
        cosines = cos_table[:, None, : head_dim // 2]
        sines = sin_table[:, None, head_dim // 2 : head_dim]
        first, second = groups[:, :, 0], groups[:, :, 1]
        return jnp.stack(
            [first * cosines + second * sines, second * cosines - first * sines], axis=2
        ).reshape(tokens, width)

    grad_qkv = jnp.concatenate(
        [turned_back(dq.astype(F32)), turned_back(grad_kv[0]), grad_kv[1]], axis=1
    ).astype(BF16)
    part_qkv = weight_part(hidden_a, grad_qkv, core, batch)
    grad_hidden_a = dot_rows(grad_qkv, w_qkv)
    norm_a, inverse_a = normalize(residual)
    grad_scale_a = per_seq(grad_hidden_a * norm_a)
    grad_shift_a = per_seq(grad_hidden_a)
    grad_inputs = grad_mixed + norm_back(norm_a, inverse_a, grad_hidden_a * (1.0 + scale_a))
    grad_mods = jnp.concatenate(
        [grad_shift_a, grad_scale_a, grad_gate_a, grad_shift_f, grad_scale_f, grad_gate_f], axis=-1
    )
    biases = [jnp.sum(g.astype(F32), axis=0) for g in (grad_qkv, grad_branch_a, grad_pre, grad_ff)]

    mod_cols = mods.shape[1] // count
    bias_sizes = [bias.shape[0] // count for bias in biases]
    own = (jnp.arange(count) == me)[:, None]
    pieces = [
        grad_mods.reshape(seqs, count, mod_cols).transpose(1, 0, 2).reshape(count, -1),
        *[bias.reshape(count, -1) for bias in biases],
        jnp.where(
            own,
            time_act.astype(F32).reshape(seqs, count, -1).transpose(1, 0, 2).reshape(count, -1),
            0.0,
        ),
    ]
    flat = jnp.concatenate(pieces, axis=1)
    size = flat.shape[1]
    flat = jnp.pad(flat, ((0, 0), (0, -size % (8 * LANES))))
    sums = small_sums(flat.reshape(count, -1, LANES), batch, 2).reshape(batch, count, -1)
    mods_all = sums[:, :, : seqs * mod_cols].reshape(batch, count, seqs, mod_cols)
    mods_all = mods_all.transpose(0, 2, 1, 3).reshape(batch * seqs, -1)
    mine = lax.dynamic_index_in_dim(sums, me, axis=1, keepdims=False)
    grad_b_mod = jnp.sum(mine[:, : seqs * mod_cols].reshape(batch * seqs, mod_cols), axis=0)
    offset = seqs * mod_cols
    bias_total = jnp.sum(mine, axis=0)
    grad_biases = []
    for bias_size in bias_sizes:
        grad_biases.append(bias_total[offset : offset + bias_size])
        offset += bias_size
    times = mine[:, offset : offset + seqs * (width // count)].reshape(batch * seqs, -1)
    grad_w_mod = dot_frames(times.astype(BF16), mods_all.astype(BF16))
    own_mods = lax.dynamic_slice_in_dim(mods_all, lax.axis_index("batch") * seqs, seqs, axis=0)
    grad_silu = dot_rows(own_mods.astype(BF16), w_mod)
    grad_time = ordered(silu_pull(grad_silu)[0])

    rows = width // count
    split_down = part_down.reshape(count, -1, rows, width // 2)
    split_down = [split_down[:, i] for i in range(split_down.shape[1])]
    parts = jnp.concatenate(
        [p.reshape(count, rows, -1) for p in (part_qkv, part_out, part_up)] + split_down, axis=2
    )
    totals = reduce_weights(parts, 512, 3).astype(F32)
    ends = [3 * width // 2, 2 * width, 3 * width]
    grad_w_qkv, grad_w_out, grad_w_up, down = [
        jnp.concatenate([piece[0], piece[1]], axis=1) for piece in jnp.split(totals, ends, axis=2)
    ]
    down = down.reshape(rows, 2, -1, width // 2).transpose(2, 0, 1, 3)
    grad_w_down = down.reshape(-1, width)
    return (
        ordered(output.reshape(seqs, frames, width)),
        ordered(grad_inputs.reshape(seqs, frames, width)),
        grad_time,
        grad_w_mod,
        grad_b_mod,
        grad_w_qkv,
        grad_biases[0],
        grad_w_out,
        grad_biases[1],
        grad_w_up,
        grad_biases[2],
        grad_w_down,
        grad_biases[3],
    )


def solution(mesh):
    frame_spec, weight_spec = P("batch", "blk", None), P("blk", None)
    return jax.shard_map(
        on_device,
        mesh=mesh,
        in_specs=(frame_spec, P("batch", None), P("batch"), frame_spec) + (P(),) * 10,
        out_specs=(frame_spec, frame_spec, P("batch", None)) + (weight_spec, P("blk")) * 5,
        check_vma=False,
    )
```

```python
from functools import partial

import jax
import jax.numpy as jnp
from jax import lax
from jax.experimental import pallas as pl
from jax.experimental.pallas import tpu as pltpu
from jax.sharding import PartitionSpec as P

HEADS = 16
EPS = 1e-06
LANES = 128
SHORT = 16
MESH = pl.DeviceIdType.MESH
BF16 = jnp.bfloat16
F32 = jnp.float32
MIB = 1 << 20


def dot(left, right):
    return jnp.dot(left, right, preferred_element_type=F32)


def dot_rows(left, right):
    return lax.dot_general(left, right, (((1,), (1,)), ((), ())), preferred_element_type=F32)


def dot_frames(left, right):
    return lax.dot_general(left, right, (((0,), (0,)), ((), ())), preferred_element_type=F32)


def normalize(rows):
    mean = jnp.mean(rows, axis=-1, keepdims=True)
    centered = rows - mean
    inverse = lax.rsqrt(jnp.mean(centered * centered, axis=-1, keepdims=True) + EPS)
    return (centered * inverse, inverse)


def norm_back(normed, inverse, grad):
    return inverse * (
        grad
        - jnp.mean(grad, axis=-1, keepdims=True)
        - normed * jnp.mean(grad * normed, axis=-1, keepdims=True)
    )


def whole(shape):
    return pl.BlockSpec(shape, lambda *_: (0,) * len(shape))


def in_hbm():
    return pl.BlockSpec(memory_space=pltpu.HBM)


def rotate(rows, cos_table, sin_table, half):
    lane = lax.broadcasted_iota(jnp.int32, rows.shape, 1)
    partner = jnp.where(
        lax.rem(lane, 2 * half) < half,
        pltpu.roll(rows, LANES - half, 1),
        pltpu.roll(rows, half, 1),
    )
    return rows * cos_table + partner * sin_table


def pre_kernel(sizes, order, x_ref, time_ref, freqs, w_mod, b_mod, w_qkv, b_qkv, mods, acts, cos_out, sin_out, hidden_t, qkv, hidden):
    seqs, frames, width, half, mod_steps, span, qkv_span, cols = sizes
    step = pl.program_id(0)
    first_frame = lax.axis_index("blk") * frames

    @pl.when(step == 0)
    def _():
        shown = time_ref[...].astype(F32)
        shown = jnp.where(order[0] == 0, shown, jnp.concatenate([shown[1:2], shown[0:1]], axis=0))
        acts[...] = (shown / (1.0 + jnp.exp(-shown))).astype(BF16)
        frame = first_frame + lax.broadcasted_iota(jnp.int32, (frames, LANES), 0)
        angle = frame.astype(F32) * freqs[...]
        lane = lax.broadcasted_iota(jnp.int32, (frames, LANES), 1)
        cos_out[...] = jnp.cos(angle)
        sines = jnp.sin(angle)
        sin_out[...] = jnp.where(lax.rem(lane, 2 * half) < half, -sines, sines)

    @pl.when(step < mod_steps)
    def _():
        cols = pl.ds(pl.multiple_of(step * span, span), span)
        mods[:, cols] = dot(acts[...], w_mod[...]) + b_mod[cols][None].astype(F32)

    @pl.when(step == mod_steps)
    def _():
        for s in range(seqs):
            normed, _ = normalize(x_ref[order[s]].astype(F32))
            shift, scale = mods[s : s + 1, :width], mods[s : s + 1, width : 2 * width]
            hidden[s * frames : (s + 1) * frames, :] = (normed * (1.0 + scale) + shift).astype(BF16)
        hidden_t[...] = hidden[...].T

    @pl.when(step >= mod_steps)
    def _():
        at = pl.multiple_of((step - mod_steps) * qkv_span, qkv_span)
        rows = dot(hidden[...], w_qkv[...]) + b_qkv[pl.ds(at, qkv_span)][None].astype(F32)
        kind = (step - mod_steps) // (width // qkv_span)

        def store(s, c, part):
            start = c * LANES % cols
            qkv[c * LANES // cols, s * frames : (s + 1) * frames, start : start + LANES] = part

        @pl.when(kind < 2)
        def _():
            factor = jnp.where(kind == 0, (2.0 * half) ** (-0.5), 1.0)
            cosines, sines = cos_out[...] * factor, sin_out[...] * factor
            for s in range(seqs):
                for c in range(qkv_span // LANES):
                    part = rows[s * frames : (s + 1) * frames, c * LANES : (c + 1) * LANES]
                    store(s, c, rotate(part, cosines, sines, half).astype(BF16))

        @pl.when(kind == 2)
        def _():
            for s in range(seqs):
                for c in range(qkv_span // LANES):
                    part = rows[s * frames : (s + 1) * frames, c * LANES : (c + 1) * LANES]
                    store(s, c, part.astype(BF16))


def pre_attention(order, inputs, time_embed, w_mod, b_mod, w_qkv, b_qkv, cols):
    seqs, frames, width = inputs.shape
    tokens = seqs * frames
    half = width // HEADS // 2
    span, qkv_span = 512, 512
    mod_steps = 2 * width // span
    per_kind = width // qkv_span
    sizes = (seqs, frames, width, half, mod_steps, span, qkv_span, cols)
    freqs = 10000.0 ** (-jnp.arange(half, dtype=F32) / half)
    freqs = jnp.tile(freqs, LANES // half)[None]

    def at(i):
        return jnp.minimum(i, mod_steps - 1)

    def past(i):
        return jnp.maximum(i - mod_steps, 0)

    return pl.pallas_call(
        partial(pre_kernel, sizes),
        grid=(mod_steps + 3 * per_kind,),
        in_specs=[
            pl.BlockSpec(memory_space=pltpu.SMEM),
            whole(inputs.shape),
            whole((seqs, width)),
            whole((1, LANES)),
            pl.BlockSpec((width, span), lambda i: (0, at(i))),
            whole(b_mod.shape),
            pl.BlockSpec((width, qkv_span), lambda i: (0, past(i))),
            whole(b_qkv.shape),
        ],
        out_specs=[
            whole((seqs, 2 * width)),
            whole((seqs, width)),
            whole((frames, LANES)),
            whole((frames, LANES)),
            whole((width, tokens)),
            pl.BlockSpec(
                (qkv_span // cols, tokens, cols),
                lambda i: (lax.rem(past(i), per_kind), 0, past(i) // per_kind),
            ),
        ],
        out_shape=[
            jax.ShapeDtypeStruct((seqs, 2 * width), F32),
            jax.ShapeDtypeStruct((seqs, width), BF16),
            jax.ShapeDtypeStruct((frames, LANES), F32),
            jax.ShapeDtypeStruct((frames, LANES), F32),
            jax.ShapeDtypeStruct((width, tokens), BF16),
            jax.ShapeDtypeStruct((width // cols, tokens, 3 * cols), BF16),
        ],
        scratch_shapes=[pltpu.VMEM((tokens, width), BF16)],
        compiler_params=pltpu.CompilerParams(vmem_limit_bytes=40 * MIB),
        name="pre_attention",
    )(order, inputs, time_embed, freqs, w_mod, b_mod, w_qkv, b_qkv)


class Spot:
    def __init__(self, count):
        b, j = lax.axis_index("batch"), lax.axis_index("blk")
        self.b, self.j = b, j
        self.core, self.half = lax.rem(b, 2), b // 2
        self.near, self.far = lax.rem(j, 2), j // 2
        self.far_count = count // 2
        self.at_core = (self.half * 2 + 1 - self.core, j)
        self.at_x = ((1 - self.half) * 2 + self.core, j)
        self.at_near = (b, self.far * 2 + 1 - self.near)
        self.far_steps = [lax.rem(self.far + step, self.far_count) for step in range(1, self.far_count)]
        self.at_far = [(b, step * 2 + self.near) for step in self.far_steps]


def add_into(target, other):
    target[...] = (target[...].astype(F32) + other.astype(F32)).astype(BF16)


class Plan:
    def __init__(self, count, frames, width):
        self.count = count
        self.frames = frames
        self.width = width
        self.groups = min(max(count // 2, 1), 4)
        self.cols = width // self.groups
        self.splits = count // self.groups
        self.total = count * frames
        self.short = self.total // SHORT
        self.short_rows = min(self.short, frames)
        self.short_blocks = -(-self.short // frames)


def greet(devices, barrier):
    for device in devices:
        pl.semaphore_signal(barrier, inc=1, device_id=device, device_id_type=MESH)
    pl.semaphore_wait(barrier, len(devices))


def push(src, dst, sems, index, device):
    copy = pltpu.make_async_remote_copy(
        src_ref=src, dst_ref=dst, send_sem=sems.at[(0,) + index], recv_sem=sems.at[(1,) + index],
        device_id=device, device_id_type=MESH,
    )
    copy.start()
    return copy


def local(src, dst, sem):
    copy = pltpu.make_async_copy(src, dst, sem)
    copy.start()
    return copy


def stacked(rows, head_dim):
    lane = lax.broadcasted_iota(jnp.int32, rows.shape, 1)
    heads = LANES // head_dim
    return jnp.concatenate(
        [jnp.where(lane // head_dim == h, rows, jnp.zeros_like(rows)) for h in range(heads)], axis=0
    )


def unstacked(turned, frames, head_dim):
    heads = LANES // head_dim
    return jnp.concatenate(
        [
            turned[h * head_dim : (h + 1) * head_dim, h * frames : (h + 1) * frames]
            for h in range(heads)
        ],
        axis=0,
    ).T


def attend(queries, keys, values_t, head_dim):
    frames = queries.shape[0]
    scores = dot_rows(keys, stacked(queries, head_dim))
    top = jnp.max(scores, axis=0, keepdims=True)
    weights = jnp.exp(scores - top)
    total = jnp.sum(weights, axis=0, keepdims=True)
    out = dot(values_t, weights.astype(BF16)) / total
    return unstacked(out, frames, head_dim).astype(BF16), top + jnp.log(total)


def attend_back(queries, grads, lse, keys, keys_t, values, head_dim):
    frames = queries.shape[0]
    q_heads, g_heads = stacked(queries, head_dim), stacked(grads, head_dim)
    probs = jnp.exp(dot_rows(keys, q_heads) - lse)
    grad_probs = dot_rows(values, g_heads)
    delta = jnp.sum(probs * grad_probs, axis=0, keepdims=True)
    grad_scores = (probs * (grad_probs - delta)).astype(BF16)
    grad_values = dot(probs.astype(BF16), g_heads)
    grad_keys = dot(grad_scores, q_heads)
    grad_queries = unstacked(dot(keys_t, grad_scores), frames, head_dim) * head_dim ** (-0.5)
    return grad_queries.astype(BF16), grad_keys, grad_values


def gelu_both(z):
    scale = (2.0 / 3.141592653589793) ** 0.5
    square = z * z
    inner = jnp.tanh(scale * z * (1.0 + 0.044715 * square))
    half = 0.5 * (1.0 + inner)
    slope = half + 0.5 * z * (1.0 - inner * inner) * (scale * (1.0 + 3.0 * 0.044715 * square))
    return z * half, slope


def core_kernel(plan, head_dim, chunk, block, *refs):
    (order, rows, hidden_t, x_ref, ct_ref, acts, b_mod_in, b_out_in, b_up_in, b_down_in, w_mod_hbm, w_out_hbm, w_up_hbm, w_down_hbm,
     output, grad_mixed, stats, dq_out, dkv_out, dshort_out, near_sums, other_t,
     w_mod, w_out, w_up, w_down, mods, attn, q_buf, kv_buf, short_buf, lse, o_buf, long_vt, short_vt,
     mixed, branch_a, hidden_f, grad_ff, grad_pre, grad_br, attn_t, hid_t, act_t, both_ff, both_pre, both_br,
     branch_f, grad_hid, parts, x_buf, grads, g_buf, dlong, dsmall, dshort_buf,
     w_sems, m_sems, q_sems, k_sems, s_sems, o_sems, h_sems, e_sems,
     bg_sems, bq_sems, bk_sems, bs_sems, x_sems, n_sems) = refs
    n, g, f, cols, width = plan.count, plan.groups, plan.frames, plan.cols, plan.width
    tokens, hidden = 2 * f, w_up.shape[1]
    half_width, half_hidden = width // 2, hidden // 2
    spot = Spot(n)
    b, me, core = spot.b, spot.j, spot.core
    group, split = lax.rem(me, g), me // g
    others = [lax.rem(me + step, n) for step in range(1, n)]
    mates = [split * g + lax.rem(group + step, g) for step in range(1, g)]
    seqs = [slice(0, f), slice(f, tokens)]
    swapped = order[0] != 0
    b_mod, b_out, b_up, b_down = [vec[...][None] for vec in (b_mod_in, b_out_in, b_up_in, b_down_in)]

    weights = [
        local(w_out_hbm, w_out, w_sems.at[0]),
        local(w_up_hbm, w_up, w_sems.at[1]),
        local(w_down_hbm, w_down, w_sems.at[2]),
    ]

    def load_mods(i):
        src = w_mod_hbm.at[:, 2 * width + i * half_width : 2 * width + (i + 1) * half_width]
        return local(src, w_mod.at[i % 2], m_sems.at[i])

    mod_copies = [load_mods(0), load_mods(1)]
    greet(
        [(b, peer) for peer in others] + [spot.at_core, spot.at_x], pltpu.get_barrier_semaphore()
    )

    waits = []
    for step, peer in enumerate(others):
        src = rows.at[lax.rem(peer, g), 0:f, cols : 3 * cols]
        waits.append(push(src, kv_buf.at[me], k_sems, (step,), (b, peer)))
    for blk in range(plan.short_blocks):

        @pl.when(me == blk)
        def _():
            for step, peer in enumerate(others):
                src = rows.at[lax.rem(peer, g), f : f + plan.short_rows, cols : 3 * cols]
                push(src, short_buf.at[blk], s_sems, (blk, step), (b, peer))

    for step, peer in enumerate(mates):
        src = rows.at[lax.rem(peer, g), :, 0:cols]
        waits.append(push(src, q_buf.at[group], q_sems, (step,), (b, peer)))
    waits.append(push(hidden_t, other_t, h_sems, (), spot.at_core))
    kv_buf[me] = rows[group, 0:f, cols : 3 * cols]
    q_buf[group] = rows[group, :, 0:cols]

    for i in range(8):
        mod_copies[i].wait()
        piece = slice(2 * width + i * half_width, 2 * width + (i + 1) * half_width)
        mods[:, i * half_width : (i + 1) * half_width] = (
            dot(acts[...], w_mod[i % 2]) + b_mod[:, piece].astype(F32)
        )
        if i + 2 < 8:
            mod_copies.append(load_mods(i + 2))

    def mod(i, s):
        return mods[s : s + 1, i * width : (i + 1) * width]

    for s, span in enumerate(seqs):
        grad_ff[span] = (mod(3, s) * ct_ref[order[s]].astype(F32)).astype(BF16)

    def core_half(which, size):
        return pl.ds(pl.multiple_of(which * size, LANES), size)

    def to_core(src, dst, index):
        return push(src, dst, e_sems, (index,), spot.at_core)

    swap_ff = to_core(grad_ff.at[:, core_half(1 - core, half_width)], both_ff.at[1], 0)
    both_ff[0] = grad_ff[:, core_half(core, half_width)]
    for copy in waits:
        copy.wait()
    for blk in range(plan.short_blocks):

        @pl.when(me == blk)
        def _():
            short_buf[blk] = rows[group, f : f + plan.short_rows, cols : 3 * cols]
            for step, peer in enumerate(others):
                src = rows.at[lax.rem(peer, g), f : f + plan.short_rows, cols : 3 * cols]
                pltpu.make_async_copy(src, src, s_sems.at[0, blk, step]).wait()

        for step, peer in enumerate(others):

            @pl.when(lax.rem(blk + step + 1, n) == me)
            def _():
                dst = short_buf.at[blk]
                pltpu.make_async_copy(dst, dst, s_sems.at[1, blk, step]).wait()

    long_vt[...] = kv_buf[:, :, cols:].reshape(plan.total, cols).T
    short_vt[...] = short_buf[:, :, cols:].reshape(plan.short, cols).T
    sends = []

    def cols_of(which):
        return pl.ds(pl.multiple_of(which * cols, LANES), cols)

    for step in range(g):
        slot = lax.rem(group + 1 + step, g)
        for u in range(cols // LANES):
            lanes = slice(u * LANES, (u + 1) * LANES)
            keys = kv_buf[:, :, lanes].reshape(plan.total, LANES)
            o_buf[slot, :f, lanes], lse[slot, u : u + 1] = attend(
                q_buf[slot, :f, lanes], keys, long_vt[lanes], head_dim
            )
            keys = short_buf[:, :, lanes].reshape(plan.short, LANES)
            row = cols // LANES + u
            o_buf[slot, f:, lanes], lse[slot, row : row + 1] = attend(
                q_buf[slot, f:, lanes], keys, short_vt[lanes], head_dim
            )
        if step == g - 1:
            attn[:, cols_of(group)] = o_buf[slot]
        else:
            dst = attn.at[:, cols_of(group)]
            sends.append(push(o_buf.at[slot], dst, o_sems, (step,), (b, mates[step])))
    long_kt, short_kt = long_vt, short_vt
    long_kt[...] = kv_buf[:, :, :cols].reshape(plan.total, cols).T
    short_kt[...] = short_buf[:, :, :cols].reshape(plan.short, cols).T
    for copy in sends:
        copy.wait()

    mine, theirs = slice(0, tokens), slice(tokens, 2 * tokens)
    weights[0].wait()
    attn_t[:, mine] = attn[...].T
    swap_attn = to_core(attn_t.at[:, mine], attn_t.at[:, theirs], 1)
    branch_a[...] = dot(attn[...], w_out[...]) + b_out.astype(F32)
    for s, span in enumerate(seqs):
        mixed[span] = x_ref[order[s]].astype(F32) + mod(0, s) * branch_a[span]
        normed, _ = normalize(mixed[span])
        hidden_f[span] = (normed * (1.0 + mod(2, s)) + mod(1, s)).astype(BF16)
    hid_t[:, mine] = hidden_f[...].T
    swap_hid = to_core(hid_t.at[:, mine], hid_t.at[:, theirs], 2)
    weights[1].wait()
    weights[2].wait()
    swap_act = []
    for i in range(hidden // block):
        span = slice(i * block, (i + 1) * block)
        act, slope = gelu_both(dot(hidden_f[...], w_up[:, span]) + b_up[:, span].astype(F32))
        act = act.astype(BF16)
        act_t[span, mine] = act.T
        swap_act.append(to_core(act_t.at[span, mine], act_t.at[span, theirs], 5 + i))
        forward = dot(act, w_down[span, :])
        grad = (dot_rows(grad_ff[...], w_down[span, :]) * slope).astype(BF16)
        grad_pre[:, span] = grad
        row, start = 9 + i * block // width, i * block % width
        stats[row : row + 1, start : start + block] = jnp.sum(grad.astype(F32), axis=0, keepdims=True)
        back = dot_rows(grad, w_up[:, span])
        if i == 0:
            branch_f[...] = forward + b_down.astype(F32)
            grad_hid[...] = back
        else:
            branch_f[...] += forward
            grad_hid[...] += back
    swap_pre = to_core(grad_pre.at[:, core_half(1 - core, half_hidden)], both_pre.at[1], 3)
    both_pre[0] = grad_pre[:, core_half(core, half_hidden)]

    n_rows = width // n
    chunks, half_chunk = parts.shape[2] // chunk, chunk // 2
    x_copies, near_copies = {}, {}

    def half_of(k, which):
        return pl.ds(pl.multiple_of(k * chunk + which * half_chunk, LANES), half_chunk)

    def start_x(k):
        src = parts.at[:, :, half_of(k, 1 - spot.half)]
        x_copies[k] = push(src, x_buf.at[k], x_sems, (k,), spot.at_x)

    def finish_x(k):
        x_copies[k].wait()
        add_into(x_buf.at[k], parts[:, :, half_of(k, spot.half)])
        src = x_buf.at[k].reshape(spot.far_count, 2, -1, half_chunk).at[:, 1 - spot.near]
        near_copies[k] = push(src, near_sums.at[k], n_sems, (k,), spot.at_near)

    def finish_near(k):
        near_copies[k].wait()
        own = x_buf.at[k].reshape(spot.far_count, 2, -1, half_chunk)[:, spot.near]
        add_into(near_sums.at[k], own)

    swap_ff.wait()
    for copy in swap_act:
        copy.wait()
    layers = hidden // width
    down = dot(act_t[...], both_ff[...].reshape(2 * tokens, half_width))
    down = down.astype(BF16).reshape(n, layers, n_rows, half_width)
    for i in range(layers):
        parts[:, :, i * half_width : (i + 1) * half_width] = down[:, i]
        start_x(i)
    swap_hid.wait()
    swap_pre.wait()
    for i in range(layers):
        grad = both_pre[:, :, i * half_width : (i + 1) * half_width].reshape(2 * tokens, half_width)
        up = dot(hid_t[...], grad).astype(BF16).reshape(n, n_rows, half_width)
        at = layers + i
        parts[:, :, at * half_width : (at + 1) * half_width] = up
        if i == 0:
            start_x(layers)

    for s, span in enumerate(seqs):
        grad_out = ct_ref[order[s]].astype(F32)
        branch, grad = branch_f[span], grad_hid[span]
        normed, inverse = normalize(mixed[span])
        stats[6 + s : 7 + s] = jnp.sum(grad_out * branch, axis=0, keepdims=True)
        stats[4 + s : 5 + s] = jnp.sum(grad * normed, axis=0, keepdims=True)
        stats[2 + s : 3 + s] = jnp.sum(grad, axis=0, keepdims=True)
        total = grad_out + norm_back(normed, inverse, grad * (1.0 + mod(2, s)))
        grad_mixed[span] = total
        stats[s : s + 1] = jnp.sum(total * branch_a[span], axis=0, keepdims=True)
        grad_br[span] = (mod(0, s) * total).astype(BF16)
    grads[...] = dot_rows(grad_br[...], w_out[...]).astype(BF16)
    waits = []
    for step, peer in enumerate(mates):
        src = grads.at[:, cols_of(lax.rem(peer, g))]
        waits.append(push(src, g_buf.at[group], bg_sems, (step,), (b, peer)))
    g_buf[group] = grads[:, cols_of(group)]
    swap_br = to_core(grad_br.at[:, core_half(1 - core, half_width)], both_br.at[1], 4)
    both_br[0] = grad_br[:, core_half(core, half_width)]
    first = mixed[seqs[0]] + mod(3, 0) * branch_f[seqs[0]]
    second = mixed[seqs[1]] + mod(3, 1) * branch_f[seqs[1]]
    output[0] = jnp.where(swapped, second, first)
    output[1] = jnp.where(swapped, first, second)
    last_row = 9 + layers
    stats[8:9] = jnp.sum(grad_br[...].astype(F32), axis=0, keepdims=True)
    stats[last_row : last_row + 1] = jnp.sum(grad_ff[...].astype(F32), axis=0, keepdims=True)
    swap_attn.wait()
    swap_br.wait()
    out_part = dot(attn_t[...], both_br[...].reshape(2 * tokens, half_width))
    parts[:, :, 2 * layers * half_width :] = out_part.astype(BF16).reshape(n, n_rows, half_width)
    for copy in waits:
        copy.wait()

    sends = []
    dq_buf = o_buf
    for step in range(g):
        slot = lax.rem(group + 1 + step, g)
        for u in range(cols // LANES):
            lanes = slice(u * LANES, (u + 1) * LANES)
            high = slice(cols + u * LANES, cols + (u + 1) * LANES)
            for span, kv, kt, row, acc in (
                (seqs[0], kv_buf, long_kt, u, dlong),
                (seqs[1], short_buf, short_kt, cols // LANES + u, dsmall),
            ):
                size = acc.shape[1]
                dq, dk, dv = attend_back(
                    q_buf[slot, span, lanes],
                    g_buf[slot, span, lanes],
                    lse[slot, row : row + 1],
                    kv[:, :, lanes].reshape(size, LANES),
                    kt[lanes],
                    kv[:, :, high].reshape(size, LANES),
                    head_dim,
                )
                dq_buf[slot, span, lanes] = dq
                if step == 0:
                    acc[0, :, lanes] = dk
                    acc[1, :, lanes] = dv
                else:
                    acc[0, :, lanes] += dk
                    acc[1, :, lanes] += dv
        if step == g - 1:
            dq_out[:, cols_of(group)] = dq_buf[slot]
        else:
            dst = dq_out.at[:, cols_of(group)]
            sends.append(push(dq_buf.at[slot], dst, bq_sems, (step,), (b, mates[step])))
        if step == 0:
            finish_x(0)
            start_x(3)
        if step == g // 2:
            finish_x(1)
            start_x(4)
    for which in range(2):
        made = slice(which * cols, (which + 1) * cols)
        kv_buf[:, :, made] = dlong[which].astype(BF16).reshape(n, f, cols)
    for step, peer in enumerate(others):
        for which in range(2):
            dst = dkv_out.at[which, split, :, cols_of(group)]
            sends.append(push(kv_buf.at[peer, :, which * cols : (which + 1) * cols], dst, bk_sems, (which, step), (b, peer)))
    for which in range(2):
        dkv_out[which, split, :, cols_of(group)] = kv_buf[me, :, which * cols : (which + 1) * cols]
    for blk in range(plan.short_blocks):
        span = slice(blk * plan.short_rows, (blk + 1) * plan.short_rows)
        dshort_buf[blk] = dsmall[:, span].astype(BF16)
        dst = dshort_out.at[:, split, :, cols_of(group)]
        for step, peer in enumerate(others):

            @pl.when(peer == blk)
            def _():
                push(dshort_buf.at[blk], dst, bs_sems, (step,), (b, peer)).wait_send()

        @pl.when(me == blk)
        def _():
            dshort_out[:, split, :, cols_of(group)] = dshort_buf[blk]
            for step in range(n - 1):
                pltpu.make_async_copy(dshort_buf.at[blk], dshort_buf.at[blk], bs_sems.at[1, step]).wait()

    for k in range(chunks):
        if k >= 2:
            finish_x(k)
        if k >= 1:
            finish_near(k - 1)
    finish_near(chunks - 1)
    for copy in sends:
        copy.wait()


def core(plan, head_dim, chunk, operands, collective_id):
    n, g, f, cols, width = plan.count, plan.groups, plan.frames, plan.cols, plan.width
    tokens, hidden, block = 2 * f, operands[12].shape[1], 512
    rows, layers = width // n, hidden // width
    wide = f * (LANES // head_dim)
    chunks = (width // 2 + hidden) // chunk
    vmem, smem = pl.BlockSpec(memory_space=pltpu.VMEM), pl.BlockSpec(memory_space=pltpu.SMEM)

    def sems(*shape):
        return pltpu.SemaphoreType.DMA(shape)

    def low(*shape):
        return pltpu.VMEM(shape, BF16)

    def high(*shape):
        return pltpu.VMEM(shape, F32)

    return pl.pallas_call(
        partial(core_kernel, plan, head_dim, chunk, block),
        in_specs=[smem] + [vmem] * 9 + [in_hbm()] * 4,
        out_specs=[vmem] * 8,
        out_shape=[
            jax.ShapeDtypeStruct((2, f, width), F32),
            jax.ShapeDtypeStruct((tokens, width), F32),
            jax.ShapeDtypeStruct((10 + layers, width), F32),
            jax.ShapeDtypeStruct((tokens, width), BF16),
            jax.ShapeDtypeStruct((2, plan.splits, f, width), BF16),
            jax.ShapeDtypeStruct((2, plan.splits, plan.short_rows, width), BF16),
            jax.ShapeDtypeStruct((chunks, n // 2, rows, chunk // 2), BF16),
            jax.ShapeDtypeStruct((width, tokens), BF16),
        ],
        scratch_shapes=[
            low(2, width, width // 2),
            low(width, width),
            low(width, hidden),
            low(hidden, width),
            high(2, 4 * width),
            low(tokens, width),
            low(g, tokens, cols),
            low(n, f, 2 * cols),
            low(plan.short_blocks, plan.short_rows, 2 * cols),
            high(g, 2 * (cols // LANES), wide),
            low(g, tokens, cols),
            low(cols, plan.total),
            low(cols, plan.short),
            high(tokens, width),
            high(tokens, width),
            low(tokens, width),
            low(tokens, width),
            low(tokens, hidden),
            low(tokens, width),
            low(width, 2 * tokens),
            low(width, 2 * tokens),
            low(hidden, 2 * tokens),
            low(2, tokens, width // 2),
            low(2, tokens, hidden // 2),
            low(2, tokens, width // 2),
            high(tokens, width),
            high(tokens, width),
            low(n, rows, chunks * chunk),
            low(chunks, n, rows, chunk // 2),
            low(tokens, width),
            low(g, tokens, cols),
            high(2, plan.total, cols),
            high(2, plan.short, cols),
            low(plan.short_blocks, 2, plan.short_rows, cols),
            sems(3),
            sems(8),
            sems(2, g - 1),
            sems(2, n - 1),
            sems(2, plan.short_blocks, n - 1),
            sems(2, g - 1),
            sems(2),
            sems(2, 5 + hidden // block),
            sems(2, g - 1),
            sems(2, g - 1),
            sems(2, 2, n - 1),
            sems(2, n - 1),
            sems(2, chunks),
            sems(2, chunks),
        ],
        compiler_params=pltpu.CompilerParams(
            collective_id=collective_id, has_side_effects=True, vmem_limit_bytes=62 * MIB
        ),
        name="core",
    )(*operands)


def tail_kernel(plan, sizes, *refs):
    (order, dq, dkv, dshort, hidden_t, other_t, x_ref, mods, grad_mixed, cos_ref, sin_ref, stats, near_sums, acts, time_ref, w_hbm, w_mod_hbm,
     totals, small_all, grad_inputs, grad_time,
     own_mods, w_mod, w_mod_sems, w_qkv, grad_qkv, both_grads, both_hidden, parts, far_one, a_one, a_two, b_one, b_two, far_two, small, small_in, mine,
     w_sem, core_sems, f1_sems, a1, a2, b1, b2, f2_sems, x_sems, c_sems, small_one, small_two, small_three) = refs
    half_dim, chunk_one, chunk, batch = sizes
    n, f = plan.count, plan.frames
    tokens, width = dq.shape
    rows = width // n
    own_cols = 3 * width // 2
    spot = Spot(n)
    b, j, core, half = spot.b, spot.j, spot.core, spot.half
    along = [(b, lax.rem(j + step, n)) for step in range(1, n)]
    across = [(lax.rem(b + step, batch), j) for step in range(1, batch)]
    weight_copy = local(w_hbm, w_qkv, w_sem)
    strip = w_mod.shape[1]

    def load_strip(i):
        return local(w_mod_hbm.at[i * strip : (i + 1) * strip], w_mod.at[i % 2], w_mod_sems.at[i % 2])

    strips = [load_strip(0), load_strip(1)]
    greet(along + across, pltpu.get_barrier_semaphore())

    def to_all(where, which):
        place = totals.at[core, :, where]
        return [
            push(place, place, x_sems, (which,), spot.at_x),
            push(place, place, c_sems, (2 * which,), spot.at_core),
        ]

    def forward(where, which):
        place = totals.at[core, :, where]
        return push(place, place, c_sems, (2 * which + 1,), spot.at_core)

    chunks_one, half_one = near_sums.shape[0], chunk_one // 2
    far_copies, last, sent = {}, [], {}
    for k in range(chunks_one):
        for step in range(spot.far_count - 1):
            far_copies[k, step] = push(
                near_sums.at[k, spot.far_steps[step]], far_one.at[k, step], f1_sems, (k, step), spot.at_far[step]
            )

    def one_cols(k, which):
        return pl.ds(pl.multiple_of(k * chunk_one + which * half_one, LANES), half_one)

    def finish_one_far(k):
        total = near_sums[k, spot.far].astype(F32)
        for step in range(spot.far_count - 1):
            far_copies[k, step].wait()
            total = total + far_one[k, step].astype(F32)
        totals[core, :, one_cols(k, half)] = total.astype(BF16)
        sent[k] = to_all(one_cols(k, half), k)

    def finish_one_x(k):
        sent[k][0].wait()
        last.append(sent[k][1])
        last.append(forward(one_cols(k, 1 - half), k))

    no_short = j >= plan.short_blocks
    grad_key = jnp.sum(dkv[0].astype(F32), axis=0)
    grad_value = jnp.sum(dkv[1].astype(F32), axis=0)
    short_key = jnp.where(no_short, 0.0, jnp.sum(dshort[0].astype(F32), axis=0))
    short_value = jnp.where(no_short, 0.0, jnp.sum(dshort[1].astype(F32), axis=0))
    for c in range(width // LANES):
        lanes = slice(c * LANES, (c + 1) * LANES)
        for s in range(2):
            span = slice(s * f, (s + 1) * f)
            turned = rotate(dq[span, lanes].astype(F32), cos_ref[...], -sin_ref[...], half_dim)
            grad_qkv[span, lanes] = turned.astype(BF16)
        lanes_k = slice(width + c * LANES, width + (c + 1) * LANES)
        turned = rotate(grad_key[:, lanes], cos_ref[...], -sin_ref[...], half_dim)
        grad_qkv[:f, lanes_k] = turned.astype(BF16)
        turned = rotate(
            short_key[:, lanes], cos_ref[: plan.short_rows], -sin_ref[: plan.short_rows], half_dim
        )
        grad_qkv[f : f + plan.short_rows, lanes_k] = turned.astype(BF16)
    grad_qkv[:f, 2 * width :] = grad_value.astype(BF16)
    grad_qkv[f : f + plan.short_rows, 2 * width :] = short_value.astype(BF16)
    if plan.short_rows < f:
        grad_qkv[f + plan.short_rows :, width:] = jnp.zeros((f - plan.short_rows, 2 * width), BF16)

    def core_half(which):
        return pl.ds(pl.multiple_of(which * own_cols, LANES), own_cols)

    swap = push(grad_qkv.at[:, core_half(1 - core)], both_grads.at[1], core_sems, (), spot.at_core)
    both_grads[0] = grad_qkv[:, core_half(core)]
    both_hidden[:, :tokens] = hidden_t[...]
    both_hidden[:, tokens:] = other_t[...]
    swap.wait()

    pairs = own_cols // chunk // 2
    half_chunk = chunk // 2
    base_two = chunks_one * chunk_one
    parts4 = parts.reshape(spot.far_count, 2, rows, own_cols)
    stage_one, stage_two, stage_far, stage_x = {}, {}, {}, {}

    def part_cols(k, second, which):
        return pl.ds(
            pl.multiple_of((k + pairs * second) * chunk + which * half_chunk, LANES), half_chunk
        )

    def total_cols(k, second, which):
        return pl.ds(
            pl.multiple_of(base_two + (k + pairs * second) * chunk + which * half_chunk, LANES), half_chunk
        )

    def start_one(k):
        for second in range(2):
            cols = slice((k + pairs * second) * chunk, (k + pairs * second + 1) * chunk)
            both = both_grads[:, :, cols].reshape(2 * tokens, chunk)
            parts[:, :, cols] = dot(both_hidden[...], both).astype(BF16).reshape(n, rows, chunk)
            if second == 0:
                src = parts.at[:, :, part_cols(k, 0, 1 - half)]
                stage_one[k, 0] = push(src, a_one.at[k], a1, (k,), spot.at_x)
            else:
                src = parts4.at[:, 1 - spot.near, :, cols]
                stage_one[k, 1] = push(src, b_one.at[k], b1, (k,), spot.at_near)

    def finish_one(k):
        stage_one[k, 0].wait()
        add_into(a_one.at[k], parts[:, :, part_cols(k, 0, half)])
        src = a_one.at[k].reshape(spot.far_count, 2, rows, half_chunk).at[:, 1 - spot.near]
        stage_two[k, 0] = push(src, a_two.at[k], a2, (k,), spot.at_near)
        stage_one[k, 1].wait()
        cols = slice((k + pairs) * chunk, (k + pairs + 1) * chunk)
        add_into(b_one.at[k], parts4[:, spot.near, :, cols])
        src = b_one.at[k, :, :, pl.ds(pl.multiple_of((1 - half) * half_chunk, LANES), half_chunk)]
        stage_two[k, 1] = push(src, b_two.at[k], b2, (k,), spot.at_x)

    def finish_two(k):
        stage_two[k, 0].wait()
        own = a_one.at[k].reshape(spot.far_count, 2, rows, half_chunk)[:, spot.near]
        add_into(a_two.at[k], own)
        stage_two[k, 1].wait()
        own = b_one[k, :, :, pl.ds(pl.multiple_of(half * half_chunk, LANES), half_chunk)]
        add_into(b_two.at[k], own)
        for second, buf in enumerate((a_two, b_two)):
            for step in range(spot.far_count - 1):
                stage_far[k, second, step] = push(
                    buf.at[k, spot.far_steps[step]],
                    far_two.at[second, k, step],
                    f2_sems,
                    (second, k, step),
                    spot.at_far[step],
                )

    def finish_far(k):
        for second, buf in enumerate((a_two, b_two)):
            total = buf[k, spot.far].astype(F32)
            for step in range(spot.far_count - 1):
                stage_far[k, second, step].wait()
                total = total + far_two[second, k, step].astype(F32)
            totals[core, :, total_cols(k, second, half)] = total.astype(BF16)
            which = chunks_one + second * pairs + k
            stage_x[k, second] = to_all(total_cols(k, second, half), which)

    def finish_x(k):
        for second in range(2):
            stage_x[k, second][0].wait()
            last.append(stage_x[k, second][1])
            which = chunks_one + second * pairs + k
            last.append(forward(total_cols(k, second, 1 - half), which))

    for k in range(pairs):
        start_one(k)

    weight_copy.wait()
    grad_hidden = dot_rows(grad_qkv[...], w_qkv[...])
    shift_rows, scale_rows, made = [], [], []
    for s in range(2):
        span = slice(s * f, (s + 1) * f)
        normed, inverse = normalize(x_ref[order[s]].astype(F32))
        grad = grad_hidden[span]
        shift_rows.append(jnp.sum(grad, axis=0, keepdims=True))
        scale_rows.append(jnp.sum(grad * normed, axis=0, keepdims=True))
        scaled = grad * (1.0 + mods[s : s + 1, width : 2 * width])
        made.append(grad_mixed[span] + norm_back(normed, inverse, scaled))
    grad_inputs[0] = jnp.where(order[0] == 0, made[0], made[1])
    grad_inputs[1] = jnp.where(order[0] == 0, made[1], made[0])
    bias = jnp.sum(grad_qkv[...].astype(F32), axis=0, keepdims=True)
    bias_rows = [bias[:, i * width : (i + 1) * width] for i in range(3)]
    kept = [stats[i : i + 1] for i in range(stats.shape[0])]
    small[...] = jnp.zeros_like(small)
    shown = jnp.where(j == 0, acts[...].astype(F32), 0.0)
    time_rows = [shown[0:1], shown[1:2]]
    for i, row in enumerate(shift_rows + scale_rows + kept[:8] + bias_rows + kept[8:] + time_rows):
        for c in range(width // LANES):
            small[i, c : c + 1] = row[:, c * LANES : (c + 1) * LANES]

    per = small.shape[0] // n
    copies = []
    for step, device in enumerate(along):
        copies.append(push(small.at[pl.ds(device[1] * per, per)], small_in.at[step], small_one, (step,), device))
    finish_one(0)
    for k in range(chunks_one):
        finish_one_far(k)
    total = small[pl.ds(j * per, per)]
    for step in range(n - 1):
        copies[step].wait()
        total = total + small_in[step]
    mine[...] = total
    own_slice = small_all.at[b, pl.ds(j * per, per)]
    own_slice[...] = total
    copies = []
    for step, device in enumerate(along):
        copies.append(push(mine, own_slice, small_two, (step,), device))
    for k in range(1, pairs):
        finish_one(k)
        finish_two(k - 1)
    for copy in copies:
        copy.wait()
    for step, device in enumerate(across):
        last.append(push(small_all.at[b], small_all.at[b], small_three, (step,), device))
    finish_two(pairs - 1)
    for k in range(chunks_one):
        finish_one_x(k)

    for i in range(12):
        for c in range(width // LANES):
            start = i // 2 * width + c * LANES
            own_mods[i % 2 : i % 2 + 1, start : start + LANES] = small_all[b, i, c : c + 1]
    shown = time_ref[...].astype(F32)
    sigmoid = 1.0 / (1.0 + jnp.exp(-shown))
    slope = sigmoid * (1.0 + shown * (1.0 - sigmoid))
    own = own_mods[...].astype(BF16)
    for i in range(width // strip):
        strips[i].wait()
        grad = dot_rows(own, w_mod[i % 2])
        grad = jnp.where(order[0] == 0, grad, jnp.concatenate([grad[1:2], grad[0:1]], axis=0))
        grad_time[:, i * strip : (i + 1) * strip] = grad * slope[:, i * strip : (i + 1) * strip]
        if i + 2 < width // strip:
            strips.append(load_strip(i + 2))
    for k in range(pairs):
        finish_far(k)
        if k >= 1:
            finish_x(k - 1)
    finish_x(pairs - 1)
    for copy in last:
        copy.wait()


def tail(plan, chunk_one, chunk, batch, half_dim, operands, collective_id):
    dq, near_sums, w_qkv = operands[1], operands[12], operands[15]
    n = plan.count
    tokens, width = dq.shape
    rows, own_cols = width // n, 3 * width // 2
    chunks_one, pairs, far = near_sums.shape[0], own_cols // chunk // 2, n // 2
    columns = chunks_one * chunk_one + own_cols
    small_rows = -(-21 // n) * n
    per = small_rows // n
    tile = (width // LANES, LANES)
    vmem = pl.BlockSpec(memory_space=pltpu.VMEM)

    def sems(*shape):
        return pltpu.SemaphoreType.DMA(shape)

    return pl.pallas_call(
        partial(tail_kernel, plan, (half_dim, chunk_one, chunk, batch)),
        in_specs=[pl.BlockSpec(memory_space=pltpu.SMEM)] + [vmem] * 14 + [in_hbm()] * 2,
        out_specs=[vmem] * 4,
        out_shape=[
            jax.ShapeDtypeStruct((2, rows, columns), BF16),
            jax.ShapeDtypeStruct((batch, small_rows) + tile, F32),
            jax.ShapeDtypeStruct((2, tokens // 2, width), F32),
            jax.ShapeDtypeStruct((2, width), F32),
        ],
        scratch_shapes=[
            pltpu.VMEM((2, 6 * width), F32),
            pltpu.VMEM((2, LANES, 6 * width), BF16),
            sems(2),
            pltpu.VMEM(w_qkv.shape, BF16),
            pltpu.VMEM((tokens, 3 * width), BF16),
            pltpu.VMEM((2, tokens, own_cols), BF16),
            pltpu.VMEM((width, 2 * tokens), BF16),
            pltpu.VMEM((n, rows, own_cols), BF16),
            pltpu.VMEM((chunks_one, far - 1, rows, chunk_one // 2), BF16),
            pltpu.VMEM((pairs, n, rows, chunk // 2), BF16),
            pltpu.VMEM((pairs, far, rows, chunk // 2), BF16),
            pltpu.VMEM((pairs, far, rows, chunk), BF16),
            pltpu.VMEM((pairs, far, rows, chunk // 2), BF16),
            pltpu.VMEM((2, pairs, far - 1, rows, chunk // 2), BF16),
            pltpu.VMEM((small_rows,) + tile, F32),
            pltpu.VMEM((n - 1, per) + tile, F32),
            pltpu.VMEM((per,) + tile, F32),
            sems(),
            sems(2),
            sems(2, chunks_one, far - 1),
            sems(2, pairs),
            sems(2, pairs),
            sems(2, pairs),
            sems(2, pairs),
            sems(2, 2, pairs, far - 1),
            sems(2, chunks_one + 2 * pairs),
            sems(2, 2 * (chunks_one + 2 * pairs)),
            sems(2, n - 1),
            sems(2, n - 1),
            sems(2, batch - 1),
        ],
        compiler_params=pltpu.CompilerParams(
            collective_id=collective_id, has_side_effects=True, vmem_limit_bytes=60 * MIB
        ),
        name="tail",
    )(*operands)


def finish_kernel(count, sizes, aligned, totals, small, *refs):
    batch, width, layers = sizes
    rows = width // count
    down, up, out, qkv, w_mod = refs[:5]
    times, mods = refs[-2:]
    me = lax.axis_index("blk")
    half = width // 2
    for core in range(2):
        for i in range(layers):
            made = totals[core, :, i * half : (i + 1) * half].astype(F32)
            down[i * rows : (i + 1) * rows, core * half : (core + 1) * half] = made
        start = layers * half
        made = totals[core, :, start : start + layers * half].astype(F32)
        up[:, core * layers * half : (core + 1) * layers * half] = made
        start = 2 * layers * half
        out[:, core * half : (core + 1) * half] = totals[core, :, start : start + half].astype(F32)
        made = totals[core, :, start + half : start + 4 * half].astype(F32)
        qkv[:, core * 3 * half : (core + 1) * 3 * half] = made
    for u in range(2 * batch):
        b, s = u // 2, u % 2
        line = small[b, 15 + 2 + layers + s, pl.ds(me * rows // LANES, 1)]
        if rows < LANES:
            line = pltpu.roll(line, LANES - lax.rem(me, LANES // rows) * rows, 1)
        times[u : u + 1] = line
        for p in range(6):
            for c in range(width // LANES):
                start = p * width + c * LANES
                mods[u : u + 1, start : start + LANES] = small[b, 2 * p + s, c : c + 1]
    w_mod[...] = dot_frames(times[:, :rows].astype(BF16), mods[...].astype(BF16))
    if aligned:
        tiles = width // LANES

        def own_lines(first, length, stride):
            lines = []
            for i in range(length // count // LANES):
                at = me * (length // count // LANES) + i
                total = jnp.zeros((1, LANES), F32)
                for b in range(batch):
                    for s in range(stride):
                        total = total + small[b, first + at // tiles * stride + s, pl.ds(lax.rem(at, tiles), 1)]
                lines.append(total)
            return lines

        firsts = [(0, 6, 2), (12, 3, 1), (15, 1, 1), (16, layers, 1), (16 + layers, 1, 1)]
        for ref, (first, many, stride) in zip(refs[5:10], firsts):
            for i, line in enumerate(own_lines(first, many * width, stride)):
                ref[i * LANES : (i + 1) * LANES] = line[0]


def finish(count, totals, small, width, layers):
    batch, rows = small.shape[0], width // count
    aligned = rows % LANES == 0
    shapes = [(layers * rows, width), (rows, layers * width), (rows, width), (rows, 3 * width), (rows, 6 * width)]
    if aligned:
        shapes += [(many * rows,) for many in (6, 3, 1, layers, 1)]
    outs = pl.pallas_call(
        partial(finish_kernel, count, (batch, width, layers), aligned),
        out_shape=[jax.ShapeDtypeStruct(shape, F32) for shape in shapes],
        scratch_shapes=[pltpu.VMEM((2 * batch, LANES), F32), pltpu.VMEM((2 * batch, 6 * width), F32)],
        compiler_params=pltpu.CompilerParams(vmem_limit_bytes=40 * MIB),
        name="finish",
    )(totals, small)
    if not aligned:
        me = lax.axis_index("blk")
        flat = jnp.sum(small.reshape(batch, -1, width), axis=0)
        mods = flat[:12].reshape(6, 2, width).sum(axis=1)
        ends = [12, 15, 16, 16 + layers, 17 + layers]
        vectors = [mods] + [flat[lo:hi] for lo, hi in zip(ends[:-1], ends[1:])]
        outs = list(outs) + [
            lax.dynamic_index_in_dim(v.reshape(count, -1), me, 0, keepdims=False) for v in vectors
        ]
    return outs


def on_device(
    inputs,
    time_embed,
    lengths,
    cotangent,
    w_mod,
    b_mod,
    w_qkv,
    b_qkv,
    w_out,
    b_out,
    w_up,
    b_up,
    w_down,
    b_down,
):
    seqs, frames, width = inputs.shape
    head_dim = width // HEADS
    count, batch = lax.axis_size("blk"), lax.axis_size("batch")
    plan = Plan(count, frames, width)
    swap = lengths[0] < lengths[1]
    order = jnp.where(swap, jnp.array([1, 0], jnp.int32), jnp.array([0, 1], jnp.int32))

    mods_a, time_act, cos_table, sin_table, hidden_t, qkv_rows = pre_attention(
        order, inputs, time_embed, w_mod, b_mod, w_qkv, b_qkv, plan.cols
    )
    output, grad_mixed, stats, dq, dkv, dshort, near_sums, other_t = core(
        plan,
        head_dim,
        512,
        (order, qkv_rows, hidden_t, inputs, cotangent, time_act, b_mod, b_out, b_up, b_down,
         w_mod, w_out, w_up, w_down),
        0,
    )
    operands = (
        order, dq, dkv, dshort, hidden_t, other_t, inputs, mods_a, grad_mixed, cos_table, sin_table, stats, near_sums,
        time_act, time_embed, w_qkv, w_mod,
    )
    totals, small, grad_inputs, grad_time = tail(plan, 512, 256, batch, head_dim // 2, operands, 1)

    down, up, out, qkv, grad_w_mod, *vectors = finish(
        count, totals, small, width, w_up.shape[1] // width
    )
    return (
        output,
        grad_inputs,
        grad_time,
        grad_w_mod,
        vectors[0],
        qkv,
        vectors[1],
        out,
        vectors[2],
        up,
        vectors[3],
        down,
        vectors[4],
    )


def solution(mesh):
    frame_spec, weight_spec = P("batch", "blk", None), P("blk", None)
    return jax.shard_map(
        on_device,
        mesh=mesh,
        in_specs=(frame_spec, P("batch", None), P("batch"), frame_spec) + (P(),) * 10,
        out_specs=(frame_spec, frame_spec, P("batch", None)) + (weight_spec, P("blk")) * 5,
        check_vma=False,
    )
```

```python
from functools import partial
from types import SimpleNamespace

import jax
import jax.numpy as jnp
from jax import lax
from jax.experimental import pallas as pl
from jax.experimental.pallas import tpu as pltpu
from jax.sharding import PartitionSpec as P

HEADS = 16
EPS = 1e-06
LANES = 128
SHORT = 16
MESH = pl.DeviceIdType.MESH
BF16 = jnp.bfloat16
F32 = jnp.float32
MIB = 1 << 20


def dot(left, right):
    return jnp.dot(left, right, preferred_element_type=F32)


def dot_rows(left, right):
    return lax.dot_general(left, right, (((1,), (1,)), ((), ())), preferred_element_type=F32)


def dot_frames(left, right):
    return lax.dot_general(left, right, (((0,), (0,)), ((), ())), preferred_element_type=F32)


def normalize(rows):
    mean = jnp.mean(rows, axis=-1, keepdims=True)
    centered = rows - mean
    inverse = lax.rsqrt(jnp.mean(centered * centered, axis=-1, keepdims=True) + EPS)
    return (centered * inverse, inverse)


def norm_back(normed, inverse, grad):
    return inverse * (
        grad
        - jnp.mean(grad, axis=-1, keepdims=True)
        - normed * jnp.mean(grad * normed, axis=-1, keepdims=True)
    )


def whole(shape):
    return pl.BlockSpec(shape, lambda *_: (0,) * len(shape))


def in_hbm():
    return pl.BlockSpec(memory_space=pltpu.HBM)


def rotate(rows, cos_table, sin_table, half):
    lane = lax.broadcasted_iota(jnp.int32, rows.shape, 1)
    partner = jnp.where(
        lax.rem(lane, 2 * half) < half,
        pltpu.roll(rows, LANES - half, 1),
        pltpu.roll(rows, half, 1),
    )
    return rows * cos_table + partner * sin_table


class Spot:
    def __init__(self, count):
        b, j = lax.axis_index("batch"), lax.axis_index("blk")
        self.b, self.j = b, j
        self.core, self.half = lax.rem(b, 2), b // 2
        self.near, self.far = lax.rem(j, 2), j // 2
        self.far_count = count // 2
        self.at_core = (self.half * 2 + 1 - self.core, j)
        self.at_x = ((1 - self.half) * 2 + self.core, j)
        self.at_both = ((1 - self.half) * 2 + 1 - self.core, j)
        self.at_near = (b, self.far * 2 + 1 - self.near)
        self.far_steps = [lax.rem(self.far + step, self.far_count) for step in range(1, self.far_count)]
        self.at_far = [(b, step * 2 + self.near) for step in self.far_steps]


def add_into(target, other):
    target[...] = (target[...].astype(F32) + other.astype(F32)).astype(BF16)


class Plan:
    def __init__(self, count, frames, width):
        self.count = count
        self.frames = frames
        self.width = width
        self.groups = min(max(count // 2, 1), 4)
        self.cols = width // self.groups
        self.splits = count // self.groups
        self.total = count * frames
        self.short = self.total // SHORT
        self.short_rows = min(self.short, frames)
        self.short_blocks = -(-self.short // frames)
        self.phases = [(lo, min(lo + 4 * self.groups, count)) for lo in range(self.groups, count, 4 * self.groups)]
        self.phases = [(0, self.groups)] + self.phases
        self.largest = max(hi - lo for lo, hi in self.phases) * frames
        self.offsets = [(d, s) for d in range(self.splits) for s in range(self.groups) if d + s > 0]

    def peer(self, device, offset):
        split = lax.rem(device // self.groups + offset[0], self.splits)
        return split * self.groups + lax.rem(lax.rem(device, self.groups) + offset[1], self.groups)


def push(src, dst, sems, index, device):
    copy = pltpu.make_async_remote_copy(
        src_ref=src, dst_ref=dst, send_sem=sems.at[(0,) + index], recv_sem=sems.at[(1,) + index],
        device_id=device, device_id_type=MESH,
    )
    copy.start()
    return copy


def local(src, dst, sem):
    copy = pltpu.make_async_copy(src, dst, sem)
    copy.start()
    return copy


def stacked(rows, head_dim):
    lane = lax.broadcasted_iota(jnp.int32, rows.shape, 1)
    heads = LANES // head_dim
    return jnp.concatenate(
        [jnp.where(lane // head_dim == h, rows, jnp.zeros_like(rows)) for h in range(heads)], axis=0
    )


def unstacked(turned, frames, head_dim):
    heads = LANES // head_dim
    return jnp.concatenate(
        [
            turned[h * head_dim : (h + 1) * head_dim, h * frames : (h + 1) * frames]
            for h in range(heads)
        ],
        axis=0,
    ).T


def attend_part(queries, keys, values_t, head_dim):
    scores = dot_rows(keys, stacked(queries, head_dim))
    top = jnp.max(scores, axis=0, keepdims=True)
    weights = jnp.exp(scores - top)
    total = jnp.sum(weights, axis=0, keepdims=True)
    return top, total, dot(values_t, weights.astype(BF16))


def attend_join(one, two):
    top = jnp.maximum(one[0], two[0])
    left, right = jnp.exp(one[0] - top), jnp.exp(two[0] - top)
    return top, one[1] * left + two[1] * right, one[2] * left + two[2] * right


def attend_end(state, frames, head_dim):
    top, total, out = state
    return unstacked(out / total, frames, head_dim).astype(BF16), top + jnp.log(total)


def delta_rows(grads, outs, head_dim):
    heads = LANES // head_dim
    lane = lax.broadcasted_iota(jnp.int32, (8, LANES), 1)
    pick = (lane // head_dim == lax.broadcasted_iota(jnp.int32, (8, LANES), 0)).astype(F32)
    product = grads.astype(F32) * outs.astype(F32)
    sums = lax.dot_general(
        pick, product, (((1,), (1,)), ((), ())), precision=lax.Precision.HIGHEST, preferred_element_type=F32
    )
    return jnp.concatenate([sums[h : h + 1] for h in range(heads)], axis=1)


def attend_back(queries, grads, lse, delta, keys, keys_t, values, head_dim):
    frames = queries.shape[0]
    q_heads, g_heads = stacked(queries, head_dim), stacked(grads, head_dim)
    probs = jnp.exp(dot_rows(keys, q_heads) - lse)
    grad_probs = dot_rows(values, g_heads)
    grad_scores = (probs * (grad_probs - delta)).astype(BF16)
    grad_values = dot(probs.astype(BF16), g_heads)
    grad_keys = dot(grad_scores, q_heads)
    grad_queries = unstacked(dot(keys_t, grad_scores), frames, head_dim) * head_dim ** (-0.5)
    return grad_queries, grad_keys, grad_values


def gelu_both(z):
    scale = (2.0 / 3.141592653589793) ** 0.5
    square = z * z
    inner = jnp.tanh(scale * z * (1.0 + 0.044715 * square))
    half = 0.5 * (1.0 + inner)
    slope = half + 0.5 * z * (1.0 - inner * inner) * (scale * (1.0 + 3.0 * 0.044715 * square))
    return z * half, slope


def layer_kernel(plan, sizes, names, *refs):
    r = SimpleNamespace(**dict(zip(names, refs)))
    heads, chunk, chunk_two, block, batch = sizes
    n, g, f, cols, width = plan.count, plan.groups, plan.frames, plan.cols, plan.width
    tokens, hidden = 2 * f, r.w_up.shape[1]
    head_dim, half_dim = width // heads, width // heads // 2
    half_width, half_hidden = width // 2, hidden // 2
    layers, n_rows, units = hidden // width, width // n, cols // LANES
    spot = Spot(n)
    b, me, core, half = spot.b, spot.j, spot.core, spot.half
    group, split = lax.rem(me, g), me // g
    others = [plan.peer(me, offset) for offset in plan.offsets]
    mates = others[: g - 1]
    along = [(b, peer) for peer in others]
    across = [(lax.rem(b + step, batch), me) for step in range(1, batch)]
    seqs = [slice(0, f), slice(f, tokens)]
    mine, theirs = slice(0, tokens), slice(tokens, 2 * tokens)
    swapped = r.lengths[0] < r.lengths[1]
    first = jnp.where(swapped, 1, 0)
    order = [first, 1 - first]

    barrier = pltpu.get_barrier_semaphore()
    for device in along + across:
        pl.semaphore_signal(barrier, inc=1, device_id=device, device_id_type=MESH)

    load_x = local(r.x_hbm, r.x, r.in_sems.at[0])
    mod_places, mod_copies = [r.w_mod.at[0], r.w_mod.at[1]], {}
    room = r.parts.reshape(width, r.parts.shape[2])
    mod_places += [room.at[:, :half_width], room.at[:, half_width:width]]
    ahead = len(mod_places)

    def mod_place(i):
        return i if i < ahead else i % 2

    def load_mod(i, place):
        return local(r.w_mod_hbm.at[:, i * half_width : (i + 1) * half_width], mod_places[place], r.m_sems.at[place])

    def next_mod(i):
        if mod_place(i) < 2:
            after = i + ahead if i < 2 else i + 2
            if after < 12:
                mod_copies[after] = load_mod(after, mod_place(after))

    def load_qkv():
        return [
            local(r.w_qkv_hbm.at[:, : 2 * width], r.w_up.at[:, : 2 * width], r.in_sems.at[1]),
            local(r.w_qkv_hbm.at[:, 2 * width :], r.w_out, r.in_sems.at[2]),
        ]

    for i in range(ahead):
        mod_copies[i] = load_mod(i, i)
    qkv_copies = load_qkv()
    load_ct = local(r.ct_hbm, r.ct, r.in_sems.at[3])
    load_down = local(r.w_down_hbm, r.w_down, r.in_sems.at[4])

    shown = r.time_embed[...].astype(F32)
    shown = jnp.where(swapped, jnp.concatenate([shown[1:2], shown[0:1]], axis=0), shown)
    r.acts[...] = (shown / (1.0 + jnp.exp(-shown))).astype(BF16)
    frame = me * f + lax.broadcasted_iota(jnp.int32, (f, LANES), 0)
    angle = frame.astype(F32) * r.freqs[...]
    lane = lax.broadcasted_iota(jnp.int32, (f, LANES), 1)
    sines = jnp.sin(angle)
    r.cos[...] = jnp.cos(angle)
    r.sin[...] = jnp.where(lax.rem(lane, 2 * half_dim) < half_dim, -sines, sines)
    r.b_row[...] = r.b_qkv[...][None].astype(F32)

    def mod_piece(i, place):
        piece = slice(i * half_width, (i + 1) * half_width)
        r.mods[:, piece] = dot(r.acts[...], mod_places[place][...]) + r.b_mod[piece][None].astype(F32)

    def mod(i, s):
        return r.mods[s : s + 1, i * width : (i + 1) * width]

    for i in range(4):
        mod_copies[i].wait()
        mod_piece(i, mod_place(i))
        next_mod(i)

    load_x.wait()
    for s, span in enumerate(seqs):
        normed, _ = normalize(r.x[order[s]].astype(F32))
        r.hidden_f[span] = (normed * (1.0 + mod(1, s)) + mod(0, s)).astype(BF16)
    for copy in qkv_copies:
        copy.wait()
    pl.semaphore_wait(barrier, len(along + across))

    def project(kind, which):
        at = pl.ds(pl.multiple_of(which * cols, LANES), cols)
        bias_at = pl.ds(pl.multiple_of(kind * width + which * cols, LANES), cols)
        weight = r.w_out[:, at] if kind == 2 else r.w_up[:, bias_at]
        made = dot(r.hidden_f[...], weight) + r.b_row[:, bias_at]
        if kind < 2:
            factor = (2.0 * half_dim) ** (-0.5) if kind == 0 else 1.0
            cosines, sines = r.cos[...] * factor, r.sin[...] * factor
        for span in seqs:
            for u in range(units):
                part = made[span, u * LANES : (u + 1) * LANES]
                if kind < 2:
                    part = rotate(part, cosines, sines, half_dim)
                start = kind * cols + u * LANES
                r.rows[which, span, start : start + LANES] = part.astype(BF16)

    near_waits = []

    def send_keys(step):
        offset = plan.offsets[step]
        src = r.rows.at[lax.rem(others[step], g), 0:f, cols : 3 * cols]
        dst = r.kv_buf.at[offset[0] * g + group]
        return push(src, dst, r.k_sems, (step,), along[step])

    inner = jnp.logical_or(lax.rem(spot.far, 4) == 1, lax.rem(spot.far, 4) == 2)
    for step in range(1, g + 1):
        which = lax.rem(group + step, g)
        project(1, which)
        project(2, which)

    @pl.when(inner)
    def _():
        for step in range(g - 1, n - 1):
            send_keys(step)

    for step in range(g - 1):
        near_waits.append(send_keys(step))
    for step in range(1, g + 1):
        which = lax.rem(group + step, g)
        project(0, which)
        if step < g:
            src = r.rows.at[which, :, 0:cols]
            near_waits.append(push(src, r.q_buf.at[group], r.q_sems, (step - 1,), along[step - 1]))

    @pl.when(jnp.logical_not(inner))
    def _():
        for step in range(g - 1, n - 1):
            send_keys(step)

    def short_rows_of(peer):
        return r.rows.at[lax.rem(peer, g), f : f + plan.short_rows, cols : 3 * cols]

    for blk in range(plan.short_blocks):

        @pl.when(me == blk)
        def _():
            for step, peer in enumerate(others):
                push(short_rows_of(peer), r.short_buf.at[blk], r.s_sems, (blk, step), along[step])

    r.both_hidden[:, mine] = r.hidden_f[...].T
    swap_hidden = push(r.both_hidden.at[:, mine], r.both_hidden.at[:, theirs], r.h_sems, (), spot.at_core)
    load_out = local(r.w_out_hbm, r.w_out, r.in_sems.at[2])
    load_up = local(r.w_up_hbm, r.w_up, r.in_sems.at[1])
    r.kv_buf[group] = r.rows[group, 0:f, cols : 3 * cols]
    r.q_buf[group] = r.rows[group, :, 0:cols]

    for i in range(4, 12):
        mod_copies[i].wait()
        mod_piece(i, mod_place(i))
        next_mod(i)

    load_ct.wait()
    for s, span in enumerate(seqs):
        r.grad_ff[span] = (mod(5, s) * r.ct[order[s]].astype(F32)).astype(BF16)

    def core_half(which, size):
        return pl.ds(pl.multiple_of(which * size, LANES), size)

    def to_core(src, dst, index):
        return push(src, dst, r.e_sems, (index,), spot.at_core)

    ff_own, ff_other = core_half(core, half_width), core_half(1 - core, half_width)
    swap_ff = [
        to_core(r.grad_ff.at[:, ff_other], r.all_ff.at[1], 0),
        push(r.grad_ff.at[:, ff_own], r.all_ff.at[2], r.ff_sems, (0,), spot.at_x),
        push(r.grad_ff.at[:, ff_other], r.all_ff.at[3], r.ff_sems, (1,), spot.at_both),
    ]
    r.all_ff[0] = r.grad_ff[:, ff_own]

    for copy in near_waits:
        copy.wait()

    def turn_values(lo, hi, start):
        part = r.kv_buf[lo:hi, :, start : start + cols].reshape((hi - lo) * f, cols)
        r.turned[:, lo * f : hi * f] = part.T

    def cols_of(which):
        return pl.ds(pl.multiple_of(which * cols, LANES), cols)

    def slot_of(step):
        return lax.rem(group + 1 + step, g)

    units = cols // LANES
    sends = []
    for phase, (lo, hi) in enumerate(plan.phases):
        last = phase == len(plan.phases) - 1
        if phase == 1:
            for step in range(g - 1, n - 1):
                src = r.rows.at[group, 0:f, cols : 3 * cols]
                pltpu.make_async_copy(src, src, r.k_sems.at[0, step]).wait()
                dst = r.kv_buf.at[plan.offsets[step][0] * g + lax.rem(group + g - plan.offsets[step][1], g)]
                pltpu.make_async_copy(dst, dst, r.k_sems.at[1, step]).wait()
        turn_values(lo, hi, cols)
        for step in range(g):
            slot = slot_of(step)
            for u in range(units):
                lanes = slice(u * LANES, (u + 1) * LANES)
                at = step * units + u
                state = attend_part(
                    r.q_buf[slot, :f, lanes],
                    r.kv_buf[lo:hi, :, lanes].reshape((hi - lo) * f, LANES),
                    r.turned[lanes, lo * f : hi * f],
                    head_dim,
                )
                if phase > 0:
                    state = attend_join((r.top_acc[at], r.total_acc[at], r.o_acc[at]), state)
                if last:
                    r.o_buf[slot, :f, lanes], r.lse[slot, u : u + 1] = attend_end(state, f, head_dim)
                else:
                    r.top_acc[at], r.total_acc[at], r.o_acc[at] = state
            if last and step == 0:
                for blk in range(plan.short_blocks):

                    @pl.when(me == blk)
                    def _():
                        r.short_buf[blk] = r.rows[group, f : f + plan.short_rows, cols : 3 * cols]

                    for i, offset in enumerate(plan.offsets):

                        @pl.when(plan.peer(blk, offset) == me)
                        def _():
                            dst = r.short_buf.at[blk]
                            pltpu.make_async_copy(dst, dst, r.s_sems.at[1, blk, i]).wait()

                r.short_turned[...] = r.short_buf[:, :, cols:].reshape(plan.short, cols).T
            if last:
                for u in range(units):
                    lanes = slice(u * LANES, (u + 1) * LANES)
                    keys = r.short_buf[:, :, lanes].reshape(plan.short, LANES)
                    state = attend_part(r.q_buf[slot, f:, lanes], keys, r.short_turned[lanes], head_dim)
                    row = units + u
                    r.o_buf[slot, f:, lanes], r.lse[slot, row : row + 1] = attend_end(state, f, head_dim)
                if step == g - 1:
                    r.attn[:, cols_of(group)] = r.o_buf[slot]
                else:
                    dst = r.attn.at[:, cols_of(group)]
                    sends.append(push(r.o_buf.at[slot], dst, r.o_sems, (step,), along[step]))
    for lo, hi in plan.phases:
        turn_values(lo, hi, 0)
    r.short_turned[...] = r.short_buf[:, :, :cols].reshape(plan.short, cols).T
    for copy in sends:
        copy.wait()
    for blk in range(plan.short_blocks):

        @pl.when(me == blk)
        def _():
            for step, peer in enumerate(others):
                src = short_rows_of(peer)
                pltpu.make_async_copy(src, src, r.s_sems.at[0, blk, step]).wait()

    load_out.wait()
    r.attn_t[:, mine] = r.attn[...].T
    swap_attn = to_core(r.attn_t.at[:, mine], r.attn_t.at[:, theirs], 1)
    r.branch_a[...] = dot(r.attn[...], r.w_out[...]) + r.b_out[...][None].astype(F32)
    for s, span in enumerate(seqs):
        r.mixed[span] = r.x[order[s]].astype(F32) + mod(2, s) * r.branch_a[span]
        normed, _ = normalize(r.mixed[span])
        r.hidden_f[span] = (normed * (1.0 + mod(4, s)) + mod(3, s)).astype(BF16)
    r.hid_t[:, mine] = r.hidden_f[...].T
    swap_hid = to_core(r.hid_t.at[:, mine], r.hid_t.at[:, theirs], 2)
    load_up.wait()
    load_down.wait()
    swap_act, act_x = [], []
    per_block = block // (layers * n_rows)
    for i in range(hidden // block):
        span = slice(i * block, (i + 1) * block)
        act, slope = gelu_both(dot(r.hidden_f[...], r.w_up[:, span]) + r.b_up[span][None].astype(F32))
        act = act.astype(BF16)
        act_t = act.T.reshape(per_block, layers, n_rows, tokens)
        held = slice(i * per_block, (i + 1) * per_block)
        r.act_own[held, :, mine] = jnp.where(half == 0, act_t[:, 0], act_t[:, 1])
        r.act_send[held] = jnp.where(half == 0, act_t[:, 1], act_t[:, 0])
        act_x.append(
            push(r.act_send.at[held], r.act_own.at[held, :, 2 * tokens : 3 * tokens], r.act_sems, (0, i), spot.at_x)
        )
        swap_act.append(
            push(r.act_own.at[held, :, mine], r.act_own.at[held, :, theirs], r.act_sems, (1, i), spot.at_core)
        )
        forward = dot(act, r.w_down[span, :])
        grad = (dot_rows(r.grad_ff[...], r.w_down[span, :]) * slope).astype(BF16)
        r.grad_pre[:, span] = grad
        row, start = 9 + i * block // width, i * block % width
        r.stats[row : row + 1, start : start + block] = jnp.sum(grad.astype(F32), axis=0, keepdims=True)
        back = dot_rows(grad, r.w_up[:, span])
        if i == 0:
            r.branch_f[...] = forward + r.b_down[...][None].astype(F32)
            r.grad_hid[...] = back
        else:
            r.branch_f[...] += forward
            r.grad_hid[...] += back
    swap_pre = to_core(r.grad_pre.at[:, core_half(1 - core, half_hidden)], r.both_pre.at[1], 3)
    r.both_pre[0] = r.grad_pre[:, core_half(core, half_hidden)]

    chunks, half_chunk = r.parts.shape[2] // chunk, chunk // 2
    base_one = layers * half_width
    x_copies, near_copies, far_copies, last, sent = {}, {}, {}, [], {}

    def half_of(k, which):
        return pl.ds(pl.multiple_of(k * chunk + which * half_chunk, LANES), half_chunk)

    def total_of(k, which):
        if k == "down":
            return core_half(which, half_width)
        return pl.ds(pl.multiple_of(base_one + k * chunk + which * half_chunk, LANES), half_chunk)

    def start_x(k):
        src = r.parts.at[:, :, half_of(k, 1 - half)]
        x_copies[k] = push(src, r.x_buf.at[k], r.x_sems, (k,), spot.at_x)

    def by_near(ref):
        return ref.reshape(spot.far_count, 2, n_rows, ref.shape[2])

    def finish_x(k):
        x_copies[k].wait()
        add_into(r.x_buf.at[k], r.parts[:, :, half_of(k, half)])
        src = by_near(r.x_buf.at[k]).at[:, 1 - spot.near]
        near_copies[k] = push(src, r.near_sums.at[k], r.n_sems, (k,), spot.at_near)

    def finish_near(k):
        near_copies[k].wait()
        whole_sum, near_sum = (r.down_sum, r.near_down) if k == "down" else (r.x_buf.at[k], r.near_sums.at[k])
        add_into(near_sum, by_near(whole_sum)[:, spot.near])
        for step in range(spot.far_count - 1):
            dst = r.far_down.at[step] if k == "down" else r.far_one.at[k, step]
            index = (chunks if k == "down" else k, step)
            far_copies[k, step] = push(near_sum.at[spot.far_steps[step]], dst, r.f1_sems, index, spot.at_far[step])

    def to_all(where, which):
        place = r.totals.at[core, :, where]
        return [
            push(place, place, r.ax_sems, (which,), spot.at_x),
            push(place, place, r.ac_sems, (2 * which,), spot.at_core),
        ]

    def forward_to_core(where, which):
        place = r.totals.at[core, :, where]
        return push(place, place, r.ac_sems, (2 * which + 1,), spot.at_core)

    def finish_far(k):
        near_sum, far_buf = (r.near_down, r.far_down) if k == "down" else (r.near_sums.at[k], r.far_one.at[k])
        total = near_sum[spot.far].astype(F32)
        for step in range(spot.far_count - 1):
            far_copies[k, step].wait()
            total = total + far_buf[step].astype(F32)
        r.totals[core, :, total_of(k, half)] = total.astype(BF16)
        sent[k] = to_all(total_of(k, half), chunks if k == "down" else k)

    def finish_all(k):
        sent[k][0].wait()
        last.append(sent[k][1])
        last.append(forward_to_core(total_of(k, 1 - half), chunks if k == "down" else k))

    for s, span in enumerate(seqs):
        grad_out = r.ct[order[s]].astype(F32)
        branch, grad = r.branch_f[span], r.grad_hid[span]
        normed, inverse = normalize(r.mixed[span])
        r.stats[6 + s : 7 + s] = jnp.sum(grad_out * branch, axis=0, keepdims=True)
        r.stats[4 + s : 5 + s] = jnp.sum(grad * normed, axis=0, keepdims=True)
        r.stats[2 + s : 3 + s] = jnp.sum(grad, axis=0, keepdims=True)
        total = grad_out + norm_back(normed, inverse, grad * (1.0 + mod(4, s)))
        r.grad_mixed[span] = total
        r.stats[s : s + 1] = jnp.sum(total * r.branch_a[span], axis=0, keepdims=True)
        r.grad_br[span] = (mod(2, s) * total).astype(BF16)
    r.grads[...] = dot_rows(r.grad_br[...], r.w_out[...]).astype(BF16)
    waits = []
    for step, peer in enumerate(mates):
        src = r.grads.at[:, cols_of(lax.rem(peer, g))]
        waits.append(push(src, r.g_buf.at[group], r.bg_sems, (step,), along[step]))
    r.g_buf[group] = r.grads[:, cols_of(group)]
    swap_br = to_core(r.grad_br.at[:, core_half(1 - core, half_width)], r.both_br.at[1], 4)
    qkv_copies = load_qkv()

    swap_hid.wait()
    swap_pre.wait()
    for i in range(layers):
        grad = r.both_pre[:, :, i * half_width : (i + 1) * half_width].reshape(2 * tokens, half_width)
        up = dot(r.hid_t[...], grad).astype(BF16).reshape(n, n_rows, half_width)
        r.parts[:, :, i * half_width : (i + 1) * half_width] = up
        start_x(i)
    for i, copy in enumerate(act_x):
        copy.wait()
        held = slice(i * per_block, (i + 1) * per_block)
        src = r.act_own.at[held, :, 2 * tokens : 3 * tokens]
        dst = r.act_own.at[held, :, 3 * tokens : 4 * tokens]
        swap_act.append(push(src, dst, r.act_sems, (2, i), spot.at_core))
    r.both_br[0] = r.grad_br[:, core_half(core, half_width)]
    swap_attn.wait()
    swap_br.wait()
    out_part = dot(r.attn_t[...], r.both_br[...].reshape(2 * tokens, half_width))
    r.parts[:, :, layers * half_width :] = out_part.astype(BF16).reshape(n, n_rows, half_width)
    start_x(layers)
    for copy in swap_ff + swap_act:
        copy.wait()
    down = dot(r.act_own[...].reshape(width, 4 * tokens), r.all_ff[...].reshape(4 * tokens, half_width))
    r.down_sum[...] = down.astype(BF16).reshape(n, n_rows, half_width)
    near_copies["down"] = push(
        by_near(r.down_sum).at[:, 1 - spot.near], r.near_down, r.n_sems, (chunks,), spot.at_near
    )
    made = [r.mixed[span] + mod(5, s) * r.branch_f[span] for s, span in enumerate(seqs)]
    r.mixed[seqs[0]] = jnp.where(swapped, made[1], made[0])
    r.mixed[seqs[1]] = jnp.where(swapped, made[0], made[1])
    last.append(local(r.mixed.reshape(2, f, width), r.output, r.in_sems.at[0]))
    last_row = 9 + layers
    r.stats[8:9] = jnp.sum(r.grad_br[...].astype(F32), axis=0, keepdims=True)
    r.stats[last_row : last_row + 1] = jnp.sum(r.grad_ff[...].astype(F32), axis=0, keepdims=True)
    for copy in waits:
        copy.wait()

    sends = []
    deltas = [
        [
            [
                delta_rows(r.g_buf[slot_of(step), span, lanes], r.o_buf[slot_of(step), span, lanes], head_dim)
                for lanes in [slice(u * LANES, (u + 1) * LANES) for u in range(units)]
            ]
            for span in seqs
        ]
        for step in range(g)
    ]
    dq_buf = r.o_buf
    for phase, (lo, hi) in enumerate(plan.phases[1:] + plan.phases[:1]):
        size = (hi - lo) * f
        for step in range(g):
            slot = slot_of(step)
            for u in range(units):
                lanes = slice(u * LANES, (u + 1) * LANES)
                high = slice(cols + u * LANES, cols + (u + 1) * LANES)
                dq, dk, dv = attend_back(
                    r.q_buf[slot, :f, lanes],
                    r.g_buf[slot, :f, lanes],
                    r.lse[slot, u : u + 1],
                    deltas[step][0][u],
                    r.kv_buf[lo:hi, :, lanes].reshape(size, LANES),
                    r.turned[lanes, lo * f : hi * f],
                    r.kv_buf[lo:hi, :, high].reshape(size, LANES),
                    head_dim,
                )
                if step == 0:
                    r.dlong[0, :size, lanes] = dk
                    r.dlong[1, :size, lanes] = dv
                else:
                    r.dlong[0, :size, lanes] += dk
                    r.dlong[1, :size, lanes] += dv
                if phase > 0:
                    dq = r.dq_acc[step, :, lanes] + dq
                r.dq_acc[step, :, lanes] = dq
                if lo > 0:
                    continue
                dq_buf[slot, :f, lanes] = dq.astype(BF16)
                row = units + u
                dq, dk, dv = attend_back(
                    r.q_buf[slot, f:, lanes],
                    r.g_buf[slot, f:, lanes],
                    r.lse[slot, row : row + 1],
                    deltas[step][1][u],
                    r.short_buf[:, :, lanes].reshape(plan.short, LANES),
                    r.short_turned[lanes],
                    r.short_buf[:, :, high].reshape(plan.short, LANES),
                    head_dim,
                )
                dq_buf[slot, f:, lanes] = dq.astype(BF16)
                if step == 0:
                    r.dsmall[0, :, lanes] = dk
                    r.dsmall[1, :, lanes] = dv
                else:
                    r.dsmall[0, :, lanes] += dk
                    r.dsmall[1, :, lanes] += dv
            if lo == 0:
                if step == g - 1:
                    r.dq_out[:, cols_of(group)] = dq_buf[slot]
                else:
                    dst = r.dq_out.at[:, cols_of(group)]
                    sends.append(push(dq_buf.at[slot], dst, r.bq_sems, (step,), along[step]))
        for which in range(2):
            made = slice(which * cols, (which + 1) * cols)
            r.kv_buf[lo:hi, :, made] = r.dlong[which, :size].astype(BF16).reshape(hi - lo, f, cols)
        for d in range(lo // g, hi // g):
            for s in range(g):
                if d == 0 and s == 0:
                    continue
                other_group = lax.rem(group + s, g)
                peer = lax.rem(split + plan.splits - d, plan.splits) * g + other_group
                for which in range(2):
                    made = slice(which * cols, (which + 1) * cols)
                    dst = r.dkv_out.at[which, split, :, cols_of(group)]
                    src = r.kv_buf.at[d * g + other_group, :, made]
                    sends.append(push(src, dst, r.bk_sems, (which, d * g + s), (b, peer)))
        if lo == 0:
            for which in range(2):
                made = slice(which * cols, (which + 1) * cols)
                r.dkv_out[which, split, :, cols_of(group)] = r.kv_buf[group, :, made]
    for blk in range(plan.short_blocks):
        span = slice(blk * plan.short_rows, (blk + 1) * plan.short_rows)
        r.dshort_buf[blk] = r.dsmall[:, span].astype(BF16)
        dst = r.dshort_out.at[:, split, :, cols_of(group)]
        for step, peer in enumerate(others):

            @pl.when(peer == blk)
            def _():
                push(r.dshort_buf.at[blk], dst, r.bs_sems, (step,), along[step])

        @pl.when(me == blk)
        def _():
            r.dshort_out[:, split, :, cols_of(group)] = r.dshort_buf[blk]

    finish_x(0)
    for copy in sends:
        copy.wait()
    for blk in range(plan.short_blocks):
        for step, peer in enumerate(others):

            @pl.when(peer == blk)
            def _():
                pltpu.make_async_copy(r.dshort_buf.at[blk], r.dshort_buf.at[blk], r.bs_sems.at[0, step]).wait()

        @pl.when(me == blk)
        def _():
            for step in range(n - 1):
                pltpu.make_async_copy(r.dshort_buf.at[blk], r.dshort_buf.at[blk], r.bs_sems.at[1, step]).wait()

    no_short = me >= plan.short_blocks
    grad_key = jnp.sum(r.dkv_out[0].astype(F32), axis=0)
    grad_value = jnp.sum(r.dkv_out[1].astype(F32), axis=0)
    short_key = jnp.where(no_short, 0.0, jnp.sum(r.dshort_out[0].astype(F32), axis=0))
    short_value = jnp.where(no_short, 0.0, jnp.sum(r.dshort_out[1].astype(F32), axis=0))
    cosines, sines = r.cos[...], -r.sin[...]
    for c in range(width // LANES):
        lanes = slice(c * LANES, (c + 1) * LANES)
        for span in seqs:
            made = rotate(r.dq_out[span, lanes].astype(F32), cosines, sines, half_dim)
            r.grad_qkv[span, lanes] = made.astype(BF16)
        lanes_k = slice(width + c * LANES, width + (c + 1) * LANES)
        made = rotate(grad_key[:, lanes], cosines, sines, half_dim)
        r.grad_qkv[:f, lanes_k] = made.astype(BF16)
        made = rotate(short_key[:, lanes], cosines[: plan.short_rows], sines[: plan.short_rows], half_dim)
        r.grad_qkv[f : f + plan.short_rows, lanes_k] = made.astype(BF16)
    r.grad_qkv[:f, 2 * width :] = grad_value.astype(BF16)
    r.grad_qkv[f : f + plan.short_rows, 2 * width :] = short_value.astype(BF16)
    if plan.short_rows < f:
        r.grad_qkv[f + plan.short_rows :, width:] = jnp.zeros((f - plan.short_rows, 2 * width), BF16)

    own_cols, piece = 3 * half_width, 3 * cols
    pieces = own_cols // piece

    def piece_of(which, i):
        return pl.ds(pl.multiple_of(which * own_cols + i * piece, LANES), piece)

    swaps = []
    for i in range(pieces):
        src = r.grad_qkv.at[:, piece_of(1 - core, i)]
        swaps.append(push(src, r.rows.at[pieces + i], r.g_sems, (i,), spot.at_core))
    for i in range(pieces):
        r.rows[i] = r.grad_qkv[:, piece_of(core, i)]
    finish_near("down")
    finish_x(1)
    finish_x(2)
    swap_hidden.wait()
    for copy in swaps:
        copy.wait()

    pairs, half_two = own_cols // chunk_two // 2, chunk_two // 2
    base_two = base_one + chunks * chunk
    parts4 = by_near(r.parts)
    stage_one, stage_two, stage_far, stage_x = {}, {}, {}, {}

    def part_cols(k, second, which):
        return pl.ds(pl.multiple_of((k + pairs * second) * chunk_two + which * half_two, LANES), half_two)

    def total_cols(k, second, which):
        start = base_two + (k + pairs * second) * chunk_two + which * half_two
        return pl.ds(pl.multiple_of(start, LANES), half_two)

    def half_two_of(which):
        return pl.ds(pl.multiple_of(which * half_two, LANES), half_two)

    def start_one(k):
        for second in range(2):
            start = (k + pairs * second) * chunk_two
            span = slice(start, start + chunk_two)
            i, at = start // piece, start % piece
            both = jnp.concatenate([r.rows[i, :, at : at + chunk_two], r.rows[pieces + i, :, at : at + chunk_two]], axis=0)
            made = dot(r.both_hidden[...], both).astype(BF16)
            r.parts[:, :, span] = made.reshape(n, n_rows, chunk_two)
            if second == 0:
                src = r.parts.at[:, :, part_cols(k, 0, 1 - half)]
                stage_one[k, 0] = push(src, r.a_one.at[k], r.a1_sems, (k,), spot.at_x)
            else:
                src = parts4.at[:, 1 - spot.near, :, span]
                stage_one[k, 1] = push(src, r.b_one.at[k], r.b1_sems, (k,), spot.at_near)

    def finish_one(k):
        stage_one[k, 0].wait()
        add_into(r.a_one.at[k], r.parts[:, :, part_cols(k, 0, half)])
        src = r.a_one.at[k].reshape(spot.far_count, 2, n_rows, half_two).at[:, 1 - spot.near]
        stage_two[k, 0] = push(src, r.a_two.at[k], r.a2_sems, (k,), spot.at_near)
        stage_one[k, 1].wait()
        span = slice((k + pairs) * chunk_two, (k + pairs + 1) * chunk_two)
        add_into(r.b_one.at[k], parts4[:, spot.near, :, span])
        src = r.b_one.at[k, :, :, half_two_of(1 - half)]
        stage_two[k, 1] = push(src, r.b_two.at[k], r.b2_sems, (k,), spot.at_x)

    def finish_two(k):
        stage_two[k, 0].wait()
        add_into(r.a_two.at[k], r.a_one.at[k].reshape(spot.far_count, 2, n_rows, half_two)[:, spot.near])
        stage_two[k, 1].wait()
        add_into(r.b_two.at[k], r.b_one[k, :, :, half_two_of(half)])
        for second, buf in enumerate((r.a_two, r.b_two)):
            for step in range(spot.far_count - 1):
                stage_far[k, second, step] = push(
                    buf.at[k, spot.far_steps[step]],
                    r.far_two.at[second, k, step],
                    r.f2_sems,
                    (second, k, step),
                    spot.at_far[step],
                )

    def finish_far_two(k):
        for second, buf in enumerate((r.a_two, r.b_two)):
            total = buf[k, spot.far].astype(F32)
            for step in range(spot.far_count - 1):
                stage_far[k, second, step].wait()
                total = total + r.far_two[second, k, step].astype(F32)
            r.totals[core, :, total_cols(k, second, half)] = total.astype(BF16)
            stage_x[k, second] = to_all(total_cols(k, second, half), chunks + 1 + second * pairs + k)

    def finish_all_two(k):
        for second in range(2):
            stage_x[k, second][0].wait()
            last.append(stage_x[k, second][1])
            last.append(forward_to_core(total_cols(k, second, 1 - half), chunks + 1 + second * pairs + k))

    for k in range(pairs):
        start_one(k)

    for copy in qkv_copies:
        copy.wait()
    strips = [load_mod(0, 0), load_mod(1, 1)]
    grad_hidden = dot_rows(r.grad_qkv[:, : 2 * width], r.w_up[:, : 2 * width]) + dot_rows(
        r.grad_qkv[:, 2 * width :], r.w_out[...]
    )
    shift_rows, scale_rows, made = [], [], []
    for s, span in enumerate(seqs):
        normed, inverse = normalize(r.x[order[s]].astype(F32))
        grad = grad_hidden[span]
        shift_rows.append(jnp.sum(grad, axis=0, keepdims=True))
        scale_rows.append(jnp.sum(grad * normed, axis=0, keepdims=True))
        made.append(r.grad_mixed[span] + norm_back(normed, inverse, grad * (1.0 + mod(1, s))))
    r.grad_mixed[seqs[0]] = jnp.where(swapped, made[1], made[0])
    r.grad_mixed[seqs[1]] = jnp.where(swapped, made[0], made[1])
    last.append(local(r.grad_mixed.reshape(2, f, width), r.grad_inputs, r.in_sems.at[3]))
    bias = jnp.sum(r.grad_qkv[...].astype(F32), axis=0, keepdims=True)
    bias_rows = [bias[:, i * width : (i + 1) * width] for i in range(3)]
    kept = [r.stats[i : i + 1] for i in range(r.stats.shape[0])]
    shown_rows = jnp.where(me == 0, r.acts[...].astype(F32), 0.0)
    time_rows = [shown_rows[0:1], shown_rows[1:2]]
    r.small[...] = jnp.zeros_like(r.small)
    for i, row in enumerate(shift_rows + scale_rows + kept[:8] + bias_rows + kept[8:] + time_rows):
        for c in range(width // LANES):
            r.small[i, c : c + 1] = row[:, c * LANES : (c + 1) * LANES]

    per = r.small.shape[0] // n
    copies = []
    for step, device in enumerate(along):
        src = r.small.at[pl.ds(device[1] * per, per)]
        copies.append(push(src, r.small_in.at[step], r.small_one, (step,), device))
    finish_near(0)
    finish_near(1)
    finish_near(2)
    finish_far("down")
    finish_one(0)
    finish_far(0)
    total = r.small[pl.ds(me * per, per)]
    for step in range(n - 1):
        copies[step].wait()
        total = total + r.small_in[step]
    r.mine[...] = total
    own_slice = r.small_all.at[b, pl.ds(me * per, per)]
    own_slice[...] = total
    copies = []
    for step, device in enumerate(along):
        copies.append(push(r.mine, own_slice, r.small_two, (step,), device))
    finish_one(1)
    finish_two(0)
    finish_far(1)
    for k in range(2, pairs):
        finish_one(k)
        finish_two(k - 1)
    for copy in copies:
        copy.wait()
    for step, device in enumerate(across):
        last.append(push(r.small_all.at[b], r.small_all.at[b], r.small_three, (step,), device))

    for i in range(12):
        for c in range(width // LANES):
            start = i // 2 * width + c * LANES
            r.mods[i % 2 : i % 2 + 1, start : start + LANES] = r.small_all[b, i, c : c + 1]
    own = r.mods[...].astype(BF16)
    grad_act = jnp.zeros((2, width), F32)
    for i in range(12):
        strips[i].wait()
        grad_act = grad_act + dot_rows(own[:, i * half_width : (i + 1) * half_width], r.w_mod[i % 2])
        if i + 2 < 12:
            strips.append(load_mod(i + 2, i % 2))
        if i == 2:
            finish_far(2)
            finish_two(pairs - 1)
        if i == 5:
            finish_all("down")
            finish_far_two(0)
            finish_all(0)
        if i == 8:
            finish_all(1)
            finish_far_two(1)
    grad_act = jnp.where(swapped, jnp.concatenate([grad_act[1:2], grad_act[0:1]], axis=0), grad_act)
    shown = r.time_embed[...].astype(F32)
    sigmoid = 1.0 / (1.0 + jnp.exp(-shown))
    r.grad_time[...] = grad_act * (sigmoid * (1.0 + shown * (1.0 - sigmoid)))

    for k in range(2, chunks):
        finish_all(k)
    finish_all_two(0)
    for k in range(2, pairs):
        finish_far_two(k)
        finish_all_two(k - 1)
    finish_all_two(pairs - 1)
    for copy in last:
        copy.wait()


def layer(plan, sizes, batch, operands, collective_id):
    heads, chunk, chunk_two, block = sizes
    n, g, f, cols, width = plan.count, plan.groups, plan.frames, plan.cols, plan.width
    hidden = operands["w_up_hbm"].shape[1]
    tokens, rows, layers, units = 2 * f, width // n, hidden // width, cols // LANES
    wide, far = f * (LANES // (width // heads)), n // 2
    chunks, pairs = (width + hidden) // 2 // chunk, 3 * width // 2 // chunk_two // 2
    small_rows = -(-(19 + layers) // n) * n
    per, tile = small_rows // n, (width // LANES, LANES)
    vmem, smem = pl.BlockSpec(memory_space=pltpu.VMEM), pl.BlockSpec(memory_space=pltpu.SMEM)

    def sems(*shape):
        return pltpu.SemaphoreType.DMA(shape)

    def low(*shape):
        return pltpu.VMEM(shape, BF16)

    def high(*shape):
        return pltpu.VMEM(shape, F32)

    outs = dict(
        output=((2, f, width), F32),
        grad_inputs=((2, f, width), F32),
        grad_time=((2, width), F32),
        totals=((2, rows, 4 * width), BF16),
        small_all=((batch, small_rows) + tile, F32),
    )
    scratch = dict(
        x=low(2, f, width),
        ct=low(2, f, width),
        w_mod=low(2, width, width // 2),
        w_out=low(width, width),
        w_up=low(width, hidden),
        w_down=low(hidden, width),
        acts=low(2, width),
        cos=high(f, LANES),
        sin=high(f, LANES),
        b_row=high(1, 3 * width),
        mods=high(2, 6 * width),
        rows=low(g, tokens, 3 * cols),
        both_hidden=low(width, 2 * tokens),
        attn=low(tokens, width),
        q_buf=low(g, tokens, cols),
        kv_buf=low(n, f, 2 * cols),
        short_buf=low(plan.short_blocks, plan.short_rows, 2 * cols),
        lse=high(g, 2 * units, wide),
        o_buf=low(g, tokens, cols),
        turned=low(cols, plan.total),
        short_turned=low(cols, plan.short),
        top_acc=high(g * units, 1, wide),
        total_acc=high(g * units, 1, wide),
        o_acc=high(g * units, LANES, wide),
        mixed=high(tokens, width),
        branch_a=high(tokens, width),
        hidden_f=low(tokens, width),
        grad_ff=low(tokens, width),
        grad_pre=low(tokens, hidden),
        grad_br=low(tokens, width),
        attn_t=low(width, 2 * tokens),
        hid_t=low(width, 2 * tokens),
        act_own=low(n, rows, 4 * tokens),
        act_send=low(n, rows, tokens),
        all_ff=low(4, tokens, width // 2),
        both_pre=low(2, tokens, hidden // 2),
        both_br=low(2, tokens, width // 2),
        branch_f=high(tokens, width),
        grad_hid=high(tokens, width),
        grad_mixed=high(tokens, width),
        stats=high(10 + layers, width),
        parts=low(n, rows, chunks * chunk),
        x_buf=low(chunks, n, rows, chunk // 2),
        down_sum=low(n, rows, width // 2),
        near_down=low(far, rows, width // 2),
        far_down=low(far - 1, rows, width // 2),
        near_sums=low(chunks, far, rows, chunk // 2),
        far_one=low(chunks, far - 1, rows, chunk // 2),
        grads=low(tokens, width),
        g_buf=low(g, tokens, cols),
        dq_acc=high(g, f, cols),
        dlong=high(2, plan.largest, cols),
        dsmall=high(2, plan.short, cols),
        dq_out=low(tokens, width),
        dkv_out=low(2, plan.splits, f, width),
        dshort_out=low(2, plan.splits, plan.short_rows, width),
        dshort_buf=low(plan.short_blocks, 2, plan.short_rows, cols),
        grad_qkv=low(tokens, 3 * width),
        a_one=low(pairs, n, rows, chunk_two // 2),
        a_two=low(pairs, far, rows, chunk_two // 2),
        b_one=low(pairs, far, rows, chunk_two),
        b_two=low(pairs, far, rows, chunk_two // 2),
        far_two=low(2, pairs, far - 1, rows, chunk_two // 2),
        small=high(small_rows, *tile),
        small_in=high(n - 1, per, *tile),
        mine=high(per, *tile),
        in_sems=sems(5),
        m_sems=sems(4),
        q_sems=sems(2, g - 1),
        k_sems=sems(2, n - 1),
        s_sems=sems(2, plan.short_blocks, n - 1),
        o_sems=sems(2, g - 1),
        h_sems=sems(2),
        e_sems=sems(2, 5),
        ff_sems=sems(2, 2),
        act_sems=sems(2, 3, hidden // block),
        bg_sems=sems(2, g - 1),
        bq_sems=sems(2, g - 1),
        bk_sems=sems(2, 2, n),
        bs_sems=sems(2, n - 1),
        x_sems=sems(2, chunks),
        n_sems=sems(2, chunks + 1),
        f1_sems=sems(2, chunks + 1, far - 1),
        g_sems=sems(2, g // 2),
        a1_sems=sems(2, pairs),
        b1_sems=sems(2, pairs),
        a2_sems=sems(2, pairs),
        b2_sems=sems(2, pairs),
        f2_sems=sems(2, 2, pairs, far - 1),
        ax_sems=sems(2, chunks + 1 + 2 * pairs),
        ac_sems=sems(2, 2 * (chunks + 1 + 2 * pairs)),
        small_one=sems(2, n - 1),
        small_two=sems(2, n - 1),
        small_three=sems(2, batch - 1),
    )
    specs = [smem if k == "lengths" else in_hbm() if k.endswith("_hbm") else vmem for k in operands]
    names = tuple(operands) + tuple(outs) + tuple(scratch)
    return pl.pallas_call(
        partial(layer_kernel, plan, (heads, chunk, chunk_two, block, batch), names),
        in_specs=specs,
        out_specs=[in_hbm() if k in ("output", "grad_inputs") else vmem for k in outs],
        out_shape=[jax.ShapeDtypeStruct(*shape) for shape in outs.values()],
        scratch_shapes=list(scratch.values()),
        compiler_params=pltpu.CompilerParams(
            collective_id=collective_id, has_side_effects=True, vmem_limit_bytes=63 * MIB
        ),
        name="layer",
    )(*operands.values())


def finish_kernel(count, sizes, aligned, names, *refs):
    r = SimpleNamespace(**dict(zip(names, refs)))
    batch, width, layers = sizes
    rows = width // count
    me = lax.axis_index("blk")
    half = width // 2
    passed = [
        local(r.totals_hbm, r.totals, r.sems.at[0]),
        local(r.small_hbm, r.small, r.sems.at[1]),
        local(r.output_hbm, r.output, r.sems.at[2]),
        local(r.grad_inputs_hbm, r.grad_inputs, r.sems.at[3]),
        local(r.grad_time_hbm, r.grad_time, r.sems.at[4]),
    ]
    passed[0].wait()
    for core in range(2):
        for i in range(layers):
            made = r.totals[core, :, i * half : (i + 1) * half].astype(F32)
            r.down_made[i * rows : (i + 1) * rows, core * half : (core + 1) * half] = made
    passed.append(local(r.down_made, r.down, r.sems.at[5]))
    for core in range(2):
        start = layers * half
        made = r.totals[core, :, start : start + layers * half].astype(F32)
        r.up_made[:, core * layers * half : (core + 1) * layers * half] = made
    passed.append(local(r.up_made, r.up, r.sems.at[6]))
    for core in range(2):
        start = 2 * layers * half
        r.out_made[:, core * half : (core + 1) * half] = r.totals[core, :, start : start + half].astype(F32)
        made = r.totals[core, :, start + half : start + 4 * half].astype(F32)
        r.qkv_made[:, core * 3 * half : (core + 1) * 3 * half] = made
    passed.append(local(r.out_made, r.out, r.sems.at[7]))
    passed.append(local(r.qkv_made, r.qkv, r.sems.at[8]))
    passed[1].wait()
    for u in range(2 * batch):
        b, s = u // 2, u % 2
        line = r.small[b, 15 + 2 + layers + s, pl.ds(me * rows // LANES, 1)]
        if rows < LANES:
            line = pltpu.roll(line, LANES - lax.rem(me, LANES // rows) * rows, 1)
        r.times[u : u + 1] = line
        for p in range(6):
            for c in range(width // LANES):
                start = p * width + c * LANES
                r.mods[u : u + 1, start : start + LANES] = r.small[b, 2 * p + s, c : c + 1]
    times, mods = r.times[:, :rows].astype(BF16), r.mods[...].astype(BF16)
    for i in range(2):
        span = slice(i * 3 * width, (i + 1) * 3 * width)
        r.w_mod_made[:, span] = dot_frames(times, mods[:, span])
        passed.append(local(r.w_mod_made.at[:, span], r.w_mod.at[:, span], r.sems.at[9 + i]))
    if aligned:
        tiles = width // LANES

        def own_lines(first, length, stride):
            lines = []
            for i in range(length // count // LANES):
                at = me * (length // count // LANES) + i
                total = jnp.zeros((1, LANES), F32)
                for b in range(batch):
                    for s in range(stride):
                        total = total + r.small[b, first + at // tiles * stride + s, pl.ds(lax.rem(at, tiles), 1)]
                lines.append(total)
            return lines

        firsts = [(0, 6, 2), (12, 3, 1), (15, 1, 1), (16, layers, 1), (16 + layers, 1, 1)]
        for which, (first, many, stride) in enumerate(firsts):
            ref = getattr(r, "vector%d" % which)
            for i, line in enumerate(own_lines(first, many * width, stride)):
                ref[i * LANES : (i + 1) * LANES] = line[0]
    for copy in passed[2:]:
        copy.wait()


def finish(count, output, grad_inputs, grad_time, totals, small, layers):
    batch, width = small.shape[0], output.shape[2]
    rows = width // count
    aligned = rows % LANES == 0
    operands = dict(
        output_hbm=output, grad_inputs_hbm=grad_inputs, grad_time_hbm=grad_time, totals_hbm=totals, small_hbm=small
    )
    shapes = dict(
        down=(layers * rows, width),
        up=(rows, layers * width),
        out=(rows, width),
        qkv=(rows, 3 * width),
        w_mod=(rows, 6 * width),
    )
    outs = dict(output=output.shape, grad_inputs=output.shape, grad_time=grad_time.shape, **shapes)
    vectors = {}
    if aligned:
        vectors = {"vector%d" % i: (many * rows,) for i, many in enumerate((6, 3, 1, layers, 1))}
    scratch = {k + "_made": pltpu.VMEM(v, F32) for k, v in shapes.items()}
    scratch.update(
        totals=pltpu.VMEM(totals.shape, BF16),
        small=pltpu.VMEM(small.shape, F32),
        times=pltpu.VMEM((2 * batch, LANES), F32),
        mods=pltpu.VMEM((2 * batch, 6 * width), F32),
        sems=pltpu.SemaphoreType.DMA((11,)),
    )
    names = tuple(operands) + tuple(outs) + tuple(vectors) + tuple(scratch)
    made = pl.pallas_call(
        partial(finish_kernel, count, (batch, width, layers), aligned, names),
        in_specs=[in_hbm()] * len(operands),
        out_specs=[in_hbm()] * len(outs) + [pl.BlockSpec(memory_space=pltpu.VMEM)] * len(vectors),
        out_shape=[jax.ShapeDtypeStruct(v, F32) for v in (outs | vectors).values()],
        scratch_shapes=list(scratch.values()),
        compiler_params=pltpu.CompilerParams(vmem_limit_bytes=40 * MIB),
        name="finish",
    )(*operands.values())
    if not aligned:
        me = lax.axis_index("blk")
        flat = jnp.sum(small.reshape(batch, -1, width), axis=0)
        mods = flat[:12].reshape(6, 2, width).sum(axis=1)
        ends = [12, 15, 16, 16 + layers, 17 + layers]
        rest = [mods] + [flat[lo:hi] for lo, hi in zip(ends[:-1], ends[1:])]
        made = list(made) + [
            lax.dynamic_index_in_dim(v.reshape(count, -1), me, 0, keepdims=False) for v in rest
        ]
    return made


def on_device(
    inputs,
    time_embed,
    lengths,
    cotangent,
    w_mod,
    b_mod,
    w_qkv,
    b_qkv,
    w_out,
    b_out,
    w_up,
    b_up,
    w_down,
    b_down,
):
    _, frames, width = inputs.shape
    half = width // HEADS // 2
    count, batch = lax.axis_size("blk"), lax.axis_size("batch")
    plan = Plan(count, frames, width)
    freqs = 10000.0 ** (-jnp.arange(half, dtype=F32) / half)
    operands = dict(
        lengths=lengths,
        time_embed=time_embed,
        freqs=jnp.tile(freqs, LANES // half)[None],
        b_mod=b_mod,
        b_qkv=b_qkv,
        b_out=b_out,
        b_up=b_up,
        b_down=b_down,
        x_hbm=inputs,
        ct_hbm=cotangent,
        w_mod_hbm=w_mod,
        w_qkv_hbm=w_qkv,
        w_out_hbm=w_out,
        w_up_hbm=w_up,
        w_down_hbm=w_down,
    )
    made = layer(plan, (HEADS, 512, 256, 512), batch, operands, 0)
    output, grad_inputs, grad_time, down, up, out, qkv, grad_w_mod, *vectors = finish(
        count, *made, w_up.shape[1] // width
    )
    return (
        output,
        grad_inputs,
        grad_time,
        grad_w_mod,
        vectors[0],
        qkv,
        vectors[1],
        out,
        vectors[2],
        up,
        vectors[3],
        down,
        vectors[4],
    )


def solution(mesh):
    frame_spec, weight_spec = P("batch", "blk", None), P("blk", None)
    return jax.shard_map(
        on_device,
        mesh=mesh,
        in_specs=(frame_spec, P("batch", None), P("batch"), frame_spec) + (P(),) * 10,
        out_specs=(frame_spec, frame_spec, P("batch", None)) + (weight_spec, P("blk")) * 5,
        check_vma=False,
    )
```

```python
from functools import partial
from types import SimpleNamespace

import jax
import jax.numpy as jnp
from jax import lax
from jax.experimental import pallas as pl
from jax.experimental.pallas import tpu as pltpu
from jax.sharding import PartitionSpec as P

HEADS = 16
EPS = 1e-06
LANES = 128
SHORT = 16
MESH = pl.DeviceIdType.MESH
BF16 = jnp.bfloat16
F32 = jnp.float32
MIB = 1 << 20


def dot(left, right):
    return jnp.dot(left, right, preferred_element_type=F32)


def dot_rows(left, right):
    return lax.dot_general(left, right, (((1,), (1,)), ((), ())), preferred_element_type=F32)


def dot_frames(left, right):
    return lax.dot_general(left, right, (((0,), (0,)), ((), ())), preferred_element_type=F32)


def normalize(rows):
    mean = jnp.mean(rows, axis=-1, keepdims=True)
    centered = rows - mean
    inverse = lax.rsqrt(jnp.mean(centered * centered, axis=-1, keepdims=True) + EPS)
    return (centered * inverse, inverse)


def norm_back(normed, inverse, grad):
    return inverse * (
        grad
        - jnp.mean(grad, axis=-1, keepdims=True)
        - normed * jnp.mean(grad * normed, axis=-1, keepdims=True)
    )


def whole(shape):
    return pl.BlockSpec(shape, lambda *_: (0,) * len(shape))


def in_hbm():
    return pl.BlockSpec(memory_space=pltpu.HBM)


def rotate(rows, cos_table, sin_table, half):
    lane = lax.broadcasted_iota(jnp.int32, rows.shape, 1)
    partner = jnp.where(
        lax.rem(lane, 2 * half) < half,
        pltpu.roll(rows, LANES - half, 1),
        pltpu.roll(rows, half, 1),
    )
    return rows * cos_table + partner * sin_table


class Spot:
    def __init__(self, count):
        b, j = lax.axis_index("batch"), lax.axis_index("blk")
        self.b, self.j = b, j
        self.core, self.half = lax.rem(b, 2), b // 2
        self.near, self.far = lax.rem(j, 2), j // 2
        self.far_count = count // 2
        self.at_core = (self.half * 2 + 1 - self.core, j)
        self.at_x = ((1 - self.half) * 2 + self.core, j)
        self.at_both = ((1 - self.half) * 2 + 1 - self.core, j)
        self.at_near = (b, self.far * 2 + 1 - self.near)
        self.far_steps = [lax.rem(self.far + step, self.far_count) for step in range(1, self.far_count)]
        self.at_far = [(b, step * 2 + self.near) for step in self.far_steps]


def add_into(target, other):
    target[...] = (target[...].astype(F32) + other.astype(F32)).astype(BF16)


class Plan:
    def __init__(self, count, frames, width):
        self.count = count
        self.frames = frames
        self.width = width
        self.groups = min(max(count // 2, 1), 4)
        self.cols = width // self.groups
        self.splits = count // self.groups
        self.total = count * frames
        self.short = self.total // SHORT
        self.short_rows = min(self.short, frames)
        self.short_blocks = -(-self.short // frames)
        self.phases = [(lo, min(lo + 4 * self.groups, count)) for lo in range(self.groups, count, 4 * self.groups)]
        self.phases = [(0, self.groups)] + self.phases
        self.largest = max(hi - lo for lo, hi in self.phases) * frames
        self.offsets = [(d, s) for d in range(self.splits) for s in range(self.groups) if d + s > 0]

    def peer(self, device, offset):
        split = lax.rem(device // self.groups + offset[0], self.splits)
        return split * self.groups + lax.rem(lax.rem(device, self.groups) + offset[1], self.groups)


def push(src, dst, sems, index, device):
    copy = pltpu.make_async_remote_copy(
        src_ref=src, dst_ref=dst, send_sem=sems.at[(0,) + index], recv_sem=sems.at[(1,) + index],
        device_id=device, device_id_type=MESH,
    )
    copy.start()
    return copy


def local(src, dst, sem):
    copy = pltpu.make_async_copy(src, dst, sem)
    copy.start()
    return copy


def stacked(rows, head_dim):
    lane = lax.broadcasted_iota(jnp.int32, rows.shape, 1)
    heads = LANES // head_dim
    return jnp.concatenate(
        [jnp.where(lane // head_dim == h, rows, jnp.zeros_like(rows)) for h in range(heads)], axis=0
    )


def unstacked(turned, frames, head_dim):
    heads = LANES // head_dim
    return jnp.concatenate(
        [
            turned[h * head_dim : (h + 1) * head_dim, h * frames : (h + 1) * frames]
            for h in range(heads)
        ],
        axis=0,
    ).T


def attend_part(queries, keys, values_t, head_dim):
    scores = dot_rows(keys, stacked(queries, head_dim))
    top = jnp.max(scores, axis=0, keepdims=True)
    weights = jnp.exp(scores - top)
    total = jnp.sum(weights, axis=0, keepdims=True)
    return top, total, dot(values_t, weights.astype(BF16))


def attend_join(one, two):
    top = jnp.maximum(one[0], two[0])
    left, right = jnp.exp(one[0] - top), jnp.exp(two[0] - top)
    return top, one[1] * left + two[1] * right, one[2] * left + two[2] * right


def attend_end(state, frames, head_dim):
    top, total, out = state
    return unstacked(out / total, frames, head_dim).astype(BF16), top + jnp.log(total)


def delta_rows(grads, outs, head_dim):
    heads = LANES // head_dim
    lane = lax.broadcasted_iota(jnp.int32, (8, LANES), 1)
    pick = (lane // head_dim == lax.broadcasted_iota(jnp.int32, (8, LANES), 0)).astype(F32)
    product = grads.astype(F32) * outs.astype(F32)
    sums = lax.dot_general(
        pick, product, (((1,), (1,)), ((), ())), precision=lax.Precision.HIGHEST, preferred_element_type=F32
    )
    return jnp.concatenate([sums[h : h + 1] for h in range(heads)], axis=1)


def attend_back(queries, grads, lse, delta, keys, keys_t, values, head_dim):
    frames = queries.shape[0]
    q_heads, g_heads = stacked(queries, head_dim), stacked(grads, head_dim)
    probs = jnp.exp(dot_rows(keys, q_heads) - lse)
    grad_probs = dot_rows(values, g_heads)
    grad_scores = (probs * (grad_probs - delta)).astype(BF16)
    grad_values = dot(probs.astype(BF16), g_heads)
    grad_keys = dot(grad_scores, q_heads)
    grad_queries = unstacked(dot(keys_t, grad_scores), frames, head_dim) * head_dim ** (-0.5)
    return grad_queries, grad_keys, grad_values


def gelu_both(z):
    scale = (2.0 / 3.141592653589793) ** 0.5
    square = z * z
    inner = jnp.tanh(scale * z * (1.0 + 0.044715 * square))
    half = 0.5 * (1.0 + inner)
    slope = half + 0.5 * z * (1.0 - inner * inner) * (scale * (1.0 + 3.0 * 0.044715 * square))
    return z * half, slope


def layer_kernel(plan, sizes, names, *refs):
    r = SimpleNamespace(**dict(zip(names, refs)))
    r.came_at = lambda kind, t: getattr(r, "came_%s_%d" % (kind, t))
    heads, chunk, chunk_two, block, batch = sizes
    n, g, f, cols, width = plan.count, plan.groups, plan.frames, plan.cols, plan.width
    tokens, hidden = 2 * f, r.w_up.shape[1]
    head_dim, half_dim = width // heads, width // heads // 2
    half_width, half_hidden = width // 2, hidden // 2
    layers, n_rows, units = hidden // width, width // n, cols // LANES
    spot = Spot(n)
    b, me, core, half = spot.b, spot.j, spot.core, spot.half
    group, split = lax.rem(me, g), me // g
    others = [plan.peer(me, offset) for offset in plan.offsets]
    mates = others[: g - 1]
    along = [(b, peer) for peer in others]
    across = [(lax.rem(b + step, batch), me) for step in range(1, batch)]
    seqs = [slice(0, f), slice(f, tokens)]
    mine, theirs = slice(0, tokens), slice(tokens, 2 * tokens)
    swapped = r.lengths[0] < r.lengths[1]
    first = jnp.where(swapped, 1, 0)
    order = [first, 1 - first]

    barrier = pltpu.get_barrier_semaphore()
    for device in along + across:
        pl.semaphore_signal(barrier, inc=1, device_id=device, device_id_type=MESH)

    load_x = local(r.x_hbm, r.x, r.in_sems.at[0])
    mod_places, mod_copies = [r.w_mod.at[0], r.w_mod.at[1]], {}
    room = r.parts.reshape(width, r.parts.shape[2])
    mod_places += [room.at[:, :half_width], room.at[:, half_width:width]]
    ahead = len(mod_places)

    def mod_place(i):
        return i if i < ahead else i % 2

    def load_mod(i, place):
        return local(r.w_mod_hbm.at[:, i * half_width : (i + 1) * half_width], mod_places[place], r.m_sems.at[place])

    def next_mod(i):
        if mod_place(i) < 2:
            after = i + ahead if i < 2 else i + 2
            if after < 12:
                mod_copies[after] = load_mod(after, mod_place(after))

    def load_qkv():
        return [
            local(r.w_qkv_hbm.at[:, : 2 * width], r.w_up.at[:, : 2 * width], r.in_sems.at[1]),
            local(r.w_qkv_hbm.at[:, 2 * width :], r.w_out, r.in_sems.at[2]),
        ]

    for i in range(ahead):
        mod_copies[i] = load_mod(i, i)
    qkv_copies = load_qkv()

    shown = r.time_embed[...].astype(F32)
    shown = jnp.where(swapped, jnp.concatenate([shown[1:2], shown[0:1]], axis=0), shown)
    r.acts[...] = (shown / (1.0 + jnp.exp(-shown))).astype(BF16)
    frame = me * f + lax.broadcasted_iota(jnp.int32, (f, LANES), 0)
    angle = frame.astype(F32) * r.freqs[...]
    lane = lax.broadcasted_iota(jnp.int32, (f, LANES), 1)
    sines = jnp.sin(angle)
    r.cos[...] = jnp.cos(angle)
    r.sin[...] = jnp.where(lax.rem(lane, 2 * half_dim) < half_dim, -sines, sines)
    r.b_row[...] = r.b_qkv[...][None].astype(F32)

    def mod_piece(i, place):
        piece = slice(i * half_width, (i + 1) * half_width)
        r.mods[:, piece] = dot(r.acts[...], mod_places[place][...]) + r.b_mod[piece][None].astype(F32)

    def mod(i, s):
        return r.mods[s : s + 1, i * width : (i + 1) * width]

    for i in range(4):
        mod_copies[i].wait()
        mod_piece(i, mod_place(i))
        next_mod(i)

    load_x.wait()
    for s, span in enumerate(seqs):
        normed, _ = normalize(r.x[order[s]].astype(F32))
        r.hidden_f[span] = (normed * (1.0 + mod(1, s)) + mod(0, s)).astype(BF16)
    for copy in qkv_copies:
        copy.wait()
    load_ct = local(r.ct_hbm, r.ct, r.in_sems.at[3])
    load_down = local(r.w_down_hbm, r.w_down, r.in_sems.at[4])
    pl.semaphore_wait(barrier, len(along + across))

    def project(kind, which):
        at = pl.ds(pl.multiple_of(which * cols, LANES), cols)
        bias_at = pl.ds(pl.multiple_of(kind * width + which * cols, LANES), cols)
        weight = r.w_out[:, at] if kind == 2 else r.w_up[:, bias_at]
        made = dot(r.hidden_f[...], weight) + r.b_row[:, bias_at]
        if kind < 2:
            factor = (2.0 * half_dim) ** (-0.5) if kind == 0 else 1.0
            cosines, sines = r.cos[...] * factor, r.sin[...] * factor
        for span in seqs:
            for u in range(units):
                part = made[span, u * LANES : (u + 1) * LANES]
                if kind < 2:
                    part = rotate(part, cosines, sines, half_dim)
                start = kind * cols + u * LANES
                r.rows[which, span, start : start + LANES] = part.astype(BF16)

    near_waits = []

    def send_keys(step):
        offset = plan.offsets[step]
        src = r.rows.at[lax.rem(others[step], g), 0:f, cols : 3 * cols]
        dst = r.kv_buf.at[offset[0] * g + group]
        return push(src, dst, r.k_sems, (step,), along[step])

    def short_rows_of(peer):
        return r.rows.at[lax.rem(peer, g), f : f + plan.short_rows, cols : 3 * cols]

    def pass_on(blk):
        for d in range(1, plan.splits):
            place = r.short_buf.at[blk]
            push(place, place, r.s_sems, (blk, g - 2 + d), along[d * g - 1])

    inner = jnp.logical_or(lax.rem(spot.far, 4) == 1, lax.rem(spot.far, 4) == 2)
    for step in range(1, g + 1):
        which = lax.rem(group + step, g)
        project(1, which)
        project(2, which)

    @pl.when(inner)
    def _():
        for step in range(g - 1, n - 1):
            send_keys(step)

    for step in range(g - 1):
        near_waits.append(send_keys(step))
    for step in range(1, g + 1):
        which = lax.rem(group + step, g)
        project(0, which)
        if step < g:
            src = r.rows.at[which, :, 0:cols]
            near_waits.append(push(src, r.q_buf.at[group], r.q_sems, (step - 1,), along[step - 1]))

    for blk in range(plan.short_blocks):

        @pl.when(me == blk)
        def _():
            for step, peer in enumerate(mates):
                push(short_rows_of(peer), r.short_buf.at[blk], r.s_sems, (blk, step), along[step])
            r.short_buf[blk] = r.rows[group, f : f + plan.short_rows, cols : 3 * cols]
            pass_on(blk)

    @pl.when(jnp.logical_not(inner))
    def _():
        for step in range(g - 1, n - 1):
            send_keys(step)

    def lot(i):
        return slice(i * tokens, (i + 1) * tokens)

    around = [spot.at_core, spot.at_x, spot.at_both]
    r.both_hidden[:, lot(0)] = r.hidden_f[...].T
    swap_hidden = [
        push(r.both_hidden.at[:, lot(0)], r.both_hidden.at[:, lot(i + 1)], r.h_sems, (i,), device)
        for i, device in enumerate(around)
    ]
    load_out = local(r.w_out_hbm, r.w_out, r.in_sems.at[2])
    load_up = local(r.w_up_hbm, r.w_up, r.in_sems.at[1])
    r.kv_buf[group] = r.rows[group, 0:f, cols : 3 * cols]
    r.q_buf[group] = r.rows[group, :, 0:cols]

    for i in range(4, 12):
        mod_copies[i].wait()
        mod_piece(i, mod_place(i))
        next_mod(i)

    load_ct.wait()
    for s, span in enumerate(seqs):
        r.grad_ff[span] = (mod(5, s) * r.ct[order[s]].astype(F32)).astype(BF16)

    def core_half(which, size):
        return pl.ds(pl.multiple_of(which * size, LANES), size)

    def to_core(src, dst, index):
        return push(src, dst, r.e_sems, (index,), spot.at_core)

    ff_own, ff_other = core_half(core, half_width), core_half(1 - core, half_width)
    swap_ff = [
        to_core(r.grad_ff.at[:, ff_other], r.all_ff.at[1], 0),
        push(r.grad_ff.at[:, ff_own], r.all_ff.at[2], r.ff_sems, (0,), spot.at_x),
        push(r.grad_ff.at[:, ff_other], r.all_ff.at[3], r.ff_sems, (1,), spot.at_both),
    ]
    r.all_ff[0] = r.grad_ff[:, ff_own]

    for copy in near_waits:
        copy.wait()
    for blk in range(plan.short_blocks):
        for step in range(g - 1):

            @pl.when(me == plan.peer(blk, plan.offsets[step]))
            def _():
                dst = r.short_buf.at[blk]
                pltpu.make_async_copy(dst, dst, r.s_sems.at[1, blk, step]).wait()
                pass_on(blk)

    def turn_values(lo, hi, start):
        part = r.kv_buf[lo:hi, :, start : start + cols].reshape((hi - lo) * f, cols)
        r.turned[:, lo * f : hi * f] = part.T

    def cols_of(which):
        return pl.ds(pl.multiple_of(which * cols, LANES), cols)

    def slot_of(step):
        return lax.rem(group + 1 + step, g)

    units = cols // LANES
    sends = []
    for phase, (lo, hi) in enumerate(plan.phases):
        last = phase == len(plan.phases) - 1
        if phase == 1:
            for step in range(g - 1, n - 1):
                src = r.rows.at[group, 0:f, cols : 3 * cols]
                pltpu.make_async_copy(src, src, r.k_sems.at[0, step]).wait()
                dst = r.kv_buf.at[plan.offsets[step][0] * g + lax.rem(group + g - plan.offsets[step][1], g)]
                pltpu.make_async_copy(dst, dst, r.k_sems.at[1, step]).wait()
        turn_values(lo, hi, cols)
        for step in range(g):
            slot = slot_of(step)
            for u in range(units):
                lanes = slice(u * LANES, (u + 1) * LANES)
                at = step * units + u
                state = attend_part(
                    r.q_buf[slot, :f, lanes],
                    r.kv_buf[lo:hi, :, lanes].reshape((hi - lo) * f, LANES),
                    r.turned[lanes, lo * f : hi * f],
                    head_dim,
                )
                if phase > 0:
                    state = attend_join((r.top_acc[at], r.total_acc[at], r.o_acc[at]), state)
                if last:
                    r.o_buf[slot, :f, lanes], r.lse[slot, u : u + 1] = attend_end(state, f, head_dim)
                else:
                    r.top_acc[at], r.total_acc[at], r.o_acc[at] = state
            if last and step == 0:
                for blk in range(plan.short_blocks):
                    for d in range(1, plan.splits):

                        @pl.when(split == (blk // g + d) % plan.splits)
                        def _():
                            dst = r.short_buf.at[blk]
                            pltpu.make_async_copy(dst, dst, r.s_sems.at[1, blk, g - 2 + d]).wait()

                r.short_turned[...] = r.short_buf[:, :, cols:].reshape(plan.short, cols).T
            if last:
                for u in range(units):
                    lanes = slice(u * LANES, (u + 1) * LANES)
                    keys = r.short_buf[:, :, lanes].reshape(plan.short, LANES)
                    state = attend_part(r.q_buf[slot, f:, lanes], keys, r.short_turned[lanes], head_dim)
                    row = units + u
                    r.o_buf[slot, f:, lanes], r.lse[slot, row : row + 1] = attend_end(state, f, head_dim)
                if step == g - 1:
                    r.attn[:, cols_of(group)] = r.o_buf[slot]
                else:
                    dst = r.attn.at[:, cols_of(group)]
                    sends.append(push(r.o_buf.at[slot], dst, r.o_sems, (step,), along[step]))
    for lo, hi in plan.phases:
        turn_values(lo, hi, 0)
    r.short_turned[...] = r.short_buf[:, :, :cols].reshape(plan.short, cols).T
    for copy in sends:
        copy.wait()
    for blk in range(plan.short_blocks):

        @pl.when(me == blk)
        def _():
            for step, peer in enumerate(mates):
                src = short_rows_of(peer)
                pltpu.make_async_copy(src, src, r.s_sems.at[0, blk, step]).wait()

        @pl.when(split == blk // g)
        def _():
            for d in range(1, plan.splits):
                src = r.short_buf.at[blk]
                pltpu.make_async_copy(src, src, r.s_sems.at[0, blk, g - 2 + d]).wait()

    load_out.wait()
    r.attn_t[:, mine] = r.attn[...].T
    swap_attn = to_core(r.attn_t.at[:, mine], r.attn_t.at[:, theirs], 1)
    r.branch_a[...] = dot(r.attn[...], r.w_out[...]) + r.b_out[...][None].astype(F32)
    for s, span in enumerate(seqs):
        r.mixed[span] = r.x[order[s]].astype(F32) + mod(2, s) * r.branch_a[span]
        normed, _ = normalize(r.mixed[span])
        r.hidden_f[span] = (normed * (1.0 + mod(4, s)) + mod(3, s)).astype(BF16)
    r.hid_t[:, mine] = r.hidden_f[...].T
    swap_hid = to_core(r.hid_t.at[:, mine], r.hid_t.at[:, theirs], 2)
    load_up.wait()
    load_down.wait()
    swap_act, act_x = [], []
    per_block = block // (layers * n_rows)
    for i in range(hidden // block):
        span = slice(i * block, (i + 1) * block)
        act, slope = gelu_both(dot(r.hidden_f[...], r.w_up[:, span]) + r.b_up[span][None].astype(F32))
        act = act.astype(BF16)
        act_t = act.T.reshape(per_block, layers, n_rows, tokens)
        held = slice(i * per_block, (i + 1) * per_block)
        r.act_own[held, :, mine] = jnp.where(half == 0, act_t[:, 0], act_t[:, 1])
        r.act_send[held] = jnp.where(half == 0, act_t[:, 1], act_t[:, 0])
        act_x.append(
            push(r.act_send.at[held], r.act_own.at[held, :, 2 * tokens : 3 * tokens], r.act_sems, (0, i), spot.at_x)
        )
        swap_act.append(
            push(r.act_own.at[held, :, mine], r.act_own.at[held, :, theirs], r.act_sems, (1, i), spot.at_core)
        )
        forward = dot(act, r.w_down[span, :])
        grad = (dot_rows(r.grad_ff[...], r.w_down[span, :]) * slope).astype(BF16)
        r.grad_pre[:, span] = grad
        row, start = 9 + i * block // width, i * block % width
        r.stats[row : row + 1, start : start + block] = jnp.sum(grad.astype(F32), axis=0, keepdims=True)
        back = dot_rows(grad, r.w_up[:, span])
        if i == 0:
            r.branch_f[...] = forward + r.b_down[...][None].astype(F32)
            r.grad_hid[...] = back
        else:
            r.branch_f[...] += forward
            r.grad_hid[...] += back
    swap_pre = to_core(r.grad_pre.at[:, core_half(1 - core, half_hidden)], r.both_pre.at[1], 3)
    r.both_pre[0] = r.grad_pre[:, core_half(core, half_hidden)]

    chunks, half_chunk = r.parts.shape[2] // chunk, chunk // 2
    base_one = layers * half_width
    x_copies, stage_copies, stage_of, last, sent = {}, {}, {}, [], {}

    def half_of(k, which):
        return pl.ds(pl.multiple_of(k * chunk + which * half_chunk, LANES), half_chunk)

    stages = range(n.bit_length() - 1)
    pieces = 3 * cols // chunk_two
    rooms = {k: (r.x_buf.at[k], [r.came_at("one", t).at[k] for t in stages], k) for k in range(chunks)}
    rooms["down"] = (r.down_sum, [r.came_at("down", t) for t in stages], chunks)
    for i in range(pieces):
        rooms["qkv", i] = (r.qkv_sum.at[i], [r.came_at("qkv", t).at[i] for t in stages], chunks + 1 + i)

    def total_of(k, which):
        if k == "down":
            return core_half(which, half_width)
        if k in range(chunks):
            return pl.ds(pl.multiple_of(base_one + k * chunk + which * half_chunk, LANES), half_chunk)
        start = base_one + chunks * chunk + which * 3 * cols + k[1] * chunk_two
        return pl.ds(pl.multiple_of(start, LANES), chunk_two)

    def start_x(k):
        src = r.parts.at[:, :, half_of(k, 1 - half)]
        x_copies[k] = push(src, r.x_buf.at[k], r.x_sems, (k,), spot.at_x)

    bits = [lax.rem(me // (1 << t), 2) for t in stages]
    partners = [(b, me + (1 - 2 * bit) * (1 << t)) for t, bit in enumerate(bits)]

    def halves(k, t):
        held = rooms[k][0] if t == 0 else rooms[k][1][t - 1]
        return held.reshape(n >> (t + 1), 2, n_rows, held.shape[2])

    def start_stage(k, t):
        _, came, number = rooms[k]
        stage_of[k] = t
        stage_copies[k] = push(halves(k, t).at[:, 1 - bits[t]], came[t], r.blk_sems, (number, t), partners[t])

    def finish_x(k):
        x_copies[k].wait()
        add_into(r.x_buf.at[k], r.parts[:, :, half_of(k, half)])
        start_stage(k, 0)

    def advance(k):
        t = stage_of[k]
        _, came, number = rooms[k]
        stage_copies[k].wait()
        if t + 1 < len(stages):
            add_into(came[t], halves(k, t)[:, bits[t]])
            start_stage(k, t + 1)
        else:
            total = came[t][0].astype(F32) + halves(k, t)[0, bits[t]].astype(F32)
            r.totals[core, :, total_of(k, half)] = total.astype(BF16)
            sent[k] = to_all(total_of(k, half), number)

    def to_all(where, which):
        place = r.totals.at[core, :, where]
        return [
            push(place, place, r.ax_sems, (which,), spot.at_x),
            push(place, place, r.ac_sems, (2 * which,), spot.at_core),
        ]

    def forward_to_core(where, which):
        place = r.totals.at[core, :, where]
        return push(place, place, r.ac_sems, (2 * which + 1,), spot.at_core)

    def finish_all(k):
        while k not in sent:
            advance(k)
        sent[k][0].wait()
        last.append(sent[k][1])
        last.append(forward_to_core(total_of(k, 1 - half), rooms[k][2]))

    for s, span in enumerate(seqs):
        grad_out = r.ct[order[s]].astype(F32)
        branch, grad = r.branch_f[span], r.grad_hid[span]
        normed, inverse = normalize(r.mixed[span])
        r.stats[6 + s : 7 + s] = jnp.sum(grad_out * branch, axis=0, keepdims=True)
        r.stats[4 + s : 5 + s] = jnp.sum(grad * normed, axis=0, keepdims=True)
        r.stats[2 + s : 3 + s] = jnp.sum(grad, axis=0, keepdims=True)
        total = grad_out + norm_back(normed, inverse, grad * (1.0 + mod(4, s)))
        r.grad_mixed[span] = total
        r.stats[s : s + 1] = jnp.sum(total * r.branch_a[span], axis=0, keepdims=True)
        r.grad_br[span] = (mod(2, s) * total).astype(BF16)
    r.grads[...] = dot_rows(r.grad_br[...], r.w_out[...]).astype(BF16)
    waits = []
    for step, peer in enumerate(mates):
        src = r.grads.at[:, cols_of(lax.rem(peer, g))]
        waits.append(push(src, r.g_buf.at[group], r.bg_sems, (step,), along[step]))
    r.g_buf[group] = r.grads[:, cols_of(group)]
    swap_br = to_core(r.grad_br.at[:, core_half(1 - core, half_width)], r.both_br.at[1], 4)
    qkv_copies = load_qkv()

    for i, copy in enumerate(act_x):
        copy.wait()
        held = slice(i * per_block, (i + 1) * per_block)
        src = r.act_own.at[held, :, 2 * tokens : 3 * tokens]
        dst = r.act_own.at[held, :, 3 * tokens : 4 * tokens]
        swap_act.append(push(src, dst, r.act_sems, (2, i), spot.at_core))
    swap_hid.wait()
    swap_pre.wait()
    for i in range(layers):
        grad = r.both_pre[:, :, i * half_width : (i + 1) * half_width].reshape(2 * tokens, half_width)
        up = dot(r.hid_t[...], grad).astype(BF16).reshape(n, n_rows, half_width)
        r.parts[:, :, i * half_width : (i + 1) * half_width] = up
        start_x(i)
    for copy in swap_ff + swap_act:
        copy.wait()
    down = dot(r.act_own[...].reshape(width, 4 * tokens), r.all_ff[...].reshape(4 * tokens, half_width))
    r.down_sum[...] = down.astype(BF16).reshape(n, n_rows, half_width)
    start_stage("down", 0)
    r.both_br[0] = r.grad_br[:, core_half(core, half_width)]
    swap_attn.wait()
    swap_br.wait()
    out_part = dot(r.attn_t[...], r.both_br[...].reshape(2 * tokens, half_width))
    r.parts[:, :, layers * half_width :] = out_part.astype(BF16).reshape(n, n_rows, half_width)
    start_x(layers)
    made = [r.mixed[span] + mod(5, s) * r.branch_f[span] for s, span in enumerate(seqs)]
    r.mixed[seqs[0]] = jnp.where(swapped, made[1], made[0])
    r.mixed[seqs[1]] = jnp.where(swapped, made[0], made[1])
    last.append(local(r.mixed.reshape(2, f, width), r.output, r.in_sems.at[0]))
    last_row = 9 + layers
    r.stats[8:9] = jnp.sum(r.grad_br[...].astype(F32), axis=0, keepdims=True)
    r.stats[last_row : last_row + 1] = jnp.sum(r.grad_ff[...].astype(F32), axis=0, keepdims=True)
    for copy in waits:
        copy.wait()

    strips = {i: load_mod(i, i % 2) for i in (4, 5)}

    sends = []
    deltas = [
        [
            [
                delta_rows(r.g_buf[slot_of(step), span, lanes], r.o_buf[slot_of(step), span, lanes], head_dim)
                for lanes in [slice(u * LANES, (u + 1) * LANES) for u in range(units)]
            ]
            for span in seqs
        ]
        for step in range(g)
    ]
    dq_buf = r.o_buf
    for step in range(g):
        slot = slot_of(step)
        for u in range(units):
            lanes = slice(u * LANES, (u + 1) * LANES)
            high = slice(cols + u * LANES, cols + (u + 1) * LANES)
            row = units + u
            dq, dk, dv = attend_back(
                r.q_buf[slot, f:, lanes],
                r.g_buf[slot, f:, lanes],
                r.lse[slot, row : row + 1],
                deltas[step][1][u],
                r.short_buf[:, :, lanes].reshape(plan.short, LANES),
                r.short_turned[lanes],
                r.short_buf[:, :, high].reshape(plan.short, LANES),
                head_dim,
            )
            dq_buf[slot, f:, lanes] = dq.astype(BF16)
            if step == 0:
                r.dsmall[0, :, lanes] = dk
                r.dsmall[1, :, lanes] = dv
            else:
                r.dsmall[0, :, lanes] += dk
                r.dsmall[1, :, lanes] += dv
    for blk in range(plan.short_blocks):
        span = slice(blk * plan.short_rows, (blk + 1) * plan.short_rows)
        r.dshort_buf[blk] = r.dsmall[:, span].astype(BF16)
        dst = r.dshort_out.at[:, split, :, cols_of(group)]
        for step, peer in enumerate(others):

            @pl.when(peer == blk)
            def _():
                push(r.dshort_buf.at[blk], dst, r.bs_sems, (step,), along[step])

        @pl.when(me == blk)
        def _():
            r.dshort_out[:, split, :, cols_of(group)] = r.dshort_buf[blk]

    for phase, (lo, hi) in enumerate(plan.phases[1:] + plan.phases[:1]):
        size = (hi - lo) * f
        for step in range(g):
            slot = slot_of(step)
            for u in range(units):
                lanes = slice(u * LANES, (u + 1) * LANES)
                high = slice(cols + u * LANES, cols + (u + 1) * LANES)
                dq, dk, dv = attend_back(
                    r.q_buf[slot, :f, lanes],
                    r.g_buf[slot, :f, lanes],
                    r.lse[slot, u : u + 1],
                    deltas[step][0][u],
                    r.kv_buf[lo:hi, :, lanes].reshape(size, LANES),
                    r.turned[lanes, lo * f : hi * f],
                    r.kv_buf[lo:hi, :, high].reshape(size, LANES),
                    head_dim,
                )
                if step == 0:
                    r.dlong[0, :size, lanes] = dk
                    r.dlong[1, :size, lanes] = dv
                else:
                    r.dlong[0, :size, lanes] += dk
                    r.dlong[1, :size, lanes] += dv
                if phase > 0:
                    dq = r.dq_acc[step, :, lanes] + dq
                r.dq_acc[step, :, lanes] = dq
                if lo > 0:
                    continue
                dq_buf[slot, :f, lanes] = dq.astype(BF16)
            if lo == 0:
                if step == g - 1:
                    r.dq_out[:, cols_of(group)] = dq_buf[slot]
                else:
                    dst = r.dq_out.at[:, cols_of(group)]
                    sends.append(push(dq_buf.at[slot], dst, r.bq_sems, (step,), along[step]))
        for which in range(2):
            made = slice(which * cols, (which + 1) * cols)
            r.kv_buf[lo:hi, :, made] = r.dlong[which, :size].astype(BF16).reshape(hi - lo, f, cols)
        for d in range(lo // g, hi // g):
            for s in range(g):
                if d == 0 and s == 0:
                    continue
                other_group = lax.rem(group + s, g)
                peer = lax.rem(split + plan.splits - d, plan.splits) * g + other_group
                for which in range(2):
                    made = slice(which * cols, (which + 1) * cols)
                    dst = r.dkv_out.at[which, split, :, cols_of(group)]
                    src = r.kv_buf.at[d * g + other_group, :, made]
                    sends.append(push(src, dst, r.bk_sems, (which, d * g + s), (b, peer)))
        if lo == 0:
            for which in range(2):
                made = slice(which * cols, (which + 1) * cols)
                r.dkv_out[which, split, :, cols_of(group)] = r.kv_buf[group, :, made]
    advance("down")

    def add_strip(total, i, rows_of):
        strips[i].wait()
        at = slice(i % 2 * half_width, (i % 2 + 1) * half_width)
        total = total + dot_rows(rows_of[:, at].astype(BF16), r.w_mod[i % 2])
        after = {10: 0, 11: 1}.get(i, i + 2)
        if after not in strips and after not in (4, 5):
            strips[after] = load_mod(after, i % 2)
        return total

    grad_act = jnp.zeros((2, width), F32)
    for i in range(4, 12):
        grad_act = add_strip(grad_act, i, r.stats[i // 2 * 2 - 4 : i // 2 * 2 - 2])
    finish_x(0)
    for copy in sends:
        copy.wait()
    for blk in range(plan.short_blocks):
        for step, peer in enumerate(others):

            @pl.when(peer == blk)
            def _():
                pltpu.make_async_copy(r.dshort_buf.at[blk], r.dshort_buf.at[blk], r.bs_sems.at[0, step]).wait()

        @pl.when(me == blk)
        def _():
            for step in range(n - 1):
                pltpu.make_async_copy(r.dshort_buf.at[blk], r.dshort_buf.at[blk], r.bs_sems.at[1, step]).wait()

    no_short = me >= plan.short_blocks
    grad_key = jnp.sum(r.dkv_out[0].astype(F32), axis=0)
    grad_value = jnp.sum(r.dkv_out[1].astype(F32), axis=0)
    short_key = jnp.where(no_short, 0.0, jnp.sum(r.dshort_out[0].astype(F32), axis=0))
    short_value = jnp.where(no_short, 0.0, jnp.sum(r.dshort_out[1].astype(F32), axis=0))
    cosines, sines = r.cos[...], -r.sin[...]
    for c in range(width // LANES):
        lanes = slice(c * LANES, (c + 1) * LANES)
        for span in seqs:
            made = rotate(r.dq_out[span, lanes].astype(F32), cosines, sines, half_dim)
            r.grad_qkv[span, lanes] = made.astype(BF16)
        lanes_k = slice(width + c * LANES, width + (c + 1) * LANES)
        made = rotate(grad_key[:, lanes], cosines, sines, half_dim)
        r.grad_qkv[:f, lanes_k] = made.astype(BF16)
        made = rotate(short_key[:, lanes], cosines[: plan.short_rows], sines[: plan.short_rows], half_dim)
        r.grad_qkv[f : f + plan.short_rows, lanes_k] = made.astype(BF16)
    r.grad_qkv[:f, 2 * width :] = grad_value.astype(BF16)
    r.grad_qkv[f : f + plan.short_rows, 2 * width :] = short_value.astype(BF16)
    if plan.short_rows < f:
        r.grad_qkv[f + plan.short_rows :, width:] = jnp.zeros((f - plan.short_rows, 2 * width), BF16)

    own_cols = 3 * cols
    pieces = own_cols // chunk_two

    def piece_of(chip, core_of, i):
        return pl.ds(pl.multiple_of((core_of * 2 + chip) * own_cols + i * chunk_two, LANES), chunk_two)

    quarters = [(half, 1 - core), (1 - half, core), (1 - half, 1 - core)]
    swaps = []
    for i in range(pieces):
        for slot, (chip, core_of) in enumerate(quarters):
            src = r.grad_qkv.at[:, piece_of(chip, core_of, i)]
            dst = r.rows.at[slot + 1, :, i * chunk_two : (i + 1) * chunk_two]
            swaps.append(push(src, dst, r.g_sems, (slot, i), around[slot]))
        r.rows[0, :, i * chunk_two : (i + 1) * chunk_two] = r.grad_qkv[:, piece_of(half, core, i)]
    advance("down")
    for k in range(1, chunks):
        finish_x(k)

    for copy in qkv_copies:
        copy.wait()
    grad_hidden = dot_rows(r.grad_qkv[:, : 2 * width], r.w_up[:, : 2 * width]) + dot_rows(
        r.grad_qkv[:, 2 * width :], r.w_out[...]
    )
    shift_rows, scale_rows, made = [], [], []
    for s, span in enumerate(seqs):
        normed, inverse = normalize(r.x[order[s]].astype(F32))
        grad = grad_hidden[span]
        shift_rows.append(jnp.sum(grad, axis=0, keepdims=True))
        scale_rows.append(jnp.sum(grad * normed, axis=0, keepdims=True))
        made.append(r.grad_mixed[span] + norm_back(normed, inverse, grad * (1.0 + mod(1, s))))
    r.grad_mixed[seqs[0]] = jnp.where(swapped, made[1], made[0])
    r.grad_mixed[seqs[1]] = jnp.where(swapped, made[0], made[1])
    last.append(local(r.grad_mixed.reshape(2, f, width), r.grad_inputs, r.in_sems.at[3]))
    bias = jnp.sum(r.grad_qkv[...].astype(F32), axis=0, keepdims=True)
    bias_rows = [bias[:, i * width : (i + 1) * width] for i in range(3)]
    kept = [r.stats[i : i + 1] for i in range(r.stats.shape[0])]
    pairs_a = [jnp.concatenate(shift_rows, axis=0), jnp.concatenate(scale_rows, axis=0)]
    for i in range(4):
        grad_act = add_strip(grad_act, i, pairs_a[i // 2])
    shown_rows = jnp.where(me == 0, r.acts[...].astype(F32), 0.0)
    time_rows = [shown_rows[0:1], shown_rows[1:2], grad_act[0:1], grad_act[1:2]]
    r.small[...] = jnp.zeros_like(r.small)
    for i, row in enumerate(shift_rows + scale_rows + kept[:8] + bias_rows + kept[8:] + time_rows):
        for c in range(width // LANES):
            r.small[i, c : c + 1] = row[:, c * LANES : (c + 1) * LANES]

    per = r.small.shape[0] // n
    copies = []
    for step, device in enumerate(along):
        src = r.small.at[pl.ds(device[1] * per, per)]
        copies.append(push(src, r.small_in.at[step], r.small_one, (step,), device))
    for copy in swap_hidden:
        copy.wait()

    def start_piece(i):
        for slot in range(3):
            swaps[3 * i + slot].wait()
        both = r.rows[:, :, i * chunk_two : (i + 1) * chunk_two].reshape(4 * tokens, chunk_two)
        made = dot(r.both_hidden[...], both).astype(BF16)
        r.qkv_sum[i] = made.reshape(n, n_rows, chunk_two)
        start_stage(("qkv", i), 0)

    queue = [("qkv", i) for i in range(pieces)]
    start_piece(0)
    advance(0)
    start_piece(1)
    advance(1)
    advance(0)
    advance("down")
    start_piece(2)
    advance(2)
    advance(queue[0])
    for k in range(3, pieces):
        start_piece(k)
    total = r.small[pl.ds(me * per, per)]
    for step in range(n - 1):
        copies[step].wait()
        total = total + r.small_in[step]
    r.mine[...] = total
    own_slice = r.small_all.at[b, pl.ds(me * per, per)]
    own_slice[...] = total
    copies = []
    for step, device in enumerate(along):
        copies.append(push(r.mine, own_slice, r.small_two, (step,), device))
    advance(1)
    advance(0)
    advance(queue[1])
    advance(queue[0])
    advance(2)
    advance(1)
    advance(queue[2])
    for copy in copies:
        copy.wait()
    for step, device in enumerate(across):
        last.append(push(r.small_all.at[b], r.small_all.at[b], r.small_three, (step,), device))
    advance(queue[1])
    advance(2)
    advance(queue[0])
    shown = r.time_embed[...].astype(F32)
    sigmoid = 1.0 / (1.0 + jnp.exp(-shown))
    slope = sigmoid * (1.0 + shown * (1.0 - sigmoid))
    row = 19 + layers
    for c in range(width // LANES):
        lanes = slice(c * LANES, (c + 1) * LANES)
        one, two = r.small_all[b, row, c : c + 1], r.small_all[b, row + 1, c : c + 1]
        upper, lower = jnp.where(swapped, two, one), jnp.where(swapped, one, two)
        r.grad_time[:, lanes] = jnp.concatenate([upper, lower], axis=0) * slope[:, lanes]
    advance(queue[2])
    finish_all("down")
    finish_all(0)
    finish_all(1)
    advance(queue[1])
    finish_all(2)

    advance(queue[2])
    for k in queue:
        finish_all(k)
    for copy in last:
        copy.wait()


def layer(plan, sizes, batch, operands, collective_id):
    heads, chunk, chunk_two, block = sizes
    n, g, f, cols, width = plan.count, plan.groups, plan.frames, plan.cols, plan.width
    hidden = operands["w_up_hbm"].shape[1]
    tokens, rows, layers, units = 2 * f, width // n, hidden // width, cols // LANES
    wide = f * (LANES // (width // heads))
    chunks, pieces = (width + hidden) // 2 // chunk, 3 * cols // chunk_two
    small_rows = -(-(21 + layers) // n) * n
    per, tile = small_rows // n, (width // LANES, LANES)
    vmem, smem = pl.BlockSpec(memory_space=pltpu.VMEM), pl.BlockSpec(memory_space=pltpu.SMEM)

    def sems(*shape):
        return pltpu.SemaphoreType.DMA(shape)

    def low(*shape):
        return pltpu.VMEM(shape, BF16)

    def high(*shape):
        return pltpu.VMEM(shape, F32)

    outs = dict(
        output=((2, f, width), F32),
        grad_inputs=((2, f, width), F32),
        grad_time=((2, width), F32),
        totals=((2, rows, 4 * width), BF16),
        small_all=((batch, small_rows) + tile, F32),
    )
    scratch = dict(
        x=low(2, f, width),
        ct=low(2, f, width),
        w_mod=low(2, width, width // 2),
        w_out=low(width, width),
        w_up=low(width, hidden),
        w_down=low(hidden, width),
        acts=low(2, width),
        cos=high(f, LANES),
        sin=high(f, LANES),
        b_row=high(1, 3 * width),
        mods=high(2, 6 * width),
        rows=low(g, tokens, 3 * cols),
        both_hidden=low(width, 4 * tokens),
        attn=low(tokens, width),
        q_buf=low(g, tokens, cols),
        kv_buf=low(n, f, 2 * cols),
        short_buf=low(plan.short_blocks, plan.short_rows, 2 * cols),
        lse=high(g, 2 * units, wide),
        o_buf=low(g, tokens, cols),
        turned=low(cols, plan.total),
        short_turned=low(cols, plan.short),
        top_acc=high(g * units, 1, wide),
        total_acc=high(g * units, 1, wide),
        o_acc=high(g * units, LANES, wide),
        mixed=high(tokens, width),
        branch_a=high(tokens, width),
        hidden_f=low(tokens, width),
        grad_ff=low(tokens, width),
        grad_pre=low(tokens, hidden),
        grad_br=low(tokens, width),
        attn_t=low(width, 2 * tokens),
        hid_t=low(width, 2 * tokens),
        act_own=low(n, rows, 4 * tokens),
        act_send=low(n, rows, tokens),
        all_ff=low(4, tokens, width // 2),
        both_pre=low(2, tokens, hidden // 2),
        both_br=low(2, tokens, width // 2),
        branch_f=high(tokens, width),
        grad_hid=high(tokens, width),
        grad_mixed=high(tokens, width),
        stats=high(10 + layers, width),
        parts=low(n, rows, chunks * chunk),
        x_buf=low(chunks, n, rows, chunk // 2),
        down_sum=low(n, rows, width // 2),
        grads=low(tokens, width),
        g_buf=low(g, tokens, cols),
        dq_acc=high(g, f, cols),
        dlong=high(2, plan.largest, cols),
        dsmall=high(2, plan.short, cols),
        dq_out=low(tokens, width),
        dkv_out=low(2, plan.splits, f, width),
        dshort_out=low(2, plan.splits, plan.short_rows, width),
        dshort_buf=low(plan.short_blocks, 2, plan.short_rows, cols),
        grad_qkv=low(tokens, 3 * width),
        qkv_sum=low(pieces, n, rows, chunk_two),
        small=high(small_rows, *tile),
        small_in=high(n - 1, per, *tile),
        mine=high(per, *tile),
        in_sems=sems(5),
        m_sems=sems(4),
        q_sems=sems(2, g - 1),
        k_sems=sems(2, n - 1),
        s_sems=sems(2, plan.short_blocks, g + plan.splits - 2),
        o_sems=sems(2, g - 1),
        h_sems=sems(2, 3),
        e_sems=sems(2, 5),
        ff_sems=sems(2, 2),
        act_sems=sems(2, 3, hidden // block),
        bg_sems=sems(2, g - 1),
        bq_sems=sems(2, g - 1),
        bk_sems=sems(2, 2, n),
        bs_sems=sems(2, n - 1),
        x_sems=sems(2, chunks),
        blk_sems=sems(2, chunks + 1 + pieces, n.bit_length() - 1),
        g_sems=sems(2, 3, pieces),
        ax_sems=sems(2, chunks + 1 + pieces),
        ac_sems=sems(2, 2 * (chunks + 1 + pieces)),
        small_one=sems(2, n - 1),
        small_two=sems(2, n - 1),
        small_three=sems(2, batch - 1),
    )
    for t in range(n.bit_length() - 1):
        scratch["came_one_%d" % t] = low(chunks, n >> (t + 1), rows, chunk // 2)
        scratch["came_down_%d" % t] = low(n >> (t + 1), rows, width // 2)
        scratch["came_qkv_%d" % t] = low(pieces, n >> (t + 1), rows, chunk_two)
    specs = [smem if k == "lengths" else in_hbm() if k.endswith("_hbm") else vmem for k in operands]
    names = tuple(operands) + tuple(outs) + tuple(scratch)
    return pl.pallas_call(
        partial(layer_kernel, plan, (heads, chunk, chunk_two, block, batch), names),
        in_specs=specs,
        out_specs=[in_hbm() if k in ("output", "grad_inputs") else vmem for k in outs],
        out_shape=[jax.ShapeDtypeStruct(*shape) for shape in outs.values()],
        scratch_shapes=list(scratch.values()),
        compiler_params=pltpu.CompilerParams(
            collective_id=collective_id, has_side_effects=True, vmem_limit_bytes=63 * MIB
        ),
        name="layer",
    )(*operands.values())


def finish_kernel(count, sizes, aligned, names, *refs):
    r = SimpleNamespace(**dict(zip(names, refs)))
    batch, width, layers = sizes
    rows = width // count
    me = lax.axis_index("blk")
    half = width // 2
    passed = [
        local(r.totals_hbm, r.totals, r.sems.at[0]),
        local(r.small_hbm, r.small, r.sems.at[1]),
        local(r.output_hbm, r.output, r.sems.at[2]),
        local(r.grad_inputs_hbm, r.grad_inputs, r.sems.at[3]),
        local(r.grad_time_hbm, r.grad_time, r.sems.at[4]),
    ]
    passed[0].wait()
    for core in range(2):
        for i in range(layers):
            made = r.totals[core, :, i * half : (i + 1) * half].astype(F32)
            r.down_made[i * rows : (i + 1) * rows, core * half : (core + 1) * half] = made
    passed.append(local(r.down_made, r.down, r.sems.at[5]))
    for core in range(2):
        start = layers * half
        made = r.totals[core, :, start : start + layers * half].astype(F32)
        r.up_made[:, core * layers * half : (core + 1) * layers * half] = made
    passed.append(local(r.up_made, r.up, r.sems.at[6]))
    for core in range(2):
        start = 2 * layers * half
        r.out_made[:, core * half : (core + 1) * half] = r.totals[core, :, start : start + half].astype(F32)
        made = r.totals[core, :, start + half : start + 4 * half].astype(F32)
        r.qkv_made[:, core * 3 * half : (core + 1) * 3 * half] = made
    passed.append(local(r.out_made, r.out, r.sems.at[7]))
    passed.append(local(r.qkv_made, r.qkv, r.sems.at[8]))
    passed[1].wait()
    for u in range(2 * batch):
        b, s = u // 2, u % 2
        line = r.small[b, 15 + 2 + layers + s, pl.ds(me * rows // LANES, 1)]
        if rows < LANES:
            line = pltpu.roll(line, LANES - lax.rem(me, LANES // rows) * rows, 1)
        r.times[u : u + 1] = line
        for p in range(6):
            for c in range(width // LANES):
                start = p * width + c * LANES
                r.mods[u : u + 1, start : start + LANES] = r.small[b, 2 * p + s, c : c + 1]
    times, mods = r.times[:, :rows].astype(BF16), r.mods[...].astype(BF16)
    for i in range(2):
        span = slice(i * 3 * width, (i + 1) * 3 * width)
        r.w_mod_made[:, span] = dot_frames(times, mods[:, span])
        passed.append(local(r.w_mod_made.at[:, span], r.w_mod.at[:, span], r.sems.at[9 + i]))
    if aligned:
        tiles = width // LANES

        def own_lines(first, length, stride):
            lines = []
            for i in range(length // count // LANES):
                at = me * (length // count // LANES) + i
                total = jnp.zeros((1, LANES), F32)
                for b in range(batch):
                    for s in range(stride):
                        total = total + r.small[b, first + at // tiles * stride + s, pl.ds(lax.rem(at, tiles), 1)]
                lines.append(total)
            return lines

        firsts = [(0, 6, 2), (12, 3, 1), (15, 1, 1), (16, layers, 1), (16 + layers, 1, 1)]
        for which, (first, many, stride) in enumerate(firsts):
            ref = getattr(r, "vector%d" % which)
            for i, line in enumerate(own_lines(first, many * width, stride)):
                ref[i * LANES : (i + 1) * LANES] = line[0]
    for copy in passed[2:]:
        copy.wait()


def finish(count, output, grad_inputs, grad_time, totals, small, layers):
    batch, width = small.shape[0], output.shape[2]
    rows = width // count
    aligned = rows % LANES == 0
    operands = dict(
        output_hbm=output, grad_inputs_hbm=grad_inputs, grad_time_hbm=grad_time, totals_hbm=totals, small_hbm=small
    )
    shapes = dict(
        down=(layers * rows, width),
        up=(rows, layers * width),
        out=(rows, width),
        qkv=(rows, 3 * width),
        w_mod=(rows, 6 * width),
    )
    outs = dict(output=output.shape, grad_inputs=output.shape, grad_time=grad_time.shape, **shapes)
    vectors = {}
    if aligned:
        vectors = {"vector%d" % i: (many * rows,) for i, many in enumerate((6, 3, 1, layers, 1))}
    scratch = {k + "_made": pltpu.VMEM(v, F32) for k, v in shapes.items()}
    scratch.update(
        totals=pltpu.VMEM(totals.shape, BF16),
        small=pltpu.VMEM(small.shape, F32),
        times=pltpu.VMEM((2 * batch, LANES), F32),
        mods=pltpu.VMEM((2 * batch, 6 * width), F32),
        sems=pltpu.SemaphoreType.DMA((11,)),
    )
    names = tuple(operands) + tuple(outs) + tuple(vectors) + tuple(scratch)
    made = pl.pallas_call(
        partial(finish_kernel, count, (batch, width, layers), aligned, names),
        in_specs=[in_hbm()] * len(operands),
        out_specs=[in_hbm()] * len(outs) + [pl.BlockSpec(memory_space=pltpu.VMEM)] * len(vectors),
        out_shape=[jax.ShapeDtypeStruct(v, F32) for v in (outs | vectors).values()],
        scratch_shapes=list(scratch.values()),
        compiler_params=pltpu.CompilerParams(vmem_limit_bytes=40 * MIB),
        name="finish",
    )(*operands.values())
    if not aligned:
        me = lax.axis_index("blk")
        flat = jnp.sum(small.reshape(batch, -1, width), axis=0)
        mods = flat[:12].reshape(6, 2, width).sum(axis=1)
        ends = [12, 15, 16, 16 + layers, 17 + layers]
        rest = [mods] + [flat[lo:hi] for lo, hi in zip(ends[:-1], ends[1:])]
        made = list(made) + [
            lax.dynamic_index_in_dim(v.reshape(count, -1), me, 0, keepdims=False) for v in rest
        ]
    return made


def on_device(
    inputs,
    time_embed,
    lengths,
    cotangent,
    w_mod,
    b_mod,
    w_qkv,
    b_qkv,
    w_out,
    b_out,
    w_up,
    b_up,
    w_down,
    b_down,
):
    _, frames, width = inputs.shape
    half = width // HEADS // 2
    count, batch = lax.axis_size("blk"), lax.axis_size("batch")
    plan = Plan(count, frames, width)
    freqs = 10000.0 ** (-jnp.arange(half, dtype=F32) / half)
    operands = dict(
        lengths=lengths,
        time_embed=time_embed,
        freqs=jnp.tile(freqs, LANES // half)[None],
        b_mod=b_mod,
        b_qkv=b_qkv,
        b_out=b_out,
        b_up=b_up,
        b_down=b_down,
        x_hbm=inputs,
        ct_hbm=cotangent,
        w_mod_hbm=w_mod,
        w_qkv_hbm=w_qkv,
        w_out_hbm=w_out,
        w_up_hbm=w_up,
        w_down_hbm=w_down,
    )
    made = layer(plan, (HEADS, 512, 256, 512), batch, operands, 0)
    output, grad_inputs, grad_time, down, up, out, qkv, grad_w_mod, *vectors = finish(
        count, *made, w_up.shape[1] // width
    )
    return (
        output,
        grad_inputs,
        grad_time,
        grad_w_mod,
        vectors[0],
        qkv,
        vectors[1],
        out,
        vectors[2],
        up,
        vectors[3],
        down,
        vectors[4],
    )


def solution(mesh):
    frame_spec, weight_spec = P("batch", "blk", None), P("blk", None)
    return jax.shard_map(
        on_device,
        mesh=mesh,
        in_specs=(frame_spec, P("batch", None), P("batch"), frame_spec) + (P(),) * 10,
        out_specs=(frame_spec, frame_spec, P("batch", None)) + (weight_spec, P("blk")) * 5,
        check_vma=False,
    )
```

```python
from functools import partial
from types import SimpleNamespace

import jax
import jax.numpy as jnp
from jax import lax
from jax.experimental import pallas as pl
from jax.experimental.pallas import tpu as pltpu
from jax.sharding import PartitionSpec as P

HEADS = 16
EPS = 1e-06
LANES = 128
SHORT = 16
MESH = pl.DeviceIdType.MESH
BF16 = jnp.bfloat16
F32 = jnp.float32
MIB = 1 << 20


def dot(left, right):
    return jnp.dot(left, right, preferred_element_type=F32)


def dot_rows(left, right):
    return lax.dot_general(left, right, (((1,), (1,)), ((), ())), preferred_element_type=F32)


def dot_frames(left, right):
    return lax.dot_general(left, right, (((0,), (0,)), ((), ())), preferred_element_type=F32)


def normalize(rows):
    mean = jnp.mean(rows, axis=-1, keepdims=True)
    centered = rows - mean
    inverse = lax.rsqrt(jnp.mean(centered * centered, axis=-1, keepdims=True) + EPS)
    return (centered * inverse, inverse)


def norm_back(normed, inverse, grad):
    return inverse * (
        grad
        - jnp.mean(grad, axis=-1, keepdims=True)
        - normed * jnp.mean(grad * normed, axis=-1, keepdims=True)
    )


def whole(shape):
    return pl.BlockSpec(shape, lambda *_: (0,) * len(shape))


def in_hbm():
    return pl.BlockSpec(memory_space=pltpu.HBM)


def rotate(rows, cos_table, sin_table, half):
    lane = lax.broadcasted_iota(jnp.int32, rows.shape, 1)
    partner = jnp.where(
        lax.rem(lane, 2 * half) < half,
        pltpu.roll(rows, LANES - half, 1),
        pltpu.roll(rows, half, 1),
    )
    return rows * cos_table + partner * sin_table


class Spot:
    def __init__(self, count):
        b, j = lax.axis_index("batch"), lax.axis_index("blk")
        self.b, self.j = b, j
        self.core, self.half = lax.rem(b, 2), b // 2
        self.near, self.far = lax.rem(j, 2), j // 2
        self.far_count = count // 2
        self.at_core = (self.half * 2 + 1 - self.core, j)
        self.at_x = ((1 - self.half) * 2 + self.core, j)
        self.at_both = ((1 - self.half) * 2 + 1 - self.core, j)
        self.at_near = (b, self.far * 2 + 1 - self.near)
        self.far_steps = [lax.rem(self.far + step, self.far_count) for step in range(1, self.far_count)]
        self.at_far = [(b, step * 2 + self.near) for step in self.far_steps]


def add_into(target, other):
    target[...] = (target[...].astype(F32) + other.astype(F32)).astype(BF16)


class Plan:
    def __init__(self, count, frames, width):
        self.count = count
        self.frames = frames
        self.width = width
        self.groups = min(max(count // 2, 1), 4)
        self.cols = width // self.groups
        self.splits = count // self.groups
        self.total = count * frames
        self.short = self.total // SHORT
        self.short_rows = min(self.short, frames)
        self.short_blocks = -(-self.short // frames)
        self.phases = [(lo, min(lo + 4 * self.groups, count)) for lo in range(self.groups, count, 4 * self.groups)]
        self.phases = [(0, self.groups)] + self.phases
        self.largest = max(hi - lo for lo, hi in self.phases) * frames
        self.offsets = [(d, s) for d in range(self.splits) for s in range(self.groups) if d + s > 0]

    def peer(self, device, offset):
        split = lax.rem(device // self.groups + offset[0], self.splits)
        return split * self.groups + lax.rem(lax.rem(device, self.groups) + offset[1], self.groups)


def push(src, dst, sems, index, device):
    copy = pltpu.make_async_remote_copy(
        src_ref=src, dst_ref=dst, send_sem=sems.at[(0,) + index], recv_sem=sems.at[(1,) + index],
        device_id=device, device_id_type=MESH,
    )
    copy.start()
    return copy


def local(src, dst, sem):
    copy = pltpu.make_async_copy(src, dst, sem)
    copy.start()
    return copy


def stacked(rows, head_dim):
    lane = lax.broadcasted_iota(jnp.int32, rows.shape, 1)
    heads = LANES // head_dim
    return jnp.concatenate(
        [jnp.where(lane // head_dim == h, rows, jnp.zeros_like(rows)) for h in range(heads)], axis=0
    )


def unstacked(turned, frames, head_dim):
    heads = LANES // head_dim
    return jnp.concatenate(
        [
            turned[h * head_dim : (h + 1) * head_dim, h * frames : (h + 1) * frames]
            for h in range(heads)
        ],
        axis=0,
    ).T


def attend_part(queries, keys, values_t, head_dim):
    scores = dot_rows(keys, stacked(queries, head_dim))
    top = jnp.max(scores, axis=0, keepdims=True)
    weights = jnp.exp(scores - top)
    total = jnp.sum(weights, axis=0, keepdims=True)
    return top, total, dot(values_t, weights.astype(BF16))


def attend_join(one, two):
    top = jnp.maximum(one[0], two[0])
    left, right = jnp.exp(one[0] - top), jnp.exp(two[0] - top)
    return top, one[1] * left + two[1] * right, one[2] * left + two[2] * right


def attend_end(state, frames, head_dim):
    top, total, out = state
    return unstacked(out / total, frames, head_dim).astype(BF16), top + jnp.log(total)


def delta_rows(grads, outs, head_dim):
    heads = LANES // head_dim
    lane = lax.broadcasted_iota(jnp.int32, (8, LANES), 1)
    pick = (lane // head_dim == lax.broadcasted_iota(jnp.int32, (8, LANES), 0)).astype(F32)
    product = grads.astype(F32) * outs.astype(F32)
    sums = lax.dot_general(
        pick, product, (((1,), (1,)), ((), ())), precision=lax.Precision.HIGHEST, preferred_element_type=F32
    )
    return jnp.concatenate([sums[h : h + 1] for h in range(heads)], axis=1)


def attend_back(queries, grads, lse, delta, keys, keys_t, values, head_dim):
    frames = queries.shape[0]
    q_heads, g_heads = stacked(queries, head_dim), stacked(grads, head_dim)
    probs = jnp.exp(dot_rows(keys, q_heads) - lse)
    grad_probs = dot_rows(values, g_heads)
    grad_scores = (probs * (grad_probs - delta)).astype(BF16)
    grad_values = dot(probs.astype(BF16), g_heads)
    grad_keys = dot(grad_scores, q_heads)
    grad_queries = unstacked(dot(keys_t, grad_scores), frames, head_dim) * head_dim ** (-0.5)
    return grad_queries, grad_keys, grad_values


def gelu_both(z):
    scale = (2.0 / 3.141592653589793) ** 0.5
    square = z * z
    inner = jnp.tanh(scale * z * (1.0 + 0.044715 * square))
    half = 0.5 * (1.0 + inner)
    slope = half + 0.5 * z * (1.0 - inner * inner) * (scale * (1.0 + 3.0 * 0.044715 * square))
    return z * half, slope


def layer_kernel(plan, sizes, names, *refs):
    r = SimpleNamespace(**dict(zip(names, refs)))
    r.came_at = lambda kind, t: getattr(r, "came_%s_%d" % (kind, t))
    heads, chunk, chunk_two, block, batch = sizes
    n, g, f, cols, width = plan.count, plan.groups, plan.frames, plan.cols, plan.width
    tokens, hidden = 2 * f, r.w_up.shape[1]
    head_dim, half_dim = width // heads, width // heads // 2
    half_width, half_hidden = width // 2, hidden // 2
    layers, n_rows, units = hidden // width, width // n, cols // LANES
    spot = Spot(n)
    b, me, core, half = spot.b, spot.j, spot.core, spot.half
    group, split = lax.rem(me, g), me // g
    others = [plan.peer(me, offset) for offset in plan.offsets]
    mates = others[: g - 1]
    along = [(b, peer) for peer in others]
    across = [(lax.rem(b + step, batch), me) for step in range(1, batch)]
    seqs = [slice(0, f), slice(f, tokens)]
    mine, theirs = slice(0, tokens), slice(tokens, 2 * tokens)
    swapped = r.lengths[0] < r.lengths[1]
    first = jnp.where(swapped, 1, 0)
    order = [first, 1 - first]

    barrier = pltpu.get_barrier_semaphore()
    for device in along + across:
        pl.semaphore_signal(barrier, inc=1, device_id=device, device_id_type=MESH)

    load_x = local(r.x_hbm, r.x, r.in_sems.at[0])
    mod_places, mod_copies = [r.w_mod.at[0], r.w_mod.at[1]], {}
    room = r.parts.reshape(width, r.parts.shape[2])
    mod_places += [room.at[:, :half_width], room.at[:, half_width:width]]
    ahead = len(mod_places)

    def mod_place(i):
        return i if i < ahead else i % 2

    def load_mod(i, place):
        return local(r.w_mod_hbm.at[:, i * half_width : (i + 1) * half_width], mod_places[place], r.m_sems.at[place])

    def next_mod(i):
        if mod_place(i) < 2:
            after = i + ahead if i < 2 else i + 2
            if after < 12:
                mod_copies[after] = load_mod(after, mod_place(after))

    def load_qkv():
        return [
            local(r.w_qkv_hbm.at[:, : 2 * width], r.w_up.at[:, : 2 * width], r.in_sems.at[1]),
            local(r.w_qkv_hbm.at[:, 2 * width :], r.w_out, r.in_sems.at[2]),
        ]

    for i in range(ahead):
        mod_copies[i] = load_mod(i, i)
    qkv_copies = load_qkv()

    shown = r.time_embed[...].astype(F32)
    shown = jnp.where(swapped, jnp.concatenate([shown[1:2], shown[0:1]], axis=0), shown)
    r.acts[...] = (shown / (1.0 + jnp.exp(-shown))).astype(BF16)
    frame = me * f + lax.broadcasted_iota(jnp.int32, (f, LANES), 0)
    lane = lax.broadcasted_iota(jnp.int32, (f, LANES), 1)
    exponent = lax.rem(lane, half_dim).astype(F32) * (-1.0 / half_dim)
    angle = frame.astype(F32) * jnp.exp(exponent * 9.210340371976184)
    sines = jnp.sin(angle)
    r.cos[...] = jnp.cos(angle)
    r.sin[...] = jnp.where(lax.rem(lane, 2 * half_dim) < half_dim, -sines, sines)
    r.b_row[...] = r.b_qkv[...][None].astype(F32)

    def mod_piece(i, place):
        piece = slice(i * half_width, (i + 1) * half_width)
        r.mods[:, piece] = dot(r.acts[...], mod_places[place][...]) + r.b_mod[piece][None].astype(F32)

    def mod(i, s):
        return r.mods[s : s + 1, i * width : (i + 1) * width]

    for i in range(4):
        mod_copies[i].wait()
        mod_piece(i, mod_place(i))
        next_mod(i)

    load_x.wait()
    for s, span in enumerate(seqs):
        normed, _ = normalize(r.x[order[s]].astype(F32))
        r.hidden_f[span] = (normed * (1.0 + mod(1, s)) + mod(0, s)).astype(BF16)
    for copy in qkv_copies:
        copy.wait()
    load_ct = local(r.ct_hbm, r.ct, r.in_sems.at[3])
    load_down = local(r.w_down_hbm, r.w_down, r.in_sems.at[4])
    pl.semaphore_wait(barrier, len(along + across))

    def project(kind, which):
        at = pl.ds(pl.multiple_of(which * cols, LANES), cols)
        bias_at = pl.ds(pl.multiple_of(kind * width + which * cols, LANES), cols)
        weight = r.w_out[:, at] if kind == 2 else r.w_up[:, bias_at]
        made = dot(r.hidden_f[...], weight) + r.b_row[:, bias_at]
        if kind < 2:
            factor = (2.0 * half_dim) ** (-0.5) if kind == 0 else 1.0
            cosines, sines = r.cos[...] * factor, r.sin[...] * factor
        for span in seqs:
            for u in range(units):
                part = made[span, u * LANES : (u + 1) * LANES]
                if kind < 2:
                    part = rotate(part, cosines, sines, half_dim)
                start = kind * cols + u * LANES
                r.rows[which, span, start : start + LANES] = part.astype(BF16)

    near_waits = []

    def send_keys(step):
        offset = plan.offsets[step]
        src = r.rows.at[lax.rem(others[step], g), 0:f, cols : 3 * cols]
        dst = r.kv_buf.at[offset[0] * g + group]
        return push(src, dst, r.k_sems, (step,), along[step])

    def short_rows_of(peer):
        return r.rows.at[lax.rem(peer, g), f : f + plan.short_rows, cols : 3 * cols]

    def pass_on(blk):
        for d in range(1, plan.splits):
            place = r.short_buf.at[blk]
            push(place, place, r.s_sems, (blk, g - 2 + d), along[d * g - 1])

    inner = jnp.logical_or(lax.rem(spot.far, 4) == 1, lax.rem(spot.far, 4) == 2)
    for step in range(1, g + 1):
        which = lax.rem(group + step, g)
        project(1, which)
        project(2, which)

        @pl.when(inner)
        def _():
            for d in range(1, plan.splits):
                send_keys(d * g + step % g - 1)

        if step < g:
            near_waits.append(send_keys(step - 1))
    for step in range(1, g + 1):
        which = lax.rem(group + step, g)
        project(0, which)
        if step < g:
            src = r.rows.at[which, :, 0:cols]
            near_waits.append(push(src, r.q_buf.at[group], r.q_sems, (step - 1,), along[step - 1]))

    for blk in range(plan.short_blocks):

        @pl.when(me == blk)
        def _():
            for step, peer in enumerate(mates):
                push(short_rows_of(peer), r.short_buf.at[blk], r.s_sems, (blk, step), along[step])
            r.short_buf[blk] = r.rows[group, f : f + plan.short_rows, cols : 3 * cols]
            pass_on(blk)

    @pl.when(jnp.logical_not(inner))
    def _():
        for step in range(g - 1, n - 1):
            send_keys(step)

    def lot(i):
        return slice(i * tokens, (i + 1) * tokens)

    around = [spot.at_core, spot.at_x, spot.at_both]
    r.both_hidden[:, lot(0)] = r.hidden_f[...].T
    swap_hidden = [
        push(r.both_hidden.at[:, lot(0)], r.both_hidden.at[:, lot(i + 1)], r.h_sems, (i,), device)
        for i, device in enumerate(around)
    ]
    load_out = local(r.w_out_hbm, r.w_out, r.in_sems.at[2])
    load_up = local(r.w_up_hbm, r.w_up, r.in_sems.at[1])
    r.kv_buf[group] = r.rows[group, 0:f, cols : 3 * cols]
    r.q_buf[group] = r.rows[group, :, 0:cols]

    for i in range(4, 12):
        mod_copies[i].wait()
        mod_piece(i, mod_place(i))
        next_mod(i)

    load_ct.wait()
    for s, span in enumerate(seqs):
        r.grad_ff[span] = (mod(5, s) * r.ct[order[s]].astype(F32)).astype(BF16)

    def core_half(which, size):
        return pl.ds(pl.multiple_of(which * size, LANES), size)

    def to_core(src, dst, index):
        return push(src, dst, r.e_sems, (index,), spot.at_core)

    ff_own, ff_other = core_half(core, half_width), core_half(1 - core, half_width)
    swap_ff = [
        to_core(r.grad_ff.at[:, ff_other], r.all_ff.at[1], 0),
        push(r.grad_ff.at[:, ff_own], r.all_ff.at[2], r.ff_sems, (0,), spot.at_x),
        push(r.grad_ff.at[:, ff_other], r.all_ff.at[3], r.ff_sems, (1,), spot.at_both),
    ]
    r.all_ff[0] = r.grad_ff[:, ff_own]

    for copy in near_waits:
        copy.wait()
    for blk in range(plan.short_blocks):
        for step in range(g - 1):

            @pl.when(me == plan.peer(blk, plan.offsets[step]))
            def _():
                dst = r.short_buf.at[blk]
                pltpu.make_async_copy(dst, dst, r.s_sems.at[1, blk, step]).wait()
                pass_on(blk)

    def turn_values(lo, hi, start):
        part = r.kv_buf[lo:hi, :, start : start + cols].reshape((hi - lo) * f, cols)
        r.turned[:, lo * f : hi * f] = part.T

    def cols_of(which):
        return pl.ds(pl.multiple_of(which * cols, LANES), cols)

    def slot_of(step):
        return lax.rem(group + 1 + step, g)

    units = cols // LANES
    sends = []
    for phase, (lo, hi) in enumerate(plan.phases):
        last = phase == len(plan.phases) - 1
        if phase == 1:
            for step in range(g - 1, n - 1):
                src = r.rows.at[group, 0:f, cols : 3 * cols]
                pltpu.make_async_copy(src, src, r.k_sems.at[0, step]).wait()
                dst = r.kv_buf.at[plan.offsets[step][0] * g + lax.rem(group + g - plan.offsets[step][1], g)]
                pltpu.make_async_copy(dst, dst, r.k_sems.at[1, step]).wait()
        turn_values(lo, hi, cols)
        for step in range(g):
            slot = slot_of(step)
            for u in range(units):
                lanes = slice(u * LANES, (u + 1) * LANES)
                at = step * units + u
                state = attend_part(
                    r.q_buf[slot, :f, lanes],
                    r.kv_buf[lo:hi, :, lanes].reshape((hi - lo) * f, LANES),
                    r.turned[lanes, lo * f : hi * f],
                    head_dim,
                )
                if phase > 0:
                    state = attend_join((r.top_acc[at], r.total_acc[at], r.o_acc[at]), state)
                if last:
                    r.o_buf[slot, :f, lanes], r.lse[slot, u : u + 1] = attend_end(state, f, head_dim)
                else:
                    r.top_acc[at], r.total_acc[at], r.o_acc[at] = state
            if last and step == 0:
                for blk in range(plan.short_blocks):
                    for d in range(1, plan.splits):

                        @pl.when(split == (blk // g + d) % plan.splits)
                        def _():
                            dst = r.short_buf.at[blk]
                            pltpu.make_async_copy(dst, dst, r.s_sems.at[1, blk, g - 2 + d]).wait()

                r.short_turned[...] = r.short_buf[:, :, cols:].reshape(plan.short, cols).T
            if last:
                for u in range(units):
                    lanes = slice(u * LANES, (u + 1) * LANES)
                    keys = r.short_buf[:, :, lanes].reshape(plan.short, LANES)
                    state = attend_part(r.q_buf[slot, f:, lanes], keys, r.short_turned[lanes], head_dim)
                    row = units + u
                    r.o_buf[slot, f:, lanes], r.lse[slot, row : row + 1] = attend_end(state, f, head_dim)
                if step == g - 1:
                    r.attn[:, cols_of(group)] = r.o_buf[slot]
                else:
                    dst = r.attn.at[:, cols_of(group)]
                    sends.append(push(r.o_buf.at[slot], dst, r.o_sems, (step,), along[step]))
    for lo, hi in plan.phases:
        turn_values(lo, hi, 0)
    r.short_turned[...] = r.short_buf[:, :, :cols].reshape(plan.short, cols).T
    for copy in sends:
        copy.wait()
    for blk in range(plan.short_blocks):

        @pl.when(me == blk)
        def _():
            for step, peer in enumerate(mates):
                src = short_rows_of(peer)
                pltpu.make_async_copy(src, src, r.s_sems.at[0, blk, step]).wait()

        @pl.when(split == blk // g)
        def _():
            for d in range(1, plan.splits):
                src = r.short_buf.at[blk]
                pltpu.make_async_copy(src, src, r.s_sems.at[0, blk, g - 2 + d]).wait()

    load_out.wait()
    r.attn_t[:, mine] = r.attn[...].T
    swap_attn = to_core(r.attn_t.at[:, mine], r.attn_t.at[:, theirs], 1)
    r.branch_a[...] = dot(r.attn[...], r.w_out[...]) + r.b_out[...][None].astype(F32)
    for s, span in enumerate(seqs):
        r.mixed[span] = r.x[order[s]].astype(F32) + mod(2, s) * r.branch_a[span]
        normed, _ = normalize(r.mixed[span])
        r.hidden_f[span] = (normed * (1.0 + mod(4, s)) + mod(3, s)).astype(BF16)
    r.hid_t[:, mine] = r.hidden_f[...].T
    swap_hid = to_core(r.hid_t.at[:, mine], r.hid_t.at[:, theirs], 2)
    load_up.wait()
    load_down.wait()
    swap_act, act_x = [], []
    per_block = block // (layers * n_rows)
    for i in range(hidden // block):
        span = slice(i * block, (i + 1) * block)
        act, slope = gelu_both(dot(r.hidden_f[...], r.w_up[:, span]) + r.b_up[span][None].astype(F32))
        act = act.astype(BF16)
        act_t = act.T.reshape(per_block, layers, n_rows, tokens)
        held = slice(i * per_block, (i + 1) * per_block)
        r.act_own[held, :, mine] = jnp.where(half == 0, act_t[:, 0], act_t[:, 1])
        r.act_send[held] = jnp.where(half == 0, act_t[:, 1], act_t[:, 0])
        act_x.append(
            push(r.act_send.at[held], r.act_own.at[held, :, 2 * tokens : 3 * tokens], r.act_sems, (0, i), spot.at_x)
        )
        swap_act.append(
            push(r.act_own.at[held, :, mine], r.act_own.at[held, :, theirs], r.act_sems, (1, i), spot.at_core)
        )
        forward = dot(act, r.w_down[span, :])
        grad = (dot_rows(r.grad_ff[...], r.w_down[span, :]) * slope).astype(BF16)
        r.grad_pre[:, span] = grad
        row, start = 9 + i * block // width, i * block % width
        r.stats[row : row + 1, start : start + block] = jnp.sum(grad.astype(F32), axis=0, keepdims=True)
        back = dot_rows(grad, r.w_up[:, span])
        if i == 0:
            r.branch_f[...] = forward + r.b_down[...][None].astype(F32)
            r.grad_hid[...] = back
        else:
            r.branch_f[...] += forward
            r.grad_hid[...] += back
    swap_pre = to_core(r.grad_pre.at[:, core_half(1 - core, half_hidden)], r.both_pre.at[1], 3)
    r.both_pre[0] = r.grad_pre[:, core_half(core, half_hidden)]

    chunks, half_chunk = r.parts.shape[2] // chunk, chunk // 2
    base_one = layers * half_width
    x_copies, stage_copies, stage_of, last, sent = {}, {}, {}, [], {}

    def half_of(k, which):
        return pl.ds(pl.multiple_of(k * chunk + which * half_chunk, LANES), half_chunk)

    stages = range(n.bit_length() - 1)
    pieces = 3 * cols // chunk_two
    rooms = {k: (r.x_buf.at[k], [r.came_at("one", t).at[k] for t in stages], k) for k in range(chunks)}
    rooms["down"] = (r.down_sum, [r.came_at("down", t) for t in stages], chunks)
    for i in range(pieces):
        rooms["qkv", i] = (r.qkv_sum.at[i], [r.came_at("qkv", t).at[i] for t in stages], chunks + 1 + i)

    def total_of(k, which):
        if k == "down":
            return core_half(which, half_width)
        if k in range(chunks):
            return pl.ds(pl.multiple_of(base_one + k * chunk + which * half_chunk, LANES), half_chunk)
        start = base_one + chunks * chunk + which * 3 * cols + k[1] * chunk_two
        return pl.ds(pl.multiple_of(start, LANES), chunk_two)

    def start_x(k):
        src = r.parts.at[:, :, half_of(k, 1 - half)]
        x_copies[k] = push(src, r.x_buf.at[k], r.x_sems, (k,), spot.at_x)

    bits = [lax.rem(me // (1 << t), 2) for t in stages]
    partners = [(b, me + (1 - 2 * bit) * (1 << t)) for t, bit in enumerate(bits)]

    def halves(k, t):
        held = rooms[k][0] if t == 0 else rooms[k][1][t - 1]
        return held.reshape(n >> (t + 1), 2, n_rows, held.shape[2])

    def start_stage(k, t):
        _, came, number = rooms[k]
        stage_of[k] = t
        stage_copies[k] = push(halves(k, t).at[:, 1 - bits[t]], came[t], r.blk_sems, (number, t), partners[t])

    def finish_x(k):
        x_copies[k].wait()
        add_into(r.x_buf.at[k], r.parts[:, :, half_of(k, half)])
        start_stage(k, 0)

    def advance(k):
        t = stage_of[k]
        _, came, number = rooms[k]
        stage_copies[k].wait()
        if t + 1 < len(stages):
            add_into(came[t], halves(k, t)[:, bits[t]])
            start_stage(k, t + 1)
        else:
            total = came[t][0].astype(F32) + halves(k, t)[0, bits[t]].astype(F32)
            r.totals[core, :, total_of(k, half)] = total.astype(BF16)
            sent[k] = to_all(total_of(k, half), number)

    def to_all(where, which):
        place = r.totals.at[core, :, where]
        return [
            push(place, place, r.ax_sems, (which,), spot.at_x),
            push(place, place, r.ac_sems, (2 * which,), spot.at_core),
        ]

    def forward_to_core(where, which):
        place = r.totals.at[core, :, where]
        return push(place, place, r.ac_sems, (2 * which + 1,), spot.at_core)

    def finish_all(k):
        while k not in sent:
            advance(k)
        sent[k][0].wait()
        last.append(sent[k][1])
        last.append(forward_to_core(total_of(k, 1 - half), rooms[k][2]))

    for s, span in enumerate(seqs):
        grad_out = r.ct[order[s]].astype(F32)
        branch, grad = r.branch_f[span], r.grad_hid[span]
        normed, inverse = normalize(r.mixed[span])
        r.stats[6 + s : 7 + s] = jnp.sum(grad_out * branch, axis=0, keepdims=True)
        r.stats[4 + s : 5 + s] = jnp.sum(grad * normed, axis=0, keepdims=True)
        r.stats[2 + s : 3 + s] = jnp.sum(grad, axis=0, keepdims=True)
        total = grad_out + norm_back(normed, inverse, grad * (1.0 + mod(4, s)))
        r.grad_mixed[span] = total
        r.stats[s : s + 1] = jnp.sum(total * r.branch_a[span], axis=0, keepdims=True)
        r.grad_br[span] = (mod(2, s) * total).astype(BF16)
    r.grads[...] = dot_rows(r.grad_br[...], r.w_out[...]).astype(BF16)
    waits = []
    for step, peer in enumerate(mates):
        src = r.grads.at[:, cols_of(lax.rem(peer, g))]
        waits.append(push(src, r.g_buf.at[group], r.bg_sems, (step,), along[step]))
    r.g_buf[group] = r.grads[:, cols_of(group)]
    swap_br = to_core(r.grad_br.at[:, core_half(1 - core, half_width)], r.both_br.at[1], 4)
    qkv_copies = load_qkv()

    for i, copy in enumerate(act_x):
        copy.wait()
        held = slice(i * per_block, (i + 1) * per_block)
        src = r.act_own.at[held, :, 2 * tokens : 3 * tokens]
        dst = r.act_own.at[held, :, 3 * tokens : 4 * tokens]
        swap_act.append(push(src, dst, r.act_sems, (2, i), spot.at_core))
    swap_hid.wait()
    swap_pre.wait()
    for i in range(layers):
        grad = r.both_pre[:, :, i * half_width : (i + 1) * half_width].reshape(2 * tokens, half_width)
        up = dot(r.hid_t[...], grad).astype(BF16).reshape(n, n_rows, half_width)
        r.parts[:, :, i * half_width : (i + 1) * half_width] = up
        start_x(i)
    for copy in swap_ff + swap_act:
        copy.wait()
    down = dot(r.act_own[...].reshape(width, 4 * tokens), r.all_ff[...].reshape(4 * tokens, half_width))
    r.down_sum[...] = down.astype(BF16).reshape(n, n_rows, half_width)
    start_stage("down", 0)
    r.both_br[0] = r.grad_br[:, core_half(core, half_width)]
    swap_attn.wait()
    swap_br.wait()
    out_part = dot(r.attn_t[...], r.both_br[...].reshape(2 * tokens, half_width))
    r.parts[:, :, layers * half_width :] = out_part.astype(BF16).reshape(n, n_rows, half_width)
    start_x(layers)
    made = [r.mixed[span] + mod(5, s) * r.branch_f[span] for s, span in enumerate(seqs)]
    r.mixed[seqs[0]] = jnp.where(swapped, made[1], made[0])
    r.mixed[seqs[1]] = jnp.where(swapped, made[0], made[1])
    last.append(local(r.mixed.reshape(2, f, width), r.output, r.in_sems.at[0]))
    last_row = 9 + layers
    r.stats[8:9] = jnp.sum(r.grad_br[...].astype(F32), axis=0, keepdims=True)
    r.stats[last_row : last_row + 1] = jnp.sum(r.grad_ff[...].astype(F32), axis=0, keepdims=True)
    for copy in waits:
        copy.wait()

    strips = {i: load_mod(i, i % 2) for i in (4, 5)}

    sends = []
    deltas = [
        [
            [
                delta_rows(r.g_buf[slot_of(step), span, lanes], r.o_buf[slot_of(step), span, lanes], head_dim)
                for lanes in [slice(u * LANES, (u + 1) * LANES) for u in range(units)]
            ]
            for span in seqs
        ]
        for step in range(g)
    ]
    dq_buf = r.o_buf
    def short_back():
        for step in range(g):
            slot = slot_of(step)
            for u in range(units):
                lanes = slice(u * LANES, (u + 1) * LANES)
                high = slice(cols + u * LANES, cols + (u + 1) * LANES)
                row = units + u
                dq, dk, dv = attend_back(
                    r.q_buf[slot, f:, lanes],
                    r.g_buf[slot, f:, lanes],
                    r.lse[slot, row : row + 1],
                    deltas[step][1][u],
                    r.short_buf[:, :, lanes].reshape(plan.short, LANES),
                    r.short_turned[lanes],
                    r.short_buf[:, :, high].reshape(plan.short, LANES),
                    head_dim,
                )
                dq_buf[slot, f:, lanes] = dq.astype(BF16)
                if step == 0:
                    r.dsmall[0, :, lanes] = dk
                    r.dsmall[1, :, lanes] = dv
                else:
                    r.dsmall[0, :, lanes] += dk
                    r.dsmall[1, :, lanes] += dv
        for blk in range(plan.short_blocks):
            span = slice(blk * plan.short_rows, (blk + 1) * plan.short_rows)
            r.dshort_buf[blk] = r.dsmall[:, span].astype(BF16)
            for d in range(1, plan.splits):
                home = blk // g

                @pl.when(split == (home + d) % plan.splits)
                def _():
                    device = (b, home * g + group)
                    push(r.dshort_buf.at[blk], r.dshort_part.at[blk, d - 1], r.bp_sems, (blk, d - 1), device)

    def short_home():
        for blk in range(plan.short_blocks):

            @pl.when(split == blk // g)
            def _():
                total = r.dshort_buf[blk].astype(F32)
                for d in range(1, plan.splits):
                    place = r.dshort_part.at[blk, d - 1]
                    pltpu.make_async_copy(place, place, r.bp_sems.at[1, blk, d - 1]).wait()
                    total = total + place[...].astype(F32)
                r.dshort_buf[blk] = total.astype(BF16)

            dst = r.dshort_out.at[:, :, cols_of(group)]
            for step, peer in enumerate(mates):

                @pl.when(peer == blk)
                def _():
                    push(r.dshort_buf.at[blk], dst, r.bs_sems, (step,), along[step])

            @pl.when(me == blk)
            def _():
                r.dshort_out[:, :, cols_of(group)] = r.dshort_buf[blk]

    for phase, (lo, hi) in enumerate(plan.phases[1:] + plan.phases[:1]):
        size = (hi - lo) * f
        if phase == 0:
            short_back()
        for step in range(g):
            slot = slot_of(step)
            for u in range(units):
                lanes = slice(u * LANES, (u + 1) * LANES)
                high = slice(cols + u * LANES, cols + (u + 1) * LANES)
                dq, dk, dv = attend_back(
                    r.q_buf[slot, :f, lanes],
                    r.g_buf[slot, :f, lanes],
                    r.lse[slot, u : u + 1],
                    deltas[step][0][u],
                    r.kv_buf[lo:hi, :, lanes].reshape(size, LANES),
                    r.turned[lanes, lo * f : hi * f],
                    r.kv_buf[lo:hi, :, high].reshape(size, LANES),
                    head_dim,
                )
                if step == 0:
                    r.dlong[0, :size, lanes] = dk
                    r.dlong[1, :size, lanes] = dv
                else:
                    r.dlong[0, :size, lanes] += dk
                    r.dlong[1, :size, lanes] += dv
                if phase > 0:
                    dq = r.dq_acc[step, :, lanes] + dq
                r.dq_acc[step, :, lanes] = dq
                if lo > 0:
                    continue
                dq_buf[slot, :f, lanes] = dq.astype(BF16)
            if lo == 0:
                if step == g - 1:
                    r.dq_out[:, cols_of(group)] = dq_buf[slot]
                else:
                    dst = r.dq_out.at[:, cols_of(group)]
                    sends.append(push(dq_buf.at[slot], dst, r.bq_sems, (step,), along[step]))
        for which in range(2):
            made = slice(which * cols, (which + 1) * cols)
            r.kv_buf[lo:hi, :, made] = r.dlong[which, :size].astype(BF16).reshape(hi - lo, f, cols)
        for d in range(lo // g, hi // g):
            for s in range(g):
                if d == 0 and s == 0:
                    continue
                other_group = lax.rem(group + s, g)
                peer = lax.rem(split + plan.splits - d, plan.splits) * g + other_group
                for which in range(2):
                    made = slice(which * cols, (which + 1) * cols)
                    dst = r.dkv_out.at[which, split, :, cols_of(group)]
                    src = r.kv_buf.at[d * g + other_group, :, made]
                    sends.append(push(src, dst, r.bk_sems, (which, d * g + s), (b, peer)))
        if lo == 0:
            for which in range(2):
                made = slice(which * cols, (which + 1) * cols)
                r.dkv_out[which, split, :, cols_of(group)] = r.kv_buf[group, :, made]
    short_home()

    def add_strip(total, i, rows_of):
        strips[i].wait()
        at = slice(i % 2 * half_width, (i % 2 + 1) * half_width)
        total = total + dot_rows(rows_of[:, at].astype(BF16), r.w_mod[i % 2])
        after = {10: 0, 11: 1}.get(i, i + 2)
        if after not in strips and after not in (4, 5):
            strips[after] = load_mod(after, i % 2)
        return total

    grad_act = jnp.zeros((2, width), F32)
    for i in range(4, 12):
        grad_act = add_strip(grad_act, i, r.stats[i // 2 * 2 - 4 : i // 2 * 2 - 2])
    advance("down")
    finish_x(0)
    for copy in sends:
        copy.wait()
    for blk in range(plan.short_blocks):
        place = r.dshort_buf.at[blk]
        for d in range(1, plan.splits):

            @pl.when(split == (blk // g + d) % plan.splits)
            def _():
                pltpu.make_async_copy(place, place, r.bp_sems.at[0, blk, d - 1]).wait()

        for step, peer in enumerate(mates):

            @pl.when(peer == blk)
            def _():
                pltpu.make_async_copy(place, place, r.bs_sems.at[0, step]).wait()

        @pl.when(me == blk)
        def _():
            for step in range(g - 1):
                pltpu.make_async_copy(place, place, r.bs_sems.at[1, step]).wait()

    no_short = me >= plan.short_blocks
    grad_key = jnp.sum(r.dkv_out[0].astype(F32), axis=0)
    grad_value = jnp.sum(r.dkv_out[1].astype(F32), axis=0)
    short_key = jnp.where(no_short, 0.0, r.dshort_out[0].astype(F32))
    short_value = jnp.where(no_short, 0.0, r.dshort_out[1].astype(F32))
    cosines, sines = r.cos[...], -r.sin[...]
    for c in range(width // LANES):
        lanes = slice(c * LANES, (c + 1) * LANES)
        for span in seqs:
            made = rotate(r.dq_out[span, lanes].astype(F32), cosines, sines, half_dim)
            r.grad_qkv[span, lanes] = made.astype(BF16)
        lanes_k = slice(width + c * LANES, width + (c + 1) * LANES)
        made = rotate(grad_key[:, lanes], cosines, sines, half_dim)
        r.grad_qkv[:f, lanes_k] = made.astype(BF16)
        made = rotate(short_key[:, lanes], cosines[: plan.short_rows], sines[: plan.short_rows], half_dim)
        r.grad_qkv[f : f + plan.short_rows, lanes_k] = made.astype(BF16)
    r.grad_qkv[:f, 2 * width :] = grad_value.astype(BF16)
    r.grad_qkv[f : f + plan.short_rows, 2 * width :] = short_value.astype(BF16)
    if plan.short_rows < f:
        r.grad_qkv[f + plan.short_rows :, width:] = jnp.zeros((f - plan.short_rows, 2 * width), BF16)

    own_cols = 3 * cols
    pieces = own_cols // chunk_two

    def piece_of(chip, core_of, i):
        return pl.ds(pl.multiple_of((core_of * 2 + chip) * own_cols + i * chunk_two, LANES), chunk_two)

    quarters = [(half, 1 - core), (1 - half, core), (1 - half, 1 - core)]
    swaps = []
    for i in range(pieces):
        for slot, (chip, core_of) in enumerate(quarters):
            src = r.grad_qkv.at[:, piece_of(chip, core_of, i)]
            dst = r.rows.at[slot + 1, :, i * chunk_two : (i + 1) * chunk_two]
            swaps.append(push(src, dst, r.g_sems, (slot, i), around[slot]))
        r.rows[0, :, i * chunk_two : (i + 1) * chunk_two] = r.grad_qkv[:, piece_of(half, core, i)]
    for k in range(1, chunks):
        finish_x(k)

    for copy in qkv_copies:
        copy.wait()
    grad_hidden = dot_rows(r.grad_qkv[:, : 2 * width], r.w_up[:, : 2 * width]) + dot_rows(
        r.grad_qkv[:, 2 * width :], r.w_out[...]
    )
    shift_rows, scale_rows, made = [], [], []
    for s, span in enumerate(seqs):
        normed, inverse = normalize(r.x[order[s]].astype(F32))
        grad = grad_hidden[span]
        shift_rows.append(jnp.sum(grad, axis=0, keepdims=True))
        scale_rows.append(jnp.sum(grad * normed, axis=0, keepdims=True))
        made.append(r.grad_mixed[span] + norm_back(normed, inverse, grad * (1.0 + mod(1, s))))
    r.grad_mixed[seqs[0]] = jnp.where(swapped, made[1], made[0])
    r.grad_mixed[seqs[1]] = jnp.where(swapped, made[0], made[1])
    last.append(local(r.grad_mixed.reshape(2, f, width), r.grad_inputs, r.in_sems.at[3]))
    bias = jnp.sum(r.grad_qkv[...].astype(F32), axis=0, keepdims=True)
    bias_rows = [bias[:, i * width : (i + 1) * width] for i in range(3)]
    kept = [r.stats[i : i + 1] for i in range(r.stats.shape[0])]
    pairs_a = [jnp.concatenate(shift_rows, axis=0), jnp.concatenate(scale_rows, axis=0)]
    for i in range(4):
        grad_act = add_strip(grad_act, i, pairs_a[i // 2])
    shown_rows = jnp.where(me == 0, r.acts[...].astype(F32), 0.0)
    time_rows = [shown_rows[0:1], shown_rows[1:2], grad_act[0:1], grad_act[1:2]]
    r.small[...] = jnp.zeros_like(r.small)
    for i, row in enumerate(shift_rows + scale_rows + kept[:8] + bias_rows + kept[8:] + time_rows):
        for c in range(width // LANES):
            r.small[i, c : c + 1] = row[:, c * LANES : (c + 1) * LANES]

    per = r.small.shape[0] // n
    copies = []
    for step, device in enumerate(along):
        src = r.small.at[pl.ds(device[1] * per, per)]
        copies.append(push(src, r.small_in.at[step], r.small_one, (step,), device))
    for copy in swap_hidden:
        copy.wait()

    def start_piece(i):
        for slot in range(3):
            swaps[3 * i + slot].wait()
        both = r.rows[:, :, i * chunk_two : (i + 1) * chunk_two].reshape(4 * tokens, chunk_two)
        made = dot(r.both_hidden[...], both).astype(BF16)
        r.qkv_sum[i] = made.reshape(n, n_rows, chunk_two)
        start_stage(("qkv", i), 0)

    queue = [("qkv", i) for i in range(pieces)]
    start_piece(0)
    advance("down")
    advance(0)
    start_piece(1)
    advance(1)
    advance(0)
    advance("down")
    start_piece(2)
    advance(2)
    advance(queue[0])
    for k in range(3, pieces):
        start_piece(k)
    total = r.small[pl.ds(me * per, per)]
    for step in range(n - 1):
        copies[step].wait()
        total = total + r.small_in[step]
    r.mine[...] = total
    own_slice = r.small_all.at[b, pl.ds(me * per, per)]
    own_slice[...] = total
    copies = []
    for step, device in enumerate(along):
        copies.append(push(r.mine, own_slice, r.small_two, (step,), device))
    advance(1)
    advance(0)
    advance(queue[1])
    advance(queue[0])
    advance(2)
    advance(1)
    advance(queue[2])
    for copy in copies:
        copy.wait()
    for step, device in enumerate(across):
        last.append(push(r.small_all.at[b], r.small_all.at[b], r.small_three, (step,), device))
    advance(queue[1])
    advance(2)
    advance(queue[0])
    shown = r.time_embed[...].astype(F32)
    sigmoid = 1.0 / (1.0 + jnp.exp(-shown))
    slope = sigmoid * (1.0 + shown * (1.0 - sigmoid))
    row = 19 + layers
    for c in range(width // LANES):
        lanes = slice(c * LANES, (c + 1) * LANES)
        one, two = r.small_all[b, row, c : c + 1], r.small_all[b, row + 1, c : c + 1]
        upper, lower = jnp.where(swapped, two, one), jnp.where(swapped, one, two)
        r.grad_time[:, lanes] = jnp.concatenate([upper, lower], axis=0) * slope[:, lanes]
    advance(queue[2])
    finish_all("down")
    finish_all(0)
    finish_all(1)
    advance(queue[1])
    finish_all(2)

    advance(queue[2])
    for k in queue:
        finish_all(k)
    for copy in last:
        copy.wait()


def layer(plan, sizes, batch, operands, collective_id):
    heads, chunk, chunk_two, block = sizes
    n, g, f, cols, width = plan.count, plan.groups, plan.frames, plan.cols, plan.width
    hidden = operands["w_up_hbm"].shape[1]
    tokens, rows, layers, units = 2 * f, width // n, hidden // width, cols // LANES
    wide = f * (LANES // (width // heads))
    chunks, pieces = (width + hidden) // 2 // chunk, 3 * cols // chunk_two
    small_rows = -(-(21 + layers) // n) * n
    per, tile = small_rows // n, (width // LANES, LANES)
    vmem, smem = pl.BlockSpec(memory_space=pltpu.VMEM), pl.BlockSpec(memory_space=pltpu.SMEM)

    def sems(*shape):
        return pltpu.SemaphoreType.DMA(shape)

    def low(*shape):
        return pltpu.VMEM(shape, BF16)

    def high(*shape):
        return pltpu.VMEM(shape, F32)

    outs = dict(
        output=((2, f, width), F32),
        grad_inputs=((2, f, width), F32),
        grad_time=((2, width), F32),
        totals=((2, rows, 4 * width), BF16),
        small_all=((batch, small_rows) + tile, F32),
    )
    scratch = dict(
        x=low(2, f, width),
        ct=low(2, f, width),
        w_mod=low(2, width, width // 2),
        w_out=low(width, width),
        w_up=low(width, hidden),
        w_down=low(hidden, width),
        acts=low(2, width),
        cos=high(f, LANES),
        sin=high(f, LANES),
        b_row=high(1, 3 * width),
        mods=high(2, 6 * width),
        rows=low(g, tokens, 3 * cols),
        both_hidden=low(width, 4 * tokens),
        attn=low(tokens, width),
        q_buf=low(g, tokens, cols),
        kv_buf=low(n, f, 2 * cols),
        short_buf=low(plan.short_blocks, plan.short_rows, 2 * cols),
        lse=high(g, 2 * units, wide),
        o_buf=low(g, tokens, cols),
        turned=low(cols, plan.total),
        short_turned=low(cols, plan.short),
        top_acc=high(g * units, 1, wide),
        total_acc=high(g * units, 1, wide),
        o_acc=high(g * units, LANES, wide),
        mixed=high(tokens, width),
        branch_a=high(tokens, width),
        hidden_f=low(tokens, width),
        grad_ff=low(tokens, width),
        grad_pre=low(tokens, hidden),
        grad_br=low(tokens, width),
        attn_t=low(width, 2 * tokens),
        hid_t=low(width, 2 * tokens),
        act_own=low(n, rows, 4 * tokens),
        act_send=low(n, rows, tokens),
        all_ff=low(4, tokens, width // 2),
        both_pre=low(2, tokens, hidden // 2),
        both_br=low(2, tokens, width // 2),
        branch_f=high(tokens, width),
        grad_hid=high(tokens, width),
        grad_mixed=high(tokens, width),
        stats=high(10 + layers, width),
        parts=low(n, rows, chunks * chunk),
        x_buf=low(chunks, n, rows, chunk // 2),
        down_sum=low(n, rows, width // 2),
        grads=low(tokens, width),
        g_buf=low(g, tokens, cols),
        dq_acc=high(g, f, cols),
        dlong=high(2, plan.largest, cols),
        dsmall=high(2, plan.short, cols),
        dq_out=low(tokens, width),
        dkv_out=low(2, plan.splits, f, width),
        dshort_out=low(2, plan.short_rows, width),
        dshort_part=low(plan.short_blocks, plan.splits - 1, 2, plan.short_rows, cols),
        dshort_buf=low(plan.short_blocks, 2, plan.short_rows, cols),
        grad_qkv=low(tokens, 3 * width),
        qkv_sum=low(pieces, n, rows, chunk_two),
        small=high(small_rows, *tile),
        small_in=high(n - 1, per, *tile),
        mine=high(per, *tile),
        in_sems=sems(5),
        m_sems=sems(4),
        q_sems=sems(2, g - 1),
        k_sems=sems(2, n - 1),
        s_sems=sems(2, plan.short_blocks, g + plan.splits - 2),
        o_sems=sems(2, g - 1),
        h_sems=sems(2, 3),
        e_sems=sems(2, 5),
        ff_sems=sems(2, 2),
        act_sems=sems(2, 3, hidden // block),
        bg_sems=sems(2, g - 1),
        bq_sems=sems(2, g - 1),
        bk_sems=sems(2, 2, n),
        bs_sems=sems(2, g - 1),
        bp_sems=sems(2, plan.short_blocks, plan.splits - 1),
        x_sems=sems(2, chunks),
        blk_sems=sems(2, chunks + 1 + pieces, n.bit_length() - 1),
        g_sems=sems(2, 3, pieces),
        ax_sems=sems(2, chunks + 1 + pieces),
        ac_sems=sems(2, 2 * (chunks + 1 + pieces)),
        small_one=sems(2, n - 1),
        small_two=sems(2, n - 1),
        small_three=sems(2, batch - 1),
    )
    for t in range(n.bit_length() - 1):
        scratch["came_one_%d" % t] = low(chunks, n >> (t + 1), rows, chunk // 2)
        scratch["came_down_%d" % t] = low(n >> (t + 1), rows, width // 2)
        scratch["came_qkv_%d" % t] = low(pieces, n >> (t + 1), rows, chunk_two)
    specs = [smem if k == "lengths" else in_hbm() if k.endswith("_hbm") else vmem for k in operands]
    names = tuple(operands) + tuple(outs) + tuple(scratch)
    return pl.pallas_call(
        partial(layer_kernel, plan, (heads, chunk, chunk_two, block, batch), names),
        in_specs=specs,
        out_specs=[in_hbm() if k in ("output", "grad_inputs") else vmem for k in outs],
        out_shape=[jax.ShapeDtypeStruct(*shape) for shape in outs.values()],
        scratch_shapes=list(scratch.values()),
        compiler_params=pltpu.CompilerParams(
            collective_id=collective_id, has_side_effects=True, vmem_limit_bytes=63 * MIB
        ),
        name="layer",
    )(*operands.values())


def finish_kernel(count, sizes, aligned, names, *refs):
    r = SimpleNamespace(**dict(zip(names, refs)))
    batch, width, layers = sizes
    rows = width // count
    me = lax.axis_index("blk")
    half = width // 2
    passed = [
        local(r.totals_hbm, r.totals, r.sems.at[0]),
        local(r.small_hbm, r.small, r.sems.at[1]),
        local(r.output_hbm, r.output_made, r.sems.at[2]),
        local(r.grad_inputs_hbm, r.grad_inputs_made, r.sems.at[3]),
        local(r.grad_time_hbm, r.grad_time_made, r.sems.at[4]),
    ]
    passed[0].wait()
    for core in range(2):
        for i in range(layers):
            made = r.totals[core, :, i * half : (i + 1) * half].astype(F32)
            r.down_made[i * rows : (i + 1) * rows, core * half : (core + 1) * half] = made
    passed.append(local(r.down_made, r.down, r.sems.at[5]))
    for core in range(2):
        start = layers * half
        made = r.totals[core, :, start : start + layers * half].astype(F32)
        r.up_made[:, core * layers * half : (core + 1) * layers * half] = made
    passed.append(local(r.up_made, r.up, r.sems.at[6]))
    for i, k in enumerate(("output", "grad_inputs", "grad_time")):
        passed[2 + i].wait()
        passed[2 + i] = local(getattr(r, k + "_made"), getattr(r, k), r.sems.at[2 + i])
    for core in range(2):
        start = 2 * layers * half
        r.out_made[:, core * half : (core + 1) * half] = r.totals[core, :, start : start + half].astype(F32)
        made = r.totals[core, :, start + half : start + 4 * half].astype(F32)
        r.qkv_made[:, core * 3 * half : (core + 1) * 3 * half] = made
    passed.append(local(r.out_made, r.out, r.sems.at[7]))
    passed.append(local(r.qkv_made, r.qkv, r.sems.at[8]))
    passed[1].wait()
    for u in range(2 * batch):
        b, s = u // 2, u % 2
        line = r.small[b, 15 + 2 + layers + s, pl.ds(me * rows // LANES, 1)]
        if rows < LANES:
            line = pltpu.roll(line, LANES - lax.rem(me, LANES // rows) * rows, 1)
        r.times[u : u + 1] = line
        for p in range(6):
            for c in range(width // LANES):
                start = p * width + c * LANES
                r.mods[u : u + 1, start : start + LANES] = r.small[b, 2 * p + s, c : c + 1]
    times, mods = r.times[:, :rows].astype(BF16), r.mods[...].astype(BF16)
    for i in range(2):
        span = slice(i * 3 * width, (i + 1) * 3 * width)
        r.w_mod_made[:, span] = dot_frames(times, mods[:, span])
        passed.append(local(r.w_mod_made.at[:, span], r.w_mod.at[:, span], r.sems.at[9 + i]))
    if aligned:
        tiles = width // LANES

        def own_lines(first, length, stride):
            lines = []
            for i in range(length // count // LANES):
                at = me * (length // count // LANES) + i
                total = jnp.zeros((1, LANES), F32)
                for b in range(batch):
                    for s in range(stride):
                        total = total + r.small[b, first + at // tiles * stride + s, pl.ds(lax.rem(at, tiles), 1)]
                lines.append(total)
            return lines

        firsts = [(0, 6, 2), (12, 3, 1), (15, 1, 1), (16, layers, 1), (16 + layers, 1, 1)]
        for which, (first, many, stride) in enumerate(firsts):
            ref = getattr(r, "vector%d" % which)
            for i, line in enumerate(own_lines(first, many * width, stride)):
                ref[i * LANES : (i + 1) * LANES] = line[0]
    for copy in passed[2:]:
        copy.wait()


def finish(count, output, grad_inputs, grad_time, totals, small, layers):
    batch, width = small.shape[0], output.shape[2]
    rows = width // count
    aligned = rows % LANES == 0
    operands = dict(
        output_hbm=output, grad_inputs_hbm=grad_inputs, grad_time_hbm=grad_time, totals_hbm=totals, small_hbm=small
    )
    shapes = dict(
        down=(layers * rows, width),
        up=(rows, layers * width),
        out=(rows, width),
        qkv=(rows, 3 * width),
        w_mod=(rows, 6 * width),
    )
    outs = dict(output=output.shape, grad_inputs=output.shape, grad_time=grad_time.shape, **shapes)
    vectors = {}
    if aligned:
        vectors = {"vector%d" % i: (many * rows,) for i, many in enumerate((6, 3, 1, layers, 1))}
    scratch = {k + "_made": pltpu.VMEM(v, F32) for k, v in outs.items()}
    scratch.update(
        totals=pltpu.VMEM(totals.shape, BF16),
        small=pltpu.VMEM(small.shape, F32),
        times=pltpu.VMEM((2 * batch, LANES), F32),
        mods=pltpu.VMEM((2 * batch, 6 * width), F32),
        sems=pltpu.SemaphoreType.DMA((11,)),
    )
    names = tuple(operands) + tuple(outs) + tuple(vectors) + tuple(scratch)
    made = pl.pallas_call(
        partial(finish_kernel, count, (batch, width, layers), aligned, names),
        in_specs=[in_hbm()] * len(operands),
        out_specs=[in_hbm()] * len(outs) + [pl.BlockSpec(memory_space=pltpu.VMEM)] * len(vectors),
        out_shape=[jax.ShapeDtypeStruct(v, F32) for v in (outs | vectors).values()],
        scratch_shapes=list(scratch.values()),
        compiler_params=pltpu.CompilerParams(vmem_limit_bytes=62 * MIB),
        name="finish",
    )(*operands.values())
    if not aligned:
        me = lax.axis_index("blk")
        flat = jnp.sum(small.reshape(batch, -1, width), axis=0)
        mods = flat[:12].reshape(6, 2, width).sum(axis=1)
        ends = [12, 15, 16, 16 + layers, 17 + layers]
        rest = [mods] + [flat[lo:hi] for lo, hi in zip(ends[:-1], ends[1:])]
        made = list(made) + [
            lax.dynamic_index_in_dim(v.reshape(count, -1), me, 0, keepdims=False) for v in rest
        ]
    return made


def on_device(
    inputs,
    time_embed,
    lengths,
    cotangent,
    w_mod,
    b_mod,
    w_qkv,
    b_qkv,
    w_out,
    b_out,
    w_up,
    b_up,
    w_down,
    b_down,
):
    _, frames, width = inputs.shape
    count, batch = lax.axis_size("blk"), lax.axis_size("batch")
    plan = Plan(count, frames, width)
    operands = dict(
        lengths=lengths,
        time_embed=time_embed,
        b_mod=b_mod,
        b_qkv=b_qkv,
        b_out=b_out,
        b_up=b_up,
        b_down=b_down,
        x_hbm=inputs,
        ct_hbm=cotangent,
        w_mod_hbm=w_mod,
        w_qkv_hbm=w_qkv,
        w_out_hbm=w_out,
        w_up_hbm=w_up,
        w_down_hbm=w_down,
    )
    made = layer(plan, (HEADS, 512, 256, 512), batch, operands, 0)
    output, grad_inputs, grad_time, down, up, out, qkv, grad_w_mod, *vectors = finish(
        count, *made, w_up.shape[1] // width
    )
    return (
        output,
        grad_inputs,
        grad_time,
        grad_w_mod,
        vectors[0],
        qkv,
        vectors[1],
        out,
        vectors[2],
        up,
        vectors[3],
        down,
        vectors[4],
    )


def solution(mesh):
    frame_spec, weight_spec = P("batch", "blk", None), P("blk", None)
    return jax.shard_map(
        on_device,
        mesh=mesh,
        in_specs=(frame_spec, P("batch", None), P("batch"), frame_spec) + (P(),) * 10,
        out_specs=(frame_spec, frame_spec, P("batch", None)) + (weight_spec, P("blk")) * 5,
        check_vma=False,
    )
```

```python
from functools import partial
from types import SimpleNamespace

import jax
import jax.numpy as jnp
from jax import lax
from jax.experimental import pallas as pl
from jax.experimental.pallas import tpu as pltpu
from jax.sharding import PartitionSpec as P

HEADS = 16
EPS = 1e-06
LANES = 128
SHORT = 16
MESH = pl.DeviceIdType.MESH
BF16 = jnp.bfloat16
F32 = jnp.float32
MIB = 1 << 20


def dot(left, right):
    return jnp.dot(left, right, preferred_element_type=F32)


def dot_rows(left, right):
    return lax.dot_general(left, right, (((1,), (1,)), ((), ())), preferred_element_type=F32)


def dot_frames(left, right):
    return lax.dot_general(left, right, (((0,), (0,)), ((), ())), preferred_element_type=F32)


def normalize(rows):
    mean = jnp.mean(rows, axis=-1, keepdims=True)
    centered = rows - mean
    inverse = lax.rsqrt(jnp.mean(centered * centered, axis=-1, keepdims=True) + EPS)
    return (centered * inverse, inverse)


def norm_back(normed, inverse, grad):
    return inverse * (
        grad
        - jnp.mean(grad, axis=-1, keepdims=True)
        - normed * jnp.mean(grad * normed, axis=-1, keepdims=True)
    )


def whole(shape):
    return pl.BlockSpec(shape, lambda *_: (0,) * len(shape))


def in_hbm():
    return pl.BlockSpec(memory_space=pltpu.HBM)


def rotate(rows, cos_table, sin_table, half):
    lane = lax.broadcasted_iota(jnp.int32, rows.shape, 1)
    partner = jnp.where(
        lax.rem(lane, 2 * half) < half,
        pltpu.roll(rows, LANES - half, 1),
        pltpu.roll(rows, half, 1),
    )
    return rows * cos_table + partner * sin_table


class Spot:
    def __init__(self, count):
        b, j = lax.axis_index("batch"), lax.axis_index("blk")
        self.b, self.j = b, j
        self.core, self.half = lax.rem(b, 2), b // 2
        self.near, self.far = lax.rem(j, 2), j // 2
        self.far_count = count // 2
        self.at_core = (self.half * 2 + 1 - self.core, j)
        self.at_x = ((1 - self.half) * 2 + self.core, j)
        self.at_both = ((1 - self.half) * 2 + 1 - self.core, j)
        self.at_near = (b, self.far * 2 + 1 - self.near)
        self.far_steps = [lax.rem(self.far + step, self.far_count) for step in range(1, self.far_count)]
        self.at_far = [(b, step * 2 + self.near) for step in self.far_steps]


def add_into(target, other):
    target[...] = (target[...].astype(F32) + other.astype(F32)).astype(BF16)


class Plan:
    def __init__(self, count, frames, width):
        self.count = count
        self.frames = frames
        self.width = width
        self.groups = min(max(count // 2, 1), 4)
        self.cols = width // self.groups
        self.splits = count // self.groups
        self.total = count * frames
        self.short = self.total // SHORT
        self.short_rows = min(self.short, frames)
        self.short_blocks = -(-self.short // frames)
        self.phases = [(lo, min(lo + 4 * self.groups, count)) for lo in range(self.groups, count, 4 * self.groups)]
        self.phases = [(0, self.groups)] + self.phases
        self.largest = max(hi - lo for lo, hi in self.phases) * frames
        self.offsets = [(d, s) for d in range(self.splits) for s in range(self.groups) if d + s > 0]

    def peer(self, device, offset):
        split = lax.rem(device // self.groups + offset[0], self.splits)
        return split * self.groups + lax.rem(lax.rem(device, self.groups) + offset[1], self.groups)


def push(src, dst, sems, index, device):
    copy = pltpu.make_async_remote_copy(
        src_ref=src, dst_ref=dst, send_sem=sems.at[(0,) + index], recv_sem=sems.at[(1,) + index],
        device_id=device, device_id_type=MESH,
    )
    copy.start()
    return copy


def local(src, dst, sem):
    copy = pltpu.make_async_copy(src, dst, sem)
    copy.start()
    return copy


def stacked(rows, head_dim):
    lane = lax.broadcasted_iota(jnp.int32, rows.shape, 1)
    heads = LANES // head_dim
    return jnp.concatenate(
        [jnp.where(lane // head_dim == h, rows, jnp.zeros_like(rows)) for h in range(heads)], axis=0
    )


def unstacked(turned, frames, head_dim):
    heads = LANES // head_dim
    return jnp.concatenate(
        [
            turned[h * head_dim : (h + 1) * head_dim, h * frames : (h + 1) * frames]
            for h in range(heads)
        ],
        axis=0,
    ).T


def attend_part(queries, keys, values_t, head_dim):
    scores = dot_rows(keys, stacked(queries, head_dim))
    top = jnp.max(scores, axis=0, keepdims=True)
    weights = jnp.exp(scores - top)
    total = jnp.sum(weights, axis=0, keepdims=True)
    return top, total, dot(values_t, weights.astype(BF16))


def attend_join(one, two):
    top = jnp.maximum(one[0], two[0])
    left, right = jnp.exp(one[0] - top), jnp.exp(two[0] - top)
    return top, one[1] * left + two[1] * right, one[2] * left + two[2] * right


def attend_end(state, frames, head_dim):
    top, total, out = state
    return unstacked(out / total, frames, head_dim).astype(BF16), top + jnp.log(total)


def delta_rows(grads, outs, head_dim):
    heads = LANES // head_dim
    lane = lax.broadcasted_iota(jnp.int32, (8, LANES), 1)
    pick = (lane // head_dim == lax.broadcasted_iota(jnp.int32, (8, LANES), 0)).astype(F32)
    product = grads.astype(F32) * outs.astype(F32)
    sums = lax.dot_general(
        pick, product, (((1,), (1,)), ((), ())), precision=lax.Precision.HIGHEST, preferred_element_type=F32
    )
    return jnp.concatenate([sums[h : h + 1] for h in range(heads)], axis=1)


def attend_back(queries, grads, lse, delta, keys, keys_t, values, head_dim):
    frames = queries.shape[0]
    q_heads, g_heads = stacked(queries, head_dim), stacked(grads, head_dim)
    probs = jnp.exp(dot_rows(keys, q_heads) - lse)
    grad_probs = dot_rows(values, g_heads)
    grad_scores = (probs * (grad_probs - delta)).astype(BF16)
    grad_values = dot(probs.astype(BF16), g_heads)
    grad_keys = dot(grad_scores, q_heads)
    grad_queries = unstacked(dot(keys_t, grad_scores), frames, head_dim) * head_dim ** (-0.5)
    return grad_queries, grad_keys, grad_values


def gelu_both(z):
    scale = (2.0 / 3.141592653589793) ** 0.5
    square = z * z
    inner = jnp.tanh(scale * z * (1.0 + 0.044715 * square))
    half = 0.5 * (1.0 + inner)
    slope = half + 0.5 * z * (1.0 - inner * inner) * (scale * (1.0 + 3.0 * 0.044715 * square))
    return z * half, slope


def layer_kernel(plan, sizes, names, *refs):
    r = SimpleNamespace(**dict(zip(names, refs)))
    r.came_at = lambda kind, t: getattr(r, "came_%s_%d" % (kind, t))
    heads, chunk, chunk_two, block, batch = sizes
    n, g, f, cols, width = plan.count, plan.groups, plan.frames, plan.cols, plan.width
    tokens, hidden = 2 * f, r.w_up.shape[1]
    head_dim, half_dim = width // heads, width // heads // 2
    half_width, half_hidden = width // 2, hidden // 2
    layers, n_rows, units = hidden // width, width // n, cols // LANES
    spot = Spot(n)
    b, me, core, half = spot.b, spot.j, spot.core, spot.half
    group, split = lax.rem(me, g), me // g
    others = [plan.peer(me, offset) for offset in plan.offsets]
    mates = others[: g - 1]
    along = [(b, peer) for peer in others]
    across = [(lax.rem(b + step, batch), me) for step in range(1, batch)]
    seqs = [slice(0, f), slice(f, tokens)]
    mine, theirs = slice(0, tokens), slice(tokens, 2 * tokens)
    swapped = r.lengths[0] < r.lengths[1]
    first = jnp.where(swapped, 1, 0)
    order = [first, 1 - first]

    barrier = pltpu.get_barrier_semaphore()
    for device in along + across:
        pl.semaphore_signal(barrier, inc=1, device_id=device, device_id_type=MESH)

    load_x = local(r.x_hbm, r.x, r.in_sems.at[0])
    mod_places, mod_copies = [r.w_mod.at[0], r.w_mod.at[1]], {}
    room = r.parts.reshape(width, r.parts.shape[2])
    mod_places += [room.at[:, :half_width], room.at[:, half_width:width]]
    ahead = len(mod_places)

    def mod_place(i):
        return i if i < ahead else i % 2

    def load_mod(i, place):
        return local(r.w_mod_hbm.at[:, i * half_width : (i + 1) * half_width], mod_places[place], r.m_sems.at[place])

    def next_mod(i):
        if mod_place(i) < 2:
            after = i + ahead if i < 2 else i + 2
            if after < 12:
                mod_copies[after] = load_mod(after, mod_place(after))

    def load_qkv():
        return [
            local(r.w_qkv_hbm.at[:, : 2 * width], r.w_up.at[:, : 2 * width], r.in_sems.at[1]),
            local(r.w_qkv_hbm.at[:, 2 * width :], r.w_out, r.in_sems.at[2]),
        ]

    for i in range(ahead):
        mod_copies[i] = load_mod(i, i)
    qkv_copies = load_qkv()

    shown = r.time_embed[...].astype(F32)
    shown = jnp.where(swapped, jnp.concatenate([shown[1:2], shown[0:1]], axis=0), shown)
    r.acts[...] = (shown / (1.0 + jnp.exp(-shown))).astype(BF16)
    frame = me * f + lax.broadcasted_iota(jnp.int32, (f, LANES), 0)
    lane = lax.broadcasted_iota(jnp.int32, (f, LANES), 1)
    exponent = lax.rem(lane, half_dim).astype(F32) * (-1.0 / half_dim)
    angle = frame.astype(F32) * jnp.exp(exponent * 9.210340371976184)
    sines = jnp.sin(angle)
    r.cos[...] = jnp.cos(angle)
    r.sin[...] = jnp.where(lax.rem(lane, 2 * half_dim) < half_dim, -sines, sines)
    r.b_row[...] = r.b_qkv[...][None].astype(F32)

    def mod_piece(i, place):
        piece = slice(i * half_width, (i + 1) * half_width)
        r.mods[:, piece] = dot(r.acts[...], mod_places[place][...]) + r.b_mod[piece][None].astype(F32)

    def mod(i, s):
        return r.mods[s : s + 1, i * width : (i + 1) * width]

    for i in range(4):
        mod_copies[i].wait()
        mod_piece(i, mod_place(i))
        next_mod(i)

    load_x.wait()
    for s, span in enumerate(seqs):
        normed, _ = normalize(r.x[order[s]].astype(F32))
        r.hidden_f[span] = (normed * (1.0 + mod(1, s)) + mod(0, s)).astype(BF16)
    for copy in qkv_copies:
        copy.wait()
    load_ct = local(r.ct_hbm, r.ct, r.in_sems.at[3])
    load_down = local(r.w_down_hbm, r.w_down, r.in_sems.at[4])
    pl.semaphore_wait(barrier, len(along + across))

    def project(kind, which):
        at = pl.ds(pl.multiple_of(which * cols, LANES), cols)
        bias_at = pl.ds(pl.multiple_of(kind * width + which * cols, LANES), cols)
        weight = r.w_out[:, at] if kind == 2 else r.w_up[:, bias_at]
        made = dot(r.hidden_f[...], weight) + r.b_row[:, bias_at]
        if kind < 2:
            factor = (2.0 * half_dim) ** (-0.5) if kind == 0 else 1.0
            cosines, sines = r.cos[...] * factor, r.sin[...] * factor
        for span in seqs:
            for u in range(units):
                part = made[span, u * LANES : (u + 1) * LANES]
                if kind < 2:
                    part = rotate(part, cosines, sines, half_dim)
                start = kind * cols + u * LANES
                r.rows[which, span, start : start + LANES] = part.astype(BF16)

    near_waits = []

    def send_keys(step):
        offset = plan.offsets[step]
        src = r.rows.at[lax.rem(others[step], g), 0:f, cols : 3 * cols]
        dst = r.kv_buf.at[offset[0] * g + group]
        return push(src, dst, r.k_sems, (step,), along[step])

    def short_rows_of(peer):
        return r.rows.at[lax.rem(peer, g), f : f + plan.short_rows, cols : 3 * cols]

    def pass_on(blk):
        for d in range(1, plan.splits):
            place = r.short_buf.at[blk]
            push(place, place, r.s_sems, (blk, g - 2 + d), along[d * g - 1])

    inner = jnp.logical_or(lax.rem(spot.far, 4) == 1, lax.rem(spot.far, 4) == 2)
    for step in range(1, g + 1):
        which = lax.rem(group + step, g)
        project(1, which)
        project(2, which)

        @pl.when(inner)
        def _():
            for d in range(1, plan.splits):
                send_keys(d * g + step % g - 1)

        if step < g:
            near_waits.append(send_keys(step - 1))
    for step in range(1, g + 1):
        which = lax.rem(group + step, g)
        project(0, which)
        if step < g:
            src = r.rows.at[which, :, 0:cols]
            near_waits.append(push(src, r.q_buf.at[group], r.q_sems, (step - 1,), along[step - 1]))

    for blk in range(plan.short_blocks):

        @pl.when(me == blk)
        def _():
            for step, peer in enumerate(mates):
                push(short_rows_of(peer), r.short_buf.at[blk], r.s_sems, (blk, step), along[step])
            r.short_buf[blk] = r.rows[group, f : f + plan.short_rows, cols : 3 * cols]
            pass_on(blk)

    @pl.when(jnp.logical_not(inner))
    def _():
        for step in range(g - 1, n - 1):
            send_keys(step)

    def lot(i):
        return slice(i * tokens, (i + 1) * tokens)

    around = [spot.at_core, spot.at_x, spot.at_both]
    r.both_hidden[:, lot(0)] = r.hidden_f[...].T
    swap_hidden = [
        push(r.both_hidden.at[:, lot(0)], r.both_hidden.at[:, lot(i + 1)], r.h_sems, (i,), device)
        for i, device in enumerate(around)
    ]
    load_out = local(r.w_out_hbm, r.w_out, r.in_sems.at[2])
    load_up = local(r.w_up_hbm, r.w_up, r.in_sems.at[1])
    r.kv_buf[group] = r.rows[group, 0:f, cols : 3 * cols]
    r.q_buf[group] = r.rows[group, :, 0:cols]

    for i in range(4, 12):
        mod_copies[i].wait()
        mod_piece(i, mod_place(i))
        next_mod(i)

    load_ct.wait()
    for s, span in enumerate(seqs):
        r.grad_ff[span] = (mod(5, s) * r.ct[order[s]].astype(F32)).astype(BF16)

    def core_half(which, size):
        return pl.ds(pl.multiple_of(which * size, LANES), size)

    def to_core(src, dst, index):
        return push(src, dst, r.e_sems, (index,), spot.at_core)

    ff_own, ff_other = core_half(core, half_width), core_half(1 - core, half_width)
    swap_ff = [
        to_core(r.grad_ff.at[:, ff_other], r.all_ff.at[1], 0),
        push(r.grad_ff.at[:, ff_own], r.all_ff.at[2], r.ff_sems, (0,), spot.at_x),
        push(r.grad_ff.at[:, ff_other], r.all_ff.at[3], r.ff_sems, (1,), spot.at_both),
    ]
    r.all_ff[0] = r.grad_ff[:, ff_own]

    for copy in near_waits:
        copy.wait()
    for blk in range(plan.short_blocks):
        for step in range(g - 1):

            @pl.when(me == plan.peer(blk, plan.offsets[step]))
            def _():
                dst = r.short_buf.at[blk]
                pltpu.make_async_copy(dst, dst, r.s_sems.at[1, blk, step]).wait()
                pass_on(blk)

    def turn_values(lo, hi, start):
        part = r.kv_buf[lo:hi, :, start : start + cols].reshape((hi - lo) * f, cols)
        r.turned[:, lo * f : hi * f] = part.T

    def cols_of(which):
        return pl.ds(pl.multiple_of(which * cols, LANES), cols)

    def slot_of(step):
        return lax.rem(group + 1 + step, g)

    units = cols // LANES
    sends = []
    for phase, (lo, hi) in enumerate(plan.phases):
        last = phase == len(plan.phases) - 1
        if phase == 1:
            for step in range(g - 1, n - 1):
                src = r.rows.at[group, 0:f, cols : 3 * cols]
                pltpu.make_async_copy(src, src, r.k_sems.at[0, step]).wait()
                dst = r.kv_buf.at[plan.offsets[step][0] * g + lax.rem(group + g - plan.offsets[step][1], g)]
                pltpu.make_async_copy(dst, dst, r.k_sems.at[1, step]).wait()
        turn_values(lo, hi, cols)
        for step in range(g):
            slot = slot_of(step)
            for u in range(units):
                lanes = slice(u * LANES, (u + 1) * LANES)
                at = step * units + u
                state = attend_part(
                    r.q_buf[slot, :f, lanes],
                    r.kv_buf[lo:hi, :, lanes].reshape((hi - lo) * f, LANES),
                    r.turned[lanes, lo * f : hi * f],
                    head_dim,
                )
                if phase > 0:
                    state = attend_join((r.top_acc[at], r.total_acc[at], r.o_acc[at]), state)
                if last:
                    r.o_buf[slot, :f, lanes], r.lse[slot, u : u + 1] = attend_end(state, f, head_dim)
                else:
                    r.top_acc[at], r.total_acc[at], r.o_acc[at] = state
            if last and step == 0:
                for blk in range(plan.short_blocks):
                    for d in range(1, plan.splits):

                        @pl.when(split == (blk // g + d) % plan.splits)
                        def _():
                            dst = r.short_buf.at[blk]
                            pltpu.make_async_copy(dst, dst, r.s_sems.at[1, blk, g - 2 + d]).wait()

                r.short_turned[...] = r.short_buf[:, :, cols:].reshape(plan.short, cols).T
            if last:
                for u in range(units):
                    lanes = slice(u * LANES, (u + 1) * LANES)
                    keys = r.short_buf[:, :, lanes].reshape(plan.short, LANES)
                    state = attend_part(r.q_buf[slot, f:, lanes], keys, r.short_turned[lanes], head_dim)
                    row = units + u
                    r.o_buf[slot, f:, lanes], r.lse[slot, row : row + 1] = attend_end(state, f, head_dim)
                if step == g - 1:
                    r.attn[:, cols_of(group)] = r.o_buf[slot]
                else:
                    dst = r.attn.at[:, cols_of(group)]
                    sends.append(push(r.o_buf.at[slot], dst, r.o_sems, (step,), along[step]))
    for lo, hi in plan.phases:
        turn_values(lo, hi, 0)
    r.short_turned[...] = r.short_buf[:, :, :cols].reshape(plan.short, cols).T
    for copy in sends:
        copy.wait()
    for blk in range(plan.short_blocks):

        @pl.when(me == blk)
        def _():
            for step, peer in enumerate(mates):
                src = short_rows_of(peer)
                pltpu.make_async_copy(src, src, r.s_sems.at[0, blk, step]).wait()

        @pl.when(split == blk // g)
        def _():
            for d in range(1, plan.splits):
                src = r.short_buf.at[blk]
                pltpu.make_async_copy(src, src, r.s_sems.at[0, blk, g - 2 + d]).wait()

    load_out.wait()
    r.attn_t[:, mine] = r.attn[...].T
    swap_attn = to_core(r.attn_t.at[:, mine], r.attn_t.at[:, theirs], 1)
    r.branch_a[...] = dot(r.attn[...], r.w_out[...]) + r.b_out[...][None].astype(F32)
    for s, span in enumerate(seqs):
        r.mixed[span] = r.x[order[s]].astype(F32) + mod(2, s) * r.branch_a[span]
        normed, _ = normalize(r.mixed[span])
        r.hidden_f[span] = (normed * (1.0 + mod(4, s)) + mod(3, s)).astype(BF16)
    r.hid_t[:, mine] = r.hidden_f[...].T
    swap_hid = to_core(r.hid_t.at[:, mine], r.hid_t.at[:, theirs], 2)
    load_up.wait()
    load_down.wait()
    swap_act, act_x = [], []
    per_block = block // (layers * n_rows)
    for i in range(hidden // block):
        span = slice(i * block, (i + 1) * block)
        act, slope = gelu_both(dot(r.hidden_f[...], r.w_up[:, span]) + r.b_up[span][None].astype(F32))
        act = act.astype(BF16)
        act_t = act.T.reshape(per_block, layers, n_rows, tokens)
        held = slice(i * per_block, (i + 1) * per_block)
        r.act_own[held, :, mine] = jnp.where(half == 0, act_t[:, 0], act_t[:, 1])
        r.act_send[held] = jnp.where(half == 0, act_t[:, 1], act_t[:, 0])
        act_x.append(
            push(r.act_send.at[held], r.act_own.at[held, :, 2 * tokens : 3 * tokens], r.act_sems, (0, i), spot.at_x)
        )
        swap_act.append(
            push(r.act_own.at[held, :, mine], r.act_own.at[held, :, theirs], r.act_sems, (1, i), spot.at_core)
        )
        forward = dot(act, r.w_down[span, :])
        grad = (dot_rows(r.grad_ff[...], r.w_down[span, :]) * slope).astype(BF16)
        r.grad_pre[:, span] = grad
        row, start = 9 + i * block // width, i * block % width
        r.stats[row : row + 1, start : start + block] = jnp.sum(grad.astype(F32), axis=0, keepdims=True)
        back = dot_rows(grad, r.w_up[:, span])
        if i == 0:
            r.branch_f[...] = forward + r.b_down[...][None].astype(F32)
            r.grad_hid[...] = back
        else:
            r.branch_f[...] += forward
            r.grad_hid[...] += back
    swap_pre = to_core(r.grad_pre.at[:, core_half(1 - core, half_hidden)], r.both_pre.at[1], 3)
    r.both_pre[0] = r.grad_pre[:, core_half(core, half_hidden)]

    chunks, half_chunk = r.parts.shape[2] // chunk, chunk // 2
    base_one = layers * half_width
    x_copies, stage_copies, stage_of, last, sent, closing = {}, {}, {}, [], {}, {}

    def half_of(k, which):
        return pl.ds(pl.multiple_of(k * chunk + which * half_chunk, LANES), half_chunk)

    stages = range(n.bit_length() - 1)
    pieces = 3 * cols // chunk_two
    rooms = {k: (r.x_buf.at[k], [r.came_at("one", t).at[k] for t in stages], k) for k in range(chunks)}
    rooms["down"] = (r.down_sum, [r.came_at("down", t) for t in stages], chunks)
    for i in range(pieces):
        rooms["qkv", i] = (r.qkv_sum.at[i], [r.came_at("qkv", t).at[i] for t in stages], chunks + 1 + i)

    def total_of(k, which):
        if k == "down":
            return core_half(which, half_width)
        if k in range(chunks):
            return pl.ds(pl.multiple_of(base_one + k * chunk + which * half_chunk, LANES), half_chunk)
        start = base_one + chunks * chunk + which * 3 * cols + k[1] * chunk_two
        return pl.ds(pl.multiple_of(start, LANES), chunk_two)

    def start_x(k):
        src = r.parts.at[:, :, half_of(k, 1 - half)]
        x_copies[k] = push(src, r.x_buf.at[k], r.x_sems, (k,), spot.at_x)

    bits = [lax.rem(me // (1 << t), 2) for t in stages]
    partners = [(b, me + (1 - 2 * bit) * (1 << t)) for t, bit in enumerate(bits)]

    def halves(k, t):
        held = rooms[k][0] if t == 0 else rooms[k][1][t - 1]
        return held.reshape(n >> (t + 1), 2, n_rows, held.shape[2])

    def start_stage(k, t):
        _, came, number = rooms[k]
        stage_of[k] = t
        stage_copies[k] = push(halves(k, t).at[:, 1 - bits[t]], came[t], r.blk_sems, (number, t), partners[t])

    def finish_x(k):
        x_copies[k].wait()
        add_into(r.x_buf.at[k], r.parts[:, :, half_of(k, half)])
        start_stage(k, 0)

    def advance(k):
        t = stage_of[k]
        _, came, number = rooms[k]
        stage_copies[k].wait()
        if t + 1 < len(stages):
            add_into(came[t], halves(k, t)[:, bits[t]])
            start_stage(k, t + 1)
        else:
            total = came[t][0].astype(F32) + halves(k, t)[0, bits[t]].astype(F32)
            r.totals[core, :, total_of(k, half)] = total.astype(BF16)
            sent[k] = to_all(total_of(k, half), number)

    def to_all(where, which):
        place = r.totals.at[core, :, where]
        return [
            push(place, place, r.ax_sems, (which,), spot.at_x),
            push(place, place, r.ac_sems, (2 * which,), spot.at_core),
        ]

    def forward_to_core(where, which):
        place = r.totals.at[core, :, where]
        return push(place, place, r.ac_sems, (2 * which + 1,), spot.at_core)

    def finish_all(k):
        while k not in sent:
            advance(k)
        sent[k][0].wait()
        closing[k] = [sent[k][1], forward_to_core(total_of(k, 1 - half), rooms[k][2])]

    for s, span in enumerate(seqs):
        grad_out = r.ct[order[s]].astype(F32)
        branch, grad = r.branch_f[span], r.grad_hid[span]
        normed, inverse = normalize(r.mixed[span])
        r.stats[6 + s : 7 + s] = jnp.sum(grad_out * branch, axis=0, keepdims=True)
        r.stats[4 + s : 5 + s] = jnp.sum(grad * normed, axis=0, keepdims=True)
        r.stats[2 + s : 3 + s] = jnp.sum(grad, axis=0, keepdims=True)
        total = grad_out + norm_back(normed, inverse, grad * (1.0 + mod(4, s)))
        r.grad_mixed[span] = total
        r.stats[s : s + 1] = jnp.sum(total * r.branch_a[span], axis=0, keepdims=True)
        r.grad_br[span] = (mod(2, s) * total).astype(BF16)
    r.grads[...] = dot_rows(r.grad_br[...], r.w_out[...]).astype(BF16)
    waits = []
    for step, peer in enumerate(mates):
        src = r.grads.at[:, cols_of(lax.rem(peer, g))]
        waits.append(push(src, r.g_buf.at[group], r.bg_sems, (step,), along[step]))
    r.g_buf[group] = r.grads[:, cols_of(group)]
    swap_br = to_core(r.grad_br.at[:, core_half(1 - core, half_width)], r.both_br.at[1], 4)
    qkv_copies = load_qkv()

    for i, copy in enumerate(act_x):
        copy.wait()
        held = slice(i * per_block, (i + 1) * per_block)
        src = r.act_own.at[held, :, 2 * tokens : 3 * tokens]
        dst = r.act_own.at[held, :, 3 * tokens : 4 * tokens]
        swap_act.append(push(src, dst, r.act_sems, (2, i), spot.at_core))
    swap_hid.wait()
    swap_pre.wait()
    for i in range(layers):
        grad = r.both_pre[:, :, i * half_width : (i + 1) * half_width].reshape(2 * tokens, half_width)
        up = dot(r.hid_t[...], grad).astype(BF16).reshape(n, n_rows, half_width)
        r.parts[:, :, i * half_width : (i + 1) * half_width] = up
        start_x(i)
    for copy in swap_ff + swap_act:
        copy.wait()
    down = dot(r.act_own[...].reshape(width, 4 * tokens), r.all_ff[...].reshape(4 * tokens, half_width))
    r.down_sum[...] = down.astype(BF16).reshape(n, n_rows, half_width)
    start_stage("down", 0)
    for copy in waits:
        copy.wait()

    strips = {i: load_mod(i, i % 2) for i in (4, 5)}

    sends = []
    deltas = [
        [
            [
                delta_rows(r.g_buf[slot_of(step), span, lanes], r.o_buf[slot_of(step), span, lanes], head_dim)
                for lanes in [slice(u * LANES, (u + 1) * LANES) for u in range(units)]
            ]
            for span in seqs
        ]
        for step in range(g)
    ]
    dq_buf = r.o_buf
    def short_back():
        for step in range(g):
            slot = slot_of(step)
            for u in range(units):
                lanes = slice(u * LANES, (u + 1) * LANES)
                high = slice(cols + u * LANES, cols + (u + 1) * LANES)
                row = units + u
                dq, dk, dv = attend_back(
                    r.q_buf[slot, f:, lanes],
                    r.g_buf[slot, f:, lanes],
                    r.lse[slot, row : row + 1],
                    deltas[step][1][u],
                    r.short_buf[:, :, lanes].reshape(plan.short, LANES),
                    r.short_turned[lanes],
                    r.short_buf[:, :, high].reshape(plan.short, LANES),
                    head_dim,
                )
                dq_buf[slot, f:, lanes] = dq.astype(BF16)
                if step == 0:
                    r.dsmall[0, :, lanes] = dk
                    r.dsmall[1, :, lanes] = dv
                else:
                    r.dsmall[0, :, lanes] += dk
                    r.dsmall[1, :, lanes] += dv
        for blk in range(plan.short_blocks):
            span = slice(blk * plan.short_rows, (blk + 1) * plan.short_rows)
            r.dshort_buf[blk] = r.dsmall[:, span].astype(BF16)
            for d in range(1, plan.splits):
                home = blk // g

                @pl.when(split == (home + d) % plan.splits)
                def _():
                    device = (b, home * g + group)
                    push(r.dshort_buf.at[blk], r.dshort_part.at[blk, d - 1], r.bp_sems, (blk, d - 1), device)

    def short_home():
        for blk in range(plan.short_blocks):

            @pl.when(split == blk // g)
            def _():
                total = r.dshort_buf[blk].astype(F32)
                for d in range(1, plan.splits):
                    place = r.dshort_part.at[blk, d - 1]
                    pltpu.make_async_copy(place, place, r.bp_sems.at[1, blk, d - 1]).wait()
                    total = total + place[...].astype(F32)
                r.dshort_buf[blk] = total.astype(BF16)

            dst = r.dshort_out.at[:, :, cols_of(group)]
            for step, peer in enumerate(mates):

                @pl.when(peer == blk)
                def _():
                    push(r.dshort_buf.at[blk], dst, r.bs_sems, (step,), along[step])

            @pl.when(me == blk)
            def _():
                r.dshort_out[:, :, cols_of(group)] = r.dshort_buf[blk]

    def send_back(lo, hi, u):
        lanes = slice(u * LANES, (u + 1) * LANES)
        back = pl.ds(pl.multiple_of(group * cols + u * LANES, LANES), LANES)
        made = [slice(which * cols + u * LANES, which * cols + (u + 1) * LANES) for which in range(2)]
        for which in range(2):
            sums = r.dlong[which, : (hi - lo) * f, lanes]
            r.kv_buf[lo:hi, :, made[which]] = sums.astype(BF16).reshape(hi - lo, f, LANES)
        for d in range(lo // g, hi // g):
            for s in range(g):
                if d == 0 and s == 0:
                    continue
                other_group = lax.rem(group + s, g)
                peer = lax.rem(split + plan.splits - d, plan.splits) * g + other_group
                for which in range(2):
                    dst = r.dkv_out.at[which, split, :, back]
                    src = r.kv_buf.at[d * g + other_group, :, made[which]]
                    sends.append(push(src, dst, r.bk_sems, (which, u, d * g + s), (b, peer)))
        if lo == 0:
            for which in range(2):
                r.dkv_out[which, split, :, back] = r.kv_buf[group, :, made[which]]

    short_back()

    r.both_br[0] = r.grad_br[:, core_half(core, half_width)]
    swap_attn.wait()
    swap_br.wait()
    out_part = dot(r.attn_t[...], r.both_br[...].reshape(2 * tokens, half_width))
    r.parts[:, :, layers * half_width :] = out_part.astype(BF16).reshape(n, n_rows, half_width)
    start_x(layers)
    made = [r.mixed[span] + mod(5, s) * r.branch_f[span] for s, span in enumerate(seqs)]
    r.mixed[seqs[0]] = jnp.where(swapped, made[1], made[0])
    r.mixed[seqs[1]] = jnp.where(swapped, made[0], made[1])
    last.append(local(r.mixed.reshape(2, f, width), r.output, r.in_sems.at[0]))
    last_row = 9 + layers
    r.stats[8:9] = jnp.sum(r.grad_br[...].astype(F32), axis=0, keepdims=True)
    r.stats[last_row : last_row + 1] = jnp.sum(r.grad_ff[...].astype(F32), axis=0, keepdims=True)

    for phase, (lo, hi) in enumerate(plan.phases[1:] + plan.phases[:1]):
        size = (hi - lo) * f
        for u in range(units):
            lanes = slice(u * LANES, (u + 1) * LANES)
            high = slice(cols + u * LANES, cols + (u + 1) * LANES)
            for step in range(g):
                slot = slot_of(step)
                dq, dk, dv = attend_back(
                    r.q_buf[slot, :f, lanes],
                    r.g_buf[slot, :f, lanes],
                    r.lse[slot, u : u + 1],
                    deltas[step][0][u],
                    r.kv_buf[lo:hi, :, lanes].reshape(size, LANES),
                    r.turned[lanes, lo * f : hi * f],
                    r.kv_buf[lo:hi, :, high].reshape(size, LANES),
                    head_dim,
                )
                if step == 0:
                    r.dlong[0, :size, lanes] = dk
                    r.dlong[1, :size, lanes] = dv
                else:
                    r.dlong[0, :size, lanes] += dk
                    r.dlong[1, :size, lanes] += dv
                if phase > 0:
                    dq = r.dq_acc[step, :, lanes] + dq
                if lo > 0:
                    r.dq_acc[step, :, lanes] = dq
                    continue
                dq_buf[slot, :f, lanes] = dq.astype(BF16)
                if u < units - 1:
                    continue
                if step == g - 1:
                    r.dq_out[:, cols_of(group)] = dq_buf[slot]
                else:
                    dst = r.dq_out.at[:, cols_of(group)]
                    sends.append(push(dq_buf.at[slot], dst, r.bq_sems, (step,), along[step]))
            send_back(lo, hi, u)

    short_home()

    def add_strip(total, i, rows_of):
        strips[i].wait()
        at = slice(i % 2 * half_width, (i % 2 + 1) * half_width)
        total = total + dot_rows(rows_of[:, at].astype(BF16), r.w_mod[i % 2])
        after = {10: 0, 11: 1}.get(i, i + 2)
        if after not in strips and after not in (4, 5):
            strips[after] = load_mod(after, i % 2)
        return total

    grad_act = jnp.zeros((2, width), F32)
    for i in range(4, 12):
        grad_act = add_strip(grad_act, i, r.stats[i // 2 * 2 - 4 : i // 2 * 2 - 2])
    advance("down")
    finish_x(0)
    for copy in sends:
        copy.wait()
    for blk in range(plan.short_blocks):
        place = r.dshort_buf.at[blk]
        for d in range(1, plan.splits):

            @pl.when(split == (blk // g + d) % plan.splits)
            def _():
                pltpu.make_async_copy(place, place, r.bp_sems.at[0, blk, d - 1]).wait()

        for step, peer in enumerate(mates):

            @pl.when(peer == blk)
            def _():
                pltpu.make_async_copy(place, place, r.bs_sems.at[0, step]).wait()

        @pl.when(me == blk)
        def _():
            for step in range(g - 1):
                pltpu.make_async_copy(place, place, r.bs_sems.at[1, step]).wait()

    no_short = me >= plan.short_blocks
    grad_key = jnp.sum(r.dkv_out[0].astype(F32), axis=0)
    grad_value = jnp.sum(r.dkv_out[1].astype(F32), axis=0)
    short_key = jnp.where(no_short, 0.0, r.dshort_out[0].astype(F32))
    short_value = jnp.where(no_short, 0.0, r.dshort_out[1].astype(F32))
    cosines, sines = r.cos[...], -r.sin[...]
    for c in range(width // LANES):
        lanes = slice(c * LANES, (c + 1) * LANES)
        for span in seqs:
            made = rotate(r.dq_out[span, lanes].astype(F32), cosines, sines, half_dim)
            r.grad_qkv[span, lanes] = made.astype(BF16)
        lanes_k = slice(width + c * LANES, width + (c + 1) * LANES)
        made = rotate(grad_key[:, lanes], cosines, sines, half_dim)
        r.grad_qkv[:f, lanes_k] = made.astype(BF16)
        made = rotate(short_key[:, lanes], cosines[: plan.short_rows], sines[: plan.short_rows], half_dim)
        r.grad_qkv[f : f + plan.short_rows, lanes_k] = made.astype(BF16)
    r.grad_qkv[:f, 2 * width :] = grad_value.astype(BF16)
    r.grad_qkv[f : f + plan.short_rows, 2 * width :] = short_value.astype(BF16)
    if plan.short_rows < f:
        r.grad_qkv[f + plan.short_rows :, width:] = jnp.zeros((f - plan.short_rows, 2 * width), BF16)

    own_cols = 3 * cols
    pieces = own_cols // chunk_two

    def piece_of(chip, core_of, i):
        return pl.ds(pl.multiple_of((core_of * 2 + chip) * own_cols + i * chunk_two, LANES), chunk_two)

    quarters = [(half, 1 - core), (1 - half, core), (1 - half, 1 - core)]
    swaps = []
    for i in range(pieces):
        for slot, (chip, core_of) in enumerate(quarters):
            src = r.grad_qkv.at[:, piece_of(chip, core_of, i)]
            dst = r.rows.at[slot + 1, :, i * chunk_two : (i + 1) * chunk_two]
            swaps.append(push(src, dst, r.g_sems, (slot, i), around[slot]))
        r.rows[0, :, i * chunk_two : (i + 1) * chunk_two] = r.grad_qkv[:, piece_of(half, core, i)]
    for k in range(1, chunks):
        finish_x(k)

    for copy in qkv_copies:
        copy.wait()
    grad_hidden = dot_rows(r.grad_qkv[:, : 2 * width], r.w_up[:, : 2 * width]) + dot_rows(
        r.grad_qkv[:, 2 * width :], r.w_out[...]
    )
    shift_rows, scale_rows, made = [], [], []
    for s, span in enumerate(seqs):
        normed, inverse = normalize(r.x[order[s]].astype(F32))
        grad = grad_hidden[span]
        shift_rows.append(jnp.sum(grad, axis=0, keepdims=True))
        scale_rows.append(jnp.sum(grad * normed, axis=0, keepdims=True))
        made.append(r.grad_mixed[span] + norm_back(normed, inverse, grad * (1.0 + mod(1, s))))
    r.grad_mixed[seqs[0]] = jnp.where(swapped, made[1], made[0])
    r.grad_mixed[seqs[1]] = jnp.where(swapped, made[0], made[1])
    last.append(local(r.grad_mixed.reshape(2, f, width), r.grad_inputs, r.in_sems.at[3]))
    bias = jnp.sum(r.grad_qkv[...].astype(F32), axis=0, keepdims=True)
    bias_rows = [bias[:, i * width : (i + 1) * width] for i in range(3)]
    kept = [r.stats[i : i + 1] for i in range(r.stats.shape[0])]
    pairs_a = [jnp.concatenate(shift_rows, axis=0), jnp.concatenate(scale_rows, axis=0)]
    for i in range(4):
        grad_act = add_strip(grad_act, i, pairs_a[i // 2])
    shown_rows = jnp.where(me == 0, r.acts[...].astype(F32), 0.0)
    time_rows = [shown_rows[0:1], shown_rows[1:2], grad_act[0:1], grad_act[1:2]]
    r.small[...] = jnp.zeros_like(r.small)
    for i, row in enumerate(shift_rows + scale_rows + kept[:8] + bias_rows + kept[8:] + time_rows):
        for c in range(width // LANES):
            r.small[i, c : c + 1] = row[:, c * LANES : (c + 1) * LANES]

    per = r.small.shape[0] // n
    copies = []
    for step, device in enumerate(along):
        src = r.small.at[pl.ds(device[1] * per, per)]
        copies.append(push(src, r.small_in.at[step], r.small_one, (step,), device))
    for copy in swap_hidden:
        copy.wait()

    def start_piece(i):
        for slot in range(3):
            swaps[3 * i + slot].wait()
        both = r.rows[:, :, i * chunk_two : (i + 1) * chunk_two].reshape(4 * tokens, chunk_two)
        made = dot(r.both_hidden[...], both).astype(BF16)
        r.qkv_sum[i] = made.reshape(n, n_rows, chunk_two)
        start_stage(("qkv", i), 0)

    def gather_small():
        total = r.small[pl.ds(me * per, per)]
        for step in range(n - 1):
            copies[step].wait()
            total = total + r.small_in[step]
        r.mine[...] = total
        own_slice = r.small_all.at[b, pl.ds(me * per, per)]
        own_slice[...] = total
        return [push(r.mine, own_slice, r.small_two, (step,), device) for step, device in enumerate(along)]

    def share_small():
        for copy in spread:
            copy.wait()
        shared = [push(r.small_all.at[b], r.small_all.at[b], r.small_three, (i,), device) for i, device in enumerate(across)]
        shown = r.time_embed[...].astype(F32)
        sigmoid = 1.0 / (1.0 + jnp.exp(-shown))
        slope = sigmoid * (1.0 + shown * (1.0 - sigmoid))
        row = 19 + layers
        for c in range(width // LANES):
            lanes = slice(c * LANES, (c + 1) * LANES)
            one, two = r.small_all[b, row, c : c + 1], r.small_all[b, row + 1, c : c + 1]
            upper, lower = jnp.where(swapped, two, one), jnp.where(swapped, one, two)
            r.grad_time[:, lanes] = jnp.concatenate([upper, lower], axis=0) * slope[:, lanes]
        return shared

    queue = [("qkv", i) for i in range(pieces)]
    start_piece(0)
    advance("down")
    advance(0)
    start_piece(1)
    advance(1)
    advance(0)
    advance("down")
    start_piece(2)
    advance(2)
    advance(queue[0])
    for k in range(3, pieces):
        start_piece(k)
    spread = gather_small()
    advance(1)
    advance(0)
    advance(queue[1])
    advance(queue[0])
    advance(2)
    advance(1)
    advance(queue[2])
    shared = share_small()
    advance(queue[1])
    advance(2)
    advance(queue[0])
    advance(queue[2])
    finish_all("down")
    finish_all(0)
    finish_all(1)
    advance(queue[1])
    finish_all(2)
    finish_all(queue[0])

    advance(queue[2])
    for k in queue[1:]:
        finish_all(k)
    for copy in shared:
        copy.wait()
    last.append(local(r.small_all, r.small_out, r.out_sems.at[len(rooms)]))
    for i, (k, copies) in enumerate(closing.items()):
        for copy in copies:
            copy.wait()
        start, size = (0, width) if k == "down" else (base_one + k * chunk, chunk) if k in range(chunks) else (0, 0)
        if k == queue[-1]:
            start, size = base_one + chunks * chunk, 6 * cols
        if size:
            region = slice(start, start + size)
            last.append(local(r.totals.at[:, :, region], r.totals_out.at[:, :, region], r.out_sems.at[i]))
    for copy in last:
        copy.wait()


def layer(plan, sizes, batch, operands, collective_id):
    heads, chunk, chunk_two, block = sizes
    n, g, f, cols, width = plan.count, plan.groups, plan.frames, plan.cols, plan.width
    hidden = operands["w_up_hbm"].shape[1]
    tokens, rows, layers, units = 2 * f, width // n, hidden // width, cols // LANES
    wide = f * (LANES // (width // heads))
    chunks, pieces = (width + hidden) // 2 // chunk, 3 * cols // chunk_two
    small_rows = -(-(21 + layers) // n) * n
    per, tile = small_rows // n, (width // LANES, LANES)
    vmem, smem = pl.BlockSpec(memory_space=pltpu.VMEM), pl.BlockSpec(memory_space=pltpu.SMEM)

    def sems(*shape):
        return pltpu.SemaphoreType.DMA(shape)

    def low(*shape):
        return pltpu.VMEM(shape, BF16)

    def high(*shape):
        return pltpu.VMEM(shape, F32)

    outs = dict(
        output=((2, f, width), F32),
        grad_inputs=((2, f, width), F32),
        grad_time=((2, width), F32),
        totals_out=((2, rows, 4 * width), BF16),
        small_out=((batch, small_rows) + tile, F32),
    )
    scratch = dict(
        totals=low(2, rows, 4 * width),
        small_all=high(batch, small_rows, *tile),
        out_sems=sems(chunks + 2 + 3 * cols // chunk_two),
        x=low(2, f, width),
        ct=low(2, f, width),
        w_mod=low(2, width, width // 2),
        w_out=low(width, width),
        w_up=low(width, hidden),
        w_down=low(hidden, width),
        acts=low(2, width),
        cos=high(f, LANES),
        sin=high(f, LANES),
        b_row=high(1, 3 * width),
        mods=high(2, 6 * width),
        rows=low(g, tokens, 3 * cols),
        both_hidden=low(width, 4 * tokens),
        attn=low(tokens, width),
        q_buf=low(g, tokens, cols),
        kv_buf=low(n, f, 2 * cols),
        short_buf=low(plan.short_blocks, plan.short_rows, 2 * cols),
        lse=high(g, 2 * units, wide),
        o_buf=low(g, tokens, cols),
        turned=low(cols, plan.total),
        short_turned=low(cols, plan.short),
        top_acc=high(g * units, 1, wide),
        total_acc=high(g * units, 1, wide),
        o_acc=high(g * units, LANES, wide),
        mixed=high(tokens, width),
        branch_a=high(tokens, width),
        hidden_f=low(tokens, width),
        grad_ff=low(tokens, width),
        grad_pre=low(tokens, hidden),
        grad_br=low(tokens, width),
        attn_t=low(width, 2 * tokens),
        hid_t=low(width, 2 * tokens),
        act_own=low(n, rows, 4 * tokens),
        act_send=low(n, rows, tokens),
        all_ff=low(4, tokens, width // 2),
        both_pre=low(2, tokens, hidden // 2),
        both_br=low(2, tokens, width // 2),
        branch_f=high(tokens, width),
        grad_hid=high(tokens, width),
        grad_mixed=high(tokens, width),
        stats=high(10 + layers, width),
        parts=low(n, rows, chunks * chunk),
        x_buf=low(chunks, n, rows, chunk // 2),
        down_sum=low(n, rows, width // 2),
        grads=low(tokens, width),
        g_buf=low(g, tokens, cols),
        dq_acc=high(g, f, cols),
        dlong=high(2, plan.largest, cols),
        dsmall=high(2, plan.short, cols),
        dq_out=low(tokens, width),
        dkv_out=low(2, plan.splits, f, width),
        dshort_out=low(2, plan.short_rows, width),
        dshort_part=low(plan.short_blocks, plan.splits - 1, 2, plan.short_rows, cols),
        dshort_buf=low(plan.short_blocks, 2, plan.short_rows, cols),
        grad_qkv=low(tokens, 3 * width),
        qkv_sum=low(pieces, n, rows, chunk_two),
        small=high(small_rows, *tile),
        small_in=high(n - 1, per, *tile),
        mine=high(per, *tile),
        in_sems=sems(5),
        m_sems=sems(4),
        q_sems=sems(2, g - 1),
        k_sems=sems(2, n - 1),
        s_sems=sems(2, plan.short_blocks, g + plan.splits - 2),
        o_sems=sems(2, g - 1),
        h_sems=sems(2, 3),
        e_sems=sems(2, 5),
        ff_sems=sems(2, 2),
        act_sems=sems(2, 3, hidden // block),
        bg_sems=sems(2, g - 1),
        bq_sems=sems(2, g - 1),
        bk_sems=sems(2, 2, units, n),
        bs_sems=sems(2, g - 1),
        bp_sems=sems(2, plan.short_blocks, plan.splits - 1),
        x_sems=sems(2, chunks),
        blk_sems=sems(2, chunks + 1 + pieces, n.bit_length() - 1),
        g_sems=sems(2, 3, pieces),
        ax_sems=sems(2, chunks + 1 + pieces),
        ac_sems=sems(2, 2 * (chunks + 1 + pieces)),
        small_one=sems(2, n - 1),
        small_two=sems(2, n - 1),
        small_three=sems(2, batch - 1),
    )
    for t in range(n.bit_length() - 1):
        scratch["came_one_%d" % t] = low(chunks, n >> (t + 1), rows, chunk // 2)
        scratch["came_down_%d" % t] = low(n >> (t + 1), rows, width // 2)
        scratch["came_qkv_%d" % t] = low(pieces, n >> (t + 1), rows, chunk_two)
    specs = [smem if k == "lengths" else in_hbm() if k.endswith("_hbm") else vmem for k in operands]
    names = tuple(operands) + tuple(outs) + tuple(scratch)
    return pl.pallas_call(
        partial(layer_kernel, plan, (heads, chunk, chunk_two, block, batch), names),
        in_specs=specs,
        out_specs=[vmem if k == "grad_time" else in_hbm() for k in outs],
        out_shape=[jax.ShapeDtypeStruct(*shape) for shape in outs.values()],
        scratch_shapes=list(scratch.values()),
        compiler_params=pltpu.CompilerParams(
            collective_id=collective_id, has_side_effects=True, vmem_limit_bytes=63 * MIB
        ),
        name="layer",
    )(*operands.values())


def finish_kernel(count, sizes, aligned, names, *refs):
    r = SimpleNamespace(**dict(zip(names, refs)))
    batch, width, layers = sizes
    rows = width // count
    me = lax.axis_index("blk")
    half = width // 2
    passed = [
        local(r.totals_hbm, r.totals, r.sems.at[0]),
        local(r.small_hbm, r.small, r.sems.at[1]),
        local(r.output_hbm, r.output_made, r.sems.at[2]),
        local(r.grad_inputs_hbm, r.grad_inputs_made, r.sems.at[3]),
        local(r.grad_time_hbm, r.grad_time_made, r.sems.at[4]),
    ]
    passed[0].wait()
    for core in range(2):
        for i in range(layers):
            made = r.totals[core, :, i * half : (i + 1) * half].astype(F32)
            r.down_made[i * rows : (i + 1) * rows, core * half : (core + 1) * half] = made
    passed.append(local(r.down_made, r.down, r.sems.at[5]))
    for core in range(2):
        start = layers * half
        made = r.totals[core, :, start : start + layers * half].astype(F32)
        r.up_made[:, core * layers * half : (core + 1) * layers * half] = made
    passed.append(local(r.up_made, r.up, r.sems.at[6]))
    for i, k in enumerate(("output", "grad_inputs", "grad_time")):
        passed[2 + i].wait()
        passed[2 + i] = local(getattr(r, k + "_made"), getattr(r, k), r.sems.at[2 + i])
    for core in range(2):
        start = 2 * layers * half
        r.out_made[:, core * half : (core + 1) * half] = r.totals[core, :, start : start + half].astype(F32)
        made = r.totals[core, :, start + half : start + 4 * half].astype(F32)
        r.qkv_made[:, core * 3 * half : (core + 1) * 3 * half] = made
    passed.append(local(r.out_made, r.out, r.sems.at[7]))
    passed.append(local(r.qkv_made, r.qkv, r.sems.at[8]))
    passed[1].wait()
    for u in range(2 * batch):
        b, s = u // 2, u % 2
        line = r.small[b, 15 + 2 + layers + s, pl.ds(me * rows // LANES, 1)]
        if rows < LANES:
            line = pltpu.roll(line, LANES - lax.rem(me, LANES // rows) * rows, 1)
        r.times[u : u + 1] = line
        for p in range(6):
            for c in range(width // LANES):
                start = p * width + c * LANES
                r.mods[u : u + 1, start : start + LANES] = r.small[b, 2 * p + s, c : c + 1]
    times, mods = r.times[:, :rows].astype(BF16), r.mods[...].astype(BF16)
    for i in range(2):
        span = slice(i * 3 * width, (i + 1) * 3 * width)
        r.w_mod_made[:, span] = dot_frames(times, mods[:, span])
        passed.append(local(r.w_mod_made.at[:, span], r.w_mod.at[:, span], r.sems.at[9 + i]))
    if aligned:
        tiles = width // LANES

        def own_lines(first, length, stride):
            lines = []
            for i in range(length // count // LANES):
                at = me * (length // count // LANES) + i
                total = jnp.zeros((1, LANES), F32)
                for b in range(batch):
                    for s in range(stride):
                        total = total + r.small[b, first + at // tiles * stride + s, pl.ds(lax.rem(at, tiles), 1)]
                lines.append(total)
            return lines

        firsts = [(0, 6, 2), (12, 3, 1), (15, 1, 1), (16, layers, 1), (16 + layers, 1, 1)]
        for which, (first, many, stride) in enumerate(firsts):
            ref = getattr(r, "vector%d" % which)
            for i, line in enumerate(own_lines(first, many * width, stride)):
                ref[i * LANES : (i + 1) * LANES] = line[0]
    for copy in passed[2:]:
        copy.wait()


def finish(count, output, grad_inputs, grad_time, totals, small, layers):
    batch, width = small.shape[0], output.shape[2]
    rows = width // count
    aligned = rows % LANES == 0
    operands = dict(
        output_hbm=output, grad_inputs_hbm=grad_inputs, grad_time_hbm=grad_time, totals_hbm=totals, small_hbm=small
    )
    shapes = dict(
        down=(layers * rows, width),
        up=(rows, layers * width),
        out=(rows, width),
        qkv=(rows, 3 * width),
        w_mod=(rows, 6 * width),
    )
    outs = dict(output=output.shape, grad_inputs=output.shape, grad_time=grad_time.shape, **shapes)
    vectors = {}
    if aligned:
        vectors = {"vector%d" % i: (many * rows,) for i, many in enumerate((6, 3, 1, layers, 1))}
    scratch = {k + "_made": pltpu.VMEM(v, F32) for k, v in outs.items()}
    scratch.update(
        totals=pltpu.VMEM(totals.shape, BF16),
        small=pltpu.VMEM(small.shape, F32),
        times=pltpu.VMEM((2 * batch, LANES), F32),
        mods=pltpu.VMEM((2 * batch, 6 * width), F32),
        sems=pltpu.SemaphoreType.DMA((11,)),
    )
    names = tuple(operands) + tuple(outs) + tuple(vectors) + tuple(scratch)
    made = pl.pallas_call(
        partial(finish_kernel, count, (batch, width, layers), aligned, names),
        in_specs=[in_hbm()] * len(operands),
        out_specs=[in_hbm()] * len(outs) + [pl.BlockSpec(memory_space=pltpu.VMEM)] * len(vectors),
        out_shape=[jax.ShapeDtypeStruct(v, F32) for v in (outs | vectors).values()],
        scratch_shapes=list(scratch.values()),
        compiler_params=pltpu.CompilerParams(vmem_limit_bytes=62 * MIB),
        name="finish",
    )(*operands.values())
    if not aligned:
        me = lax.axis_index("blk")
        flat = jnp.sum(small.reshape(batch, -1, width), axis=0)
        mods = flat[:12].reshape(6, 2, width).sum(axis=1)
        ends = [12, 15, 16, 16 + layers, 17 + layers]
        rest = [mods] + [flat[lo:hi] for lo, hi in zip(ends[:-1], ends[1:])]
        made = list(made) + [
            lax.dynamic_index_in_dim(v.reshape(count, -1), me, 0, keepdims=False) for v in rest
        ]
    return made


def on_device(
    inputs,
    time_embed,
    lengths,
    cotangent,
    w_mod,
    b_mod,
    w_qkv,
    b_qkv,
    w_out,
    b_out,
    w_up,
    b_up,
    w_down,
    b_down,
):
    _, frames, width = inputs.shape
    count, batch = lax.axis_size("blk"), lax.axis_size("batch")
    plan = Plan(count, frames, width)
    operands = dict(
        lengths=lengths,
        time_embed=time_embed,
        b_mod=b_mod,
        b_qkv=b_qkv,
        b_out=b_out,
        b_up=b_up,
        b_down=b_down,
        x_hbm=inputs,
        ct_hbm=cotangent,
        w_mod_hbm=w_mod,
        w_qkv_hbm=w_qkv,
        w_out_hbm=w_out,
        w_up_hbm=w_up,
        w_down_hbm=w_down,
    )
    made = layer(plan, (HEADS, 512, 256, 512), batch, operands, 0)
    output, grad_inputs, grad_time, down, up, out, qkv, grad_w_mod, *vectors = finish(
        count, *made, w_up.shape[1] // width
    )
    return (
        output,
        grad_inputs,
        grad_time,
        grad_w_mod,
        vectors[0],
        qkv,
        vectors[1],
        out,
        vectors[2],
        up,
        vectors[3],
        down,
        vectors[4],
    )


def solution(mesh):
    frame_spec, weight_spec = P("batch", "blk", None), P("blk", None)
    return jax.shard_map(
        on_device,
        mesh=mesh,
        in_specs=(frame_spec, P("batch", None), P("batch"), frame_spec) + (P(),) * 10,
        out_specs=(frame_spec, frame_spec, P("batch", None)) + (weight_spec, P("blk")) * 5,
        check_vma=False,
    )
```

```python
from functools import partial
from types import SimpleNamespace

import jax
import jax.numpy as jnp
from jax import lax
from jax.experimental import pallas as pl
from jax.experimental.pallas import tpu as pltpu
from jax.sharding import PartitionSpec as P

HEADS = 16
EPS = 1e-06
LANES = 128
SHORT = 16
MESH = pl.DeviceIdType.MESH
BF16 = jnp.bfloat16
F32 = jnp.float32
MIB = 1 << 20


def dot(left, right):
    return jnp.dot(left, right, preferred_element_type=F32)


def dot_rows(left, right):
    return lax.dot_general(left, right, (((1,), (1,)), ((), ())), preferred_element_type=F32)


def dot_frames(left, right):
    return lax.dot_general(left, right, (((0,), (0,)), ((), ())), preferred_element_type=F32)


def normalize(rows):
    mean = jnp.mean(rows, axis=-1, keepdims=True)
    centered = rows - mean
    inverse = lax.rsqrt(jnp.mean(centered * centered, axis=-1, keepdims=True) + EPS)
    return (centered * inverse, inverse)


def norm_back(normed, inverse, grad):
    return inverse * (
        grad
        - jnp.mean(grad, axis=-1, keepdims=True)
        - normed * jnp.mean(grad * normed, axis=-1, keepdims=True)
    )


def whole(shape):
    return pl.BlockSpec(shape, lambda *_: (0,) * len(shape))


def in_hbm():
    return pl.BlockSpec(memory_space=pltpu.HBM)


def rotate(rows, cos_table, sin_table, half):
    lane = lax.broadcasted_iota(jnp.int32, rows.shape, 1)
    partner = jnp.where(
        lax.rem(lane, 2 * half) < half,
        pltpu.roll(rows, LANES - half, 1),
        pltpu.roll(rows, half, 1),
    )
    return rows * cos_table + partner * sin_table


class Spot:
    def __init__(self, count):
        b, j = lax.axis_index("batch"), lax.axis_index("blk")
        self.b, self.j = b, j
        self.core, self.half = lax.rem(b, 2), b // 2
        self.near, self.far = lax.rem(j, 2), j // 2
        self.far_count = count // 2
        self.at_core = (self.half * 2 + 1 - self.core, j)
        self.at_x = ((1 - self.half) * 2 + self.core, j)
        self.at_both = ((1 - self.half) * 2 + 1 - self.core, j)
        self.at_near = (b, self.far * 2 + 1 - self.near)
        self.far_steps = [lax.rem(self.far + step, self.far_count) for step in range(1, self.far_count)]
        self.at_far = [(b, step * 2 + self.near) for step in self.far_steps]


def add_into(target, other):
    target[...] = (target[...].astype(F32) + other.astype(F32)).astype(BF16)


class Plan:
    def __init__(self, count, frames, width):
        self.count = count
        self.frames = frames
        self.width = width
        self.groups = min(max(count // 2, 1), 4)
        self.cols = width // self.groups
        self.splits = count // self.groups
        self.total = count * frames
        self.short = self.total // SHORT
        self.short_rows = min(self.short, frames)
        self.short_blocks = -(-self.short // frames)
        self.phases = [(lo, min(lo + 4 * self.groups, count)) for lo in range(self.groups, count, 4 * self.groups)]
        self.phases = [(0, self.groups)] + self.phases
        self.largest = max(hi - lo for lo, hi in self.phases) * frames
        self.offsets = [(d, s) for d in range(self.splits) for s in range(self.groups) if d + s > 0]

    def peer(self, device, offset):
        split = lax.rem(device // self.groups + offset[0], self.splits)
        return split * self.groups + lax.rem(lax.rem(device, self.groups) + offset[1], self.groups)


def push(src, dst, sems, index, device):
    copy = pltpu.make_async_remote_copy(
        src_ref=src, dst_ref=dst, send_sem=sems.at[(0,) + index], recv_sem=sems.at[(1,) + index],
        device_id=device, device_id_type=MESH,
    )
    copy.start()
    return copy


def local(src, dst, sem):
    copy = pltpu.make_async_copy(src, dst, sem)
    copy.start()
    return copy


def stacked(rows, head_dim):
    lane = lax.broadcasted_iota(jnp.int32, rows.shape, 1)
    heads = LANES // head_dim
    return jnp.concatenate(
        [jnp.where(lane // head_dim == h, rows, jnp.zeros_like(rows)) for h in range(heads)], axis=0
    )


def unstacked(turned, frames, head_dim):
    heads = LANES // head_dim
    return jnp.concatenate(
        [
            turned[h * head_dim : (h + 1) * head_dim, h * frames : (h + 1) * frames]
            for h in range(heads)
        ],
        axis=0,
    ).T


def attend_part(queries, keys, values_t, head_dim):
    scores = dot_rows(keys, stacked(queries, head_dim))
    top = jnp.max(scores, axis=0, keepdims=True)
    weights = jnp.exp(scores - top)
    total = jnp.sum(weights, axis=0, keepdims=True)
    return top, total, dot(values_t, weights.astype(BF16))


def attend_join(one, two):
    top = jnp.maximum(one[0], two[0])
    left, right = jnp.exp(one[0] - top), jnp.exp(two[0] - top)
    return top, one[1] * left + two[1] * right, one[2] * left + two[2] * right


def attend_end(state, frames, head_dim):
    top, total, out = state
    return unstacked(out / total, frames, head_dim).astype(BF16), top + jnp.log(total)


def delta_rows(grads, outs, head_dim):
    heads = LANES // head_dim
    lane = lax.broadcasted_iota(jnp.int32, (8, LANES), 1)
    pick = (lane // head_dim == lax.broadcasted_iota(jnp.int32, (8, LANES), 0)).astype(F32)
    product = grads.astype(F32) * outs.astype(F32)
    sums = lax.dot_general(
        pick, product, (((1,), (1,)), ((), ())), precision=lax.Precision.HIGHEST, preferred_element_type=F32
    )
    return jnp.concatenate([sums[h : h + 1] for h in range(heads)], axis=1)


def attend_back(queries, grads, lse, delta, keys, keys_t, values, head_dim):
    frames = queries.shape[0]
    q_heads, g_heads = stacked(queries, head_dim), stacked(grads, head_dim)
    probs = jnp.exp(dot_rows(keys, q_heads) - lse)
    grad_probs = dot_rows(values, g_heads)
    grad_scores = (probs * (grad_probs - delta)).astype(BF16)
    grad_values = dot(probs.astype(BF16), g_heads)
    grad_keys = dot(grad_scores, q_heads)
    grad_queries = unstacked(dot(keys_t, grad_scores), frames, head_dim) * head_dim ** (-0.5)
    return grad_queries, grad_keys, grad_values


def gelu_both(z):
    scale = (2.0 / 3.141592653589793) ** 0.5
    square = z * z
    inner = jnp.tanh(scale * z * (1.0 + 0.044715 * square))
    half = 0.5 * (1.0 + inner)
    slope = half + 0.5 * z * (1.0 - inner * inner) * (scale * (1.0 + 3.0 * 0.044715 * square))
    return z * half, slope


def layer_kernel(plan, sizes, names, *refs):
    r = SimpleNamespace(**dict(zip(names, refs)))
    r.came_at = lambda kind, t: getattr(r, "came_%s_%d" % (kind, t))
    heads, chunk, chunk_two, block, batch = sizes
    n, g, f, cols, width = plan.count, plan.groups, plan.frames, plan.cols, plan.width
    tokens, hidden = 2 * f, r.w_up.shape[1]
    head_dim, half_dim = width // heads, width // heads // 2
    half_width, half_hidden = width // 2, hidden // 2
    layers, n_rows, units = hidden // width, width // n, cols // LANES
    spot = Spot(n)
    b, me, core, half = spot.b, spot.j, spot.core, spot.half
    group, split = lax.rem(me, g), me // g
    others = [plan.peer(me, offset) for offset in plan.offsets]
    mates = others[: g - 1]
    along = [(b, peer) for peer in others]
    across = [(lax.rem(b + step, batch), me) for step in range(1, batch)]
    seqs = [slice(0, f), slice(f, tokens)]
    mine, theirs = slice(0, tokens), slice(tokens, 2 * tokens)
    swapped = r.lengths[0] < r.lengths[1]
    first = jnp.where(swapped, 1, 0)
    order = [first, 1 - first]

    barrier = pltpu.get_barrier_semaphore()
    for device in along + across:
        pl.semaphore_signal(barrier, inc=1, device_id=device, device_id_type=MESH)

    load_x = local(r.x_hbm, r.x, r.in_sems.at[0])
    mod_places, mod_copies = [r.w_mod.at[0], r.w_mod.at[1]], {}
    room = r.parts.reshape(width, r.parts.shape[2])
    mod_places += [room.at[:, :half_width], room.at[:, half_width:width]]
    ahead = len(mod_places)

    def mod_place(i):
        return i if i < ahead else i % 2

    def load_mod(i, place):
        return local(r.w_mod_hbm.at[:, i * half_width : (i + 1) * half_width], mod_places[place], r.m_sems.at[place])

    def next_mod(i):
        if mod_place(i) < 2:
            after = i + ahead if i < 2 else i + 2
            if after < 12:
                mod_copies[after] = load_mod(after, mod_place(after))

    def load_qkv():
        return [
            local(r.w_qkv_hbm.at[:, : 2 * width], r.w_up.at[:, : 2 * width], r.in_sems.at[1]),
            local(r.w_qkv_hbm.at[:, 2 * width :], r.w_out, r.in_sems.at[2]),
        ]

    for i in range(ahead):
        mod_copies[i] = load_mod(i, i)
    qkv_copies = load_qkv()

    shown = r.time_embed[...].astype(F32)
    shown = jnp.where(swapped, jnp.concatenate([shown[1:2], shown[0:1]], axis=0), shown)
    r.acts[...] = (shown / (1.0 + jnp.exp(-shown))).astype(BF16)
    frame = me * f + lax.broadcasted_iota(jnp.int32, (f, LANES), 0)
    lane = lax.broadcasted_iota(jnp.int32, (f, LANES), 1)
    exponent = lax.rem(lane, half_dim).astype(F32) * (-1.0 / half_dim)
    angle = frame.astype(F32) * jnp.exp(exponent * 9.210340371976184)
    sines = jnp.sin(angle)
    r.cos[...] = jnp.cos(angle)
    r.sin[...] = jnp.where(lax.rem(lane, 2 * half_dim) < half_dim, -sines, sines)
    r.b_row[...] = r.b_qkv[...][None].astype(F32)

    def mod_piece(i, place):
        piece = slice(i * half_width, (i + 1) * half_width)
        r.mods[:, piece] = dot(r.acts[...], mod_places[place][...]) + r.b_mod[piece][None].astype(F32)

    def mod(i, s):
        return r.mods[s : s + 1, i * width : (i + 1) * width]

    for i in range(4):
        mod_copies[i].wait()
        mod_piece(i, mod_place(i))
        next_mod(i)

    load_x.wait()
    for s, span in enumerate(seqs):
        normed, _ = normalize(r.x[order[s]].astype(F32))
        r.hidden_f[span] = (normed * (1.0 + mod(1, s)) + mod(0, s)).astype(BF16)
    for copy in qkv_copies:
        copy.wait()
    load_ct = local(r.ct_hbm, r.ct, r.in_sems.at[3])
    load_down = local(r.w_down_hbm, r.w_down, r.in_sems.at[4])
    pl.semaphore_wait(barrier, len(along + across))

    def project(kind, which):
        at = pl.ds(pl.multiple_of(which * cols, LANES), cols)
        bias_at = pl.ds(pl.multiple_of(kind * width + which * cols, LANES), cols)
        weight = r.w_out[:, at] if kind == 2 else r.w_up[:, bias_at]
        made = dot(r.hidden_f[...], weight) + r.b_row[:, bias_at]
        if kind < 2:
            factor = (2.0 * half_dim) ** (-0.5) if kind == 0 else 1.0
            cosines, sines = r.cos[...] * factor, r.sin[...] * factor
        for span in seqs:
            for u in range(units):
                part = made[span, u * LANES : (u + 1) * LANES]
                if kind < 2:
                    part = rotate(part, cosines, sines, half_dim)
                start = kind * cols + u * LANES
                r.rows[which, span, start : start + LANES] = part.astype(BF16)

    near_waits = []

    def send_keys(step):
        offset = plan.offsets[step]
        src = r.rows.at[lax.rem(others[step], g), 0:f, cols : 3 * cols]
        dst = r.kv_buf.at[offset[0] * g + group]
        return push(src, dst, r.k_sems, (step,), along[step])

    def short_rows_of(peer):
        return r.rows.at[lax.rem(peer, g), f : f + plan.short_rows, cols : 3 * cols]

    def pass_on(blk):
        for d in range(1, plan.splits):
            place = r.short_buf.at[blk]
            push(place, place, r.s_sems, (blk, g - 2 + d), along[d * g - 1])

    inner = jnp.logical_or(lax.rem(spot.far, 4) == 1, lax.rem(spot.far, 4) == 2)
    for step in range(1, g + 1):
        which = lax.rem(group + step, g)
        project(1, which)
        project(2, which)

        @pl.when(inner)
        def _():
            for d in range(1, plan.splits):
                send_keys(d * g + step % g - 1)

        if step < g:
            near_waits.append(send_keys(step - 1))
    for step in range(1, g + 1):
        which = lax.rem(group + step, g)
        project(0, which)
        if step < g:
            src = r.rows.at[which, :, 0:cols]
            near_waits.append(push(src, r.q_buf.at[group], r.q_sems, (step - 1,), along[step - 1]))

    for blk in range(plan.short_blocks):

        @pl.when(me == blk)
        def _():
            for step, peer in enumerate(mates):
                push(short_rows_of(peer), r.short_buf.at[blk], r.s_sems, (blk, step), along[step])
            r.short_buf[blk] = r.rows[group, f : f + plan.short_rows, cols : 3 * cols]
            pass_on(blk)

    @pl.when(jnp.logical_not(inner))
    def _():
        for step in range(g - 1, n - 1):
            send_keys(step)

    def lot(i):
        return slice(i * tokens, (i + 1) * tokens)

    around = [spot.at_core, spot.at_x, spot.at_both]
    r.both_hidden[:, lot(0)] = r.hidden_f[...].T
    swap_hidden = [
        push(r.both_hidden.at[:, lot(0)], r.both_hidden.at[:, lot(i + 1)], r.h_sems, (i,), device)
        for i, device in enumerate(around)
    ]
    load_out = local(r.w_out_hbm, r.w_out, r.in_sems.at[2])
    load_up = local(r.w_up_hbm, r.w_up, r.in_sems.at[1])
    r.kv_buf[group] = r.rows[group, 0:f, cols : 3 * cols]
    r.q_buf[group] = r.rows[group, :, 0:cols]

    for i in range(4, 12):
        mod_copies[i].wait()
        mod_piece(i, mod_place(i))
        next_mod(i)

    load_ct.wait()
    for s, span in enumerate(seqs):
        r.grad_ff[span] = (mod(5, s) * r.ct[order[s]].astype(F32)).astype(BF16)

    def core_half(which, size):
        return pl.ds(pl.multiple_of(which * size, LANES), size)

    def to_core(src, dst, index):
        return push(src, dst, r.e_sems, (index,), spot.at_core)

    ff_own, ff_other = core_half(core, half_width), core_half(1 - core, half_width)
    swap_ff = [
        to_core(r.grad_ff.at[:, ff_other], r.all_ff.at[1], 0),
        push(r.grad_ff.at[:, ff_own], r.all_ff.at[2], r.ff_sems, (0,), spot.at_x),
        push(r.grad_ff.at[:, ff_other], r.all_ff.at[3], r.ff_sems, (1,), spot.at_both),
    ]
    r.all_ff[0] = r.grad_ff[:, ff_own]

    for copy in near_waits:
        copy.wait()
    for blk in range(plan.short_blocks):
        for step in range(g - 1):

            @pl.when(me == plan.peer(blk, plan.offsets[step]))
            def _():
                dst = r.short_buf.at[blk]
                pltpu.make_async_copy(dst, dst, r.s_sems.at[1, blk, step]).wait()
                pass_on(blk)

    def turn_values(lo, hi, start):
        part = r.kv_buf[lo:hi, :, start : start + cols].reshape((hi - lo) * f, cols)
        r.turned[:, lo * f : hi * f] = part.T

    def cols_of(which):
        return pl.ds(pl.multiple_of(which * cols, LANES), cols)

    def slot_of(step):
        return lax.rem(group + 1 + step, g)

    units = cols // LANES
    sends = []
    for phase, (lo, hi) in enumerate(plan.phases):
        last = phase == len(plan.phases) - 1
        if phase == 1:
            for step in range(g - 1, n - 1):
                src = r.rows.at[group, 0:f, cols : 3 * cols]
                pltpu.make_async_copy(src, src, r.k_sems.at[0, step]).wait()
                dst = r.kv_buf.at[plan.offsets[step][0] * g + lax.rem(group + g - plan.offsets[step][1], g)]
                pltpu.make_async_copy(dst, dst, r.k_sems.at[1, step]).wait()
        turn_values(lo, hi, cols)
        for step in range(g):
            slot = slot_of(step)
            for u in range(units):
                lanes = slice(u * LANES, (u + 1) * LANES)
                at = step * units + u
                state = attend_part(
                    r.q_buf[slot, :f, lanes],
                    r.kv_buf[lo:hi, :, lanes].reshape((hi - lo) * f, LANES),
                    r.turned[lanes, lo * f : hi * f],
                    head_dim,
                )
                if phase > 0:
                    state = attend_join((r.top_acc[at], r.total_acc[at], r.o_acc[at]), state)
                if last:
                    r.o_buf[slot, :f, lanes], r.lse[slot, u : u + 1] = attend_end(state, f, head_dim)
                else:
                    r.top_acc[at], r.total_acc[at], r.o_acc[at] = state
            if last and step == 0:
                for blk in range(plan.short_blocks):
                    for d in range(1, plan.splits):

                        @pl.when(split == (blk // g + d) % plan.splits)
                        def _():
                            dst = r.short_buf.at[blk]
                            pltpu.make_async_copy(dst, dst, r.s_sems.at[1, blk, g - 2 + d]).wait()

                r.short_turned[...] = r.short_buf[:, :, cols:].reshape(plan.short, cols).T
            if last:
                for u in range(units):
                    lanes = slice(u * LANES, (u + 1) * LANES)
                    keys = r.short_buf[:, :, lanes].reshape(plan.short, LANES)
                    state = attend_part(r.q_buf[slot, f:, lanes], keys, r.short_turned[lanes], head_dim)
                    row = units + u
                    r.o_buf[slot, f:, lanes], r.lse[slot, row : row + 1] = attend_end(state, f, head_dim)
                if step == g - 1:
                    r.attn[:, cols_of(group)] = r.o_buf[slot]
                else:
                    dst = r.attn.at[:, cols_of(group)]
                    sends.append(push(r.o_buf.at[slot], dst, r.o_sems, (step,), along[step]))
    for lo, hi in plan.phases:
        turn_values(lo, hi, 0)
    r.short_turned[...] = r.short_buf[:, :, :cols].reshape(plan.short, cols).T
    for copy in sends:
        copy.wait()
    for blk in range(plan.short_blocks):

        @pl.when(me == blk)
        def _():
            for step, peer in enumerate(mates):
                src = short_rows_of(peer)
                pltpu.make_async_copy(src, src, r.s_sems.at[0, blk, step]).wait()

        @pl.when(split == blk // g)
        def _():
            for d in range(1, plan.splits):
                src = r.short_buf.at[blk]
                pltpu.make_async_copy(src, src, r.s_sems.at[0, blk, g - 2 + d]).wait()

    load_out.wait()
    r.attn_t[:, mine] = r.attn[...].T
    swap_attn = to_core(r.attn_t.at[:, mine], r.attn_t.at[:, theirs], 1)
    r.branch_a[...] = dot(r.attn[...], r.w_out[...]) + r.b_out[...][None].astype(F32)
    for s, span in enumerate(seqs):
        r.mixed[span] = r.x[order[s]].astype(F32) + mod(2, s) * r.branch_a[span]
        normed, _ = normalize(r.mixed[span])
        r.hidden_f[span] = (normed * (1.0 + mod(4, s)) + mod(3, s)).astype(BF16)
    r.hid_t[:, mine] = r.hidden_f[...].T
    swap_hid = to_core(r.hid_t.at[:, mine], r.hid_t.at[:, theirs], 2)
    load_up.wait()
    load_down.wait()
    swap_act, act_x = [], []
    per_block = block // (layers * n_rows)
    for i in range(hidden // block):
        span = slice(i * block, (i + 1) * block)
        act, slope = gelu_both(dot(r.hidden_f[...], r.w_up[:, span]) + r.b_up[span][None].astype(F32))
        act = act.astype(BF16)
        act_t = act.T.reshape(per_block, layers, n_rows, tokens)
        held = slice(i * per_block, (i + 1) * per_block)
        r.act_own[held, :, mine] = jnp.where(half == 0, act_t[:, 0], act_t[:, 1])
        r.act_send[held] = jnp.where(half == 0, act_t[:, 1], act_t[:, 0])
        act_x.append(
            push(r.act_send.at[held], r.act_own.at[held, :, 2 * tokens : 3 * tokens], r.act_sems, (0, i), spot.at_x)
        )
        swap_act.append(
            push(r.act_own.at[held, :, mine], r.act_own.at[held, :, theirs], r.act_sems, (1, i), spot.at_core)
        )
        forward = dot(act, r.w_down[span, :])
        grad = (dot_rows(r.grad_ff[...], r.w_down[span, :]) * slope).astype(BF16)
        r.grad_pre[:, span] = grad
        row, start = 9 + i * block // width, i * block % width
        r.stats[row : row + 1, start : start + block] = jnp.sum(grad.astype(F32), axis=0, keepdims=True)
        back = dot_rows(grad, r.w_up[:, span])
        if i == 0:
            r.branch_f[...] = forward + r.b_down[...][None].astype(F32)
            r.grad_hid[...] = back
        else:
            r.branch_f[...] += forward
            r.grad_hid[...] += back
    swap_pre = to_core(r.grad_pre.at[:, core_half(1 - core, half_hidden)], r.both_pre.at[1], 3)
    r.both_pre[0] = r.grad_pre[:, core_half(core, half_hidden)]

    chunks, half_chunk = r.parts.shape[2] // chunk, chunk // 2
    base_one = layers * half_width
    x_copies, stage_copies, stage_of, last, sent, closing = {}, {}, {}, [], {}, {}

    def half_of(k, which):
        return pl.ds(pl.multiple_of(k * chunk + which * half_chunk, LANES), half_chunk)

    stages = range(n.bit_length() - 1)
    pieces = 3 * cols // chunk_two
    rooms = {k: (r.x_buf.at[k], [r.came_at("one", t).at[k] for t in stages], k) for k in range(chunks)}
    rooms["down"] = (r.down_sum, [r.came_at("down", t) for t in stages], chunks)
    for i in range(pieces):
        rooms["qkv", i] = (r.qkv_sum.at[i], [r.came_at("qkv", t).at[i] for t in stages], chunks + 1 + i)

    def total_of(k, which):
        if k == "down":
            return core_half(which, half_width)
        if k in range(chunks):
            return pl.ds(pl.multiple_of(base_one + k * chunk + which * half_chunk, LANES), half_chunk)
        start = base_one + chunks * chunk + which * 3 * cols + k[1] * chunk_two
        return pl.ds(pl.multiple_of(start, LANES), chunk_two)

    def start_x(k):
        src = r.parts.at[:, :, half_of(k, 1 - half)]
        x_copies[k] = push(src, r.x_buf.at[k], r.x_sems, (k,), spot.at_x)

    bits = [lax.rem(me // (1 << t), 2) for t in stages]
    partners = [(b, me + (1 - 2 * bit) * (1 << t)) for t, bit in enumerate(bits)]

    def halves(k, t):
        held = rooms[k][0] if t == 0 else rooms[k][1][t - 1]
        return held.reshape(n >> (t + 1), 2, n_rows, held.shape[2])

    def start_stage(k, t):
        _, came, number = rooms[k]
        stage_of[k] = t
        stage_copies[k] = push(halves(k, t).at[:, 1 - bits[t]], came[t], r.blk_sems, (number, t), partners[t])

    def finish_x(k):
        x_copies[k].wait()
        add_into(r.x_buf.at[k], r.parts[:, :, half_of(k, half)])
        start_stage(k, 0)

    def advance(k):
        t = stage_of[k]
        _, came, number = rooms[k]
        stage_copies[k].wait()
        if t + 1 < len(stages):
            add_into(came[t], halves(k, t)[:, bits[t]])
            start_stage(k, t + 1)
        else:
            total = came[t][0].astype(F32) + halves(k, t)[0, bits[t]].astype(F32)
            r.totals[core, :, total_of(k, half)] = total.astype(BF16)
            sent[k] = to_all(total_of(k, half), number)
            if number > chunks:
                place = r.totals.at[core, :, total_of(k, half)]
                sent[k].append(push(place, place, r.ac_sems, (2 * number + 1,), spot.at_both))

    def to_all(where, which):
        place = r.totals.at[core, :, where]
        return [
            push(place, place, r.ax_sems, (which,), spot.at_x),
            push(place, place, r.ac_sems, (2 * which,), spot.at_core),
        ]

    def forward_to_core(where, which):
        place = r.totals.at[core, :, where]
        return push(place, place, r.ac_sems, (2 * which + 1,), spot.at_core)

    def finish_all(k):
        while k not in sent:
            advance(k)
        sent[k][0].wait()
        closing[k] = sent[k][1:]
        if len(closing[k]) == 1:
            closing[k].append(forward_to_core(total_of(k, 1 - half), rooms[k][2]))

    for s, span in enumerate(seqs):
        grad_out = r.ct[order[s]].astype(F32)
        branch, grad = r.branch_f[span], r.grad_hid[span]
        normed, inverse = normalize(r.mixed[span])
        r.stats[6 + s : 7 + s] = jnp.sum(grad_out * branch, axis=0, keepdims=True)
        r.stats[4 + s : 5 + s] = jnp.sum(grad * normed, axis=0, keepdims=True)
        r.stats[2 + s : 3 + s] = jnp.sum(grad, axis=0, keepdims=True)
        total = grad_out + norm_back(normed, inverse, grad * (1.0 + mod(4, s)))
        r.grad_mixed[span] = total
        r.stats[s : s + 1] = jnp.sum(total * r.branch_a[span], axis=0, keepdims=True)
        r.grad_br[span] = (mod(2, s) * total).astype(BF16)
    r.grads[...] = dot_rows(r.grad_br[...], r.w_out[...]).astype(BF16)
    waits = []
    for step, peer in enumerate(mates):
        src = r.grads.at[:, cols_of(lax.rem(peer, g))]
        waits.append(push(src, r.g_buf.at[group], r.bg_sems, (step,), along[step]))
    r.g_buf[group] = r.grads[:, cols_of(group)]
    swap_br = to_core(r.grad_br.at[:, core_half(1 - core, half_width)], r.both_br.at[1], 4)
    qkv_copies = load_qkv()

    for i, copy in enumerate(act_x):
        copy.wait()
        held = slice(i * per_block, (i + 1) * per_block)
        src = r.act_own.at[held, :, 2 * tokens : 3 * tokens]
        dst = r.act_own.at[held, :, 3 * tokens : 4 * tokens]
        swap_act.append(push(src, dst, r.act_sems, (2, i), spot.at_core))
    swap_hid.wait()
    swap_pre.wait()
    for i in range(layers):
        grad = r.both_pre[:, :, i * half_width : (i + 1) * half_width].reshape(2 * tokens, half_width)
        up = dot(r.hid_t[...], grad).astype(BF16).reshape(n, n_rows, half_width)
        r.parts[:, :, i * half_width : (i + 1) * half_width] = up
        start_x(i)
    for copy in swap_ff + swap_act:
        copy.wait()
    down = dot(r.act_own[...].reshape(width, 4 * tokens), r.all_ff[...].reshape(4 * tokens, half_width))
    r.down_sum[...] = down.astype(BF16).reshape(n, n_rows, half_width)
    start_stage("down", 0)
    for copy in waits:
        copy.wait()

    strips = {i: load_mod(i, i % 2) for i in (4, 5)}

    sends = []
    deltas = [
        [
            [
                delta_rows(r.g_buf[slot_of(step), span, lanes], r.o_buf[slot_of(step), span, lanes], head_dim)
                for lanes in [slice(u * LANES, (u + 1) * LANES) for u in range(units)]
            ]
            for span in seqs
        ]
        for step in range(g)
    ]
    dq_buf = r.o_buf
    def short_back():
        for step in range(g):
            slot = slot_of(step)
            for u in range(units):
                lanes = slice(u * LANES, (u + 1) * LANES)
                high = slice(cols + u * LANES, cols + (u + 1) * LANES)
                row = units + u
                dq, dk, dv = attend_back(
                    r.q_buf[slot, f:, lanes],
                    r.g_buf[slot, f:, lanes],
                    r.lse[slot, row : row + 1],
                    deltas[step][1][u],
                    r.short_buf[:, :, lanes].reshape(plan.short, LANES),
                    r.short_turned[lanes],
                    r.short_buf[:, :, high].reshape(plan.short, LANES),
                    head_dim,
                )
                dq_buf[slot, f:, lanes] = dq.astype(BF16)
                if step == 0:
                    r.dsmall[0, :, lanes] = dk
                    r.dsmall[1, :, lanes] = dv
                else:
                    r.dsmall[0, :, lanes] += dk
                    r.dsmall[1, :, lanes] += dv
        for blk in range(plan.short_blocks):
            span = slice(blk * plan.short_rows, (blk + 1) * plan.short_rows)
            r.dshort_buf[blk] = r.dsmall[:, span].astype(BF16)
            for d in range(1, plan.splits):
                home = blk // g

                @pl.when(split == (home + d) % plan.splits)
                def _():
                    device = (b, home * g + group)
                    push(r.dshort_buf.at[blk], r.dshort_part.at[blk, d - 1], r.bp_sems, (blk, d - 1), device)

    def short_home():
        for blk in range(plan.short_blocks):

            @pl.when(split == blk // g)
            def _():
                total = r.dshort_buf[blk].astype(F32)
                for d in range(1, plan.splits):
                    place = r.dshort_part.at[blk, d - 1]
                    pltpu.make_async_copy(place, place, r.bp_sems.at[1, blk, d - 1]).wait()
                    total = total + place[...].astype(F32)
                r.dshort_buf[blk] = total.astype(BF16)

            dst = r.dshort_out.at[:, :, cols_of(group)]
            for step, peer in enumerate(mates):

                @pl.when(peer == blk)
                def _():
                    push(r.dshort_buf.at[blk], dst, r.bs_sems, (step,), along[step])

            @pl.when(me == blk)
            def _():
                r.dshort_out[:, :, cols_of(group)] = r.dshort_buf[blk]

    def send_back(lo, hi, u):
        lanes = slice(u * LANES, (u + 1) * LANES)
        back = pl.ds(pl.multiple_of(group * cols + u * LANES, LANES), LANES)
        made = [slice(which * cols + u * LANES, which * cols + (u + 1) * LANES) for which in range(2)]
        for which in range(2):
            sums = r.dlong[which, : (hi - lo) * f, lanes]
            r.kv_buf[lo:hi, :, made[which]] = sums.astype(BF16).reshape(hi - lo, f, LANES)
        for d in range(lo // g, hi // g):
            for s in range(g):
                if d == 0 and s == 0:
                    continue
                other_group = lax.rem(group + s, g)
                peer = lax.rem(split + plan.splits - d, plan.splits) * g + other_group
                for which in range(2):
                    dst = r.dkv_out.at[which, split, :, back]
                    src = r.kv_buf.at[d * g + other_group, :, made[which]]
                    sends.append(push(src, dst, r.bk_sems, (which, u, d * g + s), (b, peer)))
        if lo == 0:
            for which in range(2):
                r.dkv_out[which, split, :, back] = r.kv_buf[group, :, made[which]]

    short_back()

    r.both_br[0] = r.grad_br[:, core_half(core, half_width)]
    swap_attn.wait()
    swap_br.wait()
    out_part = dot(r.attn_t[...], r.both_br[...].reshape(2 * tokens, half_width))
    r.parts[:, :, layers * half_width :] = out_part.astype(BF16).reshape(n, n_rows, half_width)
    start_x(layers)
    made = [r.mixed[span] + mod(5, s) * r.branch_f[span] for s, span in enumerate(seqs)]
    r.mixed[seqs[0]] = jnp.where(swapped, made[1], made[0])
    r.mixed[seqs[1]] = jnp.where(swapped, made[0], made[1])
    last.append(local(r.mixed.reshape(2, f, width), r.output, r.in_sems.at[0]))
    last_row = 9 + layers
    r.stats[8:9] = jnp.sum(r.grad_br[...].astype(F32), axis=0, keepdims=True)
    r.stats[last_row : last_row + 1] = jnp.sum(r.grad_ff[...].astype(F32), axis=0, keepdims=True)

    for phase, (lo, hi) in enumerate(plan.phases[1:] + plan.phases[:1]):
        size = (hi - lo) * f
        for u in range(units):
            lanes = slice(u * LANES, (u + 1) * LANES)
            high = slice(cols + u * LANES, cols + (u + 1) * LANES)
            for step in range(g):
                slot = slot_of(step)
                dq, dk, dv = attend_back(
                    r.q_buf[slot, :f, lanes],
                    r.g_buf[slot, :f, lanes],
                    r.lse[slot, u : u + 1],
                    deltas[step][0][u],
                    r.kv_buf[lo:hi, :, lanes].reshape(size, LANES),
                    r.turned[lanes, lo * f : hi * f],
                    r.kv_buf[lo:hi, :, high].reshape(size, LANES),
                    head_dim,
                )
                if step == 0:
                    r.dlong[0, :size, lanes] = dk
                    r.dlong[1, :size, lanes] = dv
                else:
                    r.dlong[0, :size, lanes] += dk
                    r.dlong[1, :size, lanes] += dv
                if phase > 0:
                    dq = r.dq_acc[step, :, lanes] + dq
                if lo > 0:
                    r.dq_acc[step, :, lanes] = dq
                    continue
                dq_buf[slot, :f, lanes] = dq.astype(BF16)
                if u < units - 1:
                    continue
                if step == g - 1:
                    r.dq_out[:, cols_of(group)] = dq_buf[slot]
                else:
                    dst = r.dq_out.at[:, cols_of(group)]
                    sends.append(push(dq_buf.at[slot], dst, r.bq_sems, (step,), along[step]))
            send_back(lo, hi, u)

    short_home()

    def add_strip(total, i, rows_of):
        strips[i].wait()
        at = slice(i % 2 * half_width, (i % 2 + 1) * half_width)
        total = total + dot_rows(rows_of[:, at].astype(BF16), r.w_mod[i % 2])
        after = {10: 0, 11: 1}.get(i, i + 2)
        if after not in strips and after not in (4, 5):
            strips[after] = load_mod(after, i % 2)
        return total

    grad_act = jnp.zeros((2, width), F32)
    for i in range(4, 12):
        grad_act = add_strip(grad_act, i, r.stats[i // 2 * 2 - 4 : i // 2 * 2 - 2])
    advance("down")
    finish_x(0)
    for copy in sends:
        copy.wait()
    for blk in range(plan.short_blocks):
        place = r.dshort_buf.at[blk]
        for d in range(1, plan.splits):

            @pl.when(split == (blk // g + d) % plan.splits)
            def _():
                pltpu.make_async_copy(place, place, r.bp_sems.at[0, blk, d - 1]).wait()

        for step, peer in enumerate(mates):

            @pl.when(peer == blk)
            def _():
                pltpu.make_async_copy(place, place, r.bs_sems.at[0, step]).wait()

        @pl.when(me == blk)
        def _():
            for step in range(g - 1):
                pltpu.make_async_copy(place, place, r.bs_sems.at[1, step]).wait()

    no_short = me >= plan.short_blocks
    grad_key = jnp.sum(r.dkv_out[0].astype(F32), axis=0)
    grad_value = jnp.sum(r.dkv_out[1].astype(F32), axis=0)
    short_key = jnp.where(no_short, 0.0, r.dshort_out[0].astype(F32))
    short_value = jnp.where(no_short, 0.0, r.dshort_out[1].astype(F32))
    cosines, sines = r.cos[...], -r.sin[...]
    for c in range(width // LANES):
        lanes = slice(c * LANES, (c + 1) * LANES)
        for span in seqs:
            made = rotate(r.dq_out[span, lanes].astype(F32), cosines, sines, half_dim)
            r.grad_qkv[span, lanes] = made.astype(BF16)
        lanes_k = slice(width + c * LANES, width + (c + 1) * LANES)
        made = rotate(grad_key[:, lanes], cosines, sines, half_dim)
        r.grad_qkv[:f, lanes_k] = made.astype(BF16)
        made = rotate(short_key[:, lanes], cosines[: plan.short_rows], sines[: plan.short_rows], half_dim)
        r.grad_qkv[f : f + plan.short_rows, lanes_k] = made.astype(BF16)
    r.grad_qkv[:f, 2 * width :] = grad_value.astype(BF16)
    r.grad_qkv[f : f + plan.short_rows, 2 * width :] = short_value.astype(BF16)
    if plan.short_rows < f:
        r.grad_qkv[f + plan.short_rows :, width:] = jnp.zeros((f - plan.short_rows, 2 * width), BF16)

    own_cols = 3 * cols
    pieces = own_cols // chunk_two

    def piece_of(chip, core_of, i):
        return pl.ds(pl.multiple_of((core_of * 2 + chip) * own_cols + i * chunk_two, LANES), chunk_two)

    quarters = [(half, 1 - core), (1 - half, core), (1 - half, 1 - core)]
    swaps = []
    for i in range(pieces):
        for slot, (chip, core_of) in enumerate(quarters):
            src = r.grad_qkv.at[:, piece_of(chip, core_of, i)]
            dst = r.rows.at[slot + 1, :, i * chunk_two : (i + 1) * chunk_two]
            swaps.append(push(src, dst, r.g_sems, (slot, i), around[slot]))
        r.rows[0, :, i * chunk_two : (i + 1) * chunk_two] = r.grad_qkv[:, piece_of(half, core, i)]
    for k in range(1, chunks):
        finish_x(k)

    for copy in qkv_copies:
        copy.wait()
    grad_hidden = dot_rows(r.grad_qkv[:, : 2 * width], r.w_up[:, : 2 * width]) + dot_rows(
        r.grad_qkv[:, 2 * width :], r.w_out[...]
    )
    shift_rows, scale_rows, made = [], [], []
    for s, span in enumerate(seqs):
        normed, inverse = normalize(r.x[order[s]].astype(F32))
        grad = grad_hidden[span]
        shift_rows.append(jnp.sum(grad, axis=0, keepdims=True))
        scale_rows.append(jnp.sum(grad * normed, axis=0, keepdims=True))
        made.append(r.grad_mixed[span] + norm_back(normed, inverse, grad * (1.0 + mod(1, s))))
    r.grad_mixed[seqs[0]] = jnp.where(swapped, made[1], made[0])
    r.grad_mixed[seqs[1]] = jnp.where(swapped, made[0], made[1])
    last.append(local(r.grad_mixed.reshape(2, f, width), r.grad_inputs, r.in_sems.at[3]))
    bias = jnp.sum(r.grad_qkv[...].astype(F32), axis=0, keepdims=True)
    bias_rows = [bias[:, i * width : (i + 1) * width] for i in range(3)]
    kept = [r.stats[i : i + 1] for i in range(r.stats.shape[0])]
    pairs_a = [jnp.concatenate(shift_rows, axis=0), jnp.concatenate(scale_rows, axis=0)]
    for i in range(4):
        grad_act = add_strip(grad_act, i, pairs_a[i // 2])
    shown_rows = jnp.where(me == 0, r.acts[...].astype(F32), 0.0)
    time_rows = [shown_rows[0:1], shown_rows[1:2], grad_act[0:1], grad_act[1:2]]
    r.small[...] = jnp.zeros_like(r.small)
    for i, row in enumerate(shift_rows + scale_rows + kept[:8] + bias_rows + kept[8:] + time_rows):
        for c in range(width // LANES):
            r.small[i, c : c + 1] = row[:, c * LANES : (c + 1) * LANES]

    per = r.small.shape[0] // n
    copies = []
    for step, device in enumerate(along):
        src = r.small.at[pl.ds(device[1] * per, per)]
        copies.append(push(src, r.small_in.at[step], r.small_one, (step,), device))
    for copy in swap_hidden:
        copy.wait()

    def start_piece(i):
        for slot in range(3):
            swaps[3 * i + slot].wait()
        both = r.rows[:, :, i * chunk_two : (i + 1) * chunk_two].reshape(4 * tokens, chunk_two)
        made = dot(r.both_hidden[...], both).astype(BF16)
        r.qkv_sum[i] = made.reshape(n, n_rows, chunk_two)
        start_stage(("qkv", i), 0)

    def gather_small():
        total = r.small[pl.ds(me * per, per)]
        for step in range(n - 1):
            copies[step].wait()
            total = total + r.small_in[step]
        r.mine[...] = total
        own_slice = r.small_all.at[b, pl.ds(me * per, per)]
        own_slice[...] = total
        return [push(r.mine, own_slice, r.small_two, (step,), device) for step, device in enumerate(along)]

    def share_small():
        for copy in spread:
            copy.wait()
        shared = [push(r.small_all.at[b], r.small_all.at[b], r.small_three, (i,), device) for i, device in enumerate(across)]
        shown = r.time_embed[...].astype(F32)
        sigmoid = 1.0 / (1.0 + jnp.exp(-shown))
        slope = sigmoid * (1.0 + shown * (1.0 - sigmoid))
        row = 19 + layers
        for c in range(width // LANES):
            lanes = slice(c * LANES, (c + 1) * LANES)
            one, two = r.small_all[b, row, c : c + 1], r.small_all[b, row + 1, c : c + 1]
            upper, lower = jnp.where(swapped, two, one), jnp.where(swapped, one, two)
            r.grad_time[:, lanes] = jnp.concatenate([upper, lower], axis=0) * slope[:, lanes]
        return shared

    queue = [("qkv", i) for i in range(pieces)]
    start_piece(0)
    advance("down")
    advance(0)
    start_piece(1)
    advance(1)
    advance(0)
    advance("down")
    start_piece(2)
    advance(2)
    advance(queue[0])
    for k in range(3, pieces):
        start_piece(k)
    spread = gather_small()
    advance(1)
    advance(0)
    advance(queue[1])
    advance(queue[0])
    advance(2)
    advance(1)
    advance(queue[2])
    shared = share_small()
    advance(queue[1])
    advance(2)
    advance(queue[0])
    advance(queue[2])
    finish_all("down")
    finish_all(0)
    finish_all(1)
    advance(queue[1])
    finish_all(2)
    finish_all(queue[0])

    advance(queue[2])
    for k in queue[1:]:
        finish_all(k)
    for copy in shared:
        copy.wait()
    last.append(local(r.small_all, r.small_out, r.out_sems.at[len(rooms)]))
    for i, (k, copies) in enumerate(closing.items()):
        for copy in copies:
            copy.wait()
        start, size = (0, width) if k == "down" else (base_one + k * chunk, chunk) if k in range(chunks) else (0, 0)
        if k == queue[-1]:
            start, size = base_one + chunks * chunk, 6 * cols
        if size:
            region = slice(start, start + size)
            last.append(local(r.totals.at[:, :, region], r.totals_out.at[:, :, region], r.out_sems.at[i]))
    for copy in last:
        copy.wait()


def layer(plan, sizes, batch, operands, collective_id):
    heads, chunk, chunk_two, block = sizes
    n, g, f, cols, width = plan.count, plan.groups, plan.frames, plan.cols, plan.width
    hidden = operands["w_up_hbm"].shape[1]
    tokens, rows, layers, units = 2 * f, width // n, hidden // width, cols // LANES
    wide = f * (LANES // (width // heads))
    chunks, pieces = (width + hidden) // 2 // chunk, 3 * cols // chunk_two
    small_rows = -(-(21 + layers) // n) * n
    per, tile = small_rows // n, (width // LANES, LANES)
    vmem, smem = pl.BlockSpec(memory_space=pltpu.VMEM), pl.BlockSpec(memory_space=pltpu.SMEM)

    def sems(*shape):
        return pltpu.SemaphoreType.DMA(shape)

    def low(*shape):
        return pltpu.VMEM(shape, BF16)

    def high(*shape):
        return pltpu.VMEM(shape, F32)

    outs = dict(
        output=((2, f, width), F32),
        grad_inputs=((2, f, width), F32),
        grad_time=((2, width), F32),
        totals_out=((2, rows, 4 * width), BF16),
        small_out=((batch, small_rows) + tile, F32),
    )
    scratch = dict(
        totals=low(2, rows, 4 * width),
        small_all=high(batch, small_rows, *tile),
        out_sems=sems(chunks + 2 + 3 * cols // chunk_two),
        x=low(2, f, width),
        ct=low(2, f, width),
        w_mod=low(2, width, width // 2),
        w_out=low(width, width),
        w_up=low(width, hidden),
        w_down=low(hidden, width),
        acts=low(2, width),
        cos=high(f, LANES),
        sin=high(f, LANES),
        b_row=high(1, 3 * width),
        mods=high(2, 6 * width),
        rows=low(g, tokens, 3 * cols),
        both_hidden=low(width, 4 * tokens),
        attn=low(tokens, width),
        q_buf=low(g, tokens, cols),
        kv_buf=low(n, f, 2 * cols),
        short_buf=low(plan.short_blocks, plan.short_rows, 2 * cols),
        lse=high(g, 2 * units, wide),
        o_buf=low(g, tokens, cols),
        turned=low(cols, plan.total),
        short_turned=low(cols, plan.short),
        top_acc=high(g * units, 1, wide),
        total_acc=high(g * units, 1, wide),
        o_acc=high(g * units, LANES, wide),
        mixed=high(tokens, width),
        branch_a=high(tokens, width),
        hidden_f=low(tokens, width),
        grad_ff=low(tokens, width),
        grad_pre=low(tokens, hidden),
        grad_br=low(tokens, width),
        attn_t=low(width, 2 * tokens),
        hid_t=low(width, 2 * tokens),
        act_own=low(n, rows, 4 * tokens),
        act_send=low(n, rows, tokens),
        all_ff=low(4, tokens, width // 2),
        both_pre=low(2, tokens, hidden // 2),
        both_br=low(2, tokens, width // 2),
        branch_f=high(tokens, width),
        grad_hid=high(tokens, width),
        grad_mixed=high(tokens, width),
        stats=high(10 + layers, width),
        parts=low(n, rows, chunks * chunk),
        x_buf=low(chunks, n, rows, chunk // 2),
        down_sum=low(n, rows, width // 2),
        grads=low(tokens, width),
        g_buf=low(g, tokens, cols),
        dq_acc=high(g, f, cols),
        dlong=high(2, plan.largest, cols),
        dsmall=high(2, plan.short, cols),
        dq_out=low(tokens, width),
        dkv_out=low(2, plan.splits, f, width),
        dshort_out=low(2, plan.short_rows, width),
        dshort_part=low(plan.short_blocks, plan.splits - 1, 2, plan.short_rows, cols),
        dshort_buf=low(plan.short_blocks, 2, plan.short_rows, cols),
        grad_qkv=low(tokens, 3 * width),
        qkv_sum=low(pieces, n, rows, chunk_two),
        small=high(small_rows, *tile),
        small_in=high(n - 1, per, *tile),
        mine=high(per, *tile),
        in_sems=sems(5),
        m_sems=sems(4),
        q_sems=sems(2, g - 1),
        k_sems=sems(2, n - 1),
        s_sems=sems(2, plan.short_blocks, g + plan.splits - 2),
        o_sems=sems(2, g - 1),
        h_sems=sems(2, 3),
        e_sems=sems(2, 5),
        ff_sems=sems(2, 2),
        act_sems=sems(2, 3, hidden // block),
        bg_sems=sems(2, g - 1),
        bq_sems=sems(2, g - 1),
        bk_sems=sems(2, 2, units, n),
        bs_sems=sems(2, g - 1),
        bp_sems=sems(2, plan.short_blocks, plan.splits - 1),
        x_sems=sems(2, chunks),
        blk_sems=sems(2, chunks + 1 + pieces, n.bit_length() - 1),
        g_sems=sems(2, 3, pieces),
        ax_sems=sems(2, chunks + 1 + pieces),
        ac_sems=sems(2, 2 * (chunks + 1 + pieces)),
        small_one=sems(2, n - 1),
        small_two=sems(2, n - 1),
        small_three=sems(2, batch - 1),
    )
    for t in range(n.bit_length() - 1):
        scratch["came_one_%d" % t] = low(chunks, n >> (t + 1), rows, chunk // 2)
        scratch["came_down_%d" % t] = low(n >> (t + 1), rows, width // 2)
        scratch["came_qkv_%d" % t] = low(pieces, n >> (t + 1), rows, chunk_two)
    specs = [smem if k == "lengths" else in_hbm() if k.endswith("_hbm") else vmem for k in operands]
    names = tuple(operands) + tuple(outs) + tuple(scratch)
    return pl.pallas_call(
        partial(layer_kernel, plan, (heads, chunk, chunk_two, block, batch), names),
        in_specs=specs,
        out_specs=[vmem if k == "grad_time" else in_hbm() for k in outs],
        out_shape=[jax.ShapeDtypeStruct(*shape) for shape in outs.values()],
        scratch_shapes=list(scratch.values()),
        compiler_params=pltpu.CompilerParams(
            collective_id=collective_id, has_side_effects=True, vmem_limit_bytes=63 * MIB
        ),
        name="layer",
    )(*operands.values())


def finish_kernel(count, sizes, aligned, names, *refs):
    r = SimpleNamespace(**dict(zip(names, refs)))
    batch, width, layers = sizes
    rows = width // count
    me = lax.axis_index("blk")
    half = width // 2
    passed = [
        local(r.totals_hbm, r.totals, r.sems.at[0]),
        local(r.small_hbm, r.small, r.sems.at[1]),
        local(r.output_hbm, r.output_made, r.sems.at[2]),
        local(r.grad_inputs_hbm, r.grad_inputs_made, r.sems.at[3]),
        local(r.grad_time_hbm, r.grad_time_made, r.sems.at[4]),
    ]
    passed[1].wait()
    for u in range(2 * batch):
        b, s = u // 2, u % 2
        line = r.small[b, 15 + 2 + layers + s, pl.ds(me * rows // LANES, 1)]
        if rows < LANES:
            line = pltpu.roll(line, LANES - lax.rem(me, LANES // rows) * rows, 1)
        r.times[u : u + 1] = line
        for p in range(6):
            for c in range(width // LANES):
                start = p * width + c * LANES
                r.mods[u : u + 1, start : start + LANES] = r.small[b, 2 * p + s, c : c + 1]
    times, mods = r.times[:, :rows].astype(BF16), r.mods[...].astype(BF16)
    for i in range(2):
        span = slice(i * 3 * width, (i + 1) * 3 * width)
        r.w_mod_made[:, span] = dot_frames(times, mods[:, span])
        passed.append(local(r.w_mod_made.at[:, span], r.w_mod.at[:, span], r.sems.at[9 + i]))
    passed[0].wait()
    for core in range(2):
        for i in range(layers):
            made = r.totals[core, :, i * half : (i + 1) * half].astype(F32)
            r.down_made[i * rows : (i + 1) * rows, core * half : (core + 1) * half] = made
    passed.append(local(r.down_made, r.down, r.sems.at[5]))
    for core in range(2):
        start = layers * half
        made = r.totals[core, :, start : start + layers * half].astype(F32)
        r.up_made[:, core * layers * half : (core + 1) * layers * half] = made
    passed.append(local(r.up_made, r.up, r.sems.at[6]))
    for i, k in enumerate(("output", "grad_inputs", "grad_time")):
        passed[2 + i].wait()
        passed[2 + i] = local(getattr(r, k + "_made"), getattr(r, k), r.sems.at[2 + i])
    for core in range(2):
        start = 2 * layers * half
        r.out_made[:, core * half : (core + 1) * half] = r.totals[core, :, start : start + half].astype(F32)
        made = r.totals[core, :, start + half : start + 4 * half].astype(F32)
        r.qkv_made[:, core * 3 * half : (core + 1) * 3 * half] = made
    passed.append(local(r.out_made, r.out, r.sems.at[7]))
    passed.append(local(r.qkv_made, r.qkv, r.sems.at[8]))
    if aligned:
        tiles = width // LANES

        def own_lines(first, length, stride):
            lines = []
            for i in range(length // count // LANES):
                at = me * (length // count // LANES) + i
                total = jnp.zeros((1, LANES), F32)
                for b in range(batch):
                    for s in range(stride):
                        total = total + r.small[b, first + at // tiles * stride + s, pl.ds(lax.rem(at, tiles), 1)]
                lines.append(total)
            return lines

        firsts = [(0, 6, 2), (12, 3, 1), (15, 1, 1), (16, layers, 1), (16 + layers, 1, 1)]
        for which, (first, many, stride) in enumerate(firsts):
            ref = getattr(r, "vector%d" % which)
            for i, line in enumerate(own_lines(first, many * width, stride)):
                ref[i * LANES : (i + 1) * LANES] = line[0]
    for copy in passed[2:]:
        copy.wait()


def finish(count, output, grad_inputs, grad_time, totals, small, layers):
    batch, width = small.shape[0], output.shape[2]
    rows = width // count
    aligned = rows % LANES == 0
    operands = dict(
        output_hbm=output, grad_inputs_hbm=grad_inputs, grad_time_hbm=grad_time, totals_hbm=totals, small_hbm=small
    )
    shapes = dict(
        down=(layers * rows, width),
        up=(rows, layers * width),
        out=(rows, width),
        qkv=(rows, 3 * width),
        w_mod=(rows, 6 * width),
    )
    outs = dict(output=output.shape, grad_inputs=output.shape, grad_time=grad_time.shape, **shapes)
    vectors = {}
    if aligned:
        vectors = {"vector%d" % i: (many * rows,) for i, many in enumerate((6, 3, 1, layers, 1))}
    scratch = {k + "_made": pltpu.VMEM(v, F32) for k, v in outs.items()}
    scratch.update(
        totals=pltpu.VMEM(totals.shape, BF16),
        small=pltpu.VMEM(small.shape, F32),
        times=pltpu.VMEM((2 * batch, LANES), F32),
        mods=pltpu.VMEM((2 * batch, 6 * width), F32),
        sems=pltpu.SemaphoreType.DMA((11,)),
    )
    names = tuple(operands) + tuple(outs) + tuple(vectors) + tuple(scratch)
    made = pl.pallas_call(
        partial(finish_kernel, count, (batch, width, layers), aligned, names),
        in_specs=[in_hbm()] * len(operands),
        out_specs=[in_hbm()] * len(outs) + [pl.BlockSpec(memory_space=pltpu.VMEM)] * len(vectors),
        out_shape=[jax.ShapeDtypeStruct(v, F32) for v in (outs | vectors).values()],
        scratch_shapes=list(scratch.values()),
        compiler_params=pltpu.CompilerParams(vmem_limit_bytes=62 * MIB),
        name="finish",
    )(*operands.values())
    if not aligned:
        me = lax.axis_index("blk")
        flat = jnp.sum(small.reshape(batch, -1, width), axis=0)
        mods = flat[:12].reshape(6, 2, width).sum(axis=1)
        ends = [12, 15, 16, 16 + layers, 17 + layers]
        rest = [mods] + [flat[lo:hi] for lo, hi in zip(ends[:-1], ends[1:])]
        made = list(made) + [
            lax.dynamic_index_in_dim(v.reshape(count, -1), me, 0, keepdims=False) for v in rest
        ]
    return made


def on_device(
    inputs,
    time_embed,
    lengths,
    cotangent,
    w_mod,
    b_mod,
    w_qkv,
    b_qkv,
    w_out,
    b_out,
    w_up,
    b_up,
    w_down,
    b_down,
):
    _, frames, width = inputs.shape
    count, batch = lax.axis_size("blk"), lax.axis_size("batch")
    plan = Plan(count, frames, width)
    operands = dict(
        lengths=lengths,
        time_embed=time_embed,
        b_mod=b_mod,
        b_qkv=b_qkv,
        b_out=b_out,
        b_up=b_up,
        b_down=b_down,
        x_hbm=inputs,
        ct_hbm=cotangent,
        w_mod_hbm=w_mod,
        w_qkv_hbm=w_qkv,
        w_out_hbm=w_out,
        w_up_hbm=w_up,
        w_down_hbm=w_down,
    )
    made = layer(plan, (HEADS, 512, 256, 512), batch, operands, 0)
    output, grad_inputs, grad_time, down, up, out, qkv, grad_w_mod, *vectors = finish(
        count, *made, w_up.shape[1] // width
    )
    return (
        output,
        grad_inputs,
        grad_time,
        grad_w_mod,
        vectors[0],
        qkv,
        vectors[1],
        out,
        vectors[2],
        up,
        vectors[3],
        down,
        vectors[4],
    )


def solution(mesh):
    frame_spec, weight_spec = P("batch", "blk", None), P("blk", None)
    return jax.shard_map(
        on_device,
        mesh=mesh,
        in_specs=(frame_spec, P("batch", None), P("batch"), frame_spec) + (P(),) * 10,
        out_specs=(frame_spec, frame_spec, P("batch", None)) + (weight_spec, P("blk")) * 5,
        check_vma=False,
    )
```
